32 devices in a mesh: fsdp: 4 (over z), ctx: 2 (over x), tp: 4 (over y, core).
Axes of the slice: x: 2, y: 2, z: 4, core: 2. Of those that a mesh axis runs over, the one named last changes fastest.
Arguments:
- resid_in: float32 [4, 2048, 1024], P('fsdp', 'ctx'), may hold values from -6 to 6
- segment_ids: int32 [4, 2048], P('fsdp'), may hold values from 0 to 5, never falling along the last dimension, each value on 1 to 768 neighbouring positions
- cotangent: float32 [4, 2048, 1024], P('fsdp', 'ctx'), may hold values from -6 to 6
- w_factor_a: float32 [1, 1024, 160], P(None, ('fsdp', 'ctx'), 'tp'), may hold values from -0.5 to 0.5
- w_factor_b: float32 [1, 1024, 640], P(None, ('fsdp', 'ctx', 'tp')), may hold values from -0.1875 to 0.1875
- w_out: float32 [1, 1024, 1024], P(None, 'tp', ('fsdp', 'ctx')), may hold values from -0.375 to 0.375
- w_gate_up: float32 [1, 2, 1024, 2816], P(None, None, ('fsdp', 'ctx'), 'tp'), may hold values from -0.1875 to 0.1875
- w_down: float32 [1, 2816, 1024], P(None, 'tp', ('fsdp', 'ctx')), may hold values from -0.109375 to 0.109375
- attn_gains: float32 [1, 1024], P(None, ('fsdp', 'ctx', 'tp')), may hold values from 0.25 to 1.75
- ffn_gains: float32 [1, 1024], P(None, ('fsdp', 'ctx', 'tp')), may hold values from 0.25 to 1.75
Outputs:
- block_out: float32 [4, 2048, 1024], P('fsdp', 'ctx')
- resid_grad: float32 [4, 2048, 1024], P('fsdp', 'ctx')
- grad_factor_a: float32 [1, 1024, 160], P(None, ('fsdp', 'ctx'), 'tp')
- grad_factor_b: float32 [1, 1024, 640], P(None, ('fsdp', 'ctx', 'tp'))
- grad_out: float32 [1, 1024, 1024], P(None, 'tp', ('fsdp', 'ctx'))
- grad_gate_up: float32 [1, 2, 1024, 2816], P(None, None, ('fsdp', 'ctx'), 'tp')
- grad_down: float32 [1, 2816, 1024], P(None, 'tp', ('fsdp', 'ctx'))
- grad_attn_gains: float32 [1, 1024], P(None, ('fsdp', 'ctx', 'tp'))
- grad_ffn_gains: float32 [1, 1024], P(None, ('fsdp', 'ctx', 'tp'))
The draws below stay inside these ranges and needn't reach their ends.
Inputs may be any that keep to these rules, and one draw needn't show every extreme that they name: `segment_ids`: along each row the ids never fall and run through all 6 documents; each document holds 1 to 768 tokens.
All inputs are finite; a program needn't handle non-finite values.
Results may differ from the reference program's by a relative error of at most 0.024.
The reference program's roundings to bfloat16 on the way count: a program that leaves them out, or rounds other values in their place, can miss the bound.
Values may be sent and summed in bfloat16 or wider, within the bound.
No kernel may reach another device: no remote copies, remote signals or barrier semaphores. Data moves between devices by JAX's collectives and lax.ppermute only.
A program may use at most 192 MiB of HBM per device.

```python
import math
import jax
import jax.numpy as jnp
import numpy as np
from jax import lax

D = 1024
HEADS = 16
HEAD_DIM = 64
RANK_Q = 6
RANK_KV = 2
FF = 2816
LAYERS = 1
DOCS = 6
RANKS = 10
SEQS = 4
LEN = 2048
MOST_DOC = 768
N_TP = 4


def level_of(own_key, extent, split, smallest, top_value):
    def one(position, blocks):
        heights = jax.random.uniform(jax.random.fold_in(jax.random.fold_in(own_key, 6), position), (blocks,), jnp.float32, smallest / len(split), top_value / len(split))
        return jnp.repeat(jnp.exp(heights), extent[position] // blocks).reshape((-1,) + (1,) * (len(extent) - position - 1))

    gain = one(*split[0])
    for cut in split[1:]:
        gain = gain * one(*cut)
    return gain


def split_up(amount, total, limit, lean):
    weights = [(1 << 20) // math.isqrt(grade ** lean) + 1 for grade in range(2, amount + 1)]
    spare, counts = total - limit - (amount - 1), [1] * (amount - 1)
    while spare > 0:
        candidates = [i for i in range(amount - 1) if counts[i] < limit]
        mass, left = sum([weights[i] for i in candidates]), spare
        for i in candidates:
            addition = min(limit - counts[i], max(1, left * weights[i] // mass), spare)
            counts[i] = counts[i] + addition
            spare = spare - addition
    return np.array([limit] + counts)


def ragged_sizes(own_key, amount, total, bound, skew):
    if amount == 2:
        one = jax.random.randint(own_key, (), max(1, total - bound), min(bound, total - 1) + 1)
        return jnp.stack([one, total - one])
    lengths = jnp.asarray(split_up(amount, total, bound, skew), jnp.int32)
    pairs = (amount - 1) // 2
    giver, taker = lengths[1:1 + 2 * pairs:2], lengths[2:2 + 2 * pairs:2]
    margin = jnp.minimum(giver - 1, bound - taker)
    shifted = jax.random.randint(jax.random.fold_in(own_key, 1), (pairs,), 0, 1 << 20) % (margin + 1)
    lengths = lengths.at[1:1 + 2 * pairs:2].set(giver - shifted).at[2:2 + 2 * pairs:2].set(taker + shifted)
    return lengths[jax.random.permutation(jax.random.fold_in(own_key, 2), amount)]


def centred(own_key, extent, deviation, reach, shards=(), held_as=jnp.bfloat16):
    values = deviation * jax.random.normal(own_key, extent, jnp.float32)
    if shards:
        values = values * level_of(own_key, extent, shards, -0.22, 0.18)
    return jnp.clip(values, -reach, reach).astype(held_as)


def setup_inputs(seed: int = 0) -> dict:
    arg_keys = jax.random.split(jax.random.key(seed), 11)
    resid_in = centred(arg_keys[0], (SEQS, LEN, D), 1.0, 6.0, ((0, 4), (1, 2)), jnp.float32)
    segment_ids = jax.vmap(lambda own: jnp.searchsorted(jnp.cumsum(ragged_sizes(own, DOCS, LEN, MOST_DOC, 1)), jnp.arange(LEN), side="right"))(jax.random.split(arg_keys[1], SEQS)).reshape((SEQS, LEN)).astype(jnp.int32)
    cotangent = centred(arg_keys[2], (SEQS, LEN, D), 1.0, 6.0, ((0, 4), (1, 2)), jnp.float32)
    w_factor_a = centred(arg_keys[3], (LAYERS, D, HEADS * RANKS), (D // 8) ** -0.5, 0.5, ((1, 8), (2, 4)), jnp.float32)
    w_factor_b = centred(arg_keys[4], (LAYERS, D, RANKS * HEAD_DIM), D ** -0.5, 0.1875, ((1, 32),), jnp.float32)
    w_out = centred(arg_keys[5], (LAYERS, HEADS * HEAD_DIM, D), (D // 4) ** -0.5, 0.375, ((1, 4), (2, 8)), jnp.float32)
    w_gate_up = centred(arg_keys[6], (LAYERS, 2, D, FF), D ** -0.5, 0.1875, ((2, 8), (3, 4)), jnp.float32)
    w_down = centred(arg_keys[7], (LAYERS, FF, D), FF ** -0.5, 0.109375, ((1, 4), (2, 8)), jnp.float32)
    attn_gains = jnp.clip(1.0 + 0.15 * jax.random.normal(arg_keys[8], (LAYERS, D), jnp.float32), 0.25, 1.75)
    ffn_gains = jnp.clip(1.0 + 0.15 * jax.random.normal(arg_keys[9], (LAYERS, D), jnp.float32), 0.25, 1.75)
    return {"resid_in": resid_in, "segment_ids": segment_ids, "cotangent": cotangent, "w_factor_a": w_factor_a, "w_factor_b": w_factor_b, "w_out": w_out, "w_gate_up": w_gate_up, "w_down": w_down, "attn_gains": attn_gains, "ffn_gains": ffn_gains}


EPSILON = 1e-05
PRECISE = lax.Precision.HIGHEST

@jax.custom_vjp
def low(v):
    return lax.optimization_barrier(v.astype(jnp.bfloat16)).astype(jnp.float32)

@jax.custom_vjp
def low_back(v):
    return v

def low_keep(v):
    return (low(v), None)

def low_pass(kept, grad):
    return (grad,)

def back_keep(v):
    return (v, None)

def back_low(kept, grad):
    return (low(grad),)
low.defvjp(low_keep, low_pass)
low_back.defvjp(back_keep, back_low)

def doc_positions(segment_ids):
    length = segment_ids.shape[-1]
    token_index = jnp.broadcast_to(jnp.arange(length, dtype=jnp.int32), segment_ids.shape)
    changed = jnp.concatenate([jnp.ones(segment_ids.shape[:-1] + (1,), dtype=bool), segment_ids[..., 1:] != segment_ids[..., :-1]], axis=-1)
    doc_start = lax.cummax(jnp.where(changed, token_index, 0).astype(jnp.int32), axis=segment_ids.ndim - 1)
    return (token_index - doc_start).astype(jnp.float32)

def rotate(field_value, positions, direction):
    half_width = field_value.shape[-1] // 2
    frequency = 10000.0 ** (-2.0 * jnp.arange(half_width, dtype=jnp.float32) / field_value.shape[-1])
    angles = positions[..., None, None] * frequency
    cosine = jnp.cos(angles)
    sine_part = direction * jnp.sin(angles)
    lower_half = field_value[..., :half_width]
    upper_half = field_value[..., half_width:]
    return jnp.concatenate([lower_half * cosine - upper_half * sine_part, lower_half * sine_part + upper_half * cosine], axis=-1)

def inverse_rms(values):
    return lax.rsqrt(lax.optimization_barrier(jnp.mean(values * values, axis=-1, keepdims=True)) + EPSILON)

def matmul(left, right):
    return jnp.dot(left, right, precision=PRECISE, preferred_element_type=jnp.float32)

def attend_one(packed):
    query, key_rows, value_rows, seg_row = packed
    length = query.shape[0]
    token_index = jnp.arange(length, dtype=jnp.int32)
    allowed = (token_index[None, :] <= token_index[:, None]) & (seg_row[None, :] == seg_row[:, None])
    scores = low_back(jnp.einsum('qhd,khd->hqk', query, key_rows, precision=PRECISE) / math.sqrt(HEAD_DIM))
    attn_probs = low(jax.nn.softmax(jnp.where(allowed[None], scores, -1e+30), axis=-1))
    attn_mixed = jnp.einsum('hqk,khd->qhd', attn_probs, value_rows, precision=PRECISE)
    return low_back(low(attn_mixed))

def layer_forward(resid, seg_ids, positions, weight_a, weight_b, weight_o, weight_gu, weight_d, gain_attn, gain_ffn):
    seq_count, length, model_width = resid.shape
    row_count = seq_count * length
    flat_resid = resid.reshape(row_count, model_width)
    normed = low(flat_resid * inverse_rms(flat_resid) * low(gain_attn))
    a_raw = low_back(matmul(normed, low(weight_a))).reshape(seq_count, length, N_TP, HEADS // N_TP, RANKS)
    b_raw = matmul(normed, low(weight_b)).reshape(seq_count, length, RANKS, HEAD_DIM)
    query_parts = []
    key_parts = []
    value_parts = []
    for shard_index in range(N_TP):
        b_copy = low_back(b_raw)
        a_shard = a_raw[:, :, shard_index]
        b_query = rotate(b_copy[:, :, :RANK_Q], positions, 1.0)
        b_key = low(rotate(b_copy[:, :, RANK_Q:RANK_Q + RANK_KV], positions, 1.0))
        b_value = low(b_copy[:, :, RANK_Q + RANK_KV:])
        a_key = low(a_shard[..., RANK_Q:RANK_Q + RANK_KV])
        a_value = low(a_shard[..., RANK_Q + RANK_KV:])
        query_parts.append(low(jnp.einsum('glhr,glrd->glhd', a_shard[..., :RANK_Q], b_query, precision=PRECISE) / RANK_Q))
        key_parts.append(low(jnp.einsum('glhr,glrd->glhd', a_key, b_key, precision=PRECISE) / RANK_KV))
        value_parts.append(low(jnp.einsum('glhr,glrd->glhd', a_value, b_value, precision=PRECISE) / RANK_KV))
    query = jnp.concatenate(query_parts, axis=2)
    key_rows = jnp.concatenate(key_parts, axis=2)
    value_rows = jnp.concatenate(value_parts, axis=2)
    attn_mixed = lax.map(jax.checkpoint(attend_one), (query, key_rows, value_rows, seg_ids))
    mid_resid = flat_resid + low_back(matmul(attn_mixed.reshape(row_count, HEADS * HEAD_DIM), low(weight_o)))
    normed_ffn = low(mid_resid * inverse_rms(mid_resid) * low(gain_ffn))
    gate_proj = low_back(matmul(normed_ffn, low(weight_gu[0])))
    up_proj = low_back(matmul(normed_ffn, low(weight_gu[1])))
    activated = low(jax.nn.silu(gate_proj) * up_proj)
    layer_out = mid_resid + low_back(matmul(activated, low(weight_d)))
    return layer_out.reshape(resid.shape)

def reference(resid_in, segment_ids, cotangent, w_factor_a, w_factor_b, w_out, w_gate_up, w_down, attn_gains, ffn_gains):
    group_size = math.gcd(SEQS, max(1, 4096 // LEN))
    group_count = SEQS // group_size
    positions = doc_positions(segment_ids)

    def regroup(array):
        return array.reshape((group_count, group_size) + array.shape[1:])

    def scan_step(totals, packed):
        resid_part, seg_part, pos_part, cot_part = packed

        def forward(resid_value, all_a, all_b, all_o, all_gu, all_d, all_ga, all_gf):
            for layer_index in range(LAYERS):
                resid_value = layer_forward(resid_value, seg_part, pos_part, all_a[layer_index], all_b[layer_index], all_o[layer_index], all_gu[layer_index], all_d[layer_index], all_ga[layer_index], all_gf[layer_index])
            return resid_value
        output, pullback = jax.vjp(forward, resid_part, w_factor_a, w_factor_b, w_out, w_gate_up, w_down, attn_gains, ffn_gains)
        gradients = pullback(cot_part)
        totals = tuple((total + partial_grad for total, partial_grad in zip(totals, gradients[1:])))
        return (totals, (output, gradients[0]))
    zero_start = tuple((jnp.zeros_like(weight) for weight in (w_factor_a, w_factor_b, w_out, w_gate_up, w_down, attn_gains, ffn_gains)))
    final, (outputs, resid_grads) = lax.scan(scan_step, zero_start, (regroup(resid_in), regroup(segment_ids), regroup(positions), regroup(cotangent)))
    return (outputs.reshape(resid_in.shape), resid_grads.reshape(resid_in.shape), final[0], final[1], final[2], final[3], final[4], final[5], final[6])
```

```python
import jax
import jax.numpy as jnp
from jax import lax
from jax.experimental import pallas as pl
from jax.experimental.pallas import tpu as pltpu
from jax.sharding import PartitionSpec as P

HEAD_DIM = 64
RANK_Q = 6
RANK_KV = 2
RANKS = 10
KV = 2 * RANK_KV
MOST_DOC = 768
EPSILON = 1e-05
LANES = 128
BF16 = jnp.bfloat16
F32 = jnp.float32
MASKED = -1e30


def inverse_rms(values):
    return lax.rsqrt(jnp.mean(values * values, axis=-1, keepdims=True) + EPSILON)


def norm_back(grad_value, values, inverse, gain):
    scaled = grad_value * gain
    normal = values * inverse
    return inverse * (scaled - normal * jnp.mean(scaled * normal, axis=-1, keepdims=True))


def dot(left, right, dims):
    return lax.dot_general(left, right, (dims, ((), ())), preferred_element_type=F32)


def shift(value, axes, size, step):
    return lax.ppermute(value, axes, [(i, (i + step) % size) for i in range(size)])


def swap(value, axis, size, bit):
    return lax.ppermute(value, axis, [(i, i ^ bit) for i in range(size)])


def gather_direct(value, axis, size):
    me = lax.axis_index(axis)
    parts = [(me, value)]
    for step in range(1, size):
        parts.append(((me - step) % size, shift(value, axis, size, step)))
    out = jnp.zeros((size,) + value.shape, value.dtype)
    for place, part in parts:
        out = lax.dynamic_update_slice(out, part[None], (place,) + (0,) * value.ndim)
    return out


def gather_pair(value, axis, size, bit):
    mine = (lax.axis_index(axis) // bit) % 2 == 0
    other = swap(value, axis, size, bit)
    return jnp.stack([jnp.where(mine, value, other), jnp.where(mine, other, value)])


def take(value, index):
    return lax.dynamic_index_in_dim(value, index, 0, keepdims=False)


def scatter_direct(value, axis, size):
    me = lax.axis_index(axis)
    got = [
        shift(take(value, (me + step) % size), axis, size, step) for step in range(1, size)
    ]
    total = take(value, me).astype(F32)
    for part in got:
        total = total + part.astype(F32)
    return total


def scatter_pair(value, axis, size, bit):
    mine = (lax.axis_index(axis) // bit) % 2
    got = swap(take(value, 1 - mine).astype(BF16), axis, size, bit)
    return take(value, mine).astype(F32) + got.astype(F32)


def attention_mask(first_ref, window, block):
    start = first_ref[...]
    place = lax.broadcasted_iota(jnp.int32, (window, block), 0)
    query_place = lax.broadcasted_iota(jnp.int32, (window, block), 1) + (window - block)
    return jnp.where((place >= start) & (place <= query_place), 0.0, MASKED)


def head_rows(wa_ref, wide_ref, head):
    factors = wa_ref[head].astype(F32)
    key_rows = (factors[0:1] * wide_ref[0] + factors[1:2] * wide_ref[1]) * (1.0 / RANK_KV)
    value_rows = (factors[2:3] * wide_ref[2] + factors[3:4] * wide_ref[3]) * (1.0 / RANK_KV)
    return factors, key_rows.astype(BF16), value_rows.astype(BF16)


def forward_kernel(
    first_ref, a_ref, bq_ref, wa_ref, wb_ref, mixed_ref, lse_ref, q_ref, bias_ref, wide_ref, s_ref
):
    heads = a_ref.shape[0]
    window, block = bias_ref.shape
    bias_ref[...] = attention_mask(first_ref, window, block)
    wide_ref[...] = wb_ref[...].astype(F32)
    spans = [pl.ds(j * block, block) for j in range(window // block)]

    def one_head(head, carry):
        factors = a_ref[head]
        query = factors[0:1] * bq_ref[0]
        for r in range(1, RANK_Q):
            query = query + factors[r : r + 1] * bq_ref[r]
        query = (query * (1.0 / RANK_Q)).astype(BF16) * jnp.asarray(HEAD_DIM**-0.5, BF16)
        q_ref[head] = query
        _, key_rows, value_rows = head_rows(wa_ref, wide_ref, head)
        top = jnp.full((1, block), MASKED, F32)
        for j, span in enumerate(spans):
            keys = key_rows[:, j * block : (j + 1) * block]
            scores = dot(keys, query, ((0,), (0,))) + bias_ref[span, :]
            s_ref[span, :] = scores
            top = jnp.maximum(top, jnp.max(scores, axis=0, keepdims=True))
        total = jnp.zeros((1, block), F32)
        for span in spans:
            weight = jnp.exp(s_ref[span, :] - top)
            s_ref[span, :] = weight
            total = total + jnp.sum(weight, axis=0, keepdims=True)
        lse_ref[head] = top + jnp.log(total)
        scale = 1.0 / total
        mixed = jnp.zeros((HEAD_DIM, block), F32)
        for j, span in enumerate(spans):
            probs = (s_ref[span, :] * scale).astype(BF16)
            mixed = mixed + dot(
                value_rows[:, j * block : (j + 1) * block], probs, ((1,), (0,))
            )
        mixed_ref[head] = mixed.astype(BF16)
        return carry

    lax.fori_loop(0, heads, one_head, 0)


def backward_kernel(
    first_ref,
    a_ref,
    bq_ref,
    wa_ref,
    wb_ref,
    lse_ref,
    q_ref,
    go_ref,
    ga_ref,
    gbq_ref,
    gwa_ref,
    gwb_ref,
    bias_ref,
    wide_ref,
    p_ref,
    dp_ref,
):
    heads = a_ref.shape[0]
    window, block = bias_ref.shape
    bias_ref[...] = attention_mask(first_ref, window, block)
    wide_ref[...] = wb_ref[...].astype(F32)
    gbq_ref[...] = jnp.zeros_like(gbq_ref)
    gwb_ref[...] = jnp.zeros_like(gwb_ref)
    count = window // block
    spans = [pl.ds(j * block, block) for j in range(count)]

    def one_head(head, carry):
        factors, key_rows, value_rows = head_rows(wa_ref, wide_ref, head)
        query = q_ref[head]
        grad_out = go_ref[head]
        lse = lse_ref[head]
        inner = jnp.zeros((1, block), F32)
        for j, span in enumerate(spans):
            cut = slice(j * block, (j + 1) * block)
            scores = dot(key_rows[:, cut], query, ((0,), (0,))) + bias_ref[span, :]
            probs = jnp.exp(scores - lse)
            grad_probs = dot(value_rows[:, cut], grad_out, ((0,), (0,)))
            p_ref[span, :] = probs
            dp_ref[span, :] = grad_probs
            inner = inner + jnp.sum(probs * grad_probs, axis=0, keepdims=True)
        grad_query = jnp.zeros((HEAD_DIM, block), F32)
        for j, span in enumerate(spans):
            cut = slice(j * block, (j + 1) * block)
            probs = p_ref[span, :]
            grad_scores = (probs * (dp_ref[span, :] - inner)).astype(BF16)
            grad_query = grad_query + dot(key_rows[:, cut], grad_scores, ((1,), (0,)))
            grad_keys = dot(query, grad_scores, ((1,), (1,))) * (1.0 / RANK_KV)
            grad_values = dot(grad_out, probs.astype(BF16), ((1,), (1,))) * (1.0 / RANK_KV)
            rows = []
            for r in range(KV):
                grad = grad_keys if r < RANK_KV else grad_values
                rows.append(jnp.sum(grad * wide_ref[r, :, span], axis=0, keepdims=True))
                gwb_ref[r, :, span] += factors[r : r + 1, cut] * grad
            gwa_ref[head, :, span] = jnp.concatenate(rows, axis=0)
        grad_query = grad_query * (HEAD_DIM**-0.5 / RANK_Q)
        own = a_ref[head]
        rows = []
        for r in range(RANK_Q):
            rows.append(jnp.sum(grad_query * bq_ref[r], axis=0, keepdims=True))
            gbq_ref[r] += own[r : r + 1] * grad_query
        ga_ref[head] = jnp.concatenate(rows, axis=0)
        return carry

    lax.fori_loop(0, heads, one_head, 0)


VMEM_LIMIT = 56 * 1024 * 1024


def whole_specs(count):
    return [pl.BlockSpec(memory_space=pltpu.VMEM)] * count


def attend_forward(first, a_rows, b_query, win_a, win_b):
    heads, _, block = a_rows.shape
    window = win_a.shape[-1]
    return pl.pallas_call(
        forward_kernel,
        out_shape=(
            jax.ShapeDtypeStruct((heads, HEAD_DIM, block), BF16),
            jax.ShapeDtypeStruct((heads, 1, block), F32),
            jax.ShapeDtypeStruct((heads, HEAD_DIM, block), BF16),
        ),
        in_specs=whole_specs(5),
        out_specs=tuple(whole_specs(3)),
        scratch_shapes=[
            pltpu.VMEM((window, block), F32),
            pltpu.VMEM((KV, HEAD_DIM, window), F32),
            pltpu.VMEM((window, block), F32),
        ],
        compiler_params=pltpu.CompilerParams(vmem_limit_bytes=VMEM_LIMIT),
        name="attend_forward",
    )(first, a_rows, b_query, win_a, win_b)


def attend_backward(first, a_rows, b_query, win_a, win_b, lse, query, grad_mixed):
    heads, _, block = a_rows.shape
    window = win_a.shape[-1]
    return pl.pallas_call(
        backward_kernel,
        out_shape=(
            jax.ShapeDtypeStruct((heads, RANK_Q, block), F32),
            jax.ShapeDtypeStruct((RANK_Q, HEAD_DIM, block), F32),
            jax.ShapeDtypeStruct((heads, KV, window), F32),
            jax.ShapeDtypeStruct((KV, HEAD_DIM, window), F32),
        ),
        in_specs=whole_specs(8),
        out_specs=tuple(whole_specs(4)),
        scratch_shapes=[
            pltpu.VMEM((window, block), F32),
            pltpu.VMEM((KV, HEAD_DIM, window), F32),
            pltpu.VMEM((window, block), F32),
            pltpu.VMEM((window, block), F32),
        ],
        compiler_params=pltpu.CompilerParams(vmem_limit_bytes=VMEM_LIMIT),
        name="attend_backward",
    )(first, a_rows, b_query, win_a, win_b, lse, query, grad_mixed)


def rotate(rows, cosine, sine):
    half = HEAD_DIM // 2
    lower, upper = rows[:, :half], rows[:, half:]
    return jnp.concatenate(
        [lower * cosine - upper * sine, lower * sine + upper * cosine], axis=1
    )


def make_shards(mesh):
    n_f, n_c, n_tp = mesh.shape["fsdp"], mesh.shape["ctx"], mesh.shape["tp"]
    n_hi, n_lo = 2, n_tp // 2

    def shards(
        resid_in,
        segment_ids,
        cotangent,
        w_factor_a,
        w_factor_b,
        w_out,
        w_gate_up,
        w_down,
        attn_gains,
        ffn_gains,
    ):
        seq_count, local_len, width = resid_in.shape
        assert seq_count == 1 and w_factor_a.shape[0] == 1 and n_lo == 2
        full_len = segment_ids.shape[1]
        block = local_len // n_tp
        extra = -(-(MOST_DOC - 1) // block)
        window = (extra + 1) * block
        a_cols = w_factor_a.shape[2]
        heads = n_tp * a_cols // RANKS
        b_cols = w_factor_b.shape[2]
        b_rows = w_factor_b.shape[1]
        b_parts = b_cols // LANES
        fc_cols = w_down.shape[2]
        hidden = w_down.shape[1]
        o_rows = w_out.shape[1]

        f_index, c_index, t_index = (
            lax.axis_index("fsdp"),
            lax.axis_index("ctx"),
            lax.axis_index("tp"),
        )
        hi, lo = t_index // 2, t_index % 2
        place = c_index * n_tp + t_index
        n_place = n_c * n_tp

        gains = jnp.concatenate([attn_gains, ffn_gains], axis=1).astype(BF16)
        gain_count = gains.shape[1]
        gain_rows = 16 * (-(-gain_count // (16 * LANES)))
        gains = jnp.pad(gains.reshape(-1), (0, gain_rows * LANES - gain_count))
        b_shard = w_factor_b[0].astype(BF16).reshape(b_rows, b_parts, LANES)
        a_shard = w_factor_a[0].astype(BF16).T
        pack = jnp.concatenate(
            [
                b_shard.transpose(1, 0, 2).reshape(-1, LANES),
                a_shard.reshape(-1, LANES),
                gains.reshape(-1, LANES),
            ],
            axis=0,
        )
        n_b = b_parts * b_rows
        n_a = a_cols * fc_cols // LANES
        pack = gather_direct(pack, "fsdp", n_f)
        after_pack = pack
        pack = gather_pair(pack, "ctx", n_c, 1)
        pack = gather_pair(pack, "tp", n_tp, 2)
        pack = gather_pair(pack, "tp", n_tp, 1)
        pack = pack.transpose(3, 2, 1, 0, 4, 5)
        weight_b = pack[:, :, :, :, :n_b].reshape(-1, b_parts, b_rows, LANES)
        weight_b = weight_b.transpose(0, 2, 1, 3).reshape(width, b_cols)
        weight_a = pack[:, :, :, :, n_b : n_b + n_a].reshape(n_f, n_c, n_tp, a_cols, fc_cols)
        weight_a = weight_a.transpose(2, 3, 0, 1, 4).reshape(n_tp * a_cols, width)
        gains_all = pack[:, :, :, :, n_b + n_a :].reshape(-1, gain_rows * LANES)[:, :gain_count]
        gains_all = gains_all.reshape(-1, 2, gain_count // 2).transpose(1, 0, 2)
        gains_all = gains_all.reshape(2, width).astype(F32)
        gain_attn, gain_ffn = gains_all[0:1], gains_all[1:2]

        big = jnp.concatenate(
            [
                w_gate_up[0, 0].astype(BF16).T,
                w_gate_up[0, 1].astype(BF16).T,
                w_down[0].astype(BF16),
                w_out[0].astype(BF16),
            ],
            axis=0,
        )
        big, _ = lax.optimization_barrier((big, after_pack))
        big = gather_direct(big, "fsdp", n_f)
        big = gather_pair(big, "ctx", n_c, 1)
        big = big.transpose(2, 1, 0, 3).reshape(-1, width)
        weight_g = big[:hidden]
        weight_u = big[hidden : 2 * hidden]
        weight_d = big[2 * hidden : 3 * hidden]
        weight_o = gather_pair(big[3 * hidden :], "tp", n_tp, 2)
        weight_o = gather_pair(weight_o, "tp", n_tp, 1)
        weight_o = weight_o.transpose(1, 0, 2, 3).reshape(n_tp * o_rows, width)

        seg_here = lax.dynamic_slice_in_dim(segment_ids[0], place * block, block, 0)
        first = jnp.sum((segment_ids[0][:, None] < seg_here[None, :]).astype(jnp.int32), axis=0)
        token = place * block + jnp.arange(block, dtype=jnp.int32)
        position = (token - first).astype(F32)
        first = (first - place * block + extra * block).reshape(1, block)
        frequency = 10000.0 ** (
            -2.0 * jnp.arange(HEAD_DIM // 2, dtype=F32) / HEAD_DIM
        )
        angles = frequency[:, None] * position[None, :]
        cosine, sine = jnp.cos(angles)[None], jnp.sin(angles)[None]

        stream = resid_in[0].reshape(n_tp, block, width)
        own = take(stream, t_index)
        inverse_attn = inverse_rms(own)
        normed = (own * inverse_attn * gain_attn).astype(BF16)
        a_rows = dot(weight_a, normed, ((1,), (1,))).reshape(heads, RANKS, block)
        b_raw = dot(weight_b, normed, ((0,), (1,))).reshape(RANKS, HEAD_DIM, block)
        b_rot = rotate(b_raw[: RANK_Q + RANK_KV], cosine, sine)
        b_query = b_rot[:RANK_Q]
        b_kv = jnp.concatenate([b_rot[RANK_Q:], b_raw[RANK_Q + RANK_KV :]], axis=0)
        payload = jnp.concatenate(
            [
                b_kv.reshape(KV * HEAD_DIM, block),
                a_rows[:, RANK_Q:].reshape(heads * KV, block),
            ],
            axis=0,
        ).astype(BF16)
        around = [
            lax.ppermute(
                payload, ("ctx", "tp"), [(i, i + step) for i in range(n_place - step)]
            )
            for step in range(extra, 0, -1)
        ]
        win = jnp.concatenate(around + [payload], axis=1)
        win_b = win[: KV * HEAD_DIM].reshape(KV, HEAD_DIM, window)
        win_a = win[KV * HEAD_DIM :].reshape(heads, KV, window)

        mixed, lse, query = attend_forward(first, a_rows, b_query, win_a, win_b)
        mixed = mixed.reshape(heads * HEAD_DIM, block)
        attn_out = dot(mixed, weight_o, ((0,), (0,)))
        mid = own + attn_out
        inverse_ffn = inverse_rms(mid)
        normed_ffn = (mid * inverse_ffn * gain_ffn).astype(BF16)

        near_rows = gather_pair(normed_ffn, "tp", n_tp, 1)
        far_rows = gather_pair(swap(normed_ffn, "tp", n_tp, 2), "tp", n_tp, 1)
        grad_all = cotangent[0].reshape(n_hi, n_lo * block, width)

        def half(rows, grad_rows):
            rows = rows.reshape(n_lo * block, width)
            gate = dot(rows, weight_g, ((1,), (1,)))
            up = dot(rows, weight_u, ((1,), (1,)))
            grad_act = dot(grad_rows, weight_d, ((1,), (1,)))
            squash = jax.nn.sigmoid(gate)
            act = (gate * squash * up).astype(BF16)
            grad_gate = (grad_act * up * squash * (1.0 + gate * (1.0 - squash))).astype(BF16)
            grad_up = (grad_act * gate * squash).astype(BF16)
            back = dot(grad_gate, weight_g, ((1,), (0,))) + dot(grad_up, weight_u, ((1,), (0,)))
            ahead = dot(act, weight_d, ((1,), (0,)))
            both = lambda v: v.reshape(n_lo, block, width)
            return rows, act, grad_gate, grad_up, both(back), both(ahead)

        grad_near = take(grad_all, hi).astype(BF16)
        grad_far = take(grad_all, 1 - hi).astype(BF16)
        near = half(near_rows, grad_near)
        far = half(far_rows, grad_far)
        back_far = scatter_pair(far[4], "tp", n_tp, 1).astype(BF16)
        back_far = swap(back_far, "tp", n_tp, 2)
        grad_normed_ffn = scatter_pair(near[4], "tp", n_tp, 1) + back_far.astype(F32)
        ahead_far = scatter_pair(far[5], "tp", n_tp, 1).astype(BF16)
        ahead_far = swap(ahead_far, "tp", n_tp, 2)
        ffn_out = scatter_pair(near[5], "tp", n_tp, 1) + ahead_far.astype(F32)

        def spread(value):
            beside = swap(value, "tp", n_tp, 1)
            across = swap(value, "tp", n_tp, 2)
            diagonal = swap(across, "tp", n_tp, 1)
            out = jnp.zeros((n_tp,) + value.shape, value.dtype)
            for bit, part in enumerate((value, beside, across, diagonal)):
                out = lax.dynamic_update_slice(out, part[None], (t_index ^ bit, 0, 0))
            return out.reshape(local_len, width).astype(F32)

        block_out = resid_in + spread((attn_out + ffn_out).astype(BF16))[None]

        def columns(value, which):
            value = value.reshape(value.shape[0], n_f, n_c, fc_cols)
            value = lax.dynamic_index_in_dim(value, which, 2, keepdims=False)
            return value.reshape(value.shape[0], n_f * fc_cols)

        rows_all = jnp.concatenate([near[0], far[0]], axis=0)
        act_all = jnp.concatenate([near[1], far[1]], axis=0)
        gate_all = jnp.concatenate([near[2], far[2]], axis=0)
        up_all = jnp.concatenate([near[3], far[3]], axis=0)
        cot_all = jnp.concatenate([grad_near, grad_far], axis=0)

        def big_grads(which):
            rows_cut = columns(rows_all, which)
            cot_cut = columns(cot_all, which)
            return jnp.concatenate(
                [
                    dot(gate_all, rows_cut, ((0,), (0,))),
                    dot(up_all, rows_cut, ((0,), (0,))),
                    dot(act_all, cot_cut, ((0,), (0,))),
                ],
                axis=0,
            )

        def over_fc(send, keep):
            total = keep + swap(send.astype(BF16), "ctx", n_c, 1).astype(F32)
            total = total.astype(BF16).reshape(-1, n_f, fc_cols).transpose(1, 0, 2)
            return scatter_direct(total, "fsdp", n_f)

        grad_big = over_fc(big_grads(1 - c_index), big_grads(c_index))
        grad_gate_w = grad_big[:hidden].T
        grad_up_w = grad_big[hidden : 2 * hidden].T
        grad_down_w = grad_big[2 * hidden :]

        own_cot = take(cotangent[0].reshape(n_tp, block, width), t_index)
        gain_grad_ffn = jnp.sum(grad_normed_ffn * mid * inverse_ffn, axis=0)
        delta_mid = norm_back(grad_normed_ffn, mid, inverse_ffn, gain_ffn)
        grad_attn = (own_cot + delta_mid).astype(BF16)
        grad_out = dot(mixed, grad_attn, ((1,), (0,))).reshape(n_hi, n_lo, o_rows, width)
        grad_out = scatter_pair(grad_out.transpose(1, 0, 2, 3), "tp", n_tp, 1)
        grad_out = scatter_pair(grad_out, "tp", n_tp, 2)
        grad_out = over_fc(columns(grad_out, 1 - c_index), columns(grad_out, c_index))

        grad_mixed = dot(weight_o, grad_attn, ((1,), (1,))).astype(BF16)
        ga_q, gb_q, gw_a, gw_b = attend_backward(
            first,
            a_rows,
            b_query,
            win_a,
            win_b,
            lse,
            query,
            grad_mixed.reshape(heads, HEAD_DIM, block),
        )
        gw = jnp.concatenate(
            [gw_b.reshape(KV * HEAD_DIM, window), gw_a.reshape(heads * KV, window)], axis=0
        )
        total = gw[:, extra * block :]
        for step in range(1, extra + 1):
            part = gw[:, (extra - step) * block : (extra - step + 1) * block].astype(BF16)
            part = lax.ppermute(
                part, ("ctx", "tp"), [(i + step, i) for i in range(n_place - step)]
            )
            total = total + part.astype(F32)
        gb_kv = total[: KV * HEAD_DIM].reshape(KV, HEAD_DIM, block)
        ga_kv = total[KV * HEAD_DIM :].reshape(heads, KV, block)
        grad_b = jnp.concatenate(
            [
                rotate(jnp.concatenate([gb_q, gb_kv[:RANK_KV]], axis=0), cosine, -sine),
                gb_kv[RANK_KV:],
            ],
            axis=0,
        )
        grad_b = grad_b.reshape(b_cols, block).astype(BF16)
        grad_a = jnp.concatenate([ga_q, ga_kv], axis=1).reshape(heads * RANKS, block).astype(BF16)
        grad_normed = dot(grad_a, weight_a, ((0,), (0,))) + dot(grad_b, weight_b, ((0,), (1,)))
        gain_grad_attn = jnp.sum(grad_normed * own * inverse_attn, axis=0)
        delta = delta_mid + norm_back(grad_normed, own, inverse_attn, gain_attn)
        resid_grad = cotangent + spread(delta.astype(BF16))[None]

        grad_wa = dot(grad_a, normed, ((1,), (0,))).astype(BF16)
        grad_wa = grad_wa.reshape(n_hi, n_lo, a_cols, n_f, n_c, fc_cols)
        grad_wa = grad_wa.transpose(1, 0, 4, 3, 2, 5).reshape(n_lo, n_hi, n_c, n_f, n_a, LANES)
        grad_wb = jnp.einsum(
            "pkt,td->pdk",
            grad_b.reshape(b_parts, LANES, block),
            normed,
            preferred_element_type=F32,
        ).astype(BF16)
        grad_wb = grad_wb.reshape(b_parts, n_f, n_c, n_hi, n_lo, b_rows, LANES)
        grad_wb = grad_wb.transpose(4, 3, 2, 1, 0, 5, 6)
        grad_wb = grad_wb.reshape(n_lo, n_hi, n_c, n_f, n_b, LANES)
        gain_grads = jnp.stack([gain_grad_attn, gain_grad_ffn]).astype(BF16)
        gain_grads = gain_grads.reshape(2, n_f, n_c, n_hi, n_lo, gain_count // 2)
        gain_grads = gain_grads.transpose(4, 3, 2, 1, 0, 5).reshape(
            n_lo, n_hi, n_c, n_f, gain_count
        )
        gain_grads = jnp.pad(
            gain_grads, [(0, 0)] * 4 + [(0, gain_rows * LANES - gain_count)]
        ).reshape(n_lo, n_hi, n_c, n_f, gain_rows, LANES)
        pack = jnp.concatenate([grad_wb, grad_wa, gain_grads], axis=4)
        pack = scatter_pair(pack, "tp", n_tp, 1)
        pack = scatter_pair(pack, "tp", n_tp, 2)
        pack = scatter_pair(pack, "ctx", n_c, 1).astype(BF16)
        pack = scatter_direct(pack, "fsdp", n_f)
        part_b = pack[:n_b].reshape(b_parts, b_rows, LANES).transpose(1, 0, 2)
        part_b = part_b.reshape(1, b_rows, b_cols)
        part_a = pack[n_b : n_b + n_a].reshape(a_cols, fc_cols).T[None]
        part_gain = pack[n_b + n_a :].reshape(-1)[:gain_count].reshape(2, 1, gain_count // 2)
        return (
            block_out,
            resid_grad,
            part_a,
            part_b,
            grad_out[None],
            jnp.stack([grad_gate_w, grad_up_w])[None],
            grad_down_w[None],
            part_gain[0],
            part_gain[1],
        )

    return shards


def solution(mesh):
    return jax.shard_map(
        make_shards(mesh),
        mesh=mesh,
        in_specs=(
            P("fsdp", "ctx", None),
            P("fsdp", None),
            P("fsdp", "ctx", None),
            P(None, ("fsdp", "ctx"), "tp"),
            P(None, ("fsdp", "ctx", "tp"), None),
            P(None, "tp", ("fsdp", "ctx")),
            P(None, None, ("fsdp", "ctx"), "tp"),
            P(None, "tp", ("fsdp", "ctx")),
            P(None, ("fsdp", "ctx", "tp")),
            P(None, ("fsdp", "ctx", "tp")),
        ),
        out_specs=(
            P("fsdp", "ctx", None),
            P("fsdp", "ctx", None),
            P(None, ("fsdp", "ctx"), "tp"),
            P(None, ("fsdp", "ctx", "tp"), None),
            P(None, "tp", ("fsdp", "ctx")),
            P(None, None, ("fsdp", "ctx"), "tp"),
            P(None, "tp", ("fsdp", "ctx")),
            P(None, ("fsdp", "ctx", "tp")),
            P(None, ("fsdp", "ctx", "tp")),
        ),
        check_vma=False,
    )
```

```python
import jax
import jax.numpy as jnp
from jax import lax
from jax.experimental import pallas as pl
from jax.experimental.pallas import tpu as pltpu
from jax.sharding import PartitionSpec as P

HEAD_DIM = 64
RANK_Q = 6
RANK_KV = 2
RANKS = 10
KV = 2 * RANK_KV
MOST_DOC = 768
EPSILON = 1e-05
LANES = 128
BF16 = jnp.bfloat16
F32 = jnp.float32
MASKED = -1e30


def inverse_rms(values):
    return lax.rsqrt(jnp.mean(values * values, axis=-1, keepdims=True) + EPSILON)


def norm_back(grad_value, values, inverse, gain):
    scaled = grad_value * gain
    normal = values * inverse
    return inverse * (scaled - normal * jnp.mean(scaled * normal, axis=-1, keepdims=True))


def dot(left, right, dims):
    return lax.dot_general(left, right, (dims, ((), ())), preferred_element_type=F32)


def shift(value, axes, size, step, label="shift"):
    with jax.named_scope(label):
        return lax.ppermute(value, axes, [(i, (i + step) % size) for i in range(size)])


def swap(value, axis, size, bit, label="swap"):
    with jax.named_scope(label):
        return lax.ppermute(value, axis, [(i, i ^ bit) for i in range(size)])


def gather_direct(value, axis, size):
    me = lax.axis_index(axis)
    parts = [(me, value)]
    for step in range(1, size):
        parts.append(((me - step) % size, shift(value, axis, size, step)))
    out = jnp.zeros((size,) + value.shape, value.dtype)
    for place, part in parts:
        out = lax.dynamic_update_slice(out, part[None], (place,) + (0,) * value.ndim)
    return out


def gather_pair(value, axis, size, bit):
    mine = (lax.axis_index(axis) // bit) % 2 == 0
    other = swap(value, axis, size, bit)
    return jnp.stack([jnp.where(mine, value, other), jnp.where(mine, other, value)])


def after(value, *others):
    return lax.optimization_barrier((value,) + others)[0]


def take(value, index):
    return lax.dynamic_index_in_dim(value, index, 0, keepdims=False)


def scatter_direct(value, axis, size):
    me = lax.axis_index(axis)
    got = [
        shift(take(value, (me + step) % size), axis, size, step) for step in range(1, size)
    ]
    total = take(value, me).astype(F32)
    for part in got:
        total = total + part.astype(F32)
    return total


def scatter_pair(value, axis, size, bit):
    mine = (lax.axis_index(axis) // bit) % 2
    got = swap(take(value, 1 - mine).astype(BF16), axis, size, bit)
    return take(value, mine).astype(F32) + got.astype(F32)


def attention_mask(first_ref, window, block):
    start = first_ref[...]
    place = lax.broadcasted_iota(jnp.int32, (window, block), 0)
    query_place = lax.broadcasted_iota(jnp.int32, (window, block), 1) + (window - block)
    return jnp.where((place >= start) & (place <= query_place), 0.0, MASKED)


def head_rows(wa_ref, wide_ref, head):
    factors = wa_ref[head].astype(F32)
    key_rows = (factors[0:1] * wide_ref[0] + factors[1:2] * wide_ref[1]) * (1.0 / RANK_KV)
    value_rows = (factors[2:3] * wide_ref[2] + factors[3:4] * wide_ref[3]) * (1.0 / RANK_KV)
    return factors, key_rows.astype(BF16), value_rows.astype(BF16)


def forward_kernel(
    first_ref, a_ref, bq_ref, wa_ref, wb_ref, mixed_ref, lse_ref, q_ref, bias_ref, wide_ref, s_ref
):
    heads = a_ref.shape[0]
    window, block = bias_ref.shape
    bias_ref[...] = attention_mask(first_ref, window, block)
    wide_ref[...] = wb_ref[...].astype(F32)
    spans = [pl.ds(j * block, block) for j in range(window // block)]

    def one_head(head, carry):
        factors = a_ref[head]
        query = factors[0:1] * bq_ref[0]
        for r in range(1, RANK_Q):
            query = query + factors[r : r + 1] * bq_ref[r]
        query = (query * (1.0 / RANK_Q)).astype(BF16) * jnp.asarray(HEAD_DIM**-0.5, BF16)
        q_ref[head] = query
        _, key_rows, value_rows = head_rows(wa_ref, wide_ref, head)
        top = jnp.full((1, block), MASKED, F32)
        for j, span in enumerate(spans):
            keys = key_rows[:, j * block : (j + 1) * block]
            scores = dot(keys, query, ((0,), (0,))) + bias_ref[span, :]
            s_ref[span, :] = scores
            top = jnp.maximum(top, jnp.max(scores, axis=0, keepdims=True))
        total = jnp.zeros((1, block), F32)
        for span in spans:
            weight = jnp.exp(s_ref[span, :] - top)
            s_ref[span, :] = weight
            total = total + jnp.sum(weight, axis=0, keepdims=True)
        lse_ref[head] = top + jnp.log(total)
        scale = 1.0 / total
        mixed = jnp.zeros((HEAD_DIM, block), F32)
        for j, span in enumerate(spans):
            probs = (s_ref[span, :] * scale).astype(BF16)
            mixed = mixed + dot(
                value_rows[:, j * block : (j + 1) * block], probs, ((1,), (0,))
            )
        mixed_ref[head] = mixed.astype(BF16)
        return carry

    lax.fori_loop(0, heads, one_head, 0)


def backward_kernel(
    first_ref,
    a_ref,
    bq_ref,
    wa_ref,
    wb_ref,
    lse_ref,
    q_ref,
    go_ref,
    ga_ref,
    gbq_ref,
    gwa_ref,
    gwb_ref,
    bias_ref,
    wide_ref,
    p_ref,
    dp_ref,
):
    heads = a_ref.shape[0]
    window, block = bias_ref.shape
    bias_ref[...] = attention_mask(first_ref, window, block)
    wide_ref[...] = wb_ref[...].astype(F32)
    gbq_ref[...] = jnp.zeros_like(gbq_ref)
    gwb_ref[...] = jnp.zeros_like(gwb_ref)
    count = window // block
    spans = [pl.ds(j * block, block) for j in range(count)]

    def one_head(head, carry):
        factors, key_rows, value_rows = head_rows(wa_ref, wide_ref, head)
        query = q_ref[head]
        grad_out = go_ref[head]
        lse = lse_ref[head]
        inner = jnp.zeros((1, block), F32)
        for j, span in enumerate(spans):
            cut = slice(j * block, (j + 1) * block)
            scores = dot(key_rows[:, cut], query, ((0,), (0,))) + bias_ref[span, :]
            probs = jnp.exp(scores - lse)
            grad_probs = dot(value_rows[:, cut], grad_out, ((0,), (0,)))
            p_ref[span, :] = probs
            dp_ref[span, :] = grad_probs
            inner = inner + jnp.sum(probs * grad_probs, axis=0, keepdims=True)
        grad_query = jnp.zeros((HEAD_DIM, block), F32)
        for j, span in enumerate(spans):
            cut = slice(j * block, (j + 1) * block)
            probs = p_ref[span, :]
            grad_scores = (probs * (dp_ref[span, :] - inner)).astype(BF16)
            grad_query = grad_query + dot(key_rows[:, cut], grad_scores, ((1,), (0,)))
            grad_keys = dot(query, grad_scores, ((1,), (1,))) * (1.0 / RANK_KV)
            grad_values = dot(grad_out, probs.astype(BF16), ((1,), (1,))) * (1.0 / RANK_KV)
            rows = []
            for r in range(KV):
                grad = grad_keys if r < RANK_KV else grad_values
                rows.append(jnp.sum(grad * wide_ref[r, :, span], axis=0, keepdims=True))
                gwb_ref[r, :, span] += factors[r : r + 1, cut] * grad
            gwa_ref[head, :, span] = jnp.concatenate(rows, axis=0)
        grad_query = grad_query * (HEAD_DIM**-0.5 / RANK_Q)
        own = a_ref[head]
        rows = []
        for r in range(RANK_Q):
            rows.append(jnp.sum(grad_query * bq_ref[r], axis=0, keepdims=True))
            gbq_ref[r] += own[r : r + 1] * grad_query
        ga_ref[head] = jnp.concatenate(rows, axis=0)
        return carry

    lax.fori_loop(0, heads, one_head, 0)


VMEM_LIMIT = 56 * 1024 * 1024


def whole_specs(count):
    return [pl.BlockSpec(memory_space=pltpu.VMEM)] * count


def attend_forward(first, a_rows, b_query, win_a, win_b):
    heads, _, block = a_rows.shape
    window = win_a.shape[-1]
    return pl.pallas_call(
        forward_kernel,
        out_shape=(
            jax.ShapeDtypeStruct((heads, HEAD_DIM, block), BF16),
            jax.ShapeDtypeStruct((heads, 1, block), F32),
            jax.ShapeDtypeStruct((heads, HEAD_DIM, block), BF16),
        ),
        in_specs=whole_specs(5),
        out_specs=tuple(whole_specs(3)),
        scratch_shapes=[
            pltpu.VMEM((window, block), F32),
            pltpu.VMEM((KV, HEAD_DIM, window), F32),
            pltpu.VMEM((window, block), F32),
        ],
        compiler_params=pltpu.CompilerParams(vmem_limit_bytes=VMEM_LIMIT),
        name="attend_forward",
    )(first, a_rows, b_query, win_a, win_b)


def attend_backward(first, a_rows, b_query, win_a, win_b, lse, query, grad_mixed):
    heads, _, block = a_rows.shape
    window = win_a.shape[-1]
    return pl.pallas_call(
        backward_kernel,
        out_shape=(
            jax.ShapeDtypeStruct((heads, RANK_Q, block), F32),
            jax.ShapeDtypeStruct((RANK_Q, HEAD_DIM, block), F32),
            jax.ShapeDtypeStruct((heads, KV, window), F32),
            jax.ShapeDtypeStruct((KV, HEAD_DIM, window), F32),
        ),
        in_specs=whole_specs(8),
        out_specs=tuple(whole_specs(4)),
        scratch_shapes=[
            pltpu.VMEM((window, block), F32),
            pltpu.VMEM((KV, HEAD_DIM, window), F32),
            pltpu.VMEM((window, block), F32),
            pltpu.VMEM((window, block), F32),
        ],
        compiler_params=pltpu.CompilerParams(vmem_limit_bytes=VMEM_LIMIT),
        name="attend_backward",
    )(first, a_rows, b_query, win_a, win_b, lse, query, grad_mixed)


def rotate(rows, cosine, sine):
    half = HEAD_DIM // 2
    lower, upper = rows[:, :half], rows[:, half:]
    return jnp.concatenate(
        [lower * cosine - upper * sine, lower * sine + upper * cosine], axis=1
    )


def make_general(mesh):
    n_f, n_c, n_tp = mesh.shape["fsdp"], mesh.shape["ctx"], mesh.shape["tp"]
    n_hi, n_lo = 2, n_tp // 2

    def shards(
        resid_in,
        segment_ids,
        cotangent,
        w_factor_a,
        w_factor_b,
        w_out,
        w_gate_up,
        w_down,
        attn_gains,
        ffn_gains,
    ):
        seq_count, local_len, width = resid_in.shape
        assert seq_count == 1 and w_factor_a.shape[0] == 1 and n_lo == 2
        full_len = segment_ids.shape[1]
        block = local_len // n_tp
        extra = -(-(MOST_DOC - 1) // block)
        window = (extra + 1) * block
        a_cols = w_factor_a.shape[2]
        heads = n_tp * a_cols // RANKS
        b_cols = w_factor_b.shape[2]
        b_rows = w_factor_b.shape[1]
        b_parts = b_cols // LANES
        fc_cols = w_down.shape[2]
        hidden = w_down.shape[1]
        o_rows = w_out.shape[1]

        f_index, c_index, t_index = (
            lax.axis_index("fsdp"),
            lax.axis_index("ctx"),
            lax.axis_index("tp"),
        )
        hi, lo = t_index // 2, t_index % 2
        place = c_index * n_tp + t_index
        n_place = n_c * n_tp

        gains = jnp.concatenate([attn_gains, ffn_gains], axis=1).astype(BF16)
        gain_count = gains.shape[1]
        gain_rows = 16 * (-(-gain_count // (16 * LANES)))
        gains = jnp.pad(gains.reshape(-1), (0, gain_rows * LANES - gain_count))
        b_shard = w_factor_b[0].astype(BF16).reshape(b_rows, b_parts, LANES)
        a_shard = w_factor_a[0].astype(BF16).T
        pack = jnp.concatenate(
            [
                b_shard.transpose(1, 0, 2).reshape(-1, LANES),
                a_shard.reshape(-1, LANES),
                gains.reshape(-1, LANES),
            ],
            axis=0,
        )
        n_b = b_parts * b_rows
        n_a = a_cols * fc_cols // LANES
        pack = gather_direct(pack, "fsdp", n_f)
        after_pack = pack
        pack = gather_pair(pack, "ctx", n_c, 1)
        pack = gather_pair(pack, "tp", n_tp, 2)
        pack = gather_pair(pack, "tp", n_tp, 1)
        pack = pack.transpose(3, 2, 1, 0, 4, 5)
        weight_b = pack[:, :, :, :, :n_b].reshape(-1, b_parts, b_rows, LANES)
        weight_b = weight_b.transpose(0, 2, 1, 3).reshape(width, b_cols)
        weight_a = pack[:, :, :, :, n_b : n_b + n_a].reshape(n_f, n_c, n_tp, a_cols, fc_cols)
        weight_a = weight_a.transpose(2, 3, 0, 1, 4).reshape(n_tp * a_cols, width)
        gains_all = pack[:, :, :, :, n_b + n_a :].reshape(-1, gain_rows * LANES)[:, :gain_count]
        gains_all = gains_all.reshape(-1, 2, gain_count // 2).transpose(1, 0, 2)
        gains_all = gains_all.reshape(2, width).astype(F32)
        gain_attn, gain_ffn = gains_all[0:1], gains_all[1:2]

        big = jnp.concatenate(
            [
                w_gate_up[0, 0].astype(BF16).T,
                w_gate_up[0, 1].astype(BF16).T,
                w_down[0].astype(BF16),
                w_out[0].astype(BF16),
            ],
            axis=0,
        )
        big, _ = lax.optimization_barrier((big, after_pack))
        big = gather_direct(big, "fsdp", n_f)
        big = gather_pair(big, "ctx", n_c, 1)
        big = big.transpose(2, 1, 0, 3).reshape(-1, width)
        weight_g = big[:hidden]
        weight_u = big[hidden : 2 * hidden]
        weight_d = big[2 * hidden : 3 * hidden]
        weight_o = gather_pair(big[3 * hidden :], "tp", n_tp, 2)
        weight_o = gather_pair(weight_o, "tp", n_tp, 1)
        weight_o = weight_o.transpose(1, 0, 2, 3).reshape(n_tp * o_rows, width)

        seg_here = lax.dynamic_slice_in_dim(segment_ids[0], place * block, block, 0)
        first = jnp.sum((segment_ids[0][:, None] < seg_here[None, :]).astype(jnp.int32), axis=0)
        token = place * block + jnp.arange(block, dtype=jnp.int32)
        position = (token - first).astype(F32)
        first = (first - place * block + extra * block).reshape(1, block)
        frequency = 10000.0 ** (
            -2.0 * jnp.arange(HEAD_DIM // 2, dtype=F32) / HEAD_DIM
        )
        angles = frequency[:, None] * position[None, :]
        cosine, sine = jnp.cos(angles)[None], jnp.sin(angles)[None]

        stream = resid_in[0].reshape(n_tp, block, width)
        own = take(stream, t_index)
        inverse_attn = inverse_rms(own)
        normed = (own * inverse_attn * gain_attn).astype(BF16)
        a_rows = dot(weight_a, normed, ((1,), (1,))).reshape(heads, RANKS, block)
        b_raw = dot(weight_b, normed, ((0,), (1,))).reshape(RANKS, HEAD_DIM, block)
        b_rot = rotate(b_raw[: RANK_Q + RANK_KV], cosine, sine)
        b_query = b_rot[:RANK_Q]
        b_kv = jnp.concatenate([b_rot[RANK_Q:], b_raw[RANK_Q + RANK_KV :]], axis=0)
        payload = jnp.concatenate(
            [
                b_kv.reshape(KV * HEAD_DIM, block),
                a_rows[:, RANK_Q:].reshape(heads * KV, block),
            ],
            axis=0,
        ).astype(BF16)
        around = [
            lax.ppermute(
                payload, ("ctx", "tp"), [(i, i + step) for i in range(n_place - step)]
            )
            for step in range(extra, 0, -1)
        ]
        win = jnp.concatenate(around + [payload], axis=1)
        win_b = win[: KV * HEAD_DIM].reshape(KV, HEAD_DIM, window)
        win_a = win[KV * HEAD_DIM :].reshape(heads, KV, window)

        mixed, lse, query = attend_forward(first, a_rows, b_query, win_a, win_b)
        mixed = mixed.reshape(heads * HEAD_DIM, block)
        attn_out = dot(mixed, weight_o, ((0,), (0,)))
        mid = own + attn_out
        inverse_ffn = inverse_rms(mid)
        normed_ffn = (mid * inverse_ffn * gain_ffn).astype(BF16)

        near_rows = gather_pair(normed_ffn, "tp", n_tp, 1)
        far_rows = gather_pair(swap(normed_ffn, "tp", n_tp, 2), "tp", n_tp, 1)
        grad_all = cotangent[0].reshape(n_hi, n_lo * block, width)

        def half(rows, grad_rows):
            rows = rows.reshape(n_lo * block, width)
            gate = dot(rows, weight_g, ((1,), (1,)))
            up = dot(rows, weight_u, ((1,), (1,)))
            grad_act = dot(grad_rows, weight_d, ((1,), (1,)))
            squash = jax.nn.sigmoid(gate)
            act = (gate * squash * up).astype(BF16)
            grad_gate = (grad_act * up * squash * (1.0 + gate * (1.0 - squash))).astype(BF16)
            grad_up = (grad_act * gate * squash).astype(BF16)
            back = dot(grad_gate, weight_g, ((1,), (0,))) + dot(grad_up, weight_u, ((1,), (0,)))
            ahead = dot(act, weight_d, ((1,), (0,)))
            both = lambda v: v.reshape(n_lo, block, width)
            return rows, act, grad_gate, grad_up, both(back), both(ahead)

        grad_near = take(grad_all, hi).astype(BF16)
        grad_far = take(grad_all, 1 - hi).astype(BF16)
        near = half(near_rows, grad_near)
        far = half(far_rows, grad_far)
        back_far = scatter_pair(far[4], "tp", n_tp, 1).astype(BF16)
        back_far = swap(back_far, "tp", n_tp, 2)
        grad_normed_ffn = scatter_pair(near[4], "tp", n_tp, 1) + back_far.astype(F32)
        ahead_far = scatter_pair(far[5], "tp", n_tp, 1).astype(BF16)
        ahead_far = swap(ahead_far, "tp", n_tp, 2)
        ffn_out = scatter_pair(near[5], "tp", n_tp, 1) + ahead_far.astype(F32)

        def spread(value):
            beside = swap(value, "tp", n_tp, 1)
            across = swap(value, "tp", n_tp, 2)
            diagonal = swap(across, "tp", n_tp, 1)
            out = jnp.zeros((n_tp,) + value.shape, value.dtype)
            for bit, part in enumerate((value, beside, across, diagonal)):
                out = lax.dynamic_update_slice(out, part[None], (t_index ^ bit, 0, 0))
            return out.reshape(local_len, width).astype(F32)

        block_out = resid_in + spread((attn_out + ffn_out).astype(BF16))[None]

        def columns(value, which):
            value = value.reshape(value.shape[0], n_f, n_c, fc_cols)
            value = lax.dynamic_index_in_dim(value, which, 2, keepdims=False)
            return value.reshape(value.shape[0], n_f * fc_cols)

        rows_all = jnp.concatenate([near[0], far[0]], axis=0)
        act_all = jnp.concatenate([near[1], far[1]], axis=0)
        gate_all = jnp.concatenate([near[2], far[2]], axis=0)
        up_all = jnp.concatenate([near[3], far[3]], axis=0)
        cot_all = jnp.concatenate([grad_near, grad_far], axis=0)

        def big_grads(which):
            rows_cut = columns(rows_all, which)
            cot_cut = columns(cot_all, which)
            return jnp.concatenate(
                [
                    dot(gate_all, rows_cut, ((0,), (0,))),
                    dot(up_all, rows_cut, ((0,), (0,))),
                    dot(act_all, cot_cut, ((0,), (0,))),
                ],
                axis=0,
            )

        def over_fc(send, keep):
            total = keep + swap(send.astype(BF16), "ctx", n_c, 1).astype(F32)
            total = total.astype(BF16).reshape(-1, n_f, fc_cols).transpose(1, 0, 2)
            return scatter_direct(total, "fsdp", n_f)

        grad_big = over_fc(big_grads(1 - c_index), big_grads(c_index))
        grad_gate_w = grad_big[:hidden].T
        grad_up_w = grad_big[hidden : 2 * hidden].T
        grad_down_w = grad_big[2 * hidden :]

        own_cot = take(cotangent[0].reshape(n_tp, block, width), t_index)
        gain_grad_ffn = jnp.sum(grad_normed_ffn * mid * inverse_ffn, axis=0)
        delta_mid = norm_back(grad_normed_ffn, mid, inverse_ffn, gain_ffn)
        grad_attn = (own_cot + delta_mid).astype(BF16)
        grad_out = dot(mixed, grad_attn, ((1,), (0,))).reshape(n_hi, n_lo, o_rows, width)
        grad_out = scatter_pair(grad_out.transpose(1, 0, 2, 3), "tp", n_tp, 1)
        grad_out = scatter_pair(grad_out, "tp", n_tp, 2)
        grad_out = over_fc(columns(grad_out, 1 - c_index), columns(grad_out, c_index))

        grad_mixed = dot(weight_o, grad_attn, ((1,), (1,))).astype(BF16)
        ga_q, gb_q, gw_a, gw_b = attend_backward(
            first,
            a_rows,
            b_query,
            win_a,
            win_b,
            lse,
            query,
            grad_mixed.reshape(heads, HEAD_DIM, block),
        )
        gw = jnp.concatenate(
            [gw_b.reshape(KV * HEAD_DIM, window), gw_a.reshape(heads * KV, window)], axis=0
        )
        total = gw[:, extra * block :]
        for step in range(1, extra + 1):
            part = gw[:, (extra - step) * block : (extra - step + 1) * block].astype(BF16)
            part = lax.ppermute(
                part, ("ctx", "tp"), [(i + step, i) for i in range(n_place - step)]
            )
            total = total + part.astype(F32)
        gb_kv = total[: KV * HEAD_DIM].reshape(KV, HEAD_DIM, block)
        ga_kv = total[KV * HEAD_DIM :].reshape(heads, KV, block)
        grad_b = jnp.concatenate(
            [
                rotate(jnp.concatenate([gb_q, gb_kv[:RANK_KV]], axis=0), cosine, -sine),
                gb_kv[RANK_KV:],
            ],
            axis=0,
        )
        grad_b = grad_b.reshape(b_cols, block).astype(BF16)
        grad_a = jnp.concatenate([ga_q, ga_kv], axis=1).reshape(heads * RANKS, block).astype(BF16)
        grad_normed = dot(grad_a, weight_a, ((0,), (0,))) + dot(grad_b, weight_b, ((0,), (1,)))
        gain_grad_attn = jnp.sum(grad_normed * own * inverse_attn, axis=0)
        delta = delta_mid + norm_back(grad_normed, own, inverse_attn, gain_attn)
        resid_grad = cotangent + spread(delta.astype(BF16))[None]

        grad_wa = dot(grad_a, normed, ((1,), (0,))).astype(BF16)
        grad_wa = grad_wa.reshape(n_hi, n_lo, a_cols, n_f, n_c, fc_cols)
        grad_wa = grad_wa.transpose(1, 0, 4, 3, 2, 5).reshape(n_lo, n_hi, n_c, n_f, n_a, LANES)
        grad_wb = jnp.einsum(
            "pkt,td->pdk",
            grad_b.reshape(b_parts, LANES, block),
            normed,
            preferred_element_type=F32,
        ).astype(BF16)
        grad_wb = grad_wb.reshape(b_parts, n_f, n_c, n_hi, n_lo, b_rows, LANES)
        grad_wb = grad_wb.transpose(4, 3, 2, 1, 0, 5, 6)
        grad_wb = grad_wb.reshape(n_lo, n_hi, n_c, n_f, n_b, LANES)
        gain_grads = jnp.stack([gain_grad_attn, gain_grad_ffn]).astype(BF16)
        gain_grads = gain_grads.reshape(2, n_f, n_c, n_hi, n_lo, gain_count // 2)
        gain_grads = gain_grads.transpose(4, 3, 2, 1, 0, 5).reshape(
            n_lo, n_hi, n_c, n_f, gain_count
        )
        gain_grads = jnp.pad(
            gain_grads, [(0, 0)] * 4 + [(0, gain_rows * LANES - gain_count)]
        ).reshape(n_lo, n_hi, n_c, n_f, gain_rows, LANES)
        pack = jnp.concatenate([grad_wb, grad_wa, gain_grads], axis=4)
        pack = scatter_pair(pack, "tp", n_tp, 1)
        pack = scatter_pair(pack, "tp", n_tp, 2)
        pack = scatter_pair(pack, "ctx", n_c, 1).astype(BF16)
        pack = scatter_direct(pack, "fsdp", n_f)
        part_b = pack[:n_b].reshape(b_parts, b_rows, LANES).transpose(1, 0, 2)
        part_b = part_b.reshape(1, b_rows, b_cols)
        part_a = pack[n_b : n_b + n_a].reshape(a_cols, fc_cols).T[None]
        part_gain = pack[n_b + n_a :].reshape(-1)[:gain_count].reshape(2, 1, gain_count // 2)
        return (
            block_out,
            resid_grad,
            part_a,
            part_b,
            grad_out[None],
            jnp.stack([grad_gate_w, grad_up_w])[None],
            grad_down_w[None],
            part_gain[0],
            part_gain[1],
        )

    return shards


def rotated(rows, cosine, sine):
    half = HEAD_DIM // 2
    lower, upper = rows[:half], rows[half:]
    return jnp.concatenate([lower * cosine - upper * sine, lower * sine + upper * cosine], axis=0)


def make_fused(mesh):
    n_f, n_c, n_tp = mesh.shape["fsdp"], mesh.shape["ctx"], mesh.shape["tp"]
    n_piece = n_f * n_c
    AT_TP = n_piece
    AT_ME = n_piece + n_tp

    def shards(
        resid_in,
        segment_ids,
        cotangent,
        w_factor_a,
        w_factor_b,
        w_out,
        w_gate_up,
        w_down,
        attn_gains,
        ffn_gains,
    ):
        _, local_len, width = resid_in.shape
        block = local_len // n_tp
        extra = -(-(MOST_DOC - 1) // block)
        windows = extra + 1
        a_cols = w_factor_a.shape[2]
        group = a_cols // RANKS
        heads = n_tp * group
        feats = group * HEAD_DIM
        a_pad = 16 * (-(-a_cols // 16))
        b_rows, b_cols = w_factor_b.shape[1:]
        b_parts = b_cols // LANES
        n_b = b_parts * b_rows
        pack_rows = n_b + a_pad + 16
        fc_cols = w_down.shape[2]
        hidden = w_down.shape[1]
        o_rows = w_out.shape[1]
        gain_part = attn_gains.shape[1]
        kv_b = KV * HEAD_DIM
        kv_rows = kv_b + heads * KV
        half_width = width // n_c
        assert fc_cols == LANES and o_rows == feats and n_tp == 4 and n_c == 2

        f_index, c_index, t_index = (
            lax.axis_index("fsdp"),
            lax.axis_index("ctx"),
            lax.axis_index("tp"),
        )
        place = c_index * n_tp + t_index
        n_place = n_c * n_tp
        columns = [
            ((f_index - s) % n_f) * n_c + (c_index if near == 0 else 1 - c_index)
            for near in range(n_c)
            for s in range(n_f)
        ]
        members = [t_index ^ (lo + 2 * hi) for lo in range(2) for hi in range(2)]
        meta = jnp.stack(columns + members + [t_index]).astype(jnp.int32)

        def column(meta_ref, j):
            return pl.ds(pl.multiple_of(meta_ref[j] * LANES, LANES), LANES)

        def member(meta_ref, lo, hi):
            return meta_ref[AT_TP + 2 * lo + hi]

        def to_arrival(meta_ref, load):
            return jnp.concatenate([load(column(meta_ref, j)) for j in range(n_piece)], axis=1)

        WHOLE = pl.BlockSpec(memory_space=pltpu.VMEM)
        REMOTE = pl.BlockSpec(memory_space=pl.ANY)
        OWN = pl.BlockSpec((1, block, width), lambda i, m: (0, m[AT_ME], 0))

        def call(kernel, name, outs, args, specs=None, scratch=(), grid=(1,), out_specs=None):
            return pl.pallas_call(
                kernel,
                out_shape=[jax.ShapeDtypeStruct(s, d) for s, d in outs],
                grid_spec=pltpu.PrefetchScalarGridSpec(
                    num_scalar_prefetch=1,
                    grid=grid,
                    in_specs=specs or [WHOLE] * len(args),
                    out_specs=out_specs or [WHOLE] * len(outs),
                    scratch_shapes=list(scratch),
                ),
                compiler_params=pltpu.CompilerParams(vmem_limit_bytes=VMEM_LIMIT),
                name=name,
            )(meta, *args)


        def pack_kernel(meta_ref, b_ref, a_ref, g0_ref, g1_ref, out_ref):
            for k in range(b_parts):
                out_ref[k * b_rows : (k + 1) * b_rows, :] = b_ref[
                    0, :, k * LANES : (k + 1) * LANES
                ].astype(BF16)
            a_shard = jnp.concatenate([a_ref[0], jnp.zeros((a_pad - a_cols, LANES), F32)], axis=0)
            out_ref[n_b : n_b + a_pad, :] = a_shard.astype(BF16)
            both = jnp.concatenate([g0_ref[...], g1_ref[...]], axis=0)
            both = jnp.concatenate([both, jnp.zeros((6, gain_part), F32)], axis=0)
            both = jnp.concatenate([both, jnp.zeros((8, LANES - gain_part), F32)], axis=1)
            both = pltpu.roll(both, meta_ref[AT_ME] * gain_part, 1)
            both = jnp.concatenate([both, jnp.zeros((8, LANES), F32)], axis=0)
            out_ref[n_b + a_pad :, :] = both.astype(BF16)

        def big_kernel(meta_ref, gu_ref, d_ref, out_ref):
            for k in range(2):
                out_ref[k * hidden : (k + 1) * hidden, :] = gu_ref[0, k].astype(BF16)
            out_ref[2 * hidden :, :] = d_ref[0].astype(BF16)

        def factor_kernel(
            meta_ref,
            x_ref,
            p0_ref,
            p1_ref,
            cos_ref,
            sin_ref,
            wb_ref,
            wa_ref,
            gain_ref,
            normed_ref,
            a_ref,
            bq_ref,
            pay_ref,
        ):
            gain_ref[...] = jnp.zeros_like(gain_ref)
            for lo, hi in ((0, 0), (0, 1), (1, 0), (1, 1)):
                part = (p0_ref, p1_ref)[lo]
                tp = member(meta_ref, lo, hi)
                for near in range(n_c):
                    for s in range(n_f):
                        j = near * n_f + s
                        lanes = column(meta_ref, j)
                        row = pl.multiple_of((meta_ref[j] * n_tp + tp) * b_rows, b_rows)
                        for k in range(b_parts):
                            wb_ref[pl.ds(row, b_rows), k * LANES : (k + 1) * LANES] = part[
                                near, hi, s, k * b_rows : (k + 1) * b_rows, :
                            ]
                        wa_ref[tp, :, lanes] = part[near, hi, s, n_b : n_b + a_pad, :]
                        gain_ref[:, lanes] += part[near, hi, s, n_b + a_pad :, :].astype(F32)
            x = x_ref[0]
            normed = (x * inverse_rms(x) * gain_ref[0:1]).astype(BF16)
            normed_ref[...] = normed
            cosine, sine = cos_ref[...], sin_ref[...]
            b_raw = jnp.transpose(dot(normed, wb_ref[...], ((1,), (0,))))
            for r in range(RANK_Q):
                bq_ref[r] = rotated(b_raw[r * HEAD_DIM : (r + 1) * HEAD_DIM], cosine, sine)
            for r in range(KV):
                rows = b_raw[(RANK_Q + r) * HEAD_DIM : (RANK_Q + r + 1) * HEAD_DIM]
                if r < RANK_KV:
                    rows = rotated(rows, cosine, sine)
                pay_ref[r * HEAD_DIM : (r + 1) * HEAD_DIM, :] = rows.astype(BF16)
            for tp in range(n_tp):
                a_raw = dot(wa_ref[tp], normed, ((1,), (1,)))
                a_ref[tp] = a_raw
                kv = [a_raw[g * RANKS + RANK_Q : (g + 1) * RANKS] for g in range(group)]
                start = kv_b + tp * group * KV
                pay_ref[start : start + group * KV, :] = jnp.concatenate(kv, axis=0).astype(BF16)

        def set_mask(first_ref, bias_ref):
            bias_ref[...] = attention_mask(first_ref, windows * block, block)

        def widen(win_refs, wide_ref):
            for j, ref in enumerate(win_refs):
                for r in range(KV):
                    wide_ref[j, r] = ref[r * HEAD_DIM : (r + 1) * HEAD_DIM, :].astype(F32)

        def kv_factors(win_refs, tp):
            start = pl.multiple_of(kv_b + tp * (group * KV), group * KV)
            return [ref[pl.ds(start, group * KV), :].astype(F32) for ref in win_refs]

        def kv_rows_of(factors, wide_ref, g, j):
            def mix(r):
                a0 = factors[j][g * KV + r : g * KV + r + 1]
                a1 = factors[j][g * KV + r + 1 : g * KV + r + 2]
                rows = a0 * wide_ref[j, r] + a1 * wide_ref[j, r + 1]
                return (rows * (1.0 / RANK_KV)).astype(BF16)

            return mix(0), mix(RANK_KV)

        def attention_kernel(
            meta_ref,
            first_ref,
            a_ref,
            bq_ref,
            w0_ref,
            w1_ref,
            w2_ref,
            w3_ref,
            lse_ref,
            q_ref,
            mixed_ref,
            bias_ref,
            wide_ref,
            s_ref,
        ):
            wins = (w0_ref, w1_ref, w2_ref, w3_ref)
            set_mask(first_ref, bias_ref)
            widen(wins, wide_ref)
            spans = [pl.ds(j * block, block) for j in range(windows)]

            def one_group(tp, carry):
                own = a_ref[tp]
                factors = kv_factors(wins, tp)
                for g in range(group):
                    query = own[g * RANKS : g * RANKS + 1] * bq_ref[0]
                    for r in range(1, RANK_Q):
                        query = query + own[g * RANKS + r : g * RANKS + r + 1] * bq_ref[r]
                    query = (query * (1.0 / RANK_Q)).astype(BF16)
                    query = query * jnp.asarray(HEAD_DIM**-0.5, BF16)
                    q_ref[tp, g] = query
                    top = jnp.full((1, block), MASKED, F32)
                    values = []
                    for j, span in enumerate(spans):
                        keys, rows = kv_rows_of(factors, wide_ref, g, j)
                        values.append(rows)
                        scores = dot(keys, query, ((0,), (0,))) + bias_ref[span, :]
                        s_ref[g, span, :] = scores
                        top = jnp.maximum(top, jnp.max(scores, axis=0, keepdims=True))
                    total = jnp.zeros((1, block), F32)
                    for span in spans:
                        weight = jnp.exp(s_ref[g, span, :] - top)
                        s_ref[g, span, :] = weight
                        total = total + jnp.sum(weight, axis=0, keepdims=True)
                    lse_ref[tp, g : g + 1, :] = top + jnp.log(total)
                    scale = 1.0 / total
                    mixed = jnp.zeros((HEAD_DIM, block), F32)
                    for j, span in enumerate(spans):
                        probs = (s_ref[g, span, :] * scale).astype(BF16)
                        mixed = mixed + dot(values[j], probs, ((1,), (0,)))
                    mixed_ref[tp, g * HEAD_DIM : (g + 1) * HEAD_DIM, :] = mixed.astype(BF16)
                return carry

            lax.fori_loop(0, n_tp, one_group, 0)

        def project_kernel(
            meta_ref, x_ref, mixed_ref, o0_ref, o1_ref, gain_ref, mid_ref, attn_ref, nf_ref
        ):
            attn = jnp.zeros((block, width), F32)
            for lo, ref in enumerate((o0_ref, o1_ref)):
                for hi in range(2):
                    rows = mixed_ref[member(meta_ref, lo, hi)]
                    attn = attn + dot(rows, ref[hi * o_rows : (hi + 1) * o_rows, :], ((0,), (0,)))
            attn_ref[...] = attn
            mid = to_arrival(meta_ref, lambda lanes: x_ref[0, :, lanes]) + attn
            mid_ref[...] = mid
            gain = to_arrival(meta_ref, lambda lanes: gain_ref[1:2, lanes])
            nf_ref[...] = (mid * inverse_rms(mid) * gain).astype(BF16)

        def ffn_kernel(side, meta_ref, *refs):
            n_refs = refs[:2]
            cot_ref = refs[2]
            pieces = refs[3 : 3 + n_piece]
            ht_ref, gb_ref, back0_ref, back1_ref, ahead0_ref, ahead1_ref = refs[
                3 + n_piece : 9 + n_piece
            ]
            w_ref, cot_buf, sems = refs[9 + n_piece :]
            loads = []
            for i in range(2):
                row = pl.multiple_of(member(meta_ref, i, side) * block, block)
                loads.append(
                    pltpu.make_async_copy(
                        cot_ref.at[0, pl.ds(row, block), :], cot_buf.at[i], sems.at[n_piece + i]
                    )
                )
            for j, piece in enumerate(pieces):
                loads.append(
                    pltpu.make_async_copy(
                        piece,
                        w_ref.at[:, pl.ds(j * LANES, LANES)],
                        sems.at[j],
                    )
                )
            for load in loads:
                load.start()
            for i in range(2):
                loads[i].wait()
                for j in range(n_piece):
                    gb_ref[i * block : (i + 1) * block, j * LANES : (j + 1) * LANES] = cot_buf[
                        i, :, column(meta_ref, j)
                    ].astype(BF16)
            for load in loads[2:]:
                load.wait()
            for i in range(2):
                cut = slice(i * block, (i + 1) * block)
                rows = n_refs[i][...]
                gate = dot(w_ref[0:hidden, :], rows, ((1,), (1,)))
                up = dot(w_ref[hidden : 2 * hidden, :], rows, ((1,), (1,)))
                grad_act = dot(w_ref[2 * hidden :, :], gb_ref[cut, :], ((1,), (1,)))
                squash = jax.nn.sigmoid(gate)
                soft = gate * squash
                ht_ref[2 * hidden :, cut] = (soft * up).astype(BF16)
                ht_ref[0:hidden, cut] = (
                    grad_act * up * squash * (1.0 + gate * (1.0 - squash))
                ).astype(BF16)
                ht_ref[hidden : 2 * hidden, cut] = (grad_act * soft).astype(BF16)
            back = dot(ht_ref[: 2 * hidden, :], w_ref[: 2 * hidden, :], ((0,), (0,)))
            back0_ref[...] = back[:block]
            back1_ref[...] = back[block:].astype(BF16)
            ahead = dot(ht_ref[2 * hidden :, :], w_ref[2 * hidden :, :], ((0,), (0,)))
            ahead0_ref[...] = ahead[:block]
            ahead1_ref[...] = ahead[block:].astype(BF16)

        def weight_grad_kernel(bounds, meta_ref, *refs):
            hts, n_near, n_far, gbs = refs[0:2], refs[2:4], refs[4:6], refs[6:8]
            keep_ref, send_ref = refs[8:]
            base = bounds[0][0]
            for start, stop, right in bounds:
                total = jnp.zeros((stop - start, width), F32)
                for side in range(2):
                    left = hts[side]
                    if right == 1:
                        total = total + dot(left[start:stop, :], gbs[side][...], ((1,), (0,)))
                        continue
                    for i in range(2):
                        rows = (n_near, n_far)[side][i][...]
                        cut = slice(i * block, (i + 1) * block)
                        total = total + dot(left[start:stop, cut], rows, ((1,), (0,)))
                keep_ref[start - base : stop - base, :] = total[:, :half_width].astype(BF16)
                send_ref[start - base : stop - base, :] = total[:, half_width:].astype(BF16)

        def middle_kernel(
            meta_ref,
            cot_ref,
            back_ref,
            beside_ref,
            across_ref,
            mid_ref,
            gain_ref,
            o0_ref,
            o1_ref,
            mixed_ref,
            dmid_ref,
            gg_ref,
            go_ref,
            keep_ref,
            send_ref,
        ):
            back = back_ref[...] + beside_ref[...].astype(F32) + across_ref[...].astype(F32)
            mid = mid_ref[...]
            inverse = inverse_rms(mid)
            gain = to_arrival(meta_ref, lambda lanes: gain_ref[1:2, lanes])
            normal = mid * inverse
            gains = jnp.sum(back * normal, axis=0, keepdims=True)
            for j in range(n_piece):
                gg_ref[:, column(meta_ref, j)] = jnp.broadcast_to(
                    gains[:, j * LANES : (j + 1) * LANES], (8, LANES)
                )
            scaled = back * gain
            delta = inverse * (
                scaled - normal * jnp.mean(scaled * normal, axis=-1, keepdims=True)
            )
            dmid_ref[...] = delta
            cot = to_arrival(meta_ref, lambda lanes: cot_ref[0, :, lanes])
            grad = (cot + delta).astype(BF16)
            for lo, ref in enumerate((o0_ref, o1_ref)):
                for hi in range(2):
                    tp = member(meta_ref, lo, hi)
                    cut = slice(hi * o_rows, (hi + 1) * o_rows)
                    go_ref[tp] = dot(ref[cut, :], grad, ((1,), (1,))).astype(BF16)
                    weight = dot(mixed_ref[tp], grad, ((1,), (0,))).astype(BF16)
                    (keep_ref, send_ref)[lo][cut, :] = weight

        def attention_back_kernel(
            part,
            meta_ref,
            first_ref,
            a_ref,
            bq_ref,
            w0_ref,
            w1_ref,
            w2_ref,
            w3_ref,
            lse_ref,
            q_ref,
            go_ref,
            *refs,
        ):
            bias_ref, wide_ref, p_ref, dp_ref = refs[-4:]
            if part == 0:
                ga_ref, gbq_ref, gwb_ref, gwa_ref = refs[:4]
            else:
                ga_ref, gbq_ref, *out_refs = refs[3 : 5 + windows]
                gwb_ref, gwa_ref = refs[-6:-4]
            wins = (w0_ref, w1_ref, w2_ref, w3_ref)
            set_mask(first_ref, bias_ref)
            widen(wins, wide_ref)
            if part == 0:
                gbq_ref[...] = jnp.zeros_like(gbq_ref)
                gwb_ref[...] = jnp.zeros_like(gwb_ref)
            else:
                gbq_ref[...] = refs[0][...]
                gwb_ref[...] = refs[1][...]
                gwa_ref[...] = refs[2][...]
            spans = [pl.ds(j * block, block) for j in range(windows)]
            first_tp = part * (n_tp // 2)

            def one_group(tp, carry):
                own = a_ref[tp]
                factors = kv_factors(wins, tp)
                grad_a = []
                grad_kv = [[] for _ in spans]
                for g in range(group):
                    query = q_ref[tp, g]
                    grad_out = go_ref[tp, g * HEAD_DIM : (g + 1) * HEAD_DIM, :]
                    lse = lse_ref[tp, g : g + 1, :]
                    inner = jnp.zeros((1, block), F32)
                    keys = []
                    for j, span in enumerate(spans):
                        key_rows, value_rows = kv_rows_of(factors, wide_ref, g, j)
                        keys.append(key_rows)
                        scores = dot(key_rows, query, ((0,), (0,))) + bias_ref[span, :]
                        probs = jnp.exp(scores - lse)
                        grad_probs = dot(value_rows, grad_out, ((0,), (0,)))
                        p_ref[g % 2, span, :] = probs
                        dp_ref[g % 2, span, :] = grad_probs
                        inner = inner + jnp.sum(probs * grad_probs, axis=0, keepdims=True)
                    grad_query = jnp.zeros((HEAD_DIM, block), F32)
                    for j, span in enumerate(spans):
                        probs = p_ref[g % 2, span, :]
                        grad_scores = (probs * (dp_ref[g % 2, span, :] - inner)).astype(BF16)
                        grad_query = grad_query + dot(keys[j], grad_scores, ((1,), (0,)))
                        grad_keys = dot(query, grad_scores, ((1,), (1,))) * (1.0 / RANK_KV)
                        grad_values = dot(grad_out, probs.astype(BF16), ((1,), (1,)))
                        grad_values = grad_values * (1.0 / RANK_KV)
                        for r in range(KV):
                            grad = grad_keys if r < RANK_KV else grad_values
                            grad_kv[j].append(
                                jnp.sum(grad * wide_ref[j, r], axis=0, keepdims=True)
                            )
                            gwb_ref[j, r] += factors[j][g * KV + r : g * KV + r + 1] * grad
                    grad_query = grad_query * (HEAD_DIM**-0.5 / RANK_Q)
                    for r in range(RANK_Q):
                        grad_a.append(jnp.sum(grad_query * bq_ref[r], axis=0, keepdims=True))
                        gbq_ref[r] += own[g * RANKS + r : g * RANKS + r + 1] * grad_query
                    grad_a.append(jnp.zeros((KV, block), F32))
                grad_a.append(jnp.zeros((a_pad - a_cols, block), F32))
                ga_ref[tp - first_tp] = jnp.concatenate(grad_a, axis=0)
                start = pl.multiple_of(tp * (group * KV), group * KV)
                for j in range(windows):
                    gwa_ref[j, pl.ds(start, group * KV), :] = jnp.concatenate(grad_kv[j], axis=0)
                return carry

            lax.fori_loop(first_tp, first_tp + n_tp // 2, one_group, 0)
            if part == 0:
                return
            for j, ref in enumerate(out_refs):
                for r in range(KV):
                    ref[r * HEAD_DIM : (r + 1) * HEAD_DIM, :] = gwb_ref[j, r].astype(ref.dtype)
                ref[kv_b:, :] = gwa_ref[j].astype(ref.dtype)

        def last_kernel(
            meta_ref,
            x_ref,
            own_ref,
            r1_ref,
            r2_ref,
            r3_ref,
            gbq_ref,
            ga0_ref,
            ga1_ref,
            cos_ref,
            sin_ref,
            wb_ref,
            wa_ref,
            normed_ref,
            gain_ref,
            dmid_ref,
            gg_ref,
            delta_ref,
            keep_ref,
            send_ref,
            b_buf,
            a_buf,
            d_buf,
            g_buf,
        ):
            total = own_ref[...]
            for ref in (r1_ref, r2_ref, r3_ref):
                total = total + ref[...].astype(F32)
            cosine, sine = cos_ref[...], -sin_ref[...]
            rows = [rotated(gbq_ref[r], cosine, sine) for r in range(RANK_Q)]
            for r in range(KV):
                part = total[r * HEAD_DIM : (r + 1) * HEAD_DIM]
                rows.append(rotated(part, cosine, sine) if r < RANK_KV else part)
            grad_b = jnp.transpose(jnp.concatenate(rows, axis=0)).astype(BF16)
            normed = normed_ref[...]
            back = dot(grad_b, wb_ref[...], ((1,), (1,)))
            for tp in range(n_tp):
                parts = []
                for g in range(group):
                    start = kv_b + (tp * group + g) * KV
                    parts.append(jnp.zeros((RANK_Q, block), F32))
                    parts.append(total[start : start + KV])
                parts.append(jnp.zeros((a_pad - a_cols, block), F32))
                own_a = (ga0_ref, ga1_ref)[tp // 2][tp % 2]
                grad_a = (own_a + jnp.concatenate(parts, axis=0)).astype(BF16)
                back = back + dot(grad_a, wa_ref[tp], ((0,), (0,)))
                a_buf[tp] = dot(grad_a, normed, ((1,), (0,)))
            b_buf[...] = dot(normed, grad_b, ((0,), (0,)))
            x = x_ref[0]
            inverse = inverse_rms(x)
            normal = x * inverse
            gains = jnp.sum(back * normal, axis=0, keepdims=True)
            g_buf[...] = jnp.broadcast_to(gains, (8, width))
            scaled = back * gain_ref[0:1]
            delta = inverse * (
                scaled - normal * jnp.mean(scaled * normal, axis=-1, keepdims=True)
            )
            d_buf[...] = delta
            for j in range(n_piece):
                lanes = column(meta_ref, j)
                cut = slice(j * LANES, (j + 1) * LANES)
                delta_ref[:, lanes] = (d_buf[:, lanes] + dmid_ref[:, cut]).astype(BF16)
            row_index = lax.broadcasted_iota(jnp.int32, (16, LANES), 0)
            for lo, hi in ((0, 0), (0, 1), (1, 0), (1, 1)):
                out = (keep_ref, send_ref)[lo]
                tp = member(meta_ref, lo, hi)
                for near in range(n_c):
                    for s in range(n_f):
                        j = near * n_f + s
                        lanes = column(meta_ref, j)
                        row = pl.multiple_of((meta_ref[j] * n_tp + tp) * b_rows, b_rows)
                        for k in range(b_parts):
                            out[near, hi, s, k * b_rows : (k + 1) * b_rows, :] = b_buf[
                                pl.ds(row, b_rows), k * LANES : (k + 1) * LANES
                            ].astype(BF16)
                        out[near, hi, s, n_b : n_b + a_pad, :] = a_buf[tp, :, lanes].astype(BF16)
                        pair = jnp.where(
                            row_index == 0, g_buf[0:1, lanes], gg_ref[0:1, lanes]
                        )
                        out[near, hi, s, n_b + a_pad :, :] = pair.astype(BF16)

        def add_kernel(arrival, meta_ref, x_ref, d0_ref, d1_ref, d2_ref, d3_ref, out_ref):
            step = pl.program_id(0) // 2
            rows = pl.ds(pl.multiple_of((pl.program_id(0) % 2) * (block // 2), 8), block // 2)
            for i, ref in enumerate((d0_ref, d1_ref, d2_ref, d3_ref)):

                @pl.when(step == i)
                def _(ref=ref):
                    if not arrival:
                        out_ref[0] = x_ref[0] + ref[rows, :].astype(F32)
                        return
                    for j in range(n_piece):
                        lanes = column(meta_ref, j)
                        out_ref[0, :, lanes] = x_ref[0, :, lanes] + ref[
                            rows, j * LANES : (j + 1) * LANES
                        ].astype(F32)

        def split_kernel(meta_ref, keep_ref, got_ref, *refs):
            for i, ref in enumerate(refs):
                lanes = slice(i * LANES, (i + 1) * LANES)
                total = keep_ref[:, lanes].astype(F32) + got_ref[:, lanes].astype(F32)
                ref[...] = total.astype(ref.dtype)

        def finish_kernel(meta_ref, *refs):
            first, second = refs[0:4], refs[4:8]
            gu_ref, d_ref, buf = refs[8:]
            cut = first[0].shape[0]

            def total(parts):
                out = parts[0][...].astype(F32)
                for part in parts[1:]:
                    out = out + part[...].astype(F32)
                return out

            buf[0:cut, :] = total(first)
            buf[cut:, :] = total(second)
            for k in range(2):
                gu_ref[0, k] = buf[k * hidden : (k + 1) * hidden, :]
            d_ref[0] = buf[2 * hidden :, :]

        def unpack_kernel(
            meta_ref, p_ref, r1_ref, r2_ref, r3_ref, b_ref, a_ref, g0_ref, g1_ref, o_ref
        ):
            total = p_ref[...].astype(F32)
            for ref in (r1_ref, r2_ref, r3_ref):
                total = total + ref[...].astype(F32)
            for k in range(b_parts):
                b_ref[0, :, k * LANES : (k + 1) * LANES] = total[k * b_rows : (k + 1) * b_rows]
            a_ref[0] = total[n_b : n_b + a_cols]
            rows = total[n_b + a_pad : n_b + a_pad + 8]
            rows = pltpu.roll(rows, (n_tp - meta_ref[AT_ME]) * gain_part, 1)
            g0_ref[...] = rows[0:1, :gain_part]
            g1_ref[...] = rows[1:2, :gain_part]
            o_ref[0] = total[pack_rows:]

        core = lambda v, label="row": swap(v, "tp", n_tp, 1, "core_" + label)
        chip = lambda v, label="row": swap(v, "tp", n_tp, 2, "y_" + label)
        ctx = lambda v, label="row": swap(v, "ctx", n_c, 1, "x_" + label)
        ahead = lambda v, s, label="row": shift(v, "fsdp", n_f, s, "z_" + label)

        (pack,) = call(
            pack_kernel,
            "pack",
            [((pack_rows, LANES), BF16)],
            (w_factor_b, w_factor_a.transpose(0, 2, 1), attn_gains, ffn_gains),
        )
        o_rows_all = w_out[0].astype(BF16)
        pack = jnp.stack([pack] + [ahead(pack, s, "pack") for s in range(1, n_f)])
        o_parts = [o_rows_all] + [ahead(o_rows_all, s, "wo") for s in range(1, n_f)]
        o_parts = jnp.concatenate(o_parts, axis=0)
        gu_in = after(w_gate_up.transpose(0, 1, 3, 2), pack)
        (big,) = call(
            big_kernel, "big_pack", [((3 * hidden, LANES), BF16)], (gu_in, w_down)
        )
        pack = jnp.stack([pack, ctx(pack, "pack")])
        ring = [big, ahead(big, 1, "ring1")]
        pieces_x = [ctx(big, "ring0")]
        o_across = ctx(o_parts, "wo")
        o_parts = jnp.concatenate(
            [
                half[s * o_rows : (s + 1) * o_rows]
                for half in (o_parts, o_across)
                for s in range(n_f)
            ],
            axis=1,
        )
        pack_across, ring[1], pieces_x[0] = lax.optimization_barrier(
            (chip(pack, "pack"), ring[1], pieces_x[0])
        )
        pack = jnp.stack([pack, pack_across], axis=1)
        other_pack = core(pack, "pack")
        ring.append(ahead(ring[1], 1, "ring2"))
        pieces_x.append(ctx(ring[1], "ring1"))
        o_parts = after(o_parts, other_pack)
        o_own = jnp.concatenate([o_parts, chip(o_parts, "wo")], axis=0)

        def spread_parts(delta):
            across_delta = chip(delta, "rows")
            return delta, across_delta, core(delta, "rows"), core(across_delta, "rows")

        def add_rows(whole, parts, arrival):
            rows = pl.BlockSpec(
                (1, block // 2, width), lambda i, m: (0, 2 * m[AT_TP + i // 2] + i % 2, 0)
            )
            (out,) = call(
                lambda *refs: add_kernel(arrival, *refs),
                "add_rows",
                [(whole.shape, F32)],
                (whole, *parts),
                [rows] + [WHOLE] * 4,
                (),
                (2 * n_tp,),
                [rows],
            )
            return out

        def split(keep, got):
            size = keep.shape[0]
            return call(
                split_kernel,
                "split",
                [((size, LANES), F32)] + [((size, LANES), BF16)] * (n_f - 1),
                (keep, got),
            )

        def along(parts):
            return [parts[0]] + [ahead(parts[s], n_f - s) for s in range(1, n_f)]

        seg_here = lax.dynamic_slice_in_dim(segment_ids[0], place * block, block, 0)
        first = jnp.sum((segment_ids[0][:, None] < seg_here[None, :]).astype(jnp.int32), axis=0)
        token = place * block + jnp.arange(block, dtype=jnp.int32)
        position = (token - first).astype(F32)
        first = (first - place * block + extra * block).reshape(1, block)
        frequency = 10000.0 ** (-2.0 * jnp.arange(HEAD_DIM // 2, dtype=F32) / HEAD_DIM)
        angles = frequency[:, None] * position[None, :]
        cosine, sine = jnp.cos(angles), jnp.sin(angles)

        weight_b, weight_a, gains, normed, a_rows, b_query, payload = call(
            factor_kernel,
            "factors",
            [
                ((width, b_cols), BF16),
                ((n_tp, a_pad, width), BF16),
                ((16, width), F32),
                ((block, width), BF16),
                ((n_tp, a_pad, block), F32),
                ((RANK_Q, HEAD_DIM, block), F32),
                ((kv_rows, block), BF16),
            ],
            (resid_in, pack, other_pack, cosine, sine),
            [OWN] + [WHOLE] * 4,
        )
        payload, ring[2] = lax.optimization_barrier((payload, ring[2]))
        around = [
            lax.ppermute(
                payload, ("ctx", "tp"), [(i, i + step) for i in range(n_place - step)]
            )
            for step in range(extra, 0, -1)
        ]
        ring.append(ahead(ring[2], 1, "ring3"))
        pieces_x.append(ctx(ring[2], "ring2"))
        tied = lax.optimization_barrier((*around, pieces_x[1], o_own))
        wins = list(tied[:extra]) + [payload]
        pieces_x[1], o_own = tied[extra:]
        o_other = core(o_own, "wo")
        window = windows * block
        lse, query, mixed = call(
            attention_kernel,
            "attention",
            [
                ((n_tp, group, block), F32),
                ((n_tp, group, HEAD_DIM, block), BF16),
                ((n_tp, feats, block), BF16),
            ],
            (first, a_rows, b_query, *wins),
            None,
            [
                pltpu.VMEM((window, block), F32),
                pltpu.VMEM((windows, KV, HEAD_DIM, block), F32),
                pltpu.VMEM((group, window, block), F32),
            ],
        )
        mixed, ring[3], pieces_x[2] = lax.optimization_barrier((mixed, ring[3], pieces_x[2]))
        pieces_x.append(ctx(ring[3], "ring3"))
        mid, attn_out, normed_ffn = call(
            project_kernel,
            "project",
            [((block, width), F32), ((block, width), F32), ((block, width), BF16)],
            (resid_in, mixed, o_own, o_other, gains),
            [OWN] + [WHOLE] * 4,
        )
        pieces = ring + pieces_x

        near_rows = (normed_ffn, core(normed_ffn, "nf"))
        far_own = chip(normed_ffn, "nf")

        def feed(side, rows):
            return call(
                lambda *refs: ffn_kernel(side, *refs),
                "feed_near" if side == 0 else "feed_far",
                [
                    ((3 * hidden, 2 * block), BF16),
                    ((2 * block, width), BF16),
                    ((block, width), F32),
                    ((block, width), BF16),
                    ((block, width), F32),
                    ((block, width), BF16),
                ],
                (*rows, cotangent, *pieces),
                [WHOLE] * 2 + [REMOTE] * (1 + n_piece),
                [
                    pltpu.VMEM((3 * hidden, width), BF16),
                    pltpu.VMEM((2, block, width), F32),
                    pltpu.SemaphoreType.DMA((n_piece + 2,)),
                ],
            )

        near = feed(0, near_rows)
        far_own = after(far_own, near[0])
        far_rows = (far_own, core(far_own, "nf_far"))
        far = feed(1, far_rows)
        across = (far[2] + core(far[3], "dn_far").astype(F32)).astype(BF16)
        tied_ht = after(far[0], across)
        across = chip(across, "dn")
        beside = core(near[3], "dn_near")

        def weight_grads(name, bounds):
            size = bounds[-1][1] - bounds[0][0]
            return call(
                lambda *refs: weight_grad_kernel(bounds, *refs),
                name,
                [((size, half_width), BF16)] * 2,
                (near[0], tied_ht, *near_rows, *far_rows, near[1], far[1]),
            )

        keep_a, send_a = weight_grads("weight_grads_a", [(0, hidden, 0)])
        keep_b, send_b = weight_grads(
            "weight_grads_b", [(hidden, 2 * hidden, 0), (2 * hidden, 3 * hidden, 1)]
        )

        got_a, got_b = ctx(send_a, "grads_a"), ctx(send_b, "grads_b")
        across = after(across, send_b)

        delta_mid, gain_grad, grad_mixed, keep_o, send_o = call(
            middle_kernel,
            "middle",
            [
                ((block, width), F32),
                ((8, width), F32),
                ((n_tp, feats, block), BF16),
                ((2 * o_rows, width), BF16),
                ((2 * o_rows, width), BF16),
            ],
            (cotangent, near[2], beside, across, mid, gains, o_own, o_other, mixed),
            [OWN] + [WHOLE] * 8,
        )
        ahead_sum = far[4] + core(far[5], "out_far").astype(F32)
        ahead_sum = after(ahead_sum.astype(BF16), across)
        ahead_rows = chip(ahead_sum, "out")
        back_args = (first, a_rows, b_query, *wins, lse, query, grad_mixed)
        sums = [
            ((RANK_Q, HEAD_DIM, block), F32),
            ((windows, KV, HEAD_DIM, block), F32),
            ((windows, heads * KV, block), F32),
        ]
        grad_a_out = ((n_tp // 2, a_pad, block), F32)
        back_scratch = [
            pltpu.VMEM((window, block), F32),
            pltpu.VMEM((windows, KV, HEAD_DIM, block), F32),
            pltpu.VMEM((2, window, block), F32),
            pltpu.VMEM((2, window, block), F32),
        ]
        grad_a0, *sums_out = call(
            lambda *refs: attention_back_kernel(0, *refs),
            "attention_back_a",
            [grad_a_out] + sums,
            back_args,
            None,
            back_scratch,
        )
        ffn_out = near[4] + core(near[5], "out_near").astype(F32)
        tied = lax.optimization_barrier((got_a, ahead_rows, ffn_out, grad_a0))
        got_a, ahead_rows, ffn_out = tied[:3]
        total_out = (attn_out + ffn_out + ahead_rows.astype(F32)).astype(BF16)
        big_a = split(keep_a, got_a)
        rows_o = keep_o.astype(F32) + core(send_o, "go").astype(F32)
        rows_keep, rows_send = rows_o[:, :half_width], rows_o[:, half_width:].astype(BF16)
        tied = lax.optimization_barrier((sums_out[0], total_out, rows_keep, rows_send, *big_a))
        sums_out[0], total_out, rows_keep, rows_send = tied[:4]
        big_a = along(tied[4:])
        rows_got = ctx(rows_send, "go")
        send_out = spread_parts(total_out)
        grad_a1, grad_bq, *sends = call(
            lambda *refs: attention_back_kernel(1, *refs),
            "attention_back_b",
            [grad_a_out, sums[0]] + [((kv_rows, block), BF16)] * extra + [((kv_rows, block), F32)],
            (*back_args, *sums_out),
            None,
            [pltpu.VMEM(shape, kind) for shape, kind in sums[1:]] + back_scratch,
        )
        tied = lax.optimization_barrier((*sends[:extra], *big_a, *send_out[:2]))
        sends[:extra] = tied[:extra]
        big_a = list(tied[extra : extra + n_f])
        send_out = (*tied[extra + n_f :], *send_out[2:])
        got = []
        for j in range(extra):
            with jax.named_scope("x_kv_back"):
                got.append(
                    lax.ppermute(
                        sends[j],
                        ("ctx", "tp"),
                        [(i + extra - j, i) for i in range(n_place - extra + j)],
                    )
                )
        big_b = split(after(keep_b, got[extra - 1]), got_b)
        tied = lax.optimization_barrier((*got, rows_got, *big_b))
        got, rows_got, big_b = tied[:extra], tied[extra], tied[extra + 1 :]
        big_b = along(big_b)

        delta, keep_p, send_p = call(
            last_kernel,
            "last",
            [
                ((block, width), BF16),
                ((n_c, 2, n_f, pack_rows, LANES), BF16),
                ((n_c, 2, n_f, pack_rows, LANES), BF16),
            ],
            (
                resid_in,
                sends[extra],
                *got,
                grad_bq,
                grad_a0,
                grad_a1,
                cosine,
                sine,
                weight_b,
                weight_a,
                normed,
                gains,
                delta_mid,
                gain_grad,
            ),
            [OWN] + [WHOLE] * 15,
            [
                pltpu.VMEM((width, b_cols), F32),
                pltpu.VMEM((n_tp, a_pad, width), F32),
                pltpu.VMEM((block, width), F32),
                pltpu.VMEM((8, width), F32),
            ],
        )

        send_delta = spread_parts(delta)
        part = keep_p.astype(F32) + core(send_p, "gp").astype(F32)
        part_got = ctx(part[1].astype(BF16), "gp")
        rows_o = rows_keep + rows_got.astype(F32)
        rows_go = chip(rows_o[o_rows:].astype(BF16), "go")
        block_out = add_rows(after(resid_in, part), send_out, True)
        resid_grad = add_rows(after(cotangent, block_out), send_delta, False)
        tied = lax.optimization_barrier((part_got, rows_go, *big_b, resid_grad))
        part_got, rows_go, big_b = tied[0], tied[1], tied[2 : 2 + n_f]
        part = part[0] + part_got.astype(F32)
        rows_o = rows_o[:o_rows] + rows_go.astype(F32)
        part_send = part[1].astype(BF16)
        part = part[0] + chip(part_send, "gp").astype(F32)
        rows_o = rows_o.reshape(o_rows, n_f, LANES)
        part = [jnp.concatenate([part[s], rows_o[:, s]], axis=0) for s in range(n_f)]
        part = [part[s] if s == 0 else part[s].astype(BF16) for s in range(n_f)]
        big_a[0] = after(big_a[0], *part)
        part = along(part)
        grad_gate_up, grad_down = call(
            finish_kernel,
            "finish",
            [
                ((1, 2, hidden, fc_cols), F32),
                ((1, hidden, fc_cols), F32),
            ],
            (*big_a, *big_b),
            None,
            [pltpu.VMEM((3 * hidden, LANES), F32)],
        )

        part_b, part_a, part_g0, part_g1, grad_out = call(
            unpack_kernel,
            "unpack",
            [
                ((1, b_rows, b_cols), F32),
                ((1, a_cols, fc_cols), F32),
                ((1, gain_part), F32),
                ((1, gain_part), F32),
                ((1, o_rows, LANES), F32),
            ],
            tuple(part),
        )
        return (
            block_out,
            resid_grad,
            part_a.transpose(0, 2, 1),
            part_b,
            grad_out,
            grad_gate_up.transpose(0, 1, 3, 2),
            grad_down,
            part_g0,
            part_g1,
        )

    return shards


def make_shards(mesh):
    fused, general = make_fused(mesh), make_general(mesh)

    def shards(*args):
        return (fused if args[7].shape[2] == LANES else general)(*args)

    return shards


def solution(mesh):
    return jax.shard_map(
        make_shards(mesh),
        mesh=mesh,
        in_specs=(
            P("fsdp", "ctx", None),
            P("fsdp", None),
            P("fsdp", "ctx", None),
            P(None, ("fsdp", "ctx"), "tp"),
            P(None, ("fsdp", "ctx", "tp"), None),
            P(None, "tp", ("fsdp", "ctx")),
            P(None, None, ("fsdp", "ctx"), "tp"),
            P(None, "tp", ("fsdp", "ctx")),
            P(None, ("fsdp", "ctx", "tp")),
            P(None, ("fsdp", "ctx", "tp")),
        ),
        out_specs=(
            P("fsdp", "ctx", None),
            P("fsdp", "ctx", None),
            P(None, ("fsdp", "ctx"), "tp"),
            P(None, ("fsdp", "ctx", "tp"), None),
            P(None, "tp", ("fsdp", "ctx")),
            P(None, None, ("fsdp", "ctx"), "tp"),
            P(None, "tp", ("fsdp", "ctx")),
            P(None, ("fsdp", "ctx", "tp")),
            P(None, ("fsdp", "ctx", "tp")),
        ),
        check_vma=False,
    )
```

```python
import math

import jax
import jax.numpy as jnp
from jax import lax
from jax.experimental import pallas as pl
from jax.experimental.pallas import tpu as pltpu
from jax.sharding import PartitionSpec as P

HEAD_DIM = 64
RANK_Q = 6
RANK_KV = 2
RANKS = 10
KV = 2 * RANK_KV
MOST_DOC = 768
EPSILON = 1e-05
LANES = 128
BF16 = jnp.bfloat16
F32 = jnp.float32
MASKED = -1e30


def inverse_rms(values):
    return lax.rsqrt(jnp.mean(values * values, axis=-1, keepdims=True) + EPSILON)


def norm_back(grad_value, values, inverse, gain):
    scaled = grad_value * gain
    normal = values * inverse
    return inverse * (scaled - normal * jnp.mean(scaled * normal, axis=-1, keepdims=True))


def dot(left, right, dims):
    return lax.dot_general(left, right, (dims, ((), ())), preferred_element_type=F32)


def shift(value, axes, size, step, label="shift"):
    with jax.named_scope(label):
        return lax.ppermute(value, axes, [(i, (i + step) % size) for i in range(size)])


def swap(value, axis, size, bit, label="swap"):
    with jax.named_scope(label):
        return lax.ppermute(value, axis, [(i, i ^ bit) for i in range(size)])


def gather_direct(value, axis, size):
    me = lax.axis_index(axis)
    parts = [(me, value)]
    for step in range(1, size):
        parts.append(((me - step) % size, shift(value, axis, size, step)))
    out = jnp.zeros((size,) + value.shape, value.dtype)
    for place, part in parts:
        out = lax.dynamic_update_slice(out, part[None], (place,) + (0,) * value.ndim)
    return out


def gather_pair(value, axis, size, bit):
    mine = (lax.axis_index(axis) // bit) % 2 == 0
    other = swap(value, axis, size, bit)
    return jnp.stack([jnp.where(mine, value, other), jnp.where(mine, other, value)])


def after(value, *others):
    return lax.optimization_barrier((value,) + others)[0]


def take(value, index):
    return lax.dynamic_index_in_dim(value, index, 0, keepdims=False)


def scatter_direct(value, axis, size):
    me = lax.axis_index(axis)
    got = [
        shift(take(value, (me + step) % size), axis, size, step) for step in range(1, size)
    ]
    total = take(value, me).astype(F32)
    for part in got:
        total = total + part.astype(F32)
    return total


def scatter_pair(value, axis, size, bit):
    mine = (lax.axis_index(axis) // bit) % 2
    got = swap(take(value, 1 - mine).astype(BF16), axis, size, bit)
    return take(value, mine).astype(F32) + got.astype(F32)


def attention_mask(first_ref, window, block):
    start = first_ref[...]
    place = lax.broadcasted_iota(jnp.int32, (window, block), 0)
    query_place = lax.broadcasted_iota(jnp.int32, (window, block), 1) + (window - block)
    return jnp.where((place >= start) & (place <= query_place), 0.0, MASKED)


def head_rows(wa_ref, wide_ref, head):
    factors = wa_ref[head].astype(F32)
    key_rows = (factors[0:1] * wide_ref[0] + factors[1:2] * wide_ref[1]) * (1.0 / RANK_KV)
    value_rows = (factors[2:3] * wide_ref[2] + factors[3:4] * wide_ref[3]) * (1.0 / RANK_KV)
    return factors, key_rows.astype(BF16), value_rows.astype(BF16)


def forward_kernel(
    first_ref, a_ref, bq_ref, wa_ref, wb_ref, mixed_ref, lse_ref, q_ref, bias_ref, wide_ref, s_ref
):
    heads = a_ref.shape[0]
    window, block = bias_ref.shape
    bias_ref[...] = attention_mask(first_ref, window, block)
    wide_ref[...] = wb_ref[...].astype(F32)
    spans = [pl.ds(j * block, block) for j in range(window // block)]

    def one_head(head, carry):
        factors = a_ref[head]
        query = factors[0:1] * bq_ref[0]
        for r in range(1, RANK_Q):
            query = query + factors[r : r + 1] * bq_ref[r]
        query = (query * (1.0 / RANK_Q)).astype(BF16) * jnp.asarray(HEAD_DIM**-0.5, BF16)
        q_ref[head] = query
        _, key_rows, value_rows = head_rows(wa_ref, wide_ref, head)
        top = jnp.full((1, block), MASKED, F32)
        for j, span in enumerate(spans):
            keys = key_rows[:, j * block : (j + 1) * block]
            scores = dot(keys, query, ((0,), (0,))) + bias_ref[span, :]
            s_ref[span, :] = scores
            top = jnp.maximum(top, jnp.max(scores, axis=0, keepdims=True))
        total = jnp.zeros((1, block), F32)
        for span in spans:
            weight = jnp.exp(s_ref[span, :] - top)
            s_ref[span, :] = weight
            total = total + jnp.sum(weight, axis=0, keepdims=True)
        lse_ref[head] = top + jnp.log(total)
        scale = 1.0 / total
        mixed = jnp.zeros((HEAD_DIM, block), F32)
        for j, span in enumerate(spans):
            probs = (s_ref[span, :] * scale).astype(BF16)
            mixed = mixed + dot(
                value_rows[:, j * block : (j + 1) * block], probs, ((1,), (0,))
            )
        mixed_ref[head] = mixed.astype(BF16)
        return carry

    lax.fori_loop(0, heads, one_head, 0)


def backward_kernel(
    first_ref,
    a_ref,
    bq_ref,
    wa_ref,
    wb_ref,
    lse_ref,
    q_ref,
    go_ref,
    ga_ref,
    gbq_ref,
    gwa_ref,
    gwb_ref,
    bias_ref,
    wide_ref,
    p_ref,
    dp_ref,
):
    heads = a_ref.shape[0]
    window, block = bias_ref.shape
    bias_ref[...] = attention_mask(first_ref, window, block)
    wide_ref[...] = wb_ref[...].astype(F32)
    gbq_ref[...] = jnp.zeros_like(gbq_ref)
    gwb_ref[...] = jnp.zeros_like(gwb_ref)
    count = window // block
    spans = [pl.ds(j * block, block) for j in range(count)]

    def one_head(head, carry):
        factors, key_rows, value_rows = head_rows(wa_ref, wide_ref, head)
        query = q_ref[head]
        grad_out = go_ref[head]
        lse = lse_ref[head]
        inner = jnp.zeros((1, block), F32)
        for j, span in enumerate(spans):
            cut = slice(j * block, (j + 1) * block)
            scores = dot(key_rows[:, cut], query, ((0,), (0,))) + bias_ref[span, :]
            probs = jnp.exp(scores - lse)
            grad_probs = dot(value_rows[:, cut], grad_out, ((0,), (0,)))
            p_ref[span, :] = probs
            dp_ref[span, :] = grad_probs
            inner = inner + jnp.sum(probs * grad_probs, axis=0, keepdims=True)
        grad_query = jnp.zeros((HEAD_DIM, block), F32)
        for j, span in enumerate(spans):
            cut = slice(j * block, (j + 1) * block)
            probs = p_ref[span, :]
            grad_scores = (probs * (dp_ref[span, :] - inner)).astype(BF16)
            grad_query = grad_query + dot(key_rows[:, cut], grad_scores, ((1,), (0,)))
            grad_keys = dot(query, grad_scores, ((1,), (1,))) * (1.0 / RANK_KV)
            grad_values = dot(grad_out, probs.astype(BF16), ((1,), (1,))) * (1.0 / RANK_KV)
            rows = []
            for r in range(KV):
                grad = grad_keys if r < RANK_KV else grad_values
                rows.append(jnp.sum(grad * wide_ref[r, :, span], axis=0, keepdims=True))
                gwb_ref[r, :, span] += factors[r : r + 1, cut] * grad
            gwa_ref[head, :, span] = jnp.concatenate(rows, axis=0)
        grad_query = grad_query * (HEAD_DIM**-0.5 / RANK_Q)
        own = a_ref[head]
        rows = []
        for r in range(RANK_Q):
            rows.append(jnp.sum(grad_query * bq_ref[r], axis=0, keepdims=True))
            gbq_ref[r] += own[r : r + 1] * grad_query
        ga_ref[head] = jnp.concatenate(rows, axis=0)
        return carry

    lax.fori_loop(0, heads, one_head, 0)


VMEM_LIMIT = 56 * 1024 * 1024


def whole_specs(count):
    return [pl.BlockSpec(memory_space=pltpu.VMEM)] * count


def attend_forward(first, a_rows, b_query, win_a, win_b):
    heads, _, block = a_rows.shape
    window = win_a.shape[-1]
    return pl.pallas_call(
        forward_kernel,
        out_shape=(
            jax.ShapeDtypeStruct((heads, HEAD_DIM, block), BF16),
            jax.ShapeDtypeStruct((heads, 1, block), F32),
            jax.ShapeDtypeStruct((heads, HEAD_DIM, block), BF16),
        ),
        in_specs=whole_specs(5),
        out_specs=tuple(whole_specs(3)),
        scratch_shapes=[
            pltpu.VMEM((window, block), F32),
            pltpu.VMEM((KV, HEAD_DIM, window), F32),
            pltpu.VMEM((window, block), F32),
        ],
        compiler_params=pltpu.CompilerParams(vmem_limit_bytes=VMEM_LIMIT),
        name="attend_forward",
    )(first, a_rows, b_query, win_a, win_b)


def attend_backward(first, a_rows, b_query, win_a, win_b, lse, query, grad_mixed):
    heads, _, block = a_rows.shape
    window = win_a.shape[-1]
    return pl.pallas_call(
        backward_kernel,
        out_shape=(
            jax.ShapeDtypeStruct((heads, RANK_Q, block), F32),
            jax.ShapeDtypeStruct((RANK_Q, HEAD_DIM, block), F32),
            jax.ShapeDtypeStruct((heads, KV, window), F32),
            jax.ShapeDtypeStruct((KV, HEAD_DIM, window), F32),
        ),
        in_specs=whole_specs(8),
        out_specs=tuple(whole_specs(4)),
        scratch_shapes=[
            pltpu.VMEM((window, block), F32),
            pltpu.VMEM((KV, HEAD_DIM, window), F32),
            pltpu.VMEM((window, block), F32),
            pltpu.VMEM((window, block), F32),
        ],
        compiler_params=pltpu.CompilerParams(vmem_limit_bytes=VMEM_LIMIT),
        name="attend_backward",
    )(first, a_rows, b_query, win_a, win_b, lse, query, grad_mixed)


def rotate(rows, cosine, sine):
    half = HEAD_DIM // 2
    lower, upper = rows[:, :half], rows[:, half:]
    return jnp.concatenate(
        [lower * cosine - upper * sine, lower * sine + upper * cosine], axis=1
    )


def make_general(mesh):
    n_f, n_c, n_tp = mesh.shape["fsdp"], mesh.shape["ctx"], mesh.shape["tp"]
    n_hi, n_lo = 2, n_tp // 2

    def shards(
        resid_in,
        segment_ids,
        cotangent,
        w_factor_a,
        w_factor_b,
        w_out,
        w_gate_up,
        w_down,
        attn_gains,
        ffn_gains,
    ):
        seq_count, local_len, width = resid_in.shape
        assert seq_count == 1 and w_factor_a.shape[0] == 1 and n_lo == 2
        full_len = segment_ids.shape[1]
        block = local_len // n_tp
        extra = -(-(MOST_DOC - 1) // block)
        window = (extra + 1) * block
        a_cols = w_factor_a.shape[2]
        heads = n_tp * a_cols // RANKS
        b_cols = w_factor_b.shape[2]
        b_rows = w_factor_b.shape[1]
        b_parts = b_cols // LANES
        fc_cols = w_down.shape[2]
        hidden = w_down.shape[1]
        o_rows = w_out.shape[1]

        f_index, c_index, t_index = (
            lax.axis_index("fsdp"),
            lax.axis_index("ctx"),
            lax.axis_index("tp"),
        )
        hi, lo = t_index // 2, t_index % 2
        place = c_index * n_tp + t_index
        n_place = n_c * n_tp

        gains = jnp.concatenate([attn_gains, ffn_gains], axis=1).astype(BF16)
        gain_count = gains.shape[1]
        gain_rows = 16 * (-(-gain_count // (16 * LANES)))
        gains = jnp.pad(gains.reshape(-1), (0, gain_rows * LANES - gain_count))
        b_shard = w_factor_b[0].astype(BF16).reshape(b_rows, b_parts, LANES)
        a_shard = w_factor_a[0].astype(BF16).T
        pack = jnp.concatenate(
            [
                b_shard.transpose(1, 0, 2).reshape(-1, LANES),
                a_shard.reshape(-1, LANES),
                gains.reshape(-1, LANES),
            ],
            axis=0,
        )
        n_b = b_parts * b_rows
        n_a = a_cols * fc_cols // LANES
        pack = gather_direct(pack, "fsdp", n_f)
        after_pack = pack
        pack = gather_pair(pack, "ctx", n_c, 1)
        pack = gather_pair(pack, "tp", n_tp, 2)
        pack = gather_pair(pack, "tp", n_tp, 1)
        pack = pack.transpose(3, 2, 1, 0, 4, 5)
        weight_b = pack[:, :, :, :, :n_b].reshape(-1, b_parts, b_rows, LANES)
        weight_b = weight_b.transpose(0, 2, 1, 3).reshape(width, b_cols)
        weight_a = pack[:, :, :, :, n_b : n_b + n_a].reshape(n_f, n_c, n_tp, a_cols, fc_cols)
        weight_a = weight_a.transpose(2, 3, 0, 1, 4).reshape(n_tp * a_cols, width)
        gains_all = pack[:, :, :, :, n_b + n_a :].reshape(-1, gain_rows * LANES)[:, :gain_count]
        gains_all = gains_all.reshape(-1, 2, gain_count // 2).transpose(1, 0, 2)
        gains_all = gains_all.reshape(2, width).astype(F32)
        gain_attn, gain_ffn = gains_all[0:1], gains_all[1:2]

        big = jnp.concatenate(
            [
                w_gate_up[0, 0].astype(BF16).T,
                w_gate_up[0, 1].astype(BF16).T,
                w_down[0].astype(BF16),
                w_out[0].astype(BF16),
            ],
            axis=0,
        )
        big, _ = lax.optimization_barrier((big, after_pack))
        big = gather_direct(big, "fsdp", n_f)
        big = gather_pair(big, "ctx", n_c, 1)
        big = big.transpose(2, 1, 0, 3).reshape(-1, width)
        weight_g = big[:hidden]
        weight_u = big[hidden : 2 * hidden]
        weight_d = big[2 * hidden : 3 * hidden]
        weight_o = gather_pair(big[3 * hidden :], "tp", n_tp, 2)
        weight_o = gather_pair(weight_o, "tp", n_tp, 1)
        weight_o = weight_o.transpose(1, 0, 2, 3).reshape(n_tp * o_rows, width)

        seg_here = lax.dynamic_slice_in_dim(segment_ids[0], place * block, block, 0)
        first = jnp.sum((segment_ids[0][:, None] < seg_here[None, :]).astype(jnp.int32), axis=0)
        token = place * block + jnp.arange(block, dtype=jnp.int32)
        position = (token - first).astype(F32)
        first = (first - place * block + extra * block).reshape(1, block)
        frequency = 10000.0 ** (
            -2.0 * jnp.arange(HEAD_DIM // 2, dtype=F32) / HEAD_DIM
        )
        angles = frequency[:, None] * position[None, :]
        cosine, sine = jnp.cos(angles)[None], jnp.sin(angles)[None]

        stream = resid_in[0].reshape(n_tp, block, width)
        own = take(stream, t_index)
        inverse_attn = inverse_rms(own)
        normed = (own * inverse_attn * gain_attn).astype(BF16)
        a_rows = dot(weight_a, normed, ((1,), (1,))).reshape(heads, RANKS, block)
        b_raw = dot(weight_b, normed, ((0,), (1,))).reshape(RANKS, HEAD_DIM, block)
        b_rot = rotate(b_raw[: RANK_Q + RANK_KV], cosine, sine)
        b_query = b_rot[:RANK_Q]
        b_kv = jnp.concatenate([b_rot[RANK_Q:], b_raw[RANK_Q + RANK_KV :]], axis=0)
        payload = jnp.concatenate(
            [
                b_kv.reshape(KV * HEAD_DIM, block),
                a_rows[:, RANK_Q:].reshape(heads * KV, block),
            ],
            axis=0,
        ).astype(BF16)
        around = [
            lax.ppermute(
                payload, ("ctx", "tp"), [(i, i + step) for i in range(n_place - step)]
            )
            for step in range(extra, 0, -1)
        ]
        win = jnp.concatenate(around + [payload], axis=1)
        win_b = win[: KV * HEAD_DIM].reshape(KV, HEAD_DIM, window)
        win_a = win[KV * HEAD_DIM :].reshape(heads, KV, window)

        mixed, lse, query = attend_forward(first, a_rows, b_query, win_a, win_b)
        mixed = mixed.reshape(heads * HEAD_DIM, block)
        attn_out = dot(mixed, weight_o, ((0,), (0,)))
        mid = own + attn_out
        inverse_ffn = inverse_rms(mid)
        normed_ffn = (mid * inverse_ffn * gain_ffn).astype(BF16)

        near_rows = gather_pair(normed_ffn, "tp", n_tp, 1)
        far_rows = gather_pair(swap(normed_ffn, "tp", n_tp, 2), "tp", n_tp, 1)
        grad_all = cotangent[0].reshape(n_hi, n_lo * block, width)

        def half(rows, grad_rows):
            rows = rows.reshape(n_lo * block, width)
            gate = dot(rows, weight_g, ((1,), (1,)))
            up = dot(rows, weight_u, ((1,), (1,)))
            grad_act = dot(grad_rows, weight_d, ((1,), (1,)))
            squash = jax.nn.sigmoid(gate)
            act = (gate * squash * up).astype(BF16)
            grad_gate = (grad_act * up * squash * (1.0 + gate * (1.0 - squash))).astype(BF16)
            grad_up = (grad_act * gate * squash).astype(BF16)
            back = dot(grad_gate, weight_g, ((1,), (0,))) + dot(grad_up, weight_u, ((1,), (0,)))
            ahead = dot(act, weight_d, ((1,), (0,)))
            both = lambda v: v.reshape(n_lo, block, width)
            return rows, act, grad_gate, grad_up, both(back), both(ahead)

        grad_near = take(grad_all, hi).astype(BF16)
        grad_far = take(grad_all, 1 - hi).astype(BF16)
        near = half(near_rows, grad_near)
        far = half(far_rows, grad_far)
        back_far = scatter_pair(far[4], "tp", n_tp, 1).astype(BF16)
        back_far = swap(back_far, "tp", n_tp, 2)
        grad_normed_ffn = scatter_pair(near[4], "tp", n_tp, 1) + back_far.astype(F32)
        ahead_far = scatter_pair(far[5], "tp", n_tp, 1).astype(BF16)
        ahead_far = swap(ahead_far, "tp", n_tp, 2)
        ffn_out = scatter_pair(near[5], "tp", n_tp, 1) + ahead_far.astype(F32)

        def spread(value):
            beside = swap(value, "tp", n_tp, 1)
            across = swap(value, "tp", n_tp, 2)
            diagonal = swap(across, "tp", n_tp, 1)
            out = jnp.zeros((n_tp,) + value.shape, value.dtype)
            for bit, part in enumerate((value, beside, across, diagonal)):
                out = lax.dynamic_update_slice(out, part[None], (t_index ^ bit, 0, 0))
            return out.reshape(local_len, width).astype(F32)

        block_out = resid_in + spread((attn_out + ffn_out).astype(BF16))[None]

        def columns(value, which):
            value = value.reshape(value.shape[0], n_f, n_c, fc_cols)
            value = lax.dynamic_index_in_dim(value, which, 2, keepdims=False)
            return value.reshape(value.shape[0], n_f * fc_cols)

        rows_all = jnp.concatenate([near[0], far[0]], axis=0)
        act_all = jnp.concatenate([near[1], far[1]], axis=0)
        gate_all = jnp.concatenate([near[2], far[2]], axis=0)
        up_all = jnp.concatenate([near[3], far[3]], axis=0)
        cot_all = jnp.concatenate([grad_near, grad_far], axis=0)

        def big_grads(which):
            rows_cut = columns(rows_all, which)
            cot_cut = columns(cot_all, which)
            return jnp.concatenate(
                [
                    dot(gate_all, rows_cut, ((0,), (0,))),
                    dot(up_all, rows_cut, ((0,), (0,))),
                    dot(act_all, cot_cut, ((0,), (0,))),
                ],
                axis=0,
            )

        def over_fc(send, keep):
            total = keep + swap(send.astype(BF16), "ctx", n_c, 1).astype(F32)
            total = total.astype(BF16).reshape(-1, n_f, fc_cols).transpose(1, 0, 2)
            return scatter_direct(total, "fsdp", n_f)

        grad_big = over_fc(big_grads(1 - c_index), big_grads(c_index))
        grad_gate_w = grad_big[:hidden].T
        grad_up_w = grad_big[hidden : 2 * hidden].T
        grad_down_w = grad_big[2 * hidden :]

        own_cot = take(cotangent[0].reshape(n_tp, block, width), t_index)
        gain_grad_ffn = jnp.sum(grad_normed_ffn * mid * inverse_ffn, axis=0)
        delta_mid = norm_back(grad_normed_ffn, mid, inverse_ffn, gain_ffn)
        grad_attn = (own_cot + delta_mid).astype(BF16)
        grad_out = dot(mixed, grad_attn, ((1,), (0,))).reshape(n_hi, n_lo, o_rows, width)
        grad_out = scatter_pair(grad_out.transpose(1, 0, 2, 3), "tp", n_tp, 1)
        grad_out = scatter_pair(grad_out, "tp", n_tp, 2)
        grad_out = over_fc(columns(grad_out, 1 - c_index), columns(grad_out, c_index))

        grad_mixed = dot(weight_o, grad_attn, ((1,), (1,))).astype(BF16)
        ga_q, gb_q, gw_a, gw_b = attend_backward(
            first,
            a_rows,
            b_query,
            win_a,
            win_b,
            lse,
            query,
            grad_mixed.reshape(heads, HEAD_DIM, block),
        )
        gw = jnp.concatenate(
            [gw_b.reshape(KV * HEAD_DIM, window), gw_a.reshape(heads * KV, window)], axis=0
        )
        total = gw[:, extra * block :]
        for step in range(1, extra + 1):
            part = gw[:, (extra - step) * block : (extra - step + 1) * block].astype(BF16)
            part = lax.ppermute(
                part, ("ctx", "tp"), [(i + step, i) for i in range(n_place - step)]
            )
            total = total + part.astype(F32)
        gb_kv = total[: KV * HEAD_DIM].reshape(KV, HEAD_DIM, block)
        ga_kv = total[KV * HEAD_DIM :].reshape(heads, KV, block)
        grad_b = jnp.concatenate(
            [
                rotate(jnp.concatenate([gb_q, gb_kv[:RANK_KV]], axis=0), cosine, -sine),
                gb_kv[RANK_KV:],
            ],
            axis=0,
        )
        grad_b = grad_b.reshape(b_cols, block).astype(BF16)
        grad_a = jnp.concatenate([ga_q, ga_kv], axis=1).reshape(heads * RANKS, block).astype(BF16)
        grad_normed = dot(grad_a, weight_a, ((0,), (0,))) + dot(grad_b, weight_b, ((0,), (1,)))
        gain_grad_attn = jnp.sum(grad_normed * own * inverse_attn, axis=0)
        delta = delta_mid + norm_back(grad_normed, own, inverse_attn, gain_attn)
        resid_grad = cotangent + spread(delta.astype(BF16))[None]

        grad_wa = dot(grad_a, normed, ((1,), (0,))).astype(BF16)
        grad_wa = grad_wa.reshape(n_hi, n_lo, a_cols, n_f, n_c, fc_cols)
        grad_wa = grad_wa.transpose(1, 0, 4, 3, 2, 5).reshape(n_lo, n_hi, n_c, n_f, n_a, LANES)
        grad_wb = jnp.einsum(
            "pkt,td->pdk",
            grad_b.reshape(b_parts, LANES, block),
            normed,
            preferred_element_type=F32,
        ).astype(BF16)
        grad_wb = grad_wb.reshape(b_parts, n_f, n_c, n_hi, n_lo, b_rows, LANES)
        grad_wb = grad_wb.transpose(4, 3, 2, 1, 0, 5, 6)
        grad_wb = grad_wb.reshape(n_lo, n_hi, n_c, n_f, n_b, LANES)
        gain_grads = jnp.stack([gain_grad_attn, gain_grad_ffn]).astype(BF16)
        gain_grads = gain_grads.reshape(2, n_f, n_c, n_hi, n_lo, gain_count // 2)
        gain_grads = gain_grads.transpose(4, 3, 2, 1, 0, 5).reshape(
            n_lo, n_hi, n_c, n_f, gain_count
        )
        gain_grads = jnp.pad(
            gain_grads, [(0, 0)] * 4 + [(0, gain_rows * LANES - gain_count)]
        ).reshape(n_lo, n_hi, n_c, n_f, gain_rows, LANES)
        pack = jnp.concatenate([grad_wb, grad_wa, gain_grads], axis=4)
        pack = scatter_pair(pack, "tp", n_tp, 1)
        pack = scatter_pair(pack, "tp", n_tp, 2)
        pack = scatter_pair(pack, "ctx", n_c, 1).astype(BF16)
        pack = scatter_direct(pack, "fsdp", n_f)
        part_b = pack[:n_b].reshape(b_parts, b_rows, LANES).transpose(1, 0, 2)
        part_b = part_b.reshape(1, b_rows, b_cols)
        part_a = pack[n_b : n_b + n_a].reshape(a_cols, fc_cols).T[None]
        part_gain = pack[n_b + n_a :].reshape(-1)[:gain_count].reshape(2, 1, gain_count // 2)
        return (
            block_out,
            resid_grad,
            part_a,
            part_b,
            grad_out[None],
            jnp.stack([grad_gate_w, grad_up_w])[None],
            grad_down_w[None],
            part_gain[0],
            part_gain[1],
        )

    return shards


def rotated(rows, cosine, sine):
    half = HEAD_DIM // 2
    lower, upper = rows[:half], rows[half:]
    return jnp.concatenate([lower * cosine - upper * sine, lower * sine + upper * cosine], axis=0)


def make_fused(mesh):
    n_f, n_c, n_tp = mesh.shape["fsdp"], mesh.shape["ctx"], mesh.shape["tp"]
    n_piece = n_f * n_c
    AT_TP = n_piece
    AT_ME = n_piece + n_tp

    def shards(
        resid_in,
        segment_ids,
        cotangent,
        w_factor_a,
        w_factor_b,
        w_out,
        w_gate_up,
        w_down,
        attn_gains,
        ffn_gains,
    ):
        _, local_len, width = resid_in.shape
        block = local_len // n_tp
        extra = -(-(MOST_DOC - 1) // block)
        windows = extra + 1
        a_cols = w_factor_a.shape[2]
        group = a_cols // RANKS
        heads = n_tp * group
        feats = group * HEAD_DIM
        a_pad = 16 * (-(-a_cols // 16))
        b_rows, b_cols = w_factor_b.shape[1:]
        b_parts = b_cols // LANES
        n_b = b_parts * b_rows
        pack_rows = n_b + a_pad + 16
        fc_cols = w_down.shape[2]
        hidden = w_down.shape[1]
        o_rows = w_out.shape[1]
        gain_part = attn_gains.shape[1]
        kv_b = KV * HEAD_DIM
        kv_rows = kv_b + heads * KV
        half_width = width // n_c
        assert n_f == 4 and fc_cols == LANES and o_rows == feats and n_tp == 4 and n_c == 2

        f_index, c_index, t_index = (
            lax.axis_index("fsdp"),
            lax.axis_index("ctx"),
            lax.axis_index("tp"),
        )
        place = c_index * n_tp + t_index
        n_place = n_c * n_tp
        columns = [
            ((f_index - s) % n_f) * n_c + (c_index if near == 0 else 1 - c_index)
            for near in range(n_c)
            for s in range(n_f)
        ]
        members = [t_index ^ (lo + 2 * hi) for lo in range(2) for hi in range(2)]
        beside_shift = jnp.where(f_index % 2 == 0, n_f - 1, 1)
        meta = jnp.stack(columns + members + [t_index, f_index, beside_shift]).astype(jnp.int32)

        resid_in = pltpu.with_memory_space_constraint(resid_in, pltpu.HBM)
        cotangent = pltpu.with_memory_space_constraint(cotangent, pltpu.HBM)

        def column(meta_ref, j):
            return pl.ds(pl.multiple_of(meta_ref[j] * LANES, LANES), LANES)

        def member(meta_ref, lo, hi):
            return meta_ref[AT_TP + 2 * lo + hi]

        def to_arrival(meta_ref, load):
            return jnp.concatenate([load(column(meta_ref, j)) for j in range(n_piece)], axis=1)

        WHOLE = pl.BlockSpec(memory_space=pltpu.VMEM)
        REMOTE = pl.BlockSpec(memory_space=pl.ANY)
        OWN = pl.BlockSpec((1, block, width), lambda i, m: (0, m[AT_ME], 0))

        def call(
            kernel, name, outs, args, specs=None, scratch=(), grid=(1,), out_specs=None, room=4
        ):
            held = 0
            for arg, spec in zip((*args, *args[:1]), (specs or []) + (out_specs or [])):
                if spec.block_shape:
                    held += 2 * math.prod(spec.block_shape) * arg.dtype.itemsize
            for item in scratch:
                if hasattr(item, "shape") and item.memory_space == pltpu.VMEM:
                    held += math.prod(item.shape) * jnp.dtype(item.dtype).itemsize
            limit = min(held + room * 2**20, VMEM_LIMIT)
            return pl.pallas_call(
                kernel,
                out_shape=[jax.ShapeDtypeStruct(s, d) for s, d in outs],
                grid_spec=pltpu.PrefetchScalarGridSpec(
                    num_scalar_prefetch=1,
                    grid=grid,
                    in_specs=specs or [WHOLE] * len(args),
                    out_specs=out_specs or [WHOLE] * len(outs),
                    scratch_shapes=list(scratch),
                ),
                compiler_params=pltpu.CompilerParams(vmem_limit_bytes=limit),
                name=name,
            )(meta, *args)


        def pack_kernel(meta_ref, b_ref, a_ref, g0_ref, g1_ref, out_ref):
            for k in range(b_parts):
                out_ref[k * b_rows : (k + 1) * b_rows, :] = b_ref[
                    0, :, k * LANES : (k + 1) * LANES
                ].astype(BF16)
            a_shard = jnp.concatenate([a_ref[0], jnp.zeros((a_pad - a_cols, LANES), F32)], axis=0)
            out_ref[n_b : n_b + a_pad, :] = a_shard.astype(BF16)
            both = jnp.concatenate([g0_ref[...], g1_ref[...]], axis=0)
            both = jnp.concatenate([both, jnp.zeros((6, gain_part), F32)], axis=0)
            both = jnp.concatenate([both, jnp.zeros((8, LANES - gain_part), F32)], axis=1)
            both = pltpu.roll(both, meta_ref[AT_ME] * gain_part, 1)
            both = jnp.concatenate([both, jnp.zeros((8, LANES), F32)], axis=0)
            out_ref[n_b + a_pad :, :] = both.astype(BF16)

        def big_kernel(meta_ref, gu_ref, d_ref, gu_out_ref, d_out_ref):
            for k in range(2):
                gu_out_ref[k * hidden : (k + 1) * hidden, :] = gu_ref[0, k].astype(BF16)
            d_out_ref[...] = d_ref[0].astype(BF16)

        def factor_kernel(
            meta_ref,
            x_ref,
            p0_ref,
            p1_ref,
            cos_ref,
            sin_ref,
            wb_ref,
            wa_ref,
            gain_ref,
            normed_ref,
            a_ref,
            bq_ref,
            pay_ref,
        ):
            gain_ref[...] = jnp.zeros_like(gain_ref)
            for lo, hi in ((0, 0), (0, 1), (1, 0), (1, 1)):
                part = (p0_ref, p1_ref)[lo]
                tp = member(meta_ref, lo, hi)
                for near in range(n_c):
                    for s in range(n_f):
                        j = near * n_f + s
                        lanes = column(meta_ref, j)
                        row = pl.multiple_of((meta_ref[j] * n_tp + tp) * b_rows, b_rows)
                        for k in range(b_parts):
                            wb_ref[pl.ds(row, b_rows), k * LANES : (k + 1) * LANES] = part[
                                near, hi, s, k * b_rows : (k + 1) * b_rows, :
                            ]
                        wa_ref[tp, :, lanes] = part[near, hi, s, n_b : n_b + a_pad, :]
                        gain_ref[:, lanes] += part[near, hi, s, n_b + a_pad :, :].astype(F32)
            x = x_ref[0]
            normed = (x * inverse_rms(x) * gain_ref[0:1]).astype(BF16)
            normed_ref[...] = normed
            cosine, sine = cos_ref[...], sin_ref[...]
            b_raw = jnp.transpose(dot(normed, wb_ref[...], ((1,), (0,))))
            for r in range(RANK_Q):
                bq_ref[r] = rotated(b_raw[r * HEAD_DIM : (r + 1) * HEAD_DIM], cosine, sine)
            for r in range(KV):
                rows = b_raw[(RANK_Q + r) * HEAD_DIM : (RANK_Q + r + 1) * HEAD_DIM]
                if r < RANK_KV:
                    rows = rotated(rows, cosine, sine)
                pay_ref[r * HEAD_DIM : (r + 1) * HEAD_DIM, :] = rows.astype(BF16)
            for tp in range(n_tp):
                a_raw = dot(wa_ref[tp], normed, ((1,), (1,)))
                a_ref[tp] = a_raw
                kv = [a_raw[g * RANKS + RANK_Q : (g + 1) * RANKS] for g in range(group)]
                start = kv_b + tp * group * KV
                pay_ref[start : start + group * KV, :] = jnp.concatenate(kv, axis=0).astype(BF16)

        def set_mask(first_ref, bias_ref):
            bias_ref[...] = attention_mask(first_ref, windows * block, block)

        def is_even(meta_ref):
            return lax.rem(meta_ref[AT_ME], 2) == 0

        def widen(meta_ref, arrived, win_ref, wide_ref):
            third, second, beside_second, beside, own = arrived
            win_ref[1] = second[...]
            win_ref[3] = own[...]

            @pl.when(is_even(meta_ref))
            def _():
                win_ref[0] = third[...]
                win_ref[2] = beside_second[...]

            @pl.when(jnp.logical_not(is_even(meta_ref)))
            def _():
                win_ref[0] = beside_second[...]
                win_ref[2] = beside[...]

            for j in range(windows):
                for r in range(KV):
                    wide_ref[j, r] = win_ref[j, r * HEAD_DIM : (r + 1) * HEAD_DIM, :].astype(F32)

        def kv_factors(win_ref, tp):
            start = pl.multiple_of(kv_b + tp * (group * KV), group * KV)
            return [win_ref[j, pl.ds(start, group * KV), :].astype(F32) for j in range(windows)]

        def kv_rows_of(factors, wide_ref, g, j):
            def mix(r):
                a0 = factors[j][g * KV + r : g * KV + r + 1]
                a1 = factors[j][g * KV + r + 1 : g * KV + r + 2]
                rows = a0 * wide_ref[j, r] + a1 * wide_ref[j, r + 1]
                return (rows * (1.0 / RANK_KV)).astype(BF16)

            return mix(0), mix(RANK_KV)

        def attention_kernel(
            meta_ref,
            first_ref,
            a_ref,
            bq_ref,
            w0_ref,
            w1_ref,
            w2_ref,
            w3_ref,
            w4_ref,
            lse_ref,
            q_ref,
            mixed_ref,
            win_ref,
            bias_ref,
            wide_ref,
            s_ref,
        ):
            set_mask(first_ref, bias_ref)
            widen(meta_ref, (w0_ref, w1_ref, w2_ref, w3_ref, w4_ref), win_ref, wide_ref)
            spans = [pl.ds(j * block, block) for j in range(windows)]

            def one_group(tp, carry):
                own = a_ref[tp]
                factors = kv_factors(win_ref, tp)
                for g in range(group):
                    query = own[g * RANKS : g * RANKS + 1] * bq_ref[0]
                    for r in range(1, RANK_Q):
                        query = query + own[g * RANKS + r : g * RANKS + r + 1] * bq_ref[r]
                    query = (query * (1.0 / RANK_Q)).astype(BF16)
                    query = query * jnp.asarray(HEAD_DIM**-0.5, BF16)
                    q_ref[tp, g] = query
                    top = jnp.full((1, block), MASKED, F32)
                    values = []
                    for j, span in enumerate(spans):
                        keys, rows = kv_rows_of(factors, wide_ref, g, j)
                        values.append(rows)
                        scores = dot(keys, query, ((0,), (0,))) + bias_ref[span, :]
                        s_ref[g, span, :] = scores
                        top = jnp.maximum(top, jnp.max(scores, axis=0, keepdims=True))
                    total = jnp.zeros((1, block), F32)
                    for span in spans:
                        weight = jnp.exp(s_ref[g, span, :] - top)
                        s_ref[g, span, :] = weight
                        total = total + jnp.sum(weight, axis=0, keepdims=True)
                    lse_ref[tp, g : g + 1, :] = top + jnp.log(total)
                    scale = 1.0 / total
                    mixed = jnp.zeros((HEAD_DIM, block), F32)
                    for j, span in enumerate(spans):
                        probs = (s_ref[g, span, :] * scale).astype(BF16)
                        mixed = mixed + dot(values[j], probs, ((1,), (0,)))
                    mixed_ref[tp, g * HEAD_DIM : (g + 1) * HEAD_DIM, :] = mixed.astype(BF16)
                return carry

            lax.fori_loop(0, n_tp, one_group, 0)

        def project_kernel(
            meta_ref, x_ref, mixed_ref, o0_ref, o1_ref, gain_ref, mid_ref, attn_ref, nf_ref
        ):
            attn = jnp.zeros((block, width), F32)
            for lo, ref in enumerate((o0_ref, o1_ref)):
                for hi in range(2):
                    rows = mixed_ref[member(meta_ref, lo, hi)]
                    attn = attn + dot(rows, ref[hi * o_rows : (hi + 1) * o_rows, :], ((0,), (0,)))
            attn_ref[...] = attn
            mid = to_arrival(meta_ref, lambda lanes: x_ref[0, :, lanes]) + attn
            mid_ref[...] = mid
            gain = to_arrival(meta_ref, lambda lanes: gain_ref[1:2, lanes])
            nf_ref[...] = (mid * inverse_rms(mid) * gain).astype(BF16)

        def ffn_kernel(side, meta_ref, *refs):
            n_refs = refs[:2]
            cot_ref = refs[2]
            own_gu_ref, far_gu_ref, pair_gu_ref, gu_across_ref, gu_rest_ref = refs[3:8]
            dn_refs = refs[8 : 8 + n_f]
            refs = refs[8 + n_f :]
            ht_ref, gb_ref, back0_ref, back1_ref, ahead0_ref, ahead1_ref = refs[:6]
            w_ref, cot_buf, sems = refs[6:]
            gate_up = [own_gu_ref, far_gu_ref, pair_gu_ref.at[0], pair_gu_ref.at[1], gu_across_ref]
            gate_up += [gu_rest_ref.at[s] for s in range(n_f - 1)]
            beside_shift = meta_ref[AT_ME + 2]
            arrivals = [0, 2, beside_shift, n_f - beside_shift]
            down = [ref.at[near] for near in range(n_c) for ref in dn_refs]
            loads = []
            for i in range(2):
                row = pl.multiple_of(member(meta_ref, i, side) * block, block)
                loads.append(
                    pltpu.make_async_copy(
                        cot_ref.at[0, pl.ds(row, block), :], cot_buf.at[i], sems.at[2 * n_piece + i]
                    )
                )
            for j in range(n_piece):
                lanes = pl.ds(j * LANES, LANES)
                at = pl.multiple_of((arrivals[j % n_f] + j // n_f * n_f) * LANES, LANES)
                loads.append(
                    pltpu.make_async_copy(
                        gate_up[j],
                        w_ref.at[pl.ds(0, 2 * hidden), pl.ds(at, LANES)],
                        sems.at[j],
                    )
                )
                loads.append(
                    pltpu.make_async_copy(
                        down[j], w_ref.at[pl.ds(2 * hidden, hidden), lanes], sems.at[n_piece + j]
                    )
                )
            for load in loads:
                load.start()
            for i in range(2):
                loads[i].wait()
                for j in range(n_piece):
                    gb_ref[i * block : (i + 1) * block, j * LANES : (j + 1) * LANES] = cot_buf[
                        i, :, column(meta_ref, j)
                    ].astype(BF16)
            for load in loads[2:]:
                load.wait()
            for i in range(2):
                cut = slice(i * block, (i + 1) * block)
                rows = n_refs[i][...]
                gate = dot(w_ref[0:hidden, :], rows, ((1,), (1,)))
                up = dot(w_ref[hidden : 2 * hidden, :], rows, ((1,), (1,)))
                grad_act = dot(w_ref[2 * hidden :, :], gb_ref[cut, :], ((1,), (1,)))
                squash = jax.nn.sigmoid(gate)
                soft = gate * squash
                ht_ref[2 * hidden :, cut] = (soft * up).astype(BF16)
                ht_ref[0:hidden, cut] = (
                    grad_act * up * squash * (1.0 + gate * (1.0 - squash))
                ).astype(BF16)
                ht_ref[hidden : 2 * hidden, cut] = (grad_act * soft).astype(BF16)
            back = dot(ht_ref[: 2 * hidden, :], w_ref[: 2 * hidden, :], ((0,), (0,)))
            back0_ref[...] = back[:block]
            back1_ref[...] = back[block:].astype(BF16)
            ahead = dot(ht_ref[2 * hidden :, :], w_ref[2 * hidden :, :], ((0,), (0,)))
            ahead0_ref[...] = ahead[:block]
            ahead1_ref[...] = ahead[block:].astype(BF16)

        def weight_grad(refs, start, stop, right):
            hts, n_near, n_far, gbs = refs[0:2], refs[2:4], refs[4:6], refs[6:8]
            total = jnp.zeros((stop - start, width), F32)
            for side in range(2):
                left = hts[side]
                if right == 1:
                    total = total + dot(left[start:stop, :], gbs[side][...], ((1,), (0,)))
                    continue
                for i in range(2):
                    rows = (n_near, n_far)[side][i][...]
                    cut = slice(i * block, (i + 1) * block)
                    total = total + dot(left[start:stop, cut], rows, ((1,), (0,)))
            return total

        def gate_up_grad_kernel(meta_ref, *refs):
            keep_ref, send_ref = refs[8:]
            for k in range(2):
                cut = slice(k * hidden, (k + 1) * hidden)
                total = weight_grad(refs, k * hidden, (k + 1) * hidden, 0)
                keep_ref[cut, :] = total[:, :half_width].astype(BF16)
                send_ref[cut, :] = total[:, half_width:].astype(BF16)

        def down_grad_kernel(meta_ref, *refs):
            keep_ref, send_ref = refs[8:]
            total = weight_grad(refs, 2 * hidden, 3 * hidden, 1)

            def chunk(s, near):
                start = near * half_width + s * LANES
                return total[:, start : start + LANES]

            for near in range(n_c):
                keep_ref[0, near] = chunk(0, near)
                keep_ref[1, near] = chunk(2, near)

            @pl.when(lax.rem(meta_ref[AT_ME + 1], 2) == 0)
            def _():
                for near in range(n_c):
                    send_ref[0, near] = chunk(3, near).astype(BF16)
                    send_ref[1, near] = chunk(1, near).astype(BF16)

            @pl.when(lax.rem(meta_ref[AT_ME + 1], 2) == 1)
            def _():
                for near in range(n_c):
                    send_ref[0, near] = chunk(1, near).astype(BF16)
                    send_ref[1, near] = chunk(3, near).astype(BF16)

        def middle_kernel(
            meta_ref,
            cot_ref,
            back_ref,
            beside_ref,
            across_ref,
            mid_ref,
            gain_ref,
            o0_ref,
            o1_ref,
            mixed_ref,
            dmid_ref,
            gg_ref,
            go_ref,
            keep_ref,
            send_ref,
        ):
            back = back_ref[...] + beside_ref[...].astype(F32) + across_ref[...].astype(F32)
            mid = mid_ref[...]
            inverse = inverse_rms(mid)
            gain = to_arrival(meta_ref, lambda lanes: gain_ref[1:2, lanes])
            normal = mid * inverse
            gains = jnp.sum(back * normal, axis=0, keepdims=True)
            for j in range(n_piece):
                gg_ref[:, column(meta_ref, j)] = jnp.broadcast_to(
                    gains[:, j * LANES : (j + 1) * LANES], (8, LANES)
                )
            scaled = back * gain
            delta = inverse * (
                scaled - normal * jnp.mean(scaled * normal, axis=-1, keepdims=True)
            )
            dmid_ref[...] = delta
            cot = to_arrival(meta_ref, lambda lanes: cot_ref[0, :, lanes])
            grad = (cot + delta).astype(BF16)
            for lo, ref in enumerate((o0_ref, o1_ref)):
                for hi in range(2):
                    tp = member(meta_ref, lo, hi)
                    cut = slice(hi * o_rows, (hi + 1) * o_rows)
                    go_ref[tp] = dot(ref[cut, :], grad, ((1,), (1,))).astype(BF16)
                    weight = dot(mixed_ref[tp], grad, ((1,), (0,))).astype(BF16)
                    (keep_ref, send_ref)[lo][cut, :] = weight

        def attention_back_kernel(
            part,
            meta_ref,
            first_ref,
            a_ref,
            bq_ref,
            w0_ref,
            w1_ref,
            w2_ref,
            w3_ref,
            w4_ref,
            lse_ref,
            q_ref,
            go_ref,
            *refs,
        ):
            win_ref, bias_ref, wide_ref, p_ref, dp_ref = refs[-5:]
            if part == 0:
                ga_ref, gbq_ref, gwb_ref, gwa_ref = refs[:4]
            else:
                ga_ref, gbq_ref, pair_ref, beside_ref, third_ref, own_ref = refs[3:9]
                gwb_ref, gwa_ref = refs[-7:-5]
            set_mask(first_ref, bias_ref)
            widen(meta_ref, (w0_ref, w1_ref, w2_ref, w3_ref, w4_ref), win_ref, wide_ref)
            if part == 0:
                gbq_ref[...] = jnp.zeros_like(gbq_ref)
                gwb_ref[...] = jnp.zeros_like(gwb_ref)
            else:
                gbq_ref[...] = refs[0][...]
                gwb_ref[...] = refs[1][...]
                gwa_ref[...] = refs[2][...]
            spans = [pl.ds(j * block, block) for j in range(windows)]
            first_tp = part * (n_tp // 2)

            def one_group(tp, carry):
                own = a_ref[tp]
                factors = kv_factors(win_ref, tp)
                grad_a = []
                grad_kv = [[] for _ in spans]
                for g in range(group):
                    query = q_ref[tp, g]
                    grad_out = go_ref[tp, g * HEAD_DIM : (g + 1) * HEAD_DIM, :]
                    lse = lse_ref[tp, g : g + 1, :]
                    inner = jnp.zeros((1, block), F32)
                    keys = []
                    for j, span in enumerate(spans):
                        key_rows, value_rows = kv_rows_of(factors, wide_ref, g, j)
                        keys.append(key_rows)
                        scores = dot(key_rows, query, ((0,), (0,))) + bias_ref[span, :]
                        probs = jnp.exp(scores - lse)
                        grad_probs = dot(value_rows, grad_out, ((0,), (0,)))
                        p_ref[g % 2, span, :] = probs
                        dp_ref[g % 2, span, :] = grad_probs
                        inner = inner + jnp.sum(probs * grad_probs, axis=0, keepdims=True)
                    grad_query = jnp.zeros((HEAD_DIM, block), F32)
                    for j, span in enumerate(spans):
                        probs = p_ref[g % 2, span, :]
                        grad_scores = (probs * (dp_ref[g % 2, span, :] - inner)).astype(BF16)
                        grad_query = grad_query + dot(keys[j], grad_scores, ((1,), (0,)))
                        grad_keys = dot(query, grad_scores, ((1,), (1,))) * (1.0 / RANK_KV)
                        grad_values = dot(grad_out, probs.astype(BF16), ((1,), (1,)))
                        grad_values = grad_values * (1.0 / RANK_KV)
                        for r in range(KV):
                            grad = grad_keys if r < RANK_KV else grad_values
                            grad_kv[j].append(
                                jnp.sum(grad * wide_ref[j, r], axis=0, keepdims=True)
                            )
                            gwb_ref[j, r] += factors[j][g * KV + r : g * KV + r + 1] * grad
                    grad_query = grad_query * (HEAD_DIM**-0.5 / RANK_Q)
                    for r in range(RANK_Q):
                        grad_a.append(jnp.sum(grad_query * bq_ref[r], axis=0, keepdims=True))
                        gbq_ref[r] += own[g * RANKS + r : g * RANKS + r + 1] * grad_query
                    grad_a.append(jnp.zeros((KV, block), F32))
                grad_a.append(jnp.zeros((a_pad - a_cols, block), F32))
                ga_ref[tp - first_tp] = jnp.concatenate(grad_a, axis=0)
                start = pl.multiple_of(tp * (group * KV), group * KV)
                for j in range(windows):
                    gwa_ref[j, pl.ds(start, group * KV), :] = jnp.concatenate(grad_kv[j], axis=0)
                return carry

            lax.fori_loop(first_tp, first_tp + n_tp // 2, one_group, 0)
            if part == 0:
                return

            def put(ref, start, j):
                for r in range(KV):
                    row = start + r * HEAD_DIM
                    ref[row : row + HEAD_DIM, :] = gwb_ref[j, r].astype(ref.dtype)
                ref[start + kv_b : start + kv_rows, :] = gwa_ref[j].astype(ref.dtype)

            put(own_ref, 0, 3)
            put(beside_ref, 0, 2)
            put(third_ref, 0, 0)
            put(pair_ref, 0, 1)

            @pl.when(is_even(meta_ref))
            def _():
                put(pair_ref, kv_rows, 2)

            @pl.when(jnp.logical_not(is_even(meta_ref)))
            def _():
                put(pair_ref, kv_rows, 0)

        def last_kernel(
            meta_ref,
            x_ref,
            own_ref,
            pair_ref,
            swapped_ref,
            beside_ref,
            third_ref,
            gbq_ref,
            ga0_ref,
            ga1_ref,
            cos_ref,
            sin_ref,
            wb_ref,
            wa_ref,
            normed_ref,
            gain_ref,
            dmid_ref,
            gg_ref,
            delta_ref,
            keep_ref,
            send_ref,
            b_buf,
            a_buf,
            d_buf,
            g_buf,
        ):
            total = own_ref[...] + pair_ref[:kv_rows, :].astype(F32)
            for ref in (swapped_ref, beside_ref, third_ref):
                total = total + ref[...].astype(F32)
            cosine, sine = cos_ref[...], -sin_ref[...]
            rows = [rotated(gbq_ref[r], cosine, sine) for r in range(RANK_Q)]
            for r in range(KV):
                part = total[r * HEAD_DIM : (r + 1) * HEAD_DIM]
                rows.append(rotated(part, cosine, sine) if r < RANK_KV else part)
            grad_b = jnp.transpose(jnp.concatenate(rows, axis=0)).astype(BF16)
            normed = normed_ref[...]
            back = dot(grad_b, wb_ref[...], ((1,), (1,)))
            for tp in range(n_tp):
                parts = []
                for g in range(group):
                    start = kv_b + (tp * group + g) * KV
                    parts.append(jnp.zeros((RANK_Q, block), F32))
                    parts.append(total[start : start + KV])
                parts.append(jnp.zeros((a_pad - a_cols, block), F32))
                own_a = (ga0_ref, ga1_ref)[tp // 2][tp % 2]
                grad_a = (own_a + jnp.concatenate(parts, axis=0)).astype(BF16)
                back = back + dot(grad_a, wa_ref[tp], ((0,), (0,)))
                a_buf[tp] = dot(grad_a, normed, ((1,), (0,)))
            b_buf[...] = dot(normed, grad_b, ((0,), (0,)))
            x = x_ref[0]
            inverse = inverse_rms(x)
            normal = x * inverse
            gains = jnp.sum(back * normal, axis=0, keepdims=True)
            g_buf[...] = jnp.broadcast_to(gains, (8, width))
            scaled = back * gain_ref[0:1]
            delta = inverse * (
                scaled - normal * jnp.mean(scaled * normal, axis=-1, keepdims=True)
            )
            d_buf[...] = delta
            for j in range(n_piece):
                lanes = column(meta_ref, j)
                cut = slice(j * LANES, (j + 1) * LANES)
                delta_ref[:, lanes] = (d_buf[:, lanes] + dmid_ref[:, cut]).astype(BF16)
            row_index = lax.broadcasted_iota(jnp.int32, (16, LANES), 0)
            for lo, hi in ((0, 0), (0, 1), (1, 0), (1, 1)):
                out = (keep_ref, send_ref)[lo]
                tp = member(meta_ref, lo, hi)
                for near in range(n_c):
                    for s in range(n_f):
                        j = near * n_f + s
                        lanes = column(meta_ref, j)
                        row = pl.multiple_of((meta_ref[j] * n_tp + tp) * b_rows, b_rows)
                        for k in range(b_parts):
                            out[near, hi, s, k * b_rows : (k + 1) * b_rows, :] = b_buf[
                                pl.ds(row, b_rows), k * LANES : (k + 1) * LANES
                            ].astype(BF16)
                        out[near, hi, s, n_b : n_b + a_pad, :] = a_buf[tp, :, lanes].astype(BF16)
                        pair = jnp.where(
                            row_index == 0, g_buf[0:1, lanes], gg_ref[0:1, lanes]
                        )
                        out[near, hi, s, n_b + a_pad :, :] = pair.astype(BF16)

        def add_kernel(arrival, meta_ref, x_ref, d0_ref, d1_ref, d2_ref, d3_ref, out_ref):
            step = pl.program_id(0) // 2
            rows = pl.ds(pl.multiple_of((pl.program_id(0) % 2) * (block // 2), 8), block // 2)
            for i, ref in enumerate((d0_ref, d1_ref, d2_ref, d3_ref)):

                @pl.when(step == i)
                def _(ref=ref):
                    if not arrival:
                        out_ref[0] = x_ref[0] + ref[rows, :].astype(F32)
                        return
                    for j in range(n_piece):
                        lanes = column(meta_ref, j)
                        out_ref[0, :, lanes] = x_ref[0, :, lanes] + ref[
                            rows, j * LANES : (j + 1) * LANES
                        ].astype(F32)

        def split_kernel(meta_ref, keep_ref, got_ref, own_ref, send_ref):
            def total(s):
                lanes = slice(s * LANES, (s + 1) * LANES)
                return keep_ref[:, lanes].astype(F32) + got_ref[: keep_ref.shape[0], lanes].astype(
                    F32
                )

            own_ref[0] = total(0)
            own_ref[1] = total(2)

            @pl.when(lax.rem(meta_ref[AT_ME + 1], 2) == 0)
            def _():
                send_ref[0] = total(3).astype(BF16)
                send_ref[1] = total(1).astype(BF16)

            @pl.when(lax.rem(meta_ref[AT_ME + 1], 2) == 1)
            def _():
                send_ref[0] = total(1).astype(BF16)
                send_ref[1] = total(3).astype(BF16)

        def unpack_kernel(
            meta_ref, p_ref, got_ref, b_ref, a_ref, g0_ref, g1_ref, o_ref
        ):
            total = p_ref[...].astype(F32) + got_ref[...].astype(F32)
            for k in range(b_parts):
                b_ref[0, :, k * LANES : (k + 1) * LANES] = total[k * b_rows : (k + 1) * b_rows]
            a_ref[0] = total[n_b : n_b + a_cols]
            rows = total[n_b + a_pad : n_b + a_pad + 8]
            rows = pltpu.roll(rows, (n_tp - meta_ref[AT_ME]) * gain_part, 1)
            g0_ref[...] = rows[0:1, :gain_part]
            g1_ref[...] = rows[1:2, :gain_part]
            o_ref[0] = total[pack_rows:]

        core = lambda v, label="row": swap(v, "tp", n_tp, 1, "core_" + label)
        chip = lambda v, label="row": swap(v, "tp", n_tp, 2, "y_" + label)
        ctx = lambda v, label="row": swap(v, "ctx", n_c, 1, "x_" + label)
        ahead = lambda v, s, label="row": shift(v, "fsdp", n_f, s, "z_" + label)

        (pack,) = call(
            pack_kernel,
            "pack",
            [((pack_rows, LANES), BF16)],
            (w_factor_b, w_factor_a.transpose(0, 2, 1), attn_gains, ffn_gains),
        )
        o_rows_all = w_out[0].astype(BF16)
        pack = jnp.stack([pack] + [ahead(pack, s, "pack") for s in range(1, n_f)])
        o_parts = [o_rows_all] + [ahead(o_rows_all, s, "wo") for s in range(1, n_f)]
        o_parts = jnp.concatenate(o_parts, axis=0)
        gu_in = after(w_gate_up.transpose(0, 1, 3, 2), pack)
        own_gu, own_dn = call(
            big_kernel,
            "big_pack",
            [((2 * hidden, LANES), BF16), ((hidden, LANES), BF16)],
            (gu_in, w_down),
        )
        pack = jnp.stack([pack, ctx(pack, "pack")])
        far_gu = swap(own_gu, "fsdp", n_f, 2, "z_gate_up")
        dn_pair = jnp.stack([own_dn, ctx(own_dn, "down")])
        gu_across = ctx(own_gu, "gate_up")
        o_across = ctx(o_parts, "wo")
        o_parts = jnp.concatenate(
            [
                half[s * o_rows : (s + 1) * o_rows]
                for half in (o_parts, o_across)
                for s in range(n_f)
            ],
            axis=1,
        )
        pack_across, far_gu, dn_pair, o_parts = lax.optimization_barrier(
            (chip(pack, "pack"), far_gu, dn_pair, o_parts)
        )
        pair_gu = swap(jnp.stack([own_gu, far_gu]), "fsdp", n_f, 1, "z_gate_up_pair")
        pack = jnp.stack([pack, pack_across], axis=1)
        other_pack = core(pack, "pack")

        def add_rows(whole, parts, arrival):
            rows = pl.BlockSpec(
                (1, block // 2, width), lambda i, m: (0, 2 * m[AT_TP + i // 2] + i % 2, 0)
            )
            (out,) = call(
                lambda *refs: add_kernel(arrival, *refs),
                "add_rows",
                [(whole.shape, F32)],
                (whole, *parts),
                [rows] + [WHOLE] * 4,
                (),
                (2 * n_tp,),
                [rows],
            )
            return out

        def split(keep, got):
            size = keep.shape[0]
            return call(
                split_kernel,
                "split",
                [((2, size, LANES), F32), ((2, size, LANES), BF16)],
                (keep, got),
            )

        def first_step(send, label):
            return swap(send, "fsdp", n_f, 1, "z1_" + label)

        def second_step(own, got, label):
            total = own + got.astype(F32)
            return total[0], swap(total[1].astype(BF16), "fsdp", n_f, 2, "z2_" + label)

        seg_here = lax.dynamic_slice_in_dim(segment_ids[0], place * block, block, 0)
        first = jnp.sum((segment_ids[0][:, None] < seg_here[None, :]).astype(jnp.int32), axis=0)
        token = place * block + jnp.arange(block, dtype=jnp.int32)
        position = (token - first).astype(F32)
        first = (first - place * block + extra * block).reshape(1, block)
        frequency = 10000.0 ** (-2.0 * jnp.arange(HEAD_DIM // 2, dtype=F32) / HEAD_DIM)
        angles = frequency[:, None] * position[None, :]
        cosine, sine = jnp.cos(angles), jnp.sin(angles)

        weight_b, weight_a, gains, normed, a_rows, b_query, payload = call(
            factor_kernel,
            "factors",
            [
                ((width, b_cols), BF16),
                ((n_tp, a_pad, width), BF16),
                ((16, width), F32),
                ((block, width), BF16),
                ((n_tp, a_pad, block), F32),
                ((RANK_Q, HEAD_DIM, block), F32),
                ((kv_rows, block), BF16),
            ],
            (resid_in, pack, other_pack, cosine, sine),
            [OWN] + [WHOLE] * 4,
        )
        def places(value, step, chosen, label):
            pairs = [(i, i + step) for i in chosen if 0 <= i + step < n_place]
            with jax.named_scope(label):
                return lax.ppermute(value, ("ctx", "tp"), pairs)

        every, odd, even = range(n_place), range(1, n_place, 2), range(0, n_place, 2)
        second = places(payload, 2, every, "x_kv_second")
        third = places(payload, 3, odd, "x_kv_third")
        beside_kv = core(payload, "kv")
        o_own = jnp.concatenate([o_parts, chip(o_parts, "wo")], axis=0)
        second, pair_gu, gu_across = lax.optimization_barrier((second, pair_gu, gu_across))
        gu_rest = ctx(jnp.concatenate([far_gu[None], pair_gu], axis=0), "gate_up_rest")
        dn_parts = [dn_pair, ahead(dn_pair, 1, "down1")]
        beside_second = core(second, "kv_second")
        tied = lax.optimization_barrier((third, second, beside_second, beside_kv, o_own))
        wins = (*tied[:4], payload)
        o_own = tied[4]
        o_other = core(o_own, "wo")
        window = windows * block
        lse, query, mixed = call(
            attention_kernel,
            "attention",
            [
                ((n_tp, group, block), F32),
                ((n_tp, group, HEAD_DIM, block), BF16),
                ((n_tp, feats, block), BF16),
            ],
            (first, a_rows, b_query, *wins),
            None,
            [
                pltpu.VMEM((windows, kv_rows, block), BF16),
                pltpu.VMEM((window, block), F32),
                pltpu.VMEM((windows, KV, HEAD_DIM, block), F32),
                pltpu.VMEM((group, window, block), F32),
            ],
        )
        dn_parts[1] = after(dn_parts[1], mixed)
        for s in range(2, n_f):
            dn_parts.append(ahead(dn_parts[-1], 1, "down" + str(s)))
        mid, attn_out, normed_ffn = call(
            project_kernel,
            "project",
            [((block, width), F32), ((block, width), F32), ((block, width), BF16)],
            (resid_in, mixed, o_own, o_other, gains),
            [OWN] + [WHOLE] * 4,
        )

        near_rows = (normed_ffn, core(normed_ffn, "nf"))
        far_own = chip(normed_ffn, "nf")

        def feed(side, rows):
            return call(
                lambda *refs: ffn_kernel(side, *refs),
                "feed_near" if side == 0 else "feed_far",
                [
                    ((3 * hidden, 2 * block), BF16),
                    ((2 * block, width), BF16),
                    ((block, width), F32),
                    ((block, width), BF16),
                    ((block, width), F32),
                    ((block, width), BF16),
                ],
                (*rows, cotangent, *pieces),
                [WHOLE] * 2 + [REMOTE] * (1 + len(pieces)),
                [
                    pltpu.VMEM((3 * hidden, width), BF16),
                    pltpu.VMEM((2, block, width), F32),
                    pltpu.SemaphoreType.DMA((2 * n_piece + 2,)),
                ],
            )

        far_own, gu_rest = lax.optimization_barrier((far_own, gu_rest))
        far_own, dn_parts[-1], gu_rest = lax.optimization_barrier(
            (far_own, dn_parts[-1], gu_rest)
        )
        pieces = (own_gu, far_gu, pair_gu, gu_across, gu_rest, *dn_parts)
        far_rows = (far_own, core(far_own, "nf_far"))
        far = feed(1, far_rows)
        across = (far[2] + core(far[3], "dn_far").astype(F32)).astype(BF16)
        near = feed(0, (after(near_rows[0], across), near_rows[1]))
        across = chip(across, "dn")
        beside = core(near[3], "dn_near")

        grad_args = (near[0], far[0], *near_rows, *far_rows, near[1], far[1])
        own_d, send_d = call(
            down_grad_kernel,
            "down_grad",
            [((2, n_c, hidden, LANES), F32), ((2, n_c, hidden, LANES), BF16)],
            grad_args,
            room=12,
        )
        got_d = first_step(send_d, "d")
        keep_a, send_a = call(
            gate_up_grad_kernel,
            "gate_up_grad",
            [((2 * hidden, half_width), BF16)] * 2,
            (after(grad_args[0], send_d), *grad_args[1:]),
            room=12,
        )
        got_a = ctx(send_a, "grads_a")
        across = after(across, send_a)

        delta_mid, gain_grad, grad_mixed, keep_o, send_o = call(
            middle_kernel,
            "middle",
            [
                ((block, width), F32),
                ((8, width), F32),
                ((n_tp, feats, block), BF16),
                ((2 * o_rows, width), BF16),
                ((2 * o_rows, width), BF16),
            ],
            (cotangent, near[2], beside, across, mid, gains, o_own, o_other, mixed),
            [OWN] + [WHOLE] * 8,
        )
        ahead_sum = far[4] + core(far[5], "out_far").astype(F32)
        ahead_sum = after(ahead_sum.astype(BF16), across)
        ahead_rows = chip(ahead_sum, "out")
        back_args = (first, a_rows, b_query, *wins, lse, query, grad_mixed)
        sums = [
            ((RANK_Q, HEAD_DIM, block), F32),
            ((windows, KV, HEAD_DIM, block), F32),
            ((windows, heads * KV, block), F32),
        ]
        grad_a_out = ((n_tp // 2, a_pad, block), F32)
        back_scratch = [
            pltpu.VMEM((windows, kv_rows, block), BF16),
            pltpu.VMEM((window, block), F32),
            pltpu.VMEM((windows, KV, HEAD_DIM, block), F32),
            pltpu.VMEM((2, window, block), F32),
            pltpu.VMEM((2, window, block), F32),
        ]
        grad_a0, *sums_out = call(
            lambda *refs: attention_back_kernel(0, *refs),
            "attention_back_a",
            [grad_a_out] + sums,
            back_args,
            None,
            back_scratch,
        )
        ffn_out = near[4] + core(near[5], "out_near").astype(F32)
        got_d, ahead_rows, ffn_out = lax.optimization_barrier(
            (got_d, ahead_rows, ffn_out, grad_a0)
        )[:3]
        total_out = (attn_out + ffn_out + ahead_rows.astype(F32)).astype(BF16)
        rows_o = keep_o.astype(F32) + core(send_o, "go").astype(F32)
        rows_keep, rows_send = rows_o[:, :half_width], rows_o[:, half_width:].astype(BF16)
        tied = lax.optimization_barrier((sums_out[0], total_out, rows_send, own_d, got_d))
        sums_out[0], total_out, rows_send, own_d, got_d = tied
        across_out = chip(total_out, "out_rows")
        own_d, got_d = second_step(own_d, got_d, "d")
        grad_a1, grad_bq, *sends = call(
            lambda *refs: attention_back_kernel(1, *refs),
            "attention_back_b",
            [
                grad_a_out,
                sums[0],
                ((2 * kv_rows, block), BF16),
                ((kv_rows, block), BF16),
                ((kv_rows, block), BF16),
                ((kv_rows, block), F32),
            ],
            (*back_args, *sums_out),
            None,
            [pltpu.VMEM(shape, kind) for shape, kind in sums[1:]] + back_scratch,
        )
        *sends[:3], across_out = lax.optimization_barrier((*sends[:3], across_out))
        pair_got = places(sends[0], -2, every, "x_kv_back_pair")
        third_got = places(sends[2], -3, even, "x_kv_back_third")
        with jax.named_scope("core_kv_back"):
            beside_got = lax.ppermute(sends[1], "tp", [(i, i - 1) for i in range(1, n_tp, 2)])
        own_a, send_a = split(after(keep_a, beside_got), got_a)
        total_d = own_d + after(got_d, beside_got).astype(F32)
        pair_got, third_got, own_a, send_a, total_d = lax.optimization_barrier(
            (pair_got, third_got, own_a, send_a, total_d)
        )
        swapped = core(pair_got[kv_rows:], "kv_back")
        got_a = first_step(send_a, "a")
        rows_got = ctx(after(rows_send, send_a), "go")
        got = lax.optimization_barrier((pair_got, swapped, beside_got, third_got))

        delta, keep_p, send_p = call(
            last_kernel,
            "last",
            [
                ((block, width), BF16),
                ((n_c, 2, n_f, pack_rows, LANES), BF16),
                ((n_c, 2, n_f, pack_rows, LANES), BF16),
            ],
            (
                resid_in,
                sends[3],
                *got,
                grad_bq,
                grad_a0,
                grad_a1,
                cosine,
                sine,
                weight_b,
                weight_a,
                normed,
                gains,
                delta_mid,
                gain_grad,
            ),
            [OWN] + [WHOLE] * 16,
            [
                pltpu.VMEM((width, b_cols), F32),
                pltpu.VMEM((n_tp, a_pad, width), F32),
                pltpu.VMEM((block, width), F32),
                pltpu.VMEM((8, width), F32),
            ],
        )

        send_p, delta, rows_got, got_a = lax.optimization_barrier((send_p, delta, rows_got, got_a))
        across_delta = chip(delta, "delta")
        rows_o = rows_keep + rows_got.astype(F32)
        rows_go = chip(rows_o[o_rows:].astype(BF16), "go")
        own_a, got_a = second_step(own_a, got_a, "a")
        part = keep_p.astype(F32) + core(send_p, "gp").astype(F32)
        part_send = part[1].astype(BF16)
        part_got = ctx(part_send, "gp")
        total_out = after(total_out, part_send)
        block_out = add_rows(
            resid_in,
            (
                total_out,
                across_out,
                core(total_out, "out_rows"),
                core(across_out, "out_far_rows"),
            ),
            True,
        )
        part_got, across_delta, rows_go = lax.optimization_barrier(
            (part_got, across_delta, rows_go, block_out)
        )[:3]
        rows_o = rows_o[:o_rows] + rows_go.astype(F32)
        part = part[0] + part_got.astype(F32)
        part_send = part[1].astype(BF16)
        part_got = chip(part_send, "gp")
        beside_delta = core(after(delta, part_send), "delta")
        got_last = ctx(after(total_d[1], part_send).astype(BF16), "d")
        across_delta, got_a = lax.optimization_barrier((across_delta, got_a))
        resid_grad = add_rows(
            cotangent,
            (delta, across_delta, beside_delta, core(across_delta, "delta_far")),
            False,
        )
        part_got, got_last, got_a = lax.optimization_barrier(
            (part_got, got_last, got_a, resid_grad)
        )[:3]
        part = part[0] + part_got.astype(F32)
        grad_down = total_d[0] + got_last.astype(F32)
        part = [
            jnp.concatenate([part[s], rows_o[:, s * LANES : (s + 1) * LANES]], axis=0)
            for s in range(n_f)
        ]
        is_even_f = f_index % 2 == 0
        part_send = [
            jnp.where(is_even_f, part[3], part[1]),
            jnp.where(is_even_f, part[1], part[3]),
        ]
        part_send = jnp.stack(part_send).astype(BF16)
        own_a = after(own_a, part_send)
        part_own, part_got = second_step(
            jnp.stack([part[0], part[2]]), first_step(part_send, "gp"), "gp"
        )
        grad_gate_up = (own_a + got_a.astype(F32)).reshape(1, 2, hidden, fc_cols)
        part_b, part_a, part_g0, part_g1, grad_out = call(
            unpack_kernel,
            "unpack",
            [
                ((1, b_rows, b_cols), F32),
                ((1, a_cols, fc_cols), F32),
                ((1, gain_part), F32),
                ((1, gain_part), F32),
                ((1, o_rows, LANES), F32),
            ],
            (part_own, part_got),
        )
        return (
            block_out,
            resid_grad,
            part_a.transpose(0, 2, 1),
            part_b,
            grad_out,
            grad_gate_up.transpose(0, 1, 3, 2),
            grad_down[None],
            part_g0,
            part_g1,
        )

    return shards


def make_shards(mesh):
    fused, general = make_fused(mesh), make_general(mesh)
    fits = mesh.shape["fsdp"] == 4 and mesh.shape["ctx"] == 2 and mesh.shape["tp"] == 4

    def shards(*args):
        return (fused if fits and args[7].shape[2] == LANES else general)(*args)

    return shards


def solution(mesh):
    return jax.shard_map(
        make_shards(mesh),
        mesh=mesh,
        in_specs=(
            P("fsdp", "ctx", None),
            P("fsdp", None),
            P("fsdp", "ctx", None),
            P(None, ("fsdp", "ctx"), "tp"),
            P(None, ("fsdp", "ctx", "tp"), None),
            P(None, "tp", ("fsdp", "ctx")),
            P(None, None, ("fsdp", "ctx"), "tp"),
            P(None, "tp", ("fsdp", "ctx")),
            P(None, ("fsdp", "ctx", "tp")),
            P(None, ("fsdp", "ctx", "tp")),
        ),
        out_specs=(
            P("fsdp", "ctx", None),
            P("fsdp", "ctx", None),
            P(None, ("fsdp", "ctx"), "tp"),
            P(None, ("fsdp", "ctx", "tp"), None),
            P(None, "tp", ("fsdp", "ctx")),
            P(None, None, ("fsdp", "ctx"), "tp"),
            P(None, "tp", ("fsdp", "ctx")),
            P(None, ("fsdp", "ctx", "tp")),
            P(None, ("fsdp", "ctx", "tp")),
        ),
        check_vma=False,
    )
```

```python
import math

import jax
import jax.numpy as jnp
from jax import lax
from jax.experimental import pallas as pl
from jax.experimental.pallas import tpu as pltpu
from jax.sharding import PartitionSpec as P

HEAD_DIM = 64
RANK_Q = 6
RANK_KV = 2
RANKS = 10
KV = 2 * RANK_KV
MOST_DOC = 768
EPSILON = 1e-05
LANES = 128
BF16 = jnp.bfloat16
F32 = jnp.float32
MASKED = -1e30


def inverse_rms(values):
    return lax.rsqrt(jnp.mean(values * values, axis=-1, keepdims=True) + EPSILON)


def norm_back(grad_value, values, inverse, gain):
    scaled = grad_value * gain
    normal = values * inverse
    return inverse * (scaled - normal * jnp.mean(scaled * normal, axis=-1, keepdims=True))


def dot(left, right, dims):
    return lax.dot_general(left, right, (dims, ((), ())), preferred_element_type=F32)


def shift(value, axes, size, step, label="shift"):
    with jax.named_scope(label):
        return lax.ppermute(value, axes, [(i, (i + step) % size) for i in range(size)])


def swap(value, axis, size, bit, label="swap"):
    with jax.named_scope(label):
        return lax.ppermute(value, axis, [(i, i ^ bit) for i in range(size)])


def gather_direct(value, axis, size):
    me = lax.axis_index(axis)
    parts = [(me, value)]
    for step in range(1, size):
        parts.append(((me - step) % size, shift(value, axis, size, step)))
    out = jnp.zeros((size,) + value.shape, value.dtype)
    for place, part in parts:
        out = lax.dynamic_update_slice(out, part[None], (place,) + (0,) * value.ndim)
    return out


def gather_pair(value, axis, size, bit):
    mine = (lax.axis_index(axis) // bit) % 2 == 0
    other = swap(value, axis, size, bit)
    return jnp.stack([jnp.where(mine, value, other), jnp.where(mine, other, value)])


def after(value, *others):
    return lax.optimization_barrier((value,) + others)[0]


def take(value, index):
    return lax.dynamic_index_in_dim(value, index, 0, keepdims=False)


def scatter_direct(value, axis, size):
    me = lax.axis_index(axis)
    got = [
        shift(take(value, (me + step) % size), axis, size, step) for step in range(1, size)
    ]
    total = take(value, me).astype(F32)
    for part in got:
        total = total + part.astype(F32)
    return total


def scatter_pair(value, axis, size, bit):
    mine = (lax.axis_index(axis) // bit) % 2
    got = swap(take(value, 1 - mine).astype(BF16), axis, size, bit)
    return take(value, mine).astype(F32) + got.astype(F32)


def attention_mask(first_ref, window, block):
    start = first_ref[...]
    place = lax.broadcasted_iota(jnp.int32, (window, block), 0)
    query_place = lax.broadcasted_iota(jnp.int32, (window, block), 1) + (window - block)
    return jnp.where((place >= start) & (place <= query_place), 0.0, MASKED)


def head_rows(wa_ref, wide_ref, head):
    factors = wa_ref[head].astype(F32)
    key_rows = (factors[0:1] * wide_ref[0] + factors[1:2] * wide_ref[1]) * (1.0 / RANK_KV)
    value_rows = (factors[2:3] * wide_ref[2] + factors[3:4] * wide_ref[3]) * (1.0 / RANK_KV)
    return factors, key_rows.astype(BF16), value_rows.astype(BF16)


def forward_kernel(
    first_ref, a_ref, bq_ref, wa_ref, wb_ref, mixed_ref, lse_ref, q_ref, bias_ref, wide_ref, s_ref
):
    heads = a_ref.shape[0]
    window, block = bias_ref.shape
    bias_ref[...] = attention_mask(first_ref, window, block)
    wide_ref[...] = wb_ref[...].astype(F32)
    spans = [pl.ds(j * block, block) for j in range(window // block)]

    def one_head(head, carry):
        factors = a_ref[head]
        query = factors[0:1] * bq_ref[0]
        for r in range(1, RANK_Q):
            query = query + factors[r : r + 1] * bq_ref[r]
        query = (query * (1.0 / RANK_Q)).astype(BF16) * jnp.asarray(HEAD_DIM**-0.5, BF16)
        q_ref[head] = query
        _, key_rows, value_rows = head_rows(wa_ref, wide_ref, head)
        top = jnp.full((1, block), MASKED, F32)
        for j, span in enumerate(spans):
            keys = key_rows[:, j * block : (j + 1) * block]
            scores = dot(keys, query, ((0,), (0,))) + bias_ref[span, :]
            s_ref[span, :] = scores
            top = jnp.maximum(top, jnp.max(scores, axis=0, keepdims=True))
        total = jnp.zeros((1, block), F32)
        for span in spans:
            weight = jnp.exp(s_ref[span, :] - top)
            s_ref[span, :] = weight
            total = total + jnp.sum(weight, axis=0, keepdims=True)
        lse_ref[head] = top + jnp.log(total)
        scale = 1.0 / total
        mixed = jnp.zeros((HEAD_DIM, block), F32)
        for j, span in enumerate(spans):
            probs = (s_ref[span, :] * scale).astype(BF16)
            mixed = mixed + dot(
                value_rows[:, j * block : (j + 1) * block], probs, ((1,), (0,))
            )
        mixed_ref[head] = mixed.astype(BF16)
        return carry

    lax.fori_loop(0, heads, one_head, 0)


def backward_kernel(
    first_ref,
    a_ref,
    bq_ref,
    wa_ref,
    wb_ref,
    lse_ref,
    q_ref,
    go_ref,
    ga_ref,
    gbq_ref,
    gwa_ref,
    gwb_ref,
    bias_ref,
    wide_ref,
    p_ref,
    dp_ref,
):
    heads = a_ref.shape[0]
    window, block = bias_ref.shape
    bias_ref[...] = attention_mask(first_ref, window, block)
    wide_ref[...] = wb_ref[...].astype(F32)
    gbq_ref[...] = jnp.zeros_like(gbq_ref)
    gwb_ref[...] = jnp.zeros_like(gwb_ref)
    count = window // block
    spans = [pl.ds(j * block, block) for j in range(count)]

    def one_head(head, carry):
        factors, key_rows, value_rows = head_rows(wa_ref, wide_ref, head)
        query = q_ref[head]
        grad_out = go_ref[head]
        lse = lse_ref[head]
        inner = jnp.zeros((1, block), F32)
        for j, span in enumerate(spans):
            cut = slice(j * block, (j + 1) * block)
            scores = dot(key_rows[:, cut], query, ((0,), (0,))) + bias_ref[span, :]
            probs = jnp.exp(scores - lse)
            grad_probs = dot(value_rows[:, cut], grad_out, ((0,), (0,)))
            p_ref[span, :] = probs
            dp_ref[span, :] = grad_probs
            inner = inner + jnp.sum(probs * grad_probs, axis=0, keepdims=True)
        grad_query = jnp.zeros((HEAD_DIM, block), F32)
        for j, span in enumerate(spans):
            cut = slice(j * block, (j + 1) * block)
            probs = p_ref[span, :]
            grad_scores = (probs * (dp_ref[span, :] - inner)).astype(BF16)
            grad_query = grad_query + dot(key_rows[:, cut], grad_scores, ((1,), (0,)))
            grad_keys = dot(query, grad_scores, ((1,), (1,))) * (1.0 / RANK_KV)
            grad_values = dot(grad_out, probs.astype(BF16), ((1,), (1,))) * (1.0 / RANK_KV)
            rows = []
            for r in range(KV):
                grad = grad_keys if r < RANK_KV else grad_values
                rows.append(jnp.sum(grad * wide_ref[r, :, span], axis=0, keepdims=True))
                gwb_ref[r, :, span] += factors[r : r + 1, cut] * grad
            gwa_ref[head, :, span] = jnp.concatenate(rows, axis=0)
        grad_query = grad_query * (HEAD_DIM**-0.5 / RANK_Q)
        own = a_ref[head]
        rows = []
        for r in range(RANK_Q):
            rows.append(jnp.sum(grad_query * bq_ref[r], axis=0, keepdims=True))
            gbq_ref[r] += own[r : r + 1] * grad_query
        ga_ref[head] = jnp.concatenate(rows, axis=0)
        return carry

    lax.fori_loop(0, heads, one_head, 0)


VMEM_LIMIT = 56 * 1024 * 1024


def whole_specs(count):
    return [pl.BlockSpec(memory_space=pltpu.VMEM)] * count


def attend_forward(first, a_rows, b_query, win_a, win_b):
    heads, _, block = a_rows.shape
    window = win_a.shape[-1]
    return pl.pallas_call(
        forward_kernel,
        out_shape=(
            jax.ShapeDtypeStruct((heads, HEAD_DIM, block), BF16),
            jax.ShapeDtypeStruct((heads, 1, block), F32),
            jax.ShapeDtypeStruct((heads, HEAD_DIM, block), BF16),
        ),
        in_specs=whole_specs(5),
        out_specs=tuple(whole_specs(3)),
        scratch_shapes=[
            pltpu.VMEM((window, block), F32),
            pltpu.VMEM((KV, HEAD_DIM, window), F32),
            pltpu.VMEM((window, block), F32),
        ],
        compiler_params=pltpu.CompilerParams(vmem_limit_bytes=VMEM_LIMIT),
        name="attend_forward",
    )(first, a_rows, b_query, win_a, win_b)


def attend_backward(first, a_rows, b_query, win_a, win_b, lse, query, grad_mixed):
    heads, _, block = a_rows.shape
    window = win_a.shape[-1]
    return pl.pallas_call(
        backward_kernel,
        out_shape=(
            jax.ShapeDtypeStruct((heads, RANK_Q, block), F32),
            jax.ShapeDtypeStruct((RANK_Q, HEAD_DIM, block), F32),
            jax.ShapeDtypeStruct((heads, KV, window), F32),
            jax.ShapeDtypeStruct((KV, HEAD_DIM, window), F32),
        ),
        in_specs=whole_specs(8),
        out_specs=tuple(whole_specs(4)),
        scratch_shapes=[
            pltpu.VMEM((window, block), F32),
            pltpu.VMEM((KV, HEAD_DIM, window), F32),
            pltpu.VMEM((window, block), F32),
            pltpu.VMEM((window, block), F32),
        ],
        compiler_params=pltpu.CompilerParams(vmem_limit_bytes=VMEM_LIMIT),
        name="attend_backward",
    )(first, a_rows, b_query, win_a, win_b, lse, query, grad_mixed)


def rotate(rows, cosine, sine):
    half = HEAD_DIM // 2
    lower, upper = rows[:, :half], rows[:, half:]
    return jnp.concatenate(
        [lower * cosine - upper * sine, lower * sine + upper * cosine], axis=1
    )


def make_general(mesh):
    n_f, n_c, n_tp = mesh.shape["fsdp"], mesh.shape["ctx"], mesh.shape["tp"]
    n_hi, n_lo = 2, n_tp // 2

    def shards(
        resid_in,
        segment_ids,
        cotangent,
        w_factor_a,
        w_factor_b,
        w_out,
        w_gate_up,
        w_down,
        attn_gains,
        ffn_gains,
    ):
        seq_count, local_len, width = resid_in.shape
        assert seq_count == 1 and w_factor_a.shape[0] == 1 and n_lo == 2
        full_len = segment_ids.shape[1]
        block = local_len // n_tp
        extra = -(-(MOST_DOC - 1) // block)
        window = (extra + 1) * block
        a_cols = w_factor_a.shape[2]
        heads = n_tp * a_cols // RANKS
        b_cols = w_factor_b.shape[2]
        b_rows = w_factor_b.shape[1]
        b_parts = b_cols // LANES
        fc_cols = w_down.shape[2]
        hidden = w_down.shape[1]
        o_rows = w_out.shape[1]

        f_index, c_index, t_index = (
            lax.axis_index("fsdp"),
            lax.axis_index("ctx"),
            lax.axis_index("tp"),
        )
        hi, lo = t_index // 2, t_index % 2
        place = c_index * n_tp + t_index
        n_place = n_c * n_tp

        gains = jnp.concatenate([attn_gains, ffn_gains], axis=1).astype(BF16)
        gain_count = gains.shape[1]
        gain_rows = 16 * (-(-gain_count // (16 * LANES)))
        gains = jnp.pad(gains.reshape(-1), (0, gain_rows * LANES - gain_count))
        b_shard = w_factor_b[0].astype(BF16).reshape(b_rows, b_parts, LANES)
        a_shard = w_factor_a[0].astype(BF16).T
        pack = jnp.concatenate(
            [
                b_shard.transpose(1, 0, 2).reshape(-1, LANES),
                a_shard.reshape(-1, LANES),
                gains.reshape(-1, LANES),
            ],
            axis=0,
        )
        n_b = b_parts * b_rows
        n_a = a_cols * fc_cols // LANES
        pack = gather_direct(pack, "fsdp", n_f)
        after_pack = pack
        pack = gather_pair(pack, "ctx", n_c, 1)
        pack = gather_pair(pack, "tp", n_tp, 2)
        pack = gather_pair(pack, "tp", n_tp, 1)
        pack = pack.transpose(3, 2, 1, 0, 4, 5)
        weight_b = pack[:, :, :, :, :n_b].reshape(-1, b_parts, b_rows, LANES)
        weight_b = weight_b.transpose(0, 2, 1, 3).reshape(width, b_cols)
        weight_a = pack[:, :, :, :, n_b : n_b + n_a].reshape(n_f, n_c, n_tp, a_cols, fc_cols)
        weight_a = weight_a.transpose(2, 3, 0, 1, 4).reshape(n_tp * a_cols, width)
        gains_all = pack[:, :, :, :, n_b + n_a :].reshape(-1, gain_rows * LANES)[:, :gain_count]
        gains_all = gains_all.reshape(-1, 2, gain_count // 2).transpose(1, 0, 2)
        gains_all = gains_all.reshape(2, width).astype(F32)
        gain_attn, gain_ffn = gains_all[0:1], gains_all[1:2]

        big = jnp.concatenate(
            [
                w_gate_up[0, 0].astype(BF16).T,
                w_gate_up[0, 1].astype(BF16).T,
                w_down[0].astype(BF16),
                w_out[0].astype(BF16),
            ],
            axis=0,
        )
        big, _ = lax.optimization_barrier((big, after_pack))
        big = gather_direct(big, "fsdp", n_f)
        big = gather_pair(big, "ctx", n_c, 1)
        big = big.transpose(2, 1, 0, 3).reshape(-1, width)
        weight_g = big[:hidden]
        weight_u = big[hidden : 2 * hidden]
        weight_d = big[2 * hidden : 3 * hidden]
        weight_o = gather_pair(big[3 * hidden :], "tp", n_tp, 2)
        weight_o = gather_pair(weight_o, "tp", n_tp, 1)
        weight_o = weight_o.transpose(1, 0, 2, 3).reshape(n_tp * o_rows, width)

        seg_here = lax.dynamic_slice_in_dim(segment_ids[0], place * block, block, 0)
        first = jnp.sum((segment_ids[0][:, None] < seg_here[None, :]).astype(jnp.int32), axis=0)
        token = place * block + jnp.arange(block, dtype=jnp.int32)
        position = (token - first).astype(F32)
        first = (first - place * block + extra * block).reshape(1, block)
        frequency = 10000.0 ** (
            -2.0 * jnp.arange(HEAD_DIM // 2, dtype=F32) / HEAD_DIM
        )
        angles = frequency[:, None] * position[None, :]
        cosine, sine = jnp.cos(angles)[None], jnp.sin(angles)[None]

        stream = resid_in[0].reshape(n_tp, block, width)
        own = take(stream, t_index)
        inverse_attn = inverse_rms(own)
        normed = (own * inverse_attn * gain_attn).astype(BF16)
        a_rows = dot(weight_a, normed, ((1,), (1,))).reshape(heads, RANKS, block)
        b_raw = dot(weight_b, normed, ((0,), (1,))).reshape(RANKS, HEAD_DIM, block)
        b_rot = rotate(b_raw[: RANK_Q + RANK_KV], cosine, sine)
        b_query = b_rot[:RANK_Q]
        b_kv = jnp.concatenate([b_rot[RANK_Q:], b_raw[RANK_Q + RANK_KV :]], axis=0)
        payload = jnp.concatenate(
            [
                b_kv.reshape(KV * HEAD_DIM, block),
                a_rows[:, RANK_Q:].reshape(heads * KV, block),
            ],
            axis=0,
        ).astype(BF16)
        around = [
            lax.ppermute(
                payload, ("ctx", "tp"), [(i, i + step) for i in range(n_place - step)]
            )
            for step in range(extra, 0, -1)
        ]
        win = jnp.concatenate(around + [payload], axis=1)
        win_b = win[: KV * HEAD_DIM].reshape(KV, HEAD_DIM, window)
        win_a = win[KV * HEAD_DIM :].reshape(heads, KV, window)

        mixed, lse, query = attend_forward(first, a_rows, b_query, win_a, win_b)
        mixed = mixed.reshape(heads * HEAD_DIM, block)
        attn_out = dot(mixed, weight_o, ((0,), (0,)))
        mid = own + attn_out
        inverse_ffn = inverse_rms(mid)
        normed_ffn = (mid * inverse_ffn * gain_ffn).astype(BF16)

        near_rows = gather_pair(normed_ffn, "tp", n_tp, 1)
        far_rows = gather_pair(swap(normed_ffn, "tp", n_tp, 2), "tp", n_tp, 1)
        grad_all = cotangent[0].reshape(n_hi, n_lo * block, width)

        def half(rows, grad_rows):
            rows = rows.reshape(n_lo * block, width)
            gate = dot(rows, weight_g, ((1,), (1,)))
            up = dot(rows, weight_u, ((1,), (1,)))
            grad_act = dot(grad_rows, weight_d, ((1,), (1,)))
            squash = jax.nn.sigmoid(gate)
            act = (gate * squash * up).astype(BF16)
            grad_gate = (grad_act * up * squash * (1.0 + gate * (1.0 - squash))).astype(BF16)
            grad_up = (grad_act * gate * squash).astype(BF16)
            back = dot(grad_gate, weight_g, ((1,), (0,))) + dot(grad_up, weight_u, ((1,), (0,)))
            ahead = dot(act, weight_d, ((1,), (0,)))
            both = lambda v: v.reshape(n_lo, block, width)
            return rows, act, grad_gate, grad_up, both(back), both(ahead)

        grad_near = take(grad_all, hi).astype(BF16)
        grad_far = take(grad_all, 1 - hi).astype(BF16)
        near = half(near_rows, grad_near)
        far = half(far_rows, grad_far)
        back_far = scatter_pair(far[4], "tp", n_tp, 1).astype(BF16)
        back_far = swap(back_far, "tp", n_tp, 2)
        grad_normed_ffn = scatter_pair(near[4], "tp", n_tp, 1) + back_far.astype(F32)
        ahead_far = scatter_pair(far[5], "tp", n_tp, 1).astype(BF16)
        ahead_far = swap(ahead_far, "tp", n_tp, 2)
        ffn_out = scatter_pair(near[5], "tp", n_tp, 1) + ahead_far.astype(F32)

        def spread(value):
            beside = swap(value, "tp", n_tp, 1)
            across = swap(value, "tp", n_tp, 2)
            diagonal = swap(across, "tp", n_tp, 1)
            out = jnp.zeros((n_tp,) + value.shape, value.dtype)
            for bit, part in enumerate((value, beside, across, diagonal)):
                out = lax.dynamic_update_slice(out, part[None], (t_index ^ bit, 0, 0))
            return out.reshape(local_len, width).astype(F32)

        block_out = resid_in + spread((attn_out + ffn_out).astype(BF16))[None]

        def columns(value, which):
            value = value.reshape(value.shape[0], n_f, n_c, fc_cols)
            value = lax.dynamic_index_in_dim(value, which, 2, keepdims=False)
            return value.reshape(value.shape[0], n_f * fc_cols)

        rows_all = jnp.concatenate([near[0], far[0]], axis=0)
        act_all = jnp.concatenate([near[1], far[1]], axis=0)
        gate_all = jnp.concatenate([near[2], far[2]], axis=0)
        up_all = jnp.concatenate([near[3], far[3]], axis=0)
        cot_all = jnp.concatenate([grad_near, grad_far], axis=0)

        def big_grads(which):
            rows_cut = columns(rows_all, which)
            cot_cut = columns(cot_all, which)
            return jnp.concatenate(
                [
                    dot(gate_all, rows_cut, ((0,), (0,))),
                    dot(up_all, rows_cut, ((0,), (0,))),
                    dot(act_all, cot_cut, ((0,), (0,))),
                ],
                axis=0,
            )

        def over_fc(send, keep):
            total = keep + swap(send.astype(BF16), "ctx", n_c, 1).astype(F32)
            total = total.astype(BF16).reshape(-1, n_f, fc_cols).transpose(1, 0, 2)
            return scatter_direct(total, "fsdp", n_f)

        grad_big = over_fc(big_grads(1 - c_index), big_grads(c_index))
        grad_gate_w = grad_big[:hidden].T
        grad_up_w = grad_big[hidden : 2 * hidden].T
        grad_down_w = grad_big[2 * hidden :]

        own_cot = take(cotangent[0].reshape(n_tp, block, width), t_index)
        gain_grad_ffn = jnp.sum(grad_normed_ffn * mid * inverse_ffn, axis=0)
        delta_mid = norm_back(grad_normed_ffn, mid, inverse_ffn, gain_ffn)
        grad_attn = (own_cot + delta_mid).astype(BF16)
        grad_out = dot(mixed, grad_attn, ((1,), (0,))).reshape(n_hi, n_lo, o_rows, width)
        grad_out = scatter_pair(grad_out.transpose(1, 0, 2, 3), "tp", n_tp, 1)
        grad_out = scatter_pair(grad_out, "tp", n_tp, 2)
        grad_out = over_fc(columns(grad_out, 1 - c_index), columns(grad_out, c_index))

        grad_mixed = dot(weight_o, grad_attn, ((1,), (1,))).astype(BF16)
        ga_q, gb_q, gw_a, gw_b = attend_backward(
            first,
            a_rows,
            b_query,
            win_a,
            win_b,
            lse,
            query,
            grad_mixed.reshape(heads, HEAD_DIM, block),
        )
        gw = jnp.concatenate(
            [gw_b.reshape(KV * HEAD_DIM, window), gw_a.reshape(heads * KV, window)], axis=0
        )
        total = gw[:, extra * block :]
        for step in range(1, extra + 1):
            part = gw[:, (extra - step) * block : (extra - step + 1) * block].astype(BF16)
            part = lax.ppermute(
                part, ("ctx", "tp"), [(i + step, i) for i in range(n_place - step)]
            )
            total = total + part.astype(F32)
        gb_kv = total[: KV * HEAD_DIM].reshape(KV, HEAD_DIM, block)
        ga_kv = total[KV * HEAD_DIM :].reshape(heads, KV, block)
        grad_b = jnp.concatenate(
            [
                rotate(jnp.concatenate([gb_q, gb_kv[:RANK_KV]], axis=0), cosine, -sine),
                gb_kv[RANK_KV:],
            ],
            axis=0,
        )
        grad_b = grad_b.reshape(b_cols, block).astype(BF16)
        grad_a = jnp.concatenate([ga_q, ga_kv], axis=1).reshape(heads * RANKS, block).astype(BF16)
        grad_normed = dot(grad_a, weight_a, ((0,), (0,))) + dot(grad_b, weight_b, ((0,), (1,)))
        gain_grad_attn = jnp.sum(grad_normed * own * inverse_attn, axis=0)
        delta = delta_mid + norm_back(grad_normed, own, inverse_attn, gain_attn)
        resid_grad = cotangent + spread(delta.astype(BF16))[None]

        grad_wa = dot(grad_a, normed, ((1,), (0,))).astype(BF16)
        grad_wa = grad_wa.reshape(n_hi, n_lo, a_cols, n_f, n_c, fc_cols)
        grad_wa = grad_wa.transpose(1, 0, 4, 3, 2, 5).reshape(n_lo, n_hi, n_c, n_f, n_a, LANES)
        grad_wb = jnp.einsum(
            "pkt,td->pdk",
            grad_b.reshape(b_parts, LANES, block),
            normed,
            preferred_element_type=F32,
        ).astype(BF16)
        grad_wb = grad_wb.reshape(b_parts, n_f, n_c, n_hi, n_lo, b_rows, LANES)
        grad_wb = grad_wb.transpose(4, 3, 2, 1, 0, 5, 6)
        grad_wb = grad_wb.reshape(n_lo, n_hi, n_c, n_f, n_b, LANES)
        gain_grads = jnp.stack([gain_grad_attn, gain_grad_ffn]).astype(BF16)
        gain_grads = gain_grads.reshape(2, n_f, n_c, n_hi, n_lo, gain_count // 2)
        gain_grads = gain_grads.transpose(4, 3, 2, 1, 0, 5).reshape(
            n_lo, n_hi, n_c, n_f, gain_count
        )
        gain_grads = jnp.pad(
            gain_grads, [(0, 0)] * 4 + [(0, gain_rows * LANES - gain_count)]
        ).reshape(n_lo, n_hi, n_c, n_f, gain_rows, LANES)
        pack = jnp.concatenate([grad_wb, grad_wa, gain_grads], axis=4)
        pack = scatter_pair(pack, "tp", n_tp, 1)
        pack = scatter_pair(pack, "tp", n_tp, 2)
        pack = scatter_pair(pack, "ctx", n_c, 1).astype(BF16)
        pack = scatter_direct(pack, "fsdp", n_f)
        part_b = pack[:n_b].reshape(b_parts, b_rows, LANES).transpose(1, 0, 2)
        part_b = part_b.reshape(1, b_rows, b_cols)
        part_a = pack[n_b : n_b + n_a].reshape(a_cols, fc_cols).T[None]
        part_gain = pack[n_b + n_a :].reshape(-1)[:gain_count].reshape(2, 1, gain_count // 2)
        return (
            block_out,
            resid_grad,
            part_a,
            part_b,
            grad_out[None],
            jnp.stack([grad_gate_w, grad_up_w])[None],
            grad_down_w[None],
            part_gain[0],
            part_gain[1],
        )

    return shards


def rotated(rows, cosine, sine):
    half = HEAD_DIM // 2
    lower, upper = rows[:half], rows[half:]
    return jnp.concatenate([lower * cosine - upper * sine, lower * sine + upper * cosine], axis=0)


def make_fused(mesh):
    n_f, n_c, n_tp = mesh.shape["fsdp"], mesh.shape["ctx"], mesh.shape["tp"]
    n_piece = n_f * n_c
    AT_TP = n_piece
    AT_ME = n_piece + n_tp

    def shards(
        resid_in,
        segment_ids,
        cotangent,
        w_factor_a,
        w_factor_b,
        w_out,
        w_gate_up,
        w_down,
        attn_gains,
        ffn_gains,
    ):
        _, local_len, width = resid_in.shape
        block = local_len // n_tp
        extra = -(-(MOST_DOC - 1) // block)
        windows = extra + 1
        a_cols = w_factor_a.shape[2]
        group = a_cols // RANKS
        heads = n_tp * group
        feats = group * HEAD_DIM
        a_pad = 16 * (-(-a_cols // 16))
        b_rows, b_cols = w_factor_b.shape[1:]
        b_parts = b_cols // LANES
        n_b = b_parts * b_rows
        pack_rows = n_b + a_pad + 16
        fc_cols = w_down.shape[2]
        hidden = w_down.shape[1]
        o_rows = w_out.shape[1]
        gain_part = attn_gains.shape[1]
        kv_b = KV * HEAD_DIM
        kv_rows = kv_b + heads * KV
        half_width = width // n_c
        early = 2 * hidden + 16 * (hidden // 64)
        assert n_f == 4 and fc_cols == LANES and o_rows == feats and n_tp == 4 and n_c == 2

        f_index, c_index, t_index = (
            lax.axis_index("fsdp"),
            lax.axis_index("ctx"),
            lax.axis_index("tp"),
        )
        place = c_index * n_tp + t_index
        n_place = n_c * n_tp
        columns = [
            ((f_index - s) % n_f) * n_c + (c_index if near == 0 else 1 - c_index)
            for near in range(n_c)
            for s in range(n_f)
        ]
        members = [t_index ^ (lo + 2 * hi) for lo in range(2) for hi in range(2)]
        beside_shift = jnp.where(f_index % 2 == 0, n_f - 1, 1)
        meta = jnp.stack(columns + members + [t_index, f_index, beside_shift]).astype(jnp.int32)

        resid_in = pltpu.with_memory_space_constraint(resid_in, pltpu.HBM)
        cotangent = pltpu.with_memory_space_constraint(cotangent, pltpu.HBM)

        def column(meta_ref, j):
            return pl.ds(pl.multiple_of(meta_ref[j] * LANES, LANES), LANES)

        def member(meta_ref, lo, hi):
            return meta_ref[AT_TP + 2 * lo + hi]

        def to_arrival(meta_ref, load):
            return jnp.concatenate([load(column(meta_ref, j)) for j in range(n_piece)], axis=1)

        WHOLE = pl.BlockSpec(memory_space=pltpu.VMEM)
        REMOTE = pl.BlockSpec(memory_space=pl.ANY)
        OWN = pl.BlockSpec((1, block, width), lambda i, m: (0, m[AT_ME], 0))

        def call(
            kernel, name, outs, args, specs=None, scratch=(), grid=(1,), out_specs=None, room=4
        ):
            held = 0
            for arg, spec in zip((*args, *args[:1]), (specs or []) + (out_specs or [])):
                if spec.block_shape:
                    held += 2 * math.prod(spec.block_shape) * arg.dtype.itemsize
            for item in scratch:
                if hasattr(item, "shape") and item.memory_space == pltpu.VMEM:
                    held += math.prod(item.shape) * jnp.dtype(item.dtype).itemsize
            limit = min(held + room * 2**20, VMEM_LIMIT)
            return pl.pallas_call(
                kernel,
                out_shape=[jax.ShapeDtypeStruct(s, d) for s, d in outs],
                grid_spec=pltpu.PrefetchScalarGridSpec(
                    num_scalar_prefetch=1,
                    grid=grid,
                    in_specs=specs or [WHOLE] * len(args),
                    out_specs=out_specs or [WHOLE] * len(outs),
                    scratch_shapes=list(scratch),
                ),
                compiler_params=pltpu.CompilerParams(vmem_limit_bytes=limit),
                name=name,
            )(meta, *args)


        def pack_kernel(meta_ref, b_ref, a_ref, g0_ref, g1_ref, out_ref):
            for k in range(b_parts):
                out_ref[k * b_rows : (k + 1) * b_rows, :] = b_ref[
                    0, :, k * LANES : (k + 1) * LANES
                ].astype(BF16)
            a_shard = jnp.concatenate([a_ref[0], jnp.zeros((a_pad - a_cols, LANES), F32)], axis=0)
            out_ref[n_b : n_b + a_pad, :] = a_shard.astype(BF16)
            both = jnp.concatenate([g0_ref[...], g1_ref[...]], axis=0)
            both = jnp.concatenate([both, jnp.zeros((6, gain_part), F32)], axis=0)
            both = jnp.concatenate([both, jnp.zeros((8, LANES - gain_part), F32)], axis=1)
            both = pltpu.roll(both, meta_ref[AT_ME] * gain_part, 1)
            both = jnp.concatenate([both, jnp.zeros((8, LANES), F32)], axis=0)
            out_ref[n_b + a_pad :, :] = both.astype(BF16)

        def big_kernel(meta_ref, gu_ref, d_ref, gu_out_ref, d_out_ref):
            for k in range(2):
                gu_out_ref[k * hidden : (k + 1) * hidden, :] = gu_ref[0, k].astype(BF16)
            gu_out_ref[2 * hidden :, :] = d_ref[0, : early - 2 * hidden, :].astype(BF16)
            d_out_ref[...] = d_ref[0, early - 2 * hidden :, :].astype(BF16)

        def factor_kernel(
            meta_ref,
            x_ref,
            p0_ref,
            p1_ref,
            cos_ref,
            sin_ref,
            wb_ref,
            wa_ref,
            gain_ref,
            normed_ref,
            a_ref,
            bq_ref,
            pay_ref,
        ):
            gain_ref[...] = jnp.zeros_like(gain_ref)
            for lo, hi in ((0, 0), (0, 1), (1, 0), (1, 1)):
                part = (p0_ref, p1_ref)[lo]
                tp = member(meta_ref, lo, hi)
                for near in range(n_c):
                    for s in range(n_f):
                        j = near * n_f + s
                        lanes = column(meta_ref, j)
                        row = pl.multiple_of((meta_ref[j] * n_tp + tp) * b_rows, b_rows)
                        for k in range(b_parts):
                            wb_ref[pl.ds(row, b_rows), k * LANES : (k + 1) * LANES] = part[
                                near, hi, s, k * b_rows : (k + 1) * b_rows, :
                            ]
                        wa_ref[tp, :, lanes] = part[near, hi, s, n_b : n_b + a_pad, :]
                        gain_ref[:, lanes] += part[near, hi, s, n_b + a_pad :, :].astype(F32)
            x = x_ref[0]
            normed = (x * inverse_rms(x) * gain_ref[0:1]).astype(BF16)
            normed_ref[...] = normed
            cosine, sine = cos_ref[...], sin_ref[...]
            b_raw = jnp.transpose(dot(normed, wb_ref[...], ((1,), (0,))))
            for r in range(RANK_Q):
                bq_ref[r] = rotated(b_raw[r * HEAD_DIM : (r + 1) * HEAD_DIM], cosine, sine)
            for r in range(KV):
                rows = b_raw[(RANK_Q + r) * HEAD_DIM : (RANK_Q + r + 1) * HEAD_DIM]
                if r < RANK_KV:
                    rows = rotated(rows, cosine, sine)
                pay_ref[r * HEAD_DIM : (r + 1) * HEAD_DIM, :] = rows.astype(BF16)
            for tp in range(n_tp):
                a_raw = dot(wa_ref[tp], normed, ((1,), (1,)))
                a_ref[tp] = a_raw
                kv = [a_raw[g * RANKS + RANK_Q : (g + 1) * RANKS] for g in range(group)]
                start = kv_b + tp * group * KV
                pay_ref[start : start + group * KV, :] = jnp.concatenate(kv, axis=0).astype(BF16)

        def set_mask(first_ref, bias_ref):
            bias_ref[...] = attention_mask(first_ref, windows * block, block)

        def is_even(meta_ref):
            return lax.rem(meta_ref[AT_ME], 2) == 0

        def widen(meta_ref, arrived, win_ref, wide_ref):
            third, second, beside_second, beside, own = arrived
            win_ref[1] = second[...]
            win_ref[3] = own[...]

            @pl.when(is_even(meta_ref))
            def _():
                win_ref[0] = third[...]
                win_ref[2] = beside_second[...]

            @pl.when(jnp.logical_not(is_even(meta_ref)))
            def _():
                win_ref[0] = beside_second[...]
                win_ref[2] = beside[...]

            for j in range(windows):
                for r in range(KV):
                    wide_ref[j, r] = win_ref[j, r * HEAD_DIM : (r + 1) * HEAD_DIM, :].astype(F32)

        def kv_factors(win_ref, tp):
            start = pl.multiple_of(kv_b + tp * (group * KV), group * KV)
            return [win_ref[j, pl.ds(start, group * KV), :].astype(F32) for j in range(windows)]

        def kv_rows_of(factors, wide_ref, g, j):
            def mix(r):
                a0 = factors[j][g * KV + r : g * KV + r + 1]
                a1 = factors[j][g * KV + r + 1 : g * KV + r + 2]
                rows = a0 * wide_ref[j, r] + a1 * wide_ref[j, r + 1]
                return (rows * (1.0 / RANK_KV)).astype(BF16)

            return mix(0), mix(RANK_KV)

        def attention_kernel(
            meta_ref,
            first_ref,
            a_ref,
            bq_ref,
            w0_ref,
            w1_ref,
            w2_ref,
            w3_ref,
            w4_ref,
            lse_ref,
            q_ref,
            mixed_ref,
            win_ref,
            bias_ref,
            wide_ref,
            s_ref,
        ):
            set_mask(first_ref, bias_ref)
            widen(meta_ref, (w0_ref, w1_ref, w2_ref, w3_ref, w4_ref), win_ref, wide_ref)
            spans = [pl.ds(j * block, block) for j in range(windows)]

            def one_group(tp, carry):
                own = a_ref[tp]
                factors = kv_factors(win_ref, tp)
                for g in range(group):
                    query = own[g * RANKS : g * RANKS + 1] * bq_ref[0]
                    for r in range(1, RANK_Q):
                        query = query + own[g * RANKS + r : g * RANKS + r + 1] * bq_ref[r]
                    query = (query * (1.0 / RANK_Q)).astype(BF16)
                    query = query * jnp.asarray(HEAD_DIM**-0.5, BF16)
                    q_ref[tp, g] = query
                    top = jnp.full((1, block), MASKED, F32)
                    values = []
                    for j, span in enumerate(spans):
                        keys, rows = kv_rows_of(factors, wide_ref, g, j)
                        values.append(rows)
                        scores = dot(keys, query, ((0,), (0,))) + bias_ref[span, :]
                        s_ref[g, span, :] = scores
                        top = jnp.maximum(top, jnp.max(scores, axis=0, keepdims=True))
                    total = jnp.zeros((1, block), F32)
                    for span in spans:
                        weight = jnp.exp(s_ref[g, span, :] - top)
                        s_ref[g, span, :] = weight
                        total = total + jnp.sum(weight, axis=0, keepdims=True)
                    lse_ref[tp, g : g + 1, :] = top + jnp.log(total)
                    scale = 1.0 / total
                    mixed = jnp.zeros((HEAD_DIM, block), F32)
                    for j, span in enumerate(spans):
                        probs = (s_ref[g, span, :] * scale).astype(BF16)
                        mixed = mixed + dot(values[j], probs, ((1,), (0,)))
                    mixed_ref[tp, g * HEAD_DIM : (g + 1) * HEAD_DIM, :] = mixed.astype(BF16)
                return carry

            lax.fori_loop(0, n_tp, one_group, 0)

        def project_kernel(
            meta_ref, x_ref, mixed_ref, o0_ref, o1_ref, gain_ref, mid_ref, attn_ref, nf_ref
        ):
            attn = jnp.zeros((block, width), F32)
            for lo, ref in enumerate((o0_ref, o1_ref)):
                for hi in range(2):
                    rows = mixed_ref[member(meta_ref, lo, hi)]
                    attn = attn + dot(rows, ref[hi * o_rows : (hi + 1) * o_rows, :], ((0,), (0,)))
            attn_ref[...] = attn
            mid = to_arrival(meta_ref, lambda lanes: x_ref[0, :, lanes]) + attn
            mid_ref[...] = mid
            gain = to_arrival(meta_ref, lambda lanes: gain_ref[1:2, lanes])
            nf_ref[...] = (mid * inverse_rms(mid) * gain).astype(BF16)

        def ffn_kernel(side, meta_ref, *refs):
            n_refs = refs[:2]
            cot_ref = refs[2]
            own_gu_ref, far_gu_ref, pair_gu_ref, gu_across_ref, gu_rest_ref = refs[3:8]
            dn_refs = refs[8 : 8 + n_f]
            refs = refs[8 + n_f :]
            ht_ref, gb_ref, back0_ref, back1_ref, ahead0_ref, ahead1_ref = refs[:6]
            w_ref, cot_buf, sems = refs[6:]
            gate_up = [own_gu_ref, far_gu_ref, pair_gu_ref.at[0], pair_gu_ref.at[1], gu_across_ref]
            gate_up += [gu_rest_ref.at[s] for s in range(n_f - 1)]
            beside_shift = meta_ref[AT_ME + 2]
            arrivals = [0, 2, beside_shift, n_f - beside_shift]
            down = [ref.at[near] for near in range(n_c) for ref in dn_refs]
            loads = []
            for i in range(2):
                row = pl.multiple_of(member(meta_ref, i, side) * block, block)
                loads.append(
                    pltpu.make_async_copy(
                        cot_ref.at[0, pl.ds(row, block), :], cot_buf.at[i], sems.at[2 * n_piece + i]
                    )
                )
            for j in range(n_piece):
                lanes = pl.ds(j * LANES, LANES)
                at = pl.multiple_of((arrivals[j % n_f] + j // n_f * n_f) * LANES, LANES)
                loads.append(
                    pltpu.make_async_copy(
                        gate_up[j],
                        w_ref.at[pl.ds(0, early), pl.ds(at, LANES)],
                        sems.at[j],
                    )
                )
                loads.append(
                    pltpu.make_async_copy(
                        down[j], w_ref.at[pl.ds(early, 3 * hidden - early), lanes], sems.at[n_piece + j]
                    )
                )
            for load in loads:
                load.start()
            for i in range(2):
                loads[i].wait()
                for j in range(n_piece):
                    gb_ref[i * block : (i + 1) * block, j * LANES : (j + 1) * LANES] = cot_buf[
                        i, :, column(meta_ref, j)
                    ].astype(BF16)
            for load in loads[2:]:
                load.wait()
            for i in range(2):
                cut = slice(i * block, (i + 1) * block)
                rows = n_refs[i][...]
                gate = dot(w_ref[0:hidden, :], rows, ((1,), (1,)))
                up = dot(w_ref[hidden : 2 * hidden, :], rows, ((1,), (1,)))
                grad_act = dot(w_ref[2 * hidden :, :], gb_ref[cut, :], ((1,), (1,)))
                squash = jax.nn.sigmoid(gate)
                soft = gate * squash
                ht_ref[2 * hidden :, cut] = (soft * up).astype(BF16)
                ht_ref[0:hidden, cut] = (
                    grad_act * up * squash * (1.0 + gate * (1.0 - squash))
                ).astype(BF16)
                ht_ref[hidden : 2 * hidden, cut] = (grad_act * soft).astype(BF16)
            back = dot(ht_ref[: 2 * hidden, :], w_ref[: 2 * hidden, :], ((0,), (0,)))
            back0_ref[...] = back[:block]
            back1_ref[...] = back[block:].astype(BF16)
            ahead = dot(ht_ref[2 * hidden :, :], w_ref[2 * hidden :, :], ((0,), (0,)))
            ahead0_ref[...] = ahead[:block]
            ahead1_ref[...] = ahead[block:].astype(BF16)

        def weight_grad(refs, start, stop, right):
            hts, n_near, n_far, gbs = refs[0:2], refs[2:4], refs[4:6], refs[6:8]
            total = jnp.zeros((stop - start, width), F32)
            for side in range(2):
                left = hts[side]
                if right == 1:
                    total = total + dot(left[start:stop, :], gbs[side][...], ((1,), (0,)))
                    continue
                for i in range(2):
                    rows = (n_near, n_far)[side][i][...]
                    cut = slice(i * block, (i + 1) * block)
                    total = total + dot(left[start:stop, cut], rows, ((1,), (0,)))
            return total

        def gate_up_grad_kernel(meta_ref, *refs):
            keep_ref, send_ref = refs[8:]
            for k in range(2):
                cut = slice(k * hidden, (k + 1) * hidden)
                total = weight_grad(refs, k * hidden, (k + 1) * hidden, 0)
                keep_ref[cut, :] = total[:, :half_width].astype(BF16)
                send_ref[cut, :] = total[:, half_width:].astype(BF16)

        def down_grad_kernel(meta_ref, *refs):
            keep_ref, send_ref = refs[8:]
            total = weight_grad(refs, 2 * hidden, 3 * hidden, 1)

            def chunk(s, near):
                start = near * half_width + s * LANES
                return total[:, start : start + LANES]

            for near in range(n_c):
                keep_ref[0, near] = chunk(0, near)
                keep_ref[1, near] = chunk(2, near)

            @pl.when(lax.rem(meta_ref[AT_ME + 1], 2) == 0)
            def _():
                for near in range(n_c):
                    send_ref[0, near] = chunk(3, near).astype(BF16)
                    send_ref[1, near] = chunk(1, near).astype(BF16)

            @pl.when(lax.rem(meta_ref[AT_ME + 1], 2) == 1)
            def _():
                for near in range(n_c):
                    send_ref[0, near] = chunk(1, near).astype(BF16)
                    send_ref[1, near] = chunk(3, near).astype(BF16)

        def middle_kernel(
            meta_ref,
            cot_ref,
            back_ref,
            beside_ref,
            across_ref,
            mid_ref,
            gain_ref,
            o0_ref,
            o1_ref,
            mixed_ref,
            dmid_ref,
            gg_ref,
            go_ref,
            keep_ref,
            send_ref,
        ):
            back = back_ref[...] + beside_ref[...].astype(F32) + across_ref[...].astype(F32)
            mid = mid_ref[...]
            inverse = inverse_rms(mid)
            gain = to_arrival(meta_ref, lambda lanes: gain_ref[1:2, lanes])
            normal = mid * inverse
            gains = jnp.sum(back * normal, axis=0, keepdims=True)
            for j in range(n_piece):
                gg_ref[:, column(meta_ref, j)] = jnp.broadcast_to(
                    gains[:, j * LANES : (j + 1) * LANES], (8, LANES)
                )
            scaled = back * gain
            delta = inverse * (
                scaled - normal * jnp.mean(scaled * normal, axis=-1, keepdims=True)
            )
            dmid_ref[...] = delta
            cot = to_arrival(meta_ref, lambda lanes: cot_ref[0, :, lanes])
            grad = (cot + delta).astype(BF16)
            for lo, ref in enumerate((o0_ref, o1_ref)):
                for hi in range(2):
                    tp = member(meta_ref, lo, hi)
                    cut = slice(hi * o_rows, (hi + 1) * o_rows)
                    go_ref[tp] = dot(ref[cut, :], grad, ((1,), (1,))).astype(BF16)
                    weight = dot(mixed_ref[tp], grad, ((1,), (0,))).astype(BF16)
                    (keep_ref, send_ref)[lo][cut, :] = weight

        def attention_back_kernel(
            part,
            meta_ref,
            first_ref,
            a_ref,
            bq_ref,
            w0_ref,
            w1_ref,
            w2_ref,
            w3_ref,
            w4_ref,
            lse_ref,
            q_ref,
            go_ref,
            *refs,
        ):
            win_ref, bias_ref, wide_ref, p_ref, dp_ref = refs[-5:]
            if part == 0:
                ga_ref, gbq_ref, gwb_ref, gwa_ref = refs[:4]
            else:
                ga_ref, gbq_ref, second_ref, beside_ref, third_ref, own_ref = refs[3:9]
                gwb_ref, gwa_ref = refs[-7:-5]
            set_mask(first_ref, bias_ref)
            widen(meta_ref, (w0_ref, w1_ref, w2_ref, w3_ref, w4_ref), win_ref, wide_ref)
            if part == 0:
                gbq_ref[...] = jnp.zeros_like(gbq_ref)
                gwb_ref[...] = jnp.zeros_like(gwb_ref)
            else:
                gbq_ref[...] = refs[0][...]
                gwb_ref[...] = refs[1][...]
                gwa_ref[...] = refs[2][...]
            spans = [pl.ds(j * block, block) for j in range(windows)]
            first_tp = part * (n_tp // 2)

            def one_group(tp, carry):
                own = a_ref[tp]
                factors = kv_factors(win_ref, tp)
                grad_a = []
                grad_kv = [[] for _ in spans]
                for g in range(group):
                    query = q_ref[tp, g]
                    grad_out = go_ref[tp, g * HEAD_DIM : (g + 1) * HEAD_DIM, :]
                    lse = lse_ref[tp, g : g + 1, :]
                    inner = jnp.zeros((1, block), F32)
                    keys = []
                    for j, span in enumerate(spans):
                        key_rows, value_rows = kv_rows_of(factors, wide_ref, g, j)
                        keys.append(key_rows)
                        scores = dot(key_rows, query, ((0,), (0,))) + bias_ref[span, :]
                        probs = jnp.exp(scores - lse)
                        grad_probs = dot(value_rows, grad_out, ((0,), (0,)))
                        p_ref[g % 2, span, :] = probs
                        dp_ref[g % 2, span, :] = grad_probs
                        inner = inner + jnp.sum(probs * grad_probs, axis=0, keepdims=True)
                    grad_query = jnp.zeros((HEAD_DIM, block), F32)
                    for j, span in enumerate(spans):
                        probs = p_ref[g % 2, span, :]
                        grad_scores = (probs * (dp_ref[g % 2, span, :] - inner)).astype(BF16)
                        grad_query = grad_query + dot(keys[j], grad_scores, ((1,), (0,)))
                        grad_keys = dot(query, grad_scores, ((1,), (1,))) * (1.0 / RANK_KV)
                        grad_values = dot(grad_out, probs.astype(BF16), ((1,), (1,)))
                        grad_values = grad_values * (1.0 / RANK_KV)
                        for r in range(KV):
                            grad = grad_keys if r < RANK_KV else grad_values
                            grad_kv[j].append(
                                jnp.sum(grad * wide_ref[j, r], axis=0, keepdims=True)
                            )
                            gwb_ref[j, r] += factors[j][g * KV + r : g * KV + r + 1] * grad
                    grad_query = grad_query * (HEAD_DIM**-0.5 / RANK_Q)
                    for r in range(RANK_Q):
                        grad_a.append(jnp.sum(grad_query * bq_ref[r], axis=0, keepdims=True))
                        gbq_ref[r] += own[g * RANKS + r : g * RANKS + r + 1] * grad_query
                    grad_a.append(jnp.zeros((KV, block), F32))
                grad_a.append(jnp.zeros((a_pad - a_cols, block), F32))
                ga_ref[tp - first_tp] = jnp.concatenate(grad_a, axis=0)
                start = pl.multiple_of(tp * (group * KV), group * KV)
                for j in range(windows):
                    gwa_ref[j, pl.ds(start, group * KV), :] = jnp.concatenate(grad_kv[j], axis=0)
                return carry

            lax.fori_loop(first_tp, first_tp + n_tp // 2, one_group, 0)
            if part == 0:
                return

            def put(ref, start, j):
                for r in range(KV):
                    row = start + r * HEAD_DIM
                    ref[row : row + HEAD_DIM, :] = gwb_ref[j, r].astype(ref.dtype)
                ref[start + kv_b : start + kv_rows, :] = gwa_ref[j].astype(ref.dtype)

            put(own_ref, 0, 3)
            put(beside_ref, 0, 2)
            put(third_ref, 0, 0)
            put(second_ref, 0, 1)

        def last_kernel(
            meta_ref,
            x_ref,
            own_ref,
            second_ref,
            beside_ref,
            third_ref,
            gbq_ref,
            ga0_ref,
            ga1_ref,
            cos_ref,
            sin_ref,
            wb_ref,
            wa_ref,
            normed_ref,
            gain_ref,
            dmid_ref,
            gg_ref,
            delta_ref,
            keep0_ref,
            keep1_ref,
            send0_ref,
            send1_ref,
            b_buf,
            a_buf,
            d_buf,
            g_buf,
        ):
            total = own_ref[...]
            for ref in (second_ref, beside_ref, third_ref):
                total = total + ref[...].astype(F32)
            cosine, sine = cos_ref[...], -sin_ref[...]
            rows = [rotated(gbq_ref[r], cosine, sine) for r in range(RANK_Q)]
            for r in range(KV):
                part = total[r * HEAD_DIM : (r + 1) * HEAD_DIM]
                rows.append(rotated(part, cosine, sine) if r < RANK_KV else part)
            grad_b = jnp.transpose(jnp.concatenate(rows, axis=0)).astype(BF16)
            normed = normed_ref[...]
            back = dot(grad_b, wb_ref[...], ((1,), (1,)))
            for tp in range(n_tp):
                parts = []
                for g in range(group):
                    start = kv_b + (tp * group + g) * KV
                    parts.append(jnp.zeros((RANK_Q, block), F32))
                    parts.append(total[start : start + KV])
                parts.append(jnp.zeros((a_pad - a_cols, block), F32))
                own_a = (ga0_ref, ga1_ref)[tp // 2][tp % 2]
                grad_a = (own_a + jnp.concatenate(parts, axis=0)).astype(BF16)
                back = back + dot(grad_a, wa_ref[tp], ((0,), (0,)))
                a_buf[tp] = dot(grad_a, normed, ((1,), (0,)))
            b_buf[...] = dot(normed, grad_b, ((0,), (0,)))
            x = x_ref[0]
            inverse = inverse_rms(x)
            normal = x * inverse
            gains = jnp.sum(back * normal, axis=0, keepdims=True)
            g_buf[...] = jnp.broadcast_to(gains, (8, width))
            scaled = back * gain_ref[0:1]
            delta = inverse * (
                scaled - normal * jnp.mean(scaled * normal, axis=-1, keepdims=True)
            )
            d_buf[...] = delta
            for j in range(n_piece):
                lanes = column(meta_ref, j)
                cut = slice(j * LANES, (j + 1) * LANES)
                delta_ref[:, lanes] = (d_buf[:, lanes] + dmid_ref[:, cut]).astype(BF16)
            row_index = lax.broadcasted_iota(jnp.int32, (16, LANES), 0)
            for lo, hi in ((0, 0), (0, 1), (1, 0), (1, 1)):
                outs = ((keep0_ref, keep1_ref), (send0_ref, send1_ref))[lo]
                tp = member(meta_ref, lo, hi)
                for near in range(n_c):
                    out = outs[near]
                    for s in range(n_f):
                        j = near * n_f + s
                        lanes = column(meta_ref, j)
                        row = pl.multiple_of((meta_ref[j] * n_tp + tp) * b_rows, b_rows)
                        for k in range(b_parts):
                            out[hi, s, k * b_rows : (k + 1) * b_rows, :] = b_buf[
                                pl.ds(row, b_rows), k * LANES : (k + 1) * LANES
                            ].astype(BF16)
                        out[hi, s, n_b : n_b + a_pad, :] = a_buf[tp, :, lanes].astype(BF16)
                        pair = jnp.where(
                            row_index == 0, g_buf[0:1, lanes], gg_ref[0:1, lanes]
                        )
                        out[hi, s, n_b + a_pad :, :] = pair.astype(BF16)

        def add_kernel(arrival, meta_ref, x_ref, d0_ref, d1_ref, d2_ref, d3_ref, out_ref):
            step = pl.program_id(0) // 2
            rows = pl.ds(pl.multiple_of((pl.program_id(0) % 2) * (block // 2), 8), block // 2)
            for i, ref in enumerate((d0_ref, d1_ref, d2_ref, d3_ref)):

                @pl.when(step == i)
                def _(ref=ref):
                    if not arrival:
                        out_ref[0] = x_ref[0] + ref[rows, :].astype(F32)
                        return
                    for j in range(n_piece):
                        lanes = column(meta_ref, j)
                        out_ref[0, :, lanes] = x_ref[0, :, lanes] + ref[
                            rows, j * LANES : (j + 1) * LANES
                        ].astype(F32)

        def split_kernel(meta_ref, keep_ref, got_ref, own_ref, send_ref):
            def total(s):
                lanes = slice(s * LANES, (s + 1) * LANES)
                return keep_ref[:, lanes].astype(F32) + got_ref[: keep_ref.shape[0], lanes].astype(
                    F32
                )

            own_ref[0] = total(0)
            own_ref[1] = total(2)

            @pl.when(lax.rem(meta_ref[AT_ME + 1], 2) == 0)
            def _():
                send_ref[0] = total(3).astype(BF16)
                send_ref[1] = total(1).astype(BF16)

            @pl.when(lax.rem(meta_ref[AT_ME + 1], 2) == 1)
            def _():
                send_ref[0] = total(1).astype(BF16)
                send_ref[1] = total(3).astype(BF16)

        def unpack_kernel(
            meta_ref, p_ref, got_ref, b_ref, a_ref, g0_ref, g1_ref, o_ref
        ):
            total = p_ref[...].astype(F32) + got_ref[...].astype(F32)
            for k in range(b_parts):
                b_ref[0, :, k * LANES : (k + 1) * LANES] = total[k * b_rows : (k + 1) * b_rows]
            a_ref[0] = total[n_b : n_b + a_cols]
            rows = total[n_b + a_pad : n_b + a_pad + 8]
            rows = pltpu.roll(rows, (n_tp - meta_ref[AT_ME]) * gain_part, 1)
            g0_ref[...] = rows[0:1, :gain_part]
            g1_ref[...] = rows[1:2, :gain_part]
            o_ref[0] = total[pack_rows:]

        core = lambda v, label="row": swap(v, "tp", n_tp, 1, "core_" + label)
        chip = lambda v, label="row": swap(v, "tp", n_tp, 2, "y_" + label)
        ctx = lambda v, label="row": swap(v, "ctx", n_c, 1, "x_" + label)
        ahead = lambda v, s, label="row": shift(v, "fsdp", n_f, s, "z_" + label)

        (pack,) = call(
            pack_kernel,
            "pack",
            [((pack_rows, LANES), BF16)],
            (w_factor_b, w_factor_a.transpose(0, 2, 1), attn_gains, ffn_gains),
        )
        o_rows_all = w_out[0].astype(BF16)
        pack = jnp.stack([pack] + [ahead(pack, s, "pack") for s in range(1, n_f)])
        o_parts = [o_rows_all] + [ahead(o_rows_all, s, "wo") for s in range(1, n_f)]
        o_parts = jnp.concatenate(o_parts, axis=0)
        gu_in = after(w_gate_up.transpose(0, 1, 3, 2), pack)
        own_gu, own_dn = call(
            big_kernel,
            "big_pack",
            [((early, LANES), BF16), ((3 * hidden - early, LANES), BF16)],
            (gu_in, w_down),
        )
        pack = jnp.stack([pack, ctx(pack, "pack")])
        far_gu = swap(own_gu, "fsdp", n_f, 2, "z_gate_up")
        dn_pair = jnp.stack([own_dn, ctx(own_dn, "down")])
        gu_across = ctx(own_gu, "gate_up")
        o_across = ctx(o_parts, "wo")
        o_parts = jnp.concatenate(
            [
                half[s * o_rows : (s + 1) * o_rows]
                for half in (o_parts, o_across)
                for s in range(n_f)
            ],
            axis=1,
        )
        pack_across, far_gu, dn_pair, o_parts = lax.optimization_barrier(
            (chip(pack, "pack"), far_gu, dn_pair, o_parts)
        )
        pair_gu = swap(jnp.stack([own_gu, far_gu]), "fsdp", n_f, 1, "z_gate_up_pair")
        pack = jnp.stack([pack, pack_across], axis=1)
        other_pack = core(pack, "pack")

        def add_rows(whole, parts, arrival):
            rows = pl.BlockSpec(
                (1, block // 2, width), lambda i, m: (0, 2 * m[AT_TP + i // 2] + i % 2, 0)
            )
            (out,) = call(
                lambda *refs: add_kernel(arrival, *refs),
                "add_rows",
                [(whole.shape, F32)],
                (whole, *parts),
                [rows] + [WHOLE] * 4,
                (),
                (2 * n_tp,),
                [rows],
            )
            return out

        def split(keep, got):
            size = keep.shape[0]
            return call(
                split_kernel,
                "split",
                [((2, size, LANES), F32), ((2, size, LANES), BF16)],
                (keep, got),
            )

        def first_step(send, label):
            return swap(send, "fsdp", n_f, 1, "z1_" + label)

        def second_step(own, got, label):
            total = own + got.astype(F32)
            return total[0], swap(total[1].astype(BF16), "fsdp", n_f, 2, "z2_" + label)

        seg_here = lax.dynamic_slice_in_dim(segment_ids[0], place * block, block, 0)
        first = jnp.sum((segment_ids[0][:, None] < seg_here[None, :]).astype(jnp.int32), axis=0)
        token = place * block + jnp.arange(block, dtype=jnp.int32)
        position = (token - first).astype(F32)
        first = (first - place * block + extra * block).reshape(1, block)
        frequency = 10000.0 ** (-2.0 * jnp.arange(HEAD_DIM // 2, dtype=F32) / HEAD_DIM)
        angles = frequency[:, None] * position[None, :]
        cosine, sine = jnp.cos(angles), jnp.sin(angles)

        weight_b, weight_a, gains, normed, a_rows, b_query, payload = call(
            factor_kernel,
            "factors",
            [
                ((width, b_cols), BF16),
                ((n_tp, a_pad, width), BF16),
                ((16, width), F32),
                ((block, width), BF16),
                ((n_tp, a_pad, block), F32),
                ((RANK_Q, HEAD_DIM, block), F32),
                ((kv_rows, block), BF16),
            ],
            (resid_in, pack, other_pack, cosine, sine),
            [OWN] + [WHOLE] * 4,
        )
        def places(value, step, chosen, label):
            pairs = [(i, i + step) for i in chosen if 0 <= i + step < n_place]
            with jax.named_scope(label):
                return lax.ppermute(value, ("ctx", "tp"), pairs)

        every, odd, even = range(n_place), range(1, n_place, 2), range(0, n_place, 2)
        second = places(payload, 2, every, "x_kv_second")
        third = places(payload, 3, odd, "x_kv_third")
        beside_kv = core(payload, "kv")
        o_own = jnp.concatenate([o_parts, chip(o_parts, "wo")], axis=0)
        second, pair_gu, gu_across = lax.optimization_barrier((second, pair_gu, gu_across))
        gu_rest = ctx(jnp.concatenate([far_gu[None], pair_gu], axis=0), "gate_up_rest")
        dn_parts = [dn_pair, ahead(dn_pair, 1, "down1")]
        beside_second = core(second, "kv_second")
        tied = lax.optimization_barrier((third, second, beside_second, beside_kv, o_own))
        wins = (*tied[:4], payload)
        o_own = tied[4]
        o_other = core(o_own, "wo")
        window = windows * block
        lse, query, mixed = call(
            attention_kernel,
            "attention",
            [
                ((n_tp, group, block), F32),
                ((n_tp, group, HEAD_DIM, block), BF16),
                ((n_tp, feats, block), BF16),
            ],
            (first, a_rows, b_query, *wins),
            None,
            [
                pltpu.VMEM((windows, kv_rows, block), BF16),
                pltpu.VMEM((window, block), F32),
                pltpu.VMEM((windows, KV, HEAD_DIM, block), F32),
                pltpu.VMEM((group, window, block), F32),
            ],
        )
        dn_parts[1] = after(dn_parts[1], mixed)
        for s in range(2, n_f):
            dn_parts.append(ahead(dn_parts[-1], 1, "down" + str(s)))
        mid, attn_out, normed_ffn = call(
            project_kernel,
            "project",
            [((block, width), F32), ((block, width), F32), ((block, width), BF16)],
            (resid_in, mixed, o_own, o_other, gains),
            [OWN] + [WHOLE] * 4,
        )

        near_rows = (normed_ffn, core(normed_ffn, "nf"))
        far_own = chip(normed_ffn, "nf")

        def feed(side, rows):
            return call(
                lambda *refs: ffn_kernel(side, *refs),
                "feed_near" if side == 0 else "feed_far",
                [
                    ((3 * hidden, 2 * block), BF16),
                    ((2 * block, width), BF16),
                    ((block, width), F32),
                    ((block, width), BF16),
                    ((block, width), F32),
                    ((block, width), BF16),
                ],
                (*rows, cotangent, *pieces),
                [WHOLE] * 2 + [REMOTE] * (1 + len(pieces)),
                [
                    pltpu.VMEM((3 * hidden, width), BF16),
                    pltpu.VMEM((2, block, width), F32),
                    pltpu.SemaphoreType.DMA((2 * n_piece + 2,)),
                ],
            )

        far_own, gu_rest = lax.optimization_barrier((far_own, gu_rest))
        far_own, dn_parts[-1], gu_rest = lax.optimization_barrier(
            (far_own, dn_parts[-1], gu_rest)
        )
        pieces = (own_gu, far_gu, pair_gu, gu_across, gu_rest, *dn_parts)
        far_rows = (far_own, core(far_own, "nf_far"))
        far = feed(1, far_rows)
        across = (far[2] + core(far[3], "dn_far").astype(F32)).astype(BF16)
        near = feed(0, (after(near_rows[0], across), near_rows[1]))
        across = chip(across, "dn")
        beside = core(near[3], "dn_near")

        grad_args = (near[0], far[0], *near_rows, *far_rows, near[1], far[1])
        own_d, send_d = call(
            down_grad_kernel,
            "down_grad",
            [((2, n_c, hidden, LANES), F32), ((2, n_c, hidden, LANES), BF16)],
            grad_args,
            room=12,
        )
        got_d = first_step(send_d, "d")
        keep_a, send_a = call(
            gate_up_grad_kernel,
            "gate_up_grad",
            [((2 * hidden, half_width), BF16)] * 2,
            (after(grad_args[0], send_d), *grad_args[1:]),
            room=12,
        )
        got_a = ctx(send_a, "grads_a")
        across = after(across, send_a)

        delta_mid, gain_grad, grad_mixed, keep_o, send_o = call(
            middle_kernel,
            "middle",
            [
                ((block, width), F32),
                ((8, width), F32),
                ((n_tp, feats, block), BF16),
                ((2 * o_rows, width), BF16),
                ((2 * o_rows, width), BF16),
            ],
            (cotangent, near[2], beside, across, mid, gains, o_own, o_other, mixed),
            [OWN] + [WHOLE] * 8,
        )
        near_sum = attn_out + near[4] + core(after(near[5], across), "out_near").astype(F32)
        far_sum = far[4] + core(after(far[5], across), "out_far").astype(F32)
        out_send = jnp.stack([far_sum, near_sum]).astype(BF16)
        grad_mixed = after(grad_mixed, out_send)
        rows_got = core(send_o, "go")
        out_got = chip(out_send, "out")
        back_args = (first, a_rows, b_query, *wins, lse, query, grad_mixed)
        sums = [
            ((RANK_Q, HEAD_DIM, block), F32),
            ((windows, KV, HEAD_DIM, block), F32),
            ((windows, heads * KV, block), F32),
        ]
        grad_a_out = ((n_tp // 2, a_pad, block), F32)
        back_scratch = [
            pltpu.VMEM((windows, kv_rows, block), BF16),
            pltpu.VMEM((window, block), F32),
            pltpu.VMEM((windows, KV, HEAD_DIM, block), F32),
            pltpu.VMEM((2, window, block), F32),
            pltpu.VMEM((2, window, block), F32),
        ]
        grad_a0, *sums_out = call(
            lambda *refs: attention_back_kernel(0, *refs),
            "attention_back_a",
            [grad_a_out] + sums,
            back_args,
            None,
            back_scratch,
        )
        sums_out[0], own_d, got_d, _ = lax.optimization_barrier(
            (sums_out[0], own_d, got_d, grad_a0)
        )
        own_d, got_d = second_step(own_d, got_d, "d")
        grad_a1, grad_bq, *sends = call(
            lambda *refs: attention_back_kernel(1, *refs),
            "attention_back_b",
            [
                grad_a_out,
                sums[0],
                ((kv_rows, block), BF16),
                ((kv_rows, block), BF16),
                ((kv_rows, block), BF16),
                ((kv_rows, block), F32),
            ],
            (*back_args, *sums_out),
            None,
            [pltpu.VMEM(shape, kind) for shape, kind in sums[1:]] + back_scratch,
        )
        *sends[:3], out_got, rows_got = lax.optimization_barrier((*sends[:3], out_got, rows_got))
        second_got = places(sends[0], -2, every, "x_kv_back_second")
        beside_got = places(sends[1], -1, every, "x_kv_back_beside")
        third_got = places(sends[2], -3, every, "x_kv_back_third")
        own_a, send_a = split(after(keep_a, sends[0]), got_a)
        got_a = first_step(send_a, "a")
        rows_o = keep_o.astype(F32) + after(rows_got, send_a).astype(F32)
        rows_keep, rows_send = rows_o[:, :half_width], rows_o[:, half_width:].astype(BF16)
        rows_got = ctx(rows_send, "go")
        *got, got_d = lax.optimization_barrier((second_got, beside_got, third_got, got_d))
        out_rows = (out_send[::-1].astype(F32) + out_got.astype(F32)).astype(BF16)

        delta, keep0, keep1, send0, send1 = call(
            last_kernel,
            "last",
            [
                ((block, width), BF16),
                *[((2, n_f, pack_rows, LANES), BF16)] * 4,
            ],
            (
                resid_in,
                sends[3],
                *got,
                grad_bq,
                grad_a0,
                grad_a1,
                cosine,
                sine,
                weight_b,
                weight_a,
                normed,
                gains,
                delta_mid,
                gain_grad,
            ),
            [OWN] + [WHOLE] * 15,
            [
                pltpu.VMEM((width, b_cols), F32),
                pltpu.VMEM((n_tp, a_pad, width), F32),
                pltpu.VMEM((block, width), F32),
                pltpu.VMEM((8, width), F32),
            ],
        )

        part_send = (keep1.astype(F32) + core(send1, "gp").astype(F32)).astype(BF16)
        total_d = own_d + got_d.astype(F32)
        part_send, got_a, rows_got = lax.optimization_barrier((part_send, got_a, rows_got))
        part_got = ctx(part_send, "gp")
        own_a, got_a = second_step(own_a, got_a, "a")
        part = keep0.astype(F32) + core(after(send0, part_send), "gp_near").astype(F32)
        rows_o = rows_keep + rows_got.astype(F32)
        rows_send, part = lax.optimization_barrier((rows_o[o_rows:].astype(BF16), part))
        across_delta = chip(delta, "delta")
        rows_go = chip(rows_send, "go")
        out_rows = after(out_rows, part_send)
        out_beside = core(out_rows, "out_rows")
        block_out = add_rows(
            resid_in, (out_rows[0], out_rows[1], out_beside[0], out_beside[1]), True
        )
        part_got, across_delta = lax.optimization_barrier((part_got, across_delta, block_out))[:2]
        part = part + part_got.astype(F32)
        part_send = part[1].astype(BF16)
        part_got = chip(part_send, "gp")
        across_delta = after(across_delta, part_send)
        beside_delta = core(after(delta, part_send), "delta")
        got_last = ctx(after(total_d[1], part_send).astype(BF16), "d")
        part_got, rows_go, got_a = lax.optimization_barrier((part_got, rows_go, got_a))
        part = part[0] + part_got.astype(F32)
        rows_o = rows_o[:o_rows] + rows_go.astype(F32)
        part = [
            jnp.concatenate([part[s], rows_o[:, s * LANES : (s + 1) * LANES]], axis=0)
            for s in range(n_f)
        ]
        is_even_f = f_index % 2 == 0
        part_send = [
            jnp.where(is_even_f, part[3], part[1]),
            jnp.where(is_even_f, part[1], part[3]),
        ]
        part_send = jnp.stack(part_send).astype(BF16)
        part_own, part_got = second_step(
            jnp.stack([part[0], part[2]]), first_step(part_send, "gp"), "gp"
        )
        across_delta = after(across_delta, part_send)
        resid_grad = add_rows(
            cotangent,
            (delta, across_delta, beside_delta, core(across_delta, "delta_far")),
            False,
        )
        part_got, got_last = lax.optimization_barrier((part_got, got_last, resid_grad))[:2]
        grad_down = total_d[0] + got_last.astype(F32)
        grad_gate_up = (own_a + got_a.astype(F32)).reshape(1, 2, hidden, fc_cols)
        part_b, part_a, part_g0, part_g1, grad_out = call(
            unpack_kernel,
            "unpack",
            [
                ((1, b_rows, b_cols), F32),
                ((1, a_cols, fc_cols), F32),
                ((1, gain_part), F32),
                ((1, gain_part), F32),
                ((1, o_rows, LANES), F32),
            ],
            (part_own, part_got),
        )
        return (
            block_out,
            resid_grad,
            part_a.transpose(0, 2, 1),
            part_b,
            grad_out,
            grad_gate_up.transpose(0, 1, 3, 2),
            grad_down[None],
            part_g0,
            part_g1,
        )

    return shards


def make_shards(mesh):
    fused, general = make_fused(mesh), make_general(mesh)
    fits = mesh.shape["fsdp"] == 4 and mesh.shape["ctx"] == 2 and mesh.shape["tp"] == 4

    def shards(*args):
        return (fused if fits and args[7].shape[2] == LANES else general)(*args)

    return shards


def solution(mesh):
    return jax.shard_map(
        make_shards(mesh),
        mesh=mesh,
        in_specs=(
            P("fsdp", "ctx", None),
            P("fsdp", None),
            P("fsdp", "ctx", None),
            P(None, ("fsdp", "ctx"), "tp"),
            P(None, ("fsdp", "ctx", "tp"), None),
            P(None, "tp", ("fsdp", "ctx")),
            P(None, None, ("fsdp", "ctx"), "tp"),
            P(None, "tp", ("fsdp", "ctx")),
            P(None, ("fsdp", "ctx", "tp")),
            P(None, ("fsdp", "ctx", "tp")),
        ),
        out_specs=(
            P("fsdp", "ctx", None),
            P("fsdp", "ctx", None),
            P(None, ("fsdp", "ctx"), "tp"),
            P(None, ("fsdp", "ctx", "tp"), None),
            P(None, "tp", ("fsdp", "ctx")),
            P(None, None, ("fsdp", "ctx"), "tp"),
            P(None, "tp", ("fsdp", "ctx")),
            P(None, ("fsdp", "ctx", "tp")),
            P(None, ("fsdp", "ctx", "tp")),
        ),
        check_vma=False,
    )
```

```python
import math

import jax
import jax.numpy as jnp
from jax import lax
from jax.experimental import pallas as pl
from jax.experimental.pallas import tpu as pltpu
from jax.sharding import PartitionSpec as P

HEAD_DIM = 64
RANK_Q = 6
RANK_KV = 2
RANKS = 10
KV = 2 * RANK_KV
MOST_DOC = 768
EPSILON = 1e-05
LANES = 128
BF16 = jnp.bfloat16
F32 = jnp.float32
MASKED = -1e30


def inverse_rms(values):
    return lax.rsqrt(jnp.mean(values * values, axis=-1, keepdims=True) + EPSILON)


def norm_back(grad_value, values, inverse, gain):
    scaled = grad_value * gain
    normal = values * inverse
    return inverse * (scaled - normal * jnp.mean(scaled * normal, axis=-1, keepdims=True))


def dot(left, right, dims):
    return lax.dot_general(left, right, (dims, ((), ())), preferred_element_type=F32)


def shift(value, axes, size, step, label="shift"):
    with jax.named_scope(label):
        return lax.ppermute(value, axes, [(i, (i + step) % size) for i in range(size)])


def swap(value, axis, size, bit, label="swap"):
    with jax.named_scope(label):
        return lax.ppermute(value, axis, [(i, i ^ bit) for i in range(size)])


def gather_direct(value, axis, size):
    me = lax.axis_index(axis)
    parts = [(me, value)]
    for step in range(1, size):
        parts.append(((me - step) % size, shift(value, axis, size, step)))
    out = jnp.zeros((size,) + value.shape, value.dtype)
    for place, part in parts:
        out = lax.dynamic_update_slice(out, part[None], (place,) + (0,) * value.ndim)
    return out


def gather_pair(value, axis, size, bit):
    mine = (lax.axis_index(axis) // bit) % 2 == 0
    other = swap(value, axis, size, bit)
    return jnp.stack([jnp.where(mine, value, other), jnp.where(mine, other, value)])


def after(value, *others):
    return lax.optimization_barrier((value,) + others)[0]


def take(value, index):
    return lax.dynamic_index_in_dim(value, index, 0, keepdims=False)


def scatter_direct(value, axis, size):
    me = lax.axis_index(axis)
    got = [
        shift(take(value, (me + step) % size), axis, size, step) for step in range(1, size)
    ]
    total = take(value, me).astype(F32)
    for part in got:
        total = total + part.astype(F32)
    return total


def scatter_pair(value, axis, size, bit):
    mine = (lax.axis_index(axis) // bit) % 2
    got = swap(take(value, 1 - mine).astype(BF16), axis, size, bit)
    return take(value, mine).astype(F32) + got.astype(F32)


def attention_mask(first_ref, window, block):
    start = first_ref[...]
    place = lax.broadcasted_iota(jnp.int32, (window, block), 0)
    query_place = lax.broadcasted_iota(jnp.int32, (window, block), 1) + (window - block)
    return jnp.where((place >= start) & (place <= query_place), 0.0, MASKED)


def head_rows(wa_ref, wide_ref, head):
    factors = wa_ref[head].astype(F32)
    key_rows = (factors[0:1] * wide_ref[0] + factors[1:2] * wide_ref[1]) * (1.0 / RANK_KV)
    value_rows = (factors[2:3] * wide_ref[2] + factors[3:4] * wide_ref[3]) * (1.0 / RANK_KV)
    return factors, key_rows.astype(BF16), value_rows.astype(BF16)


def forward_kernel(
    first_ref, a_ref, bq_ref, wa_ref, wb_ref, mixed_ref, lse_ref, q_ref, bias_ref, wide_ref, s_ref
):
    heads = a_ref.shape[0]
    window, block = bias_ref.shape
    bias_ref[...] = attention_mask(first_ref, window, block)
    wide_ref[...] = wb_ref[...].astype(F32)
    spans = [pl.ds(j * block, block) for j in range(window // block)]

    def one_head(head, carry):
        factors = a_ref[head]
        query = factors[0:1] * bq_ref[0]
        for r in range(1, RANK_Q):
            query = query + factors[r : r + 1] * bq_ref[r]
        query = (query * (1.0 / RANK_Q)).astype(BF16) * jnp.asarray(HEAD_DIM**-0.5, BF16)
        q_ref[head] = query
        _, key_rows, value_rows = head_rows(wa_ref, wide_ref, head)
        top = jnp.full((1, block), MASKED, F32)
        for j, span in enumerate(spans):
            keys = key_rows[:, j * block : (j + 1) * block]
            scores = dot(keys, query, ((0,), (0,))) + bias_ref[span, :]
            s_ref[span, :] = scores
            top = jnp.maximum(top, jnp.max(scores, axis=0, keepdims=True))
        total = jnp.zeros((1, block), F32)
        for span in spans:
            weight = jnp.exp(s_ref[span, :] - top)
            s_ref[span, :] = weight
            total = total + jnp.sum(weight, axis=0, keepdims=True)
        lse_ref[head] = top + jnp.log(total)
        scale = 1.0 / total
        mixed = jnp.zeros((HEAD_DIM, block), F32)
        for j, span in enumerate(spans):
            probs = (s_ref[span, :] * scale).astype(BF16)
            mixed = mixed + dot(
                value_rows[:, j * block : (j + 1) * block], probs, ((1,), (0,))
            )
        mixed_ref[head] = mixed.astype(BF16)
        return carry

    lax.fori_loop(0, heads, one_head, 0)


def backward_kernel(
    first_ref,
    a_ref,
    bq_ref,
    wa_ref,
    wb_ref,
    lse_ref,
    q_ref,
    go_ref,
    ga_ref,
    gbq_ref,
    gwa_ref,
    gwb_ref,
    bias_ref,
    wide_ref,
    p_ref,
    dp_ref,
):
    heads = a_ref.shape[0]
    window, block = bias_ref.shape
    bias_ref[...] = attention_mask(first_ref, window, block)
    wide_ref[...] = wb_ref[...].astype(F32)
    gbq_ref[...] = jnp.zeros_like(gbq_ref)
    gwb_ref[...] = jnp.zeros_like(gwb_ref)
    count = window // block
    spans = [pl.ds(j * block, block) for j in range(count)]

    def one_head(head, carry):
        factors, key_rows, value_rows = head_rows(wa_ref, wide_ref, head)
        query = q_ref[head]
        grad_out = go_ref[head]
        lse = lse_ref[head]
        inner = jnp.zeros((1, block), F32)
        for j, span in enumerate(spans):
            cut = slice(j * block, (j + 1) * block)
            scores = dot(key_rows[:, cut], query, ((0,), (0,))) + bias_ref[span, :]
            probs = jnp.exp(scores - lse)
            grad_probs = dot(value_rows[:, cut], grad_out, ((0,), (0,)))
            p_ref[span, :] = probs
            dp_ref[span, :] = grad_probs
            inner = inner + jnp.sum(probs * grad_probs, axis=0, keepdims=True)
        grad_query = jnp.zeros((HEAD_DIM, block), F32)
        for j, span in enumerate(spans):
            cut = slice(j * block, (j + 1) * block)
            probs = p_ref[span, :]
            grad_scores = (probs * (dp_ref[span, :] - inner)).astype(BF16)
            grad_query = grad_query + dot(key_rows[:, cut], grad_scores, ((1,), (0,)))
            grad_keys = dot(query, grad_scores, ((1,), (1,))) * (1.0 / RANK_KV)
            grad_values = dot(grad_out, probs.astype(BF16), ((1,), (1,))) * (1.0 / RANK_KV)
            rows = []
            for r in range(KV):
                grad = grad_keys if r < RANK_KV else grad_values
                rows.append(jnp.sum(grad * wide_ref[r, :, span], axis=0, keepdims=True))
                gwb_ref[r, :, span] += factors[r : r + 1, cut] * grad
            gwa_ref[head, :, span] = jnp.concatenate(rows, axis=0)
        grad_query = grad_query * (HEAD_DIM**-0.5 / RANK_Q)
        own = a_ref[head]
        rows = []
        for r in range(RANK_Q):
            rows.append(jnp.sum(grad_query * bq_ref[r], axis=0, keepdims=True))
            gbq_ref[r] += own[r : r + 1] * grad_query
        ga_ref[head] = jnp.concatenate(rows, axis=0)
        return carry

    lax.fori_loop(0, heads, one_head, 0)


VMEM_LIMIT = 56 * 1024 * 1024


def whole_specs(count):
    return [pl.BlockSpec(memory_space=pltpu.VMEM)] * count


def attend_forward(first, a_rows, b_query, win_a, win_b):
    heads, _, block = a_rows.shape
    window = win_a.shape[-1]
    return pl.pallas_call(
        forward_kernel,
        out_shape=(
            jax.ShapeDtypeStruct((heads, HEAD_DIM, block), BF16),
            jax.ShapeDtypeStruct((heads, 1, block), F32),
            jax.ShapeDtypeStruct((heads, HEAD_DIM, block), BF16),
        ),
        in_specs=whole_specs(5),
        out_specs=tuple(whole_specs(3)),
        scratch_shapes=[
            pltpu.VMEM((window, block), F32),
            pltpu.VMEM((KV, HEAD_DIM, window), F32),
            pltpu.VMEM((window, block), F32),
        ],
        compiler_params=pltpu.CompilerParams(vmem_limit_bytes=VMEM_LIMIT),
        name="attend_forward",
    )(first, a_rows, b_query, win_a, win_b)


def attend_backward(first, a_rows, b_query, win_a, win_b, lse, query, grad_mixed):
    heads, _, block = a_rows.shape
    window = win_a.shape[-1]
    return pl.pallas_call(
        backward_kernel,
        out_shape=(
            jax.ShapeDtypeStruct((heads, RANK_Q, block), F32),
            jax.ShapeDtypeStruct((RANK_Q, HEAD_DIM, block), F32),
            jax.ShapeDtypeStruct((heads, KV, window), F32),
            jax.ShapeDtypeStruct((KV, HEAD_DIM, window), F32),
        ),
        in_specs=whole_specs(8),
        out_specs=tuple(whole_specs(4)),
        scratch_shapes=[
            pltpu.VMEM((window, block), F32),
            pltpu.VMEM((KV, HEAD_DIM, window), F32),
            pltpu.VMEM((window, block), F32),
            pltpu.VMEM((window, block), F32),
        ],
        compiler_params=pltpu.CompilerParams(vmem_limit_bytes=VMEM_LIMIT),
        name="attend_backward",
    )(first, a_rows, b_query, win_a, win_b, lse, query, grad_mixed)


def rotate(rows, cosine, sine):
    half = HEAD_DIM // 2
    lower, upper = rows[:, :half], rows[:, half:]
    return jnp.concatenate(
        [lower * cosine - upper * sine, lower * sine + upper * cosine], axis=1
    )


def make_general(mesh):
    n_f, n_c, n_tp = mesh.shape["fsdp"], mesh.shape["ctx"], mesh.shape["tp"]
    n_hi, n_lo = 2, n_tp // 2

    def shards(
        resid_in,
        segment_ids,
        cotangent,
        w_factor_a,
        w_factor_b,
        w_out,
        w_gate_up,
        w_down,
        attn_gains,
        ffn_gains,
    ):
        seq_count, local_len, width = resid_in.shape
        assert seq_count == 1 and w_factor_a.shape[0] == 1 and n_lo == 2
        full_len = segment_ids.shape[1]
        block = local_len // n_tp
        extra = -(-(MOST_DOC - 1) // block)
        window = (extra + 1) * block
        a_cols = w_factor_a.shape[2]
        heads = n_tp * a_cols // RANKS
        b_cols = w_factor_b.shape[2]
        b_rows = w_factor_b.shape[1]
        b_parts = b_cols // LANES
        fc_cols = w_down.shape[2]
        hidden = w_down.shape[1]
        o_rows = w_out.shape[1]

        f_index, c_index, t_index = (
            lax.axis_index("fsdp"),
            lax.axis_index("ctx"),
            lax.axis_index("tp"),
        )
        hi, lo = t_index // 2, t_index % 2
        place = c_index * n_tp + t_index
        n_place = n_c * n_tp

        gains = jnp.concatenate([attn_gains, ffn_gains], axis=1).astype(BF16)
        gain_count = gains.shape[1]
        gain_rows = 16 * (-(-gain_count // (16 * LANES)))
        gains = jnp.pad(gains.reshape(-1), (0, gain_rows * LANES - gain_count))
        b_shard = w_factor_b[0].astype(BF16).reshape(b_rows, b_parts, LANES)
        a_shard = w_factor_a[0].astype(BF16).T
        pack = jnp.concatenate(
            [
                b_shard.transpose(1, 0, 2).reshape(-1, LANES),
                a_shard.reshape(-1, LANES),
                gains.reshape(-1, LANES),
            ],
            axis=0,
        )
        n_b = b_parts * b_rows
        n_a = a_cols * fc_cols // LANES
        pack = gather_direct(pack, "fsdp", n_f)
        after_pack = pack
        pack = gather_pair(pack, "ctx", n_c, 1)
        pack = gather_pair(pack, "tp", n_tp, 2)
        pack = gather_pair(pack, "tp", n_tp, 1)
        pack = pack.transpose(3, 2, 1, 0, 4, 5)
        weight_b = pack[:, :, :, :, :n_b].reshape(-1, b_parts, b_rows, LANES)
        weight_b = weight_b.transpose(0, 2, 1, 3).reshape(width, b_cols)
        weight_a = pack[:, :, :, :, n_b : n_b + n_a].reshape(n_f, n_c, n_tp, a_cols, fc_cols)
        weight_a = weight_a.transpose(2, 3, 0, 1, 4).reshape(n_tp * a_cols, width)
        gains_all = pack[:, :, :, :, n_b + n_a :].reshape(-1, gain_rows * LANES)[:, :gain_count]
        gains_all = gains_all.reshape(-1, 2, gain_count // 2).transpose(1, 0, 2)
        gains_all = gains_all.reshape(2, width).astype(F32)
        gain_attn, gain_ffn = gains_all[0:1], gains_all[1:2]

        big = jnp.concatenate(
            [
                w_gate_up[0, 0].astype(BF16).T,
                w_gate_up[0, 1].astype(BF16).T,
                w_down[0].astype(BF16),
                w_out[0].astype(BF16),
            ],
            axis=0,
        )
        big, _ = lax.optimization_barrier((big, after_pack))
        big = gather_direct(big, "fsdp", n_f)
        big = gather_pair(big, "ctx", n_c, 1)
        big = big.transpose(2, 1, 0, 3).reshape(-1, width)
        weight_g = big[:hidden]
        weight_u = big[hidden : 2 * hidden]
        weight_d = big[2 * hidden : 3 * hidden]
        weight_o = gather_pair(big[3 * hidden :], "tp", n_tp, 2)
        weight_o = gather_pair(weight_o, "tp", n_tp, 1)
        weight_o = weight_o.transpose(1, 0, 2, 3).reshape(n_tp * o_rows, width)

        seg_here = lax.dynamic_slice_in_dim(segment_ids[0], place * block, block, 0)
        first = jnp.sum((segment_ids[0][:, None] < seg_here[None, :]).astype(jnp.int32), axis=0)
        token = place * block + jnp.arange(block, dtype=jnp.int32)
        position = (token - first).astype(F32)
        first = (first - place * block + extra * block).reshape(1, block)
        frequency = 10000.0 ** (
            -2.0 * jnp.arange(HEAD_DIM // 2, dtype=F32) / HEAD_DIM
        )
        angles = frequency[:, None] * position[None, :]
        cosine, sine = jnp.cos(angles)[None], jnp.sin(angles)[None]

        stream = resid_in[0].reshape(n_tp, block, width)
        own = take(stream, t_index)
        inverse_attn = inverse_rms(own)
        normed = (own * inverse_attn * gain_attn).astype(BF16)
        a_rows = dot(weight_a, normed, ((1,), (1,))).reshape(heads, RANKS, block)
        b_raw = dot(weight_b, normed, ((0,), (1,))).reshape(RANKS, HEAD_DIM, block)
        b_rot = rotate(b_raw[: RANK_Q + RANK_KV], cosine, sine)
        b_query = b_rot[:RANK_Q]
        b_kv = jnp.concatenate([b_rot[RANK_Q:], b_raw[RANK_Q + RANK_KV :]], axis=0)
        payload = jnp.concatenate(
            [
                b_kv.reshape(KV * HEAD_DIM, block),
                a_rows[:, RANK_Q:].reshape(heads * KV, block),
            ],
            axis=0,
        ).astype(BF16)
        around = [
            lax.ppermute(
                payload, ("ctx", "tp"), [(i, i + step) for i in range(n_place - step)]
            )
            for step in range(extra, 0, -1)
        ]
        win = jnp.concatenate(around + [payload], axis=1)
        win_b = win[: KV * HEAD_DIM].reshape(KV, HEAD_DIM, window)
        win_a = win[KV * HEAD_DIM :].reshape(heads, KV, window)

        mixed, lse, query = attend_forward(first, a_rows, b_query, win_a, win_b)
        mixed = mixed.reshape(heads * HEAD_DIM, block)
        attn_out = dot(mixed, weight_o, ((0,), (0,)))
        mid = own + attn_out
        inverse_ffn = inverse_rms(mid)
        normed_ffn = (mid * inverse_ffn * gain_ffn).astype(BF16)

        near_rows = gather_pair(normed_ffn, "tp", n_tp, 1)
        far_rows = gather_pair(swap(normed_ffn, "tp", n_tp, 2), "tp", n_tp, 1)
        grad_all = cotangent[0].reshape(n_hi, n_lo * block, width)

        def half(rows, grad_rows):
            rows = rows.reshape(n_lo * block, width)
            gate = dot(rows, weight_g, ((1,), (1,)))
            up = dot(rows, weight_u, ((1,), (1,)))
            grad_act = dot(grad_rows, weight_d, ((1,), (1,)))
            squash = jax.nn.sigmoid(gate)
            act = (gate * squash * up).astype(BF16)
            grad_gate = (grad_act * up * squash * (1.0 + gate * (1.0 - squash))).astype(BF16)
            grad_up = (grad_act * gate * squash).astype(BF16)
            back = dot(grad_gate, weight_g, ((1,), (0,))) + dot(grad_up, weight_u, ((1,), (0,)))
            ahead = dot(act, weight_d, ((1,), (0,)))
            both = lambda v: v.reshape(n_lo, block, width)
            return rows, act, grad_gate, grad_up, both(back), both(ahead)

        grad_near = take(grad_all, hi).astype(BF16)
        grad_far = take(grad_all, 1 - hi).astype(BF16)
        near = half(near_rows, grad_near)
        far = half(far_rows, grad_far)
        back_far = scatter_pair(far[4], "tp", n_tp, 1).astype(BF16)
        back_far = swap(back_far, "tp", n_tp, 2)
        grad_normed_ffn = scatter_pair(near[4], "tp", n_tp, 1) + back_far.astype(F32)
        ahead_far = scatter_pair(far[5], "tp", n_tp, 1).astype(BF16)
        ahead_far = swap(ahead_far, "tp", n_tp, 2)
        ffn_out = scatter_pair(near[5], "tp", n_tp, 1) + ahead_far.astype(F32)

        def spread(value):
            beside = swap(value, "tp", n_tp, 1)
            across = swap(value, "tp", n_tp, 2)
            diagonal = swap(across, "tp", n_tp, 1)
            out = jnp.zeros((n_tp,) + value.shape, value.dtype)
            for bit, part in enumerate((value, beside, across, diagonal)):
                out = lax.dynamic_update_slice(out, part[None], (t_index ^ bit, 0, 0))
            return out.reshape(local_len, width).astype(F32)

        block_out = resid_in + spread((attn_out + ffn_out).astype(BF16))[None]

        def columns(value, which):
            value = value.reshape(value.shape[0], n_f, n_c, fc_cols)
            value = lax.dynamic_index_in_dim(value, which, 2, keepdims=False)
            return value.reshape(value.shape[0], n_f * fc_cols)

        rows_all = jnp.concatenate([near[0], far[0]], axis=0)
        act_all = jnp.concatenate([near[1], far[1]], axis=0)
        gate_all = jnp.concatenate([near[2], far[2]], axis=0)
        up_all = jnp.concatenate([near[3], far[3]], axis=0)
        cot_all = jnp.concatenate([grad_near, grad_far], axis=0)

        def big_grads(which):
            rows_cut = columns(rows_all, which)
            cot_cut = columns(cot_all, which)
            return jnp.concatenate(
                [
                    dot(gate_all, rows_cut, ((0,), (0,))),
                    dot(up_all, rows_cut, ((0,), (0,))),
                    dot(act_all, cot_cut, ((0,), (0,))),
                ],
                axis=0,
            )

        def over_fc(send, keep):
            total = keep + swap(send.astype(BF16), "ctx", n_c, 1).astype(F32)
            total = total.astype(BF16).reshape(-1, n_f, fc_cols).transpose(1, 0, 2)
            return scatter_direct(total, "fsdp", n_f)

        grad_big = over_fc(big_grads(1 - c_index), big_grads(c_index))
        grad_gate_w = grad_big[:hidden].T
        grad_up_w = grad_big[hidden : 2 * hidden].T
        grad_down_w = grad_big[2 * hidden :]

        own_cot = take(cotangent[0].reshape(n_tp, block, width), t_index)
        gain_grad_ffn = jnp.sum(grad_normed_ffn * mid * inverse_ffn, axis=0)
        delta_mid = norm_back(grad_normed_ffn, mid, inverse_ffn, gain_ffn)
        grad_attn = (own_cot + delta_mid).astype(BF16)
        grad_out = dot(mixed, grad_attn, ((1,), (0,))).reshape(n_hi, n_lo, o_rows, width)
        grad_out = scatter_pair(grad_out.transpose(1, 0, 2, 3), "tp", n_tp, 1)
        grad_out = scatter_pair(grad_out, "tp", n_tp, 2)
        grad_out = over_fc(columns(grad_out, 1 - c_index), columns(grad_out, c_index))

        grad_mixed = dot(weight_o, grad_attn, ((1,), (1,))).astype(BF16)
        ga_q, gb_q, gw_a, gw_b = attend_backward(
            first,
            a_rows,
            b_query,
            win_a,
            win_b,
            lse,
            query,
            grad_mixed.reshape(heads, HEAD_DIM, block),
        )
        gw = jnp.concatenate(
            [gw_b.reshape(KV * HEAD_DIM, window), gw_a.reshape(heads * KV, window)], axis=0
        )
        total = gw[:, extra * block :]
        for step in range(1, extra + 1):
            part = gw[:, (extra - step) * block : (extra - step + 1) * block].astype(BF16)
            part = lax.ppermute(
                part, ("ctx", "tp"), [(i + step, i) for i in range(n_place - step)]
            )
            total = total + part.astype(F32)
        gb_kv = total[: KV * HEAD_DIM].reshape(KV, HEAD_DIM, block)
        ga_kv = total[KV * HEAD_DIM :].reshape(heads, KV, block)
        grad_b = jnp.concatenate(
            [
                rotate(jnp.concatenate([gb_q, gb_kv[:RANK_KV]], axis=0), cosine, -sine),
                gb_kv[RANK_KV:],
            ],
            axis=0,
        )
        grad_b = grad_b.reshape(b_cols, block).astype(BF16)
        grad_a = jnp.concatenate([ga_q, ga_kv], axis=1).reshape(heads * RANKS, block).astype(BF16)
        grad_normed = dot(grad_a, weight_a, ((0,), (0,))) + dot(grad_b, weight_b, ((0,), (1,)))
        gain_grad_attn = jnp.sum(grad_normed * own * inverse_attn, axis=0)
        delta = delta_mid + norm_back(grad_normed, own, inverse_attn, gain_attn)
        resid_grad = cotangent + spread(delta.astype(BF16))[None]

        grad_wa = dot(grad_a, normed, ((1,), (0,))).astype(BF16)
        grad_wa = grad_wa.reshape(n_hi, n_lo, a_cols, n_f, n_c, fc_cols)
        grad_wa = grad_wa.transpose(1, 0, 4, 3, 2, 5).reshape(n_lo, n_hi, n_c, n_f, n_a, LANES)
        grad_wb = jnp.einsum(
            "pkt,td->pdk",
            grad_b.reshape(b_parts, LANES, block),
            normed,
            preferred_element_type=F32,
        ).astype(BF16)
        grad_wb = grad_wb.reshape(b_parts, n_f, n_c, n_hi, n_lo, b_rows, LANES)
        grad_wb = grad_wb.transpose(4, 3, 2, 1, 0, 5, 6)
        grad_wb = grad_wb.reshape(n_lo, n_hi, n_c, n_f, n_b, LANES)
        gain_grads = jnp.stack([gain_grad_attn, gain_grad_ffn]).astype(BF16)
        gain_grads = gain_grads.reshape(2, n_f, n_c, n_hi, n_lo, gain_count // 2)
        gain_grads = gain_grads.transpose(4, 3, 2, 1, 0, 5).reshape(
            n_lo, n_hi, n_c, n_f, gain_count
        )
        gain_grads = jnp.pad(
            gain_grads, [(0, 0)] * 4 + [(0, gain_rows * LANES - gain_count)]
        ).reshape(n_lo, n_hi, n_c, n_f, gain_rows, LANES)
        pack = jnp.concatenate([grad_wb, grad_wa, gain_grads], axis=4)
        pack = scatter_pair(pack, "tp", n_tp, 1)
        pack = scatter_pair(pack, "tp", n_tp, 2)
        pack = scatter_pair(pack, "ctx", n_c, 1).astype(BF16)
        pack = scatter_direct(pack, "fsdp", n_f)
        part_b = pack[:n_b].reshape(b_parts, b_rows, LANES).transpose(1, 0, 2)
        part_b = part_b.reshape(1, b_rows, b_cols)
        part_a = pack[n_b : n_b + n_a].reshape(a_cols, fc_cols).T[None]
        part_gain = pack[n_b + n_a :].reshape(-1)[:gain_count].reshape(2, 1, gain_count // 2)
        return (
            block_out,
            resid_grad,
            part_a,
            part_b,
            grad_out[None],
            jnp.stack([grad_gate_w, grad_up_w])[None],
            grad_down_w[None],
            part_gain[0],
            part_gain[1],
        )

    return shards


def rotated(rows, cosine, sine):
    half = HEAD_DIM // 2
    lower, upper = rows[:half], rows[half:]
    return jnp.concatenate([lower * cosine - upper * sine, lower * sine + upper * cosine], axis=0)


def make_fused(mesh):
    n_f, n_c, n_tp = mesh.shape["fsdp"], mesh.shape["ctx"], mesh.shape["tp"]
    n_piece = n_f * n_c
    AT_TP = n_piece
    AT_ME = n_piece + n_tp

    def shards(
        resid_in,
        segment_ids,
        cotangent,
        w_factor_a,
        w_factor_b,
        w_out,
        w_gate_up,
        w_down,
        attn_gains,
        ffn_gains,
    ):
        _, local_len, width = resid_in.shape
        block = local_len // n_tp
        extra = -(-(MOST_DOC - 1) // block)
        windows = extra + 1
        a_cols = w_factor_a.shape[2]
        group = a_cols // RANKS
        heads = n_tp * group
        feats = group * HEAD_DIM
        a_pad = 16 * (-(-a_cols // 16))
        b_rows, b_cols = w_factor_b.shape[1:]
        b_parts = b_cols // LANES
        n_b = b_parts * b_rows
        pack_rows = n_b + a_pad + 16
        fc_cols = w_down.shape[2]
        hidden = w_down.shape[1]
        o_rows = w_out.shape[1]
        gain_part = attn_gains.shape[1]
        kv_b = KV * HEAD_DIM
        kv_rows = kv_b + heads * KV
        half_width = width // n_c
        early = 2 * hidden + 16 * (hidden // 64)
        assert n_f == 4 and fc_cols == LANES and o_rows == feats and n_tp == 4 and n_c == 2

        f_index, c_index, t_index = (
            lax.axis_index("fsdp"),
            lax.axis_index("ctx"),
            lax.axis_index("tp"),
        )
        place = c_index * n_tp + t_index
        n_place = n_c * n_tp
        columns = [
            ((f_index - s) % n_f) * n_c + (c_index if near == 0 else 1 - c_index)
            for near in range(n_c)
            for s in range(n_f)
        ]
        members = [t_index ^ (lo + 2 * hi) for lo in range(2) for hi in range(2)]
        beside_shift = jnp.where(f_index % 2 == 0, n_f - 1, 1)
        meta = jnp.stack(columns + members + [t_index, f_index, beside_shift]).astype(jnp.int32)

        resid_in = pltpu.with_memory_space_constraint(resid_in, pltpu.HBM)
        cotangent = pltpu.with_memory_space_constraint(cotangent, pltpu.HBM)

        def column(meta_ref, j):
            return pl.ds(pl.multiple_of(meta_ref[j] * LANES, LANES), LANES)

        def member(meta_ref, lo, hi):
            return meta_ref[AT_TP + 2 * lo + hi]

        def to_arrival(meta_ref, load):
            return jnp.concatenate([load(column(meta_ref, j)) for j in range(n_piece)], axis=1)

        WHOLE = pl.BlockSpec(memory_space=pltpu.VMEM)
        REMOTE = pl.BlockSpec(memory_space=pl.ANY)

        def call(
            kernel, name, outs, args, specs=None, scratch=(), grid=(1,), out_specs=None, room=4,
            scalars=meta,
        ):
            held = 0
            for arg, spec in zip((*args, *args[:1]), (specs or []) + (out_specs or [])):
                if spec.block_shape:
                    held += 2 * math.prod(spec.block_shape) * arg.dtype.itemsize
            for item in scratch:
                if hasattr(item, "shape") and item.memory_space == pltpu.VMEM:
                    held += math.prod(item.shape) * jnp.dtype(item.dtype).itemsize
            limit = min(held + room * 2**20, VMEM_LIMIT)
            return pl.pallas_call(
                kernel,
                out_shape=[jax.ShapeDtypeStruct(s, d) for s, d in outs],
                grid_spec=pltpu.PrefetchScalarGridSpec(
                    num_scalar_prefetch=1,
                    grid=grid,
                    in_specs=specs or [WHOLE] * len(args),
                    out_specs=out_specs or [WHOLE] * len(outs),
                    scratch_shapes=list(scratch),
                ),
                compiler_params=pltpu.CompilerParams(vmem_limit_bytes=limit),
                name=name,
            )(scalars, *args)


        def pack_kernel(meta_ref, b_ref, a_ref, g0_ref, g1_ref, out_ref):
            for k in range(b_parts):
                out_ref[k * b_rows : (k + 1) * b_rows, :] = b_ref[
                    0, :, k * LANES : (k + 1) * LANES
                ].astype(BF16)
            a_shard = jnp.concatenate([a_ref[0], jnp.zeros((a_pad - a_cols, LANES), F32)], axis=0)
            out_ref[n_b : n_b + a_pad, :] = a_shard.astype(BF16)
            both = jnp.concatenate([g0_ref[...], g1_ref[...]], axis=0)
            both = jnp.concatenate([both, jnp.zeros((6, gain_part), F32)], axis=0)
            both = jnp.concatenate([both, jnp.zeros((8, LANES - gain_part), F32)], axis=1)
            both = pltpu.roll(both, meta_ref[AT_ME] * gain_part, 1)
            both = jnp.concatenate([both, jnp.zeros((8, LANES), F32)], axis=0)
            out_ref[n_b + a_pad :, :] = both.astype(BF16)

        def big_kernel(meta_ref, gu_ref, d_ref, gu_out_ref, d_out_ref):
            for k in range(2):
                gu_out_ref[k * hidden : (k + 1) * hidden, :] = gu_ref[0, k].astype(BF16)
            gu_out_ref[2 * hidden :, :] = d_ref[0, : early - 2 * hidden, :].astype(BF16)
            d_out_ref[...] = d_ref[0, early - 2 * hidden :, :].astype(BF16)

        def factor_kernel(
            meta_ref,
            x_ref,
            p0_ref,
            p1_ref,
            cos_ref,
            sin_ref,
            wb_ref,
            wa_ref,
            gain_ref,
            normed_ref,
            a_ref,
            bq_ref,
            pay_ref,
        ):
            gain_ref[...] = jnp.zeros_like(gain_ref)
            for lo, hi in ((0, 0), (0, 1), (1, 0), (1, 1)):
                part = (p0_ref, p1_ref)[lo]
                tp = member(meta_ref, lo, hi)
                for near in range(n_c):
                    for s in range(n_f):
                        j = near * n_f + s
                        lanes = column(meta_ref, j)
                        row = pl.multiple_of((meta_ref[j] * n_tp + tp) * b_rows, b_rows)
                        for k in range(b_parts):
                            wb_ref[pl.ds(row, b_rows), k * LANES : (k + 1) * LANES] = part[
                                near, hi, s, k * b_rows : (k + 1) * b_rows, :
                            ]
                        wa_ref[tp, :, lanes] = part[near, hi, s, n_b : n_b + a_pad, :]
                        gain_ref[:, lanes] += part[near, hi, s, n_b + a_pad :, :].astype(F32)
            x = x_ref[...]
            normed = (x * inverse_rms(x) * gain_ref[0:1]).astype(BF16)
            normed_ref[...] = normed
            cosine, sine = cos_ref[...], sin_ref[...]
            b_raw = jnp.transpose(dot(normed, wb_ref[...], ((1,), (0,))))
            for r in range(RANK_Q):
                bq_ref[r] = rotated(b_raw[r * HEAD_DIM : (r + 1) * HEAD_DIM], cosine, sine)
            for r in range(KV):
                rows = b_raw[(RANK_Q + r) * HEAD_DIM : (RANK_Q + r + 1) * HEAD_DIM]
                if r < RANK_KV:
                    rows = rotated(rows, cosine, sine)
                pay_ref[r * HEAD_DIM : (r + 1) * HEAD_DIM, :] = rows.astype(BF16)
            for tp in range(n_tp):
                a_raw = dot(wa_ref[tp], normed, ((1,), (1,)))
                a_ref[tp] = a_raw
                kv = [a_raw[g * RANKS + RANK_Q : (g + 1) * RANKS] for g in range(group)]
                start = kv_b + tp * group * KV
                pay_ref[start : start + group * KV, :] = jnp.concatenate(kv, axis=0).astype(BF16)

        def set_mask(first_ref, bias_ref):
            bias_ref[...] = attention_mask(first_ref, windows * block, block)

        def is_even(meta_ref):
            return lax.rem(meta_ref[AT_ME], 2) == 0

        def widen(meta_ref, arrived, win_ref, wide_ref):
            third, second, beside_second, beside, own = arrived
            win_ref[1] = second[...]
            win_ref[3] = own[...]

            @pl.when(is_even(meta_ref))
            def _():
                win_ref[0] = third[...]
                win_ref[2] = beside_second[...]

            @pl.when(jnp.logical_not(is_even(meta_ref)))
            def _():
                win_ref[0] = beside_second[...]
                win_ref[2] = beside[...]

            for j in range(windows):
                for r in range(KV):
                    wide_ref[j, r] = win_ref[j, r * HEAD_DIM : (r + 1) * HEAD_DIM, :].astype(F32)

        def kv_factors(win_ref, tp):
            start = pl.multiple_of(kv_b + tp * (group * KV), group * KV)
            return [win_ref[j, pl.ds(start, group * KV), :].astype(F32) for j in range(windows)]

        def kv_rows_of(factors, wide_ref, g, j):
            def mix(r):
                a0 = factors[j][g * KV + r : g * KV + r + 1]
                a1 = factors[j][g * KV + r + 1 : g * KV + r + 2]
                rows = a0 * wide_ref[j, r] + a1 * wide_ref[j, r + 1]
                return (rows * (1.0 / RANK_KV)).astype(BF16)

            return mix(0), mix(RANK_KV)

        def attention_kernel(
            meta_ref,
            first_ref,
            a_ref,
            bq_ref,
            w0_ref,
            w1_ref,
            w2_ref,
            w3_ref,
            w4_ref,
            lse_ref,
            q_ref,
            mixed_ref,
            win_ref,
            bias_ref,
            wide_ref,
            s_ref,
        ):
            set_mask(first_ref, bias_ref)
            widen(meta_ref, (w0_ref, w1_ref, w2_ref, w3_ref, w4_ref), win_ref, wide_ref)
            spans = [pl.ds(j * block, block) for j in range(windows)]

            def one_group(tp, carry):
                own = a_ref[tp]
                factors = kv_factors(win_ref, tp)
                for g in range(group):
                    query = own[g * RANKS : g * RANKS + 1] * bq_ref[0]
                    for r in range(1, RANK_Q):
                        query = query + own[g * RANKS + r : g * RANKS + r + 1] * bq_ref[r]
                    query = (query * (1.0 / RANK_Q)).astype(BF16)
                    query = query * jnp.asarray(HEAD_DIM**-0.5, BF16)
                    q_ref[tp, g] = query
                    top = jnp.full((1, block), MASKED, F32)
                    values = []
                    for j, span in enumerate(spans):
                        keys, rows = kv_rows_of(factors, wide_ref, g, j)
                        values.append(rows)
                        scores = dot(keys, query, ((0,), (0,))) + bias_ref[span, :]
                        s_ref[g, span, :] = scores
                        top = jnp.maximum(top, jnp.max(scores, axis=0, keepdims=True))
                    total = jnp.zeros((1, block), F32)
                    for span in spans:
                        weight = jnp.exp(s_ref[g, span, :] - top)
                        s_ref[g, span, :] = weight
                        total = total + jnp.sum(weight, axis=0, keepdims=True)
                    lse_ref[tp, g : g + 1, :] = top + jnp.log(total)
                    scale = 1.0 / total
                    mixed = jnp.zeros((HEAD_DIM, block), F32)
                    for j, span in enumerate(spans):
                        probs = (s_ref[g, span, :] * scale).astype(BF16)
                        mixed = mixed + dot(values[j], probs, ((1,), (0,)))
                    mixed_ref[tp, g * HEAD_DIM : (g + 1) * HEAD_DIM, :] = mixed.astype(BF16)
                return carry

            lax.fori_loop(0, n_tp, one_group, 0)

        def project_kernel(
            meta_ref, x_ref, mixed_ref, o0_ref, o1_ref, gain_ref, mid_ref, attn_ref, nf_ref
        ):
            attn = jnp.zeros((block, width), F32)
            for lo, ref in enumerate((o0_ref, o1_ref)):
                for hi in range(2):
                    rows = mixed_ref[member(meta_ref, lo, hi)]
                    attn = attn + dot(rows, ref[hi * o_rows : (hi + 1) * o_rows, :], ((0,), (0,)))
            attn_ref[...] = attn
            mid = to_arrival(meta_ref, lambda lanes: x_ref[:, lanes]) + attn
            mid_ref[...] = mid
            gain = to_arrival(meta_ref, lambda lanes: gain_ref[1:2, lanes])
            nf_ref[...] = (mid * inverse_rms(mid) * gain).astype(BF16)

        def rows_kernel(
            meta_ref, x_hbm, cot_ref, x_ref, own_ref, near_ref, far_ref, cot_buf, sems
        ):
            row = pl.multiple_of(meta_ref[AT_ME] * block, block)
            own_load = pltpu.make_async_copy(x_hbm.at[0, pl.ds(row, block), :], x_ref, sems.at[4])
            own_load.start()
            loads = []
            for side in range(2):
                for i in range(2):
                    row = pl.multiple_of(member(meta_ref, i, side) * block, block)
                    k = 2 * side + i
                    loads.append(
                        pltpu.make_async_copy(
                            cot_ref.at[0, pl.ds(row, block), :], cot_buf.at[k], sems.at[k]
                        )
                    )
                    loads[-1].start()
            for k, load in enumerate(loads):
                load.wait()
                out_ref = (near_ref, far_ref)[k // 2]
                rows = slice(k % 2 * block, (k % 2 + 1) * block)
                for j in range(n_piece):
                    lanes = slice(j * LANES, (j + 1) * LANES)
                    part = cot_buf[k, :, column(meta_ref, j)]
                    out_ref[rows, lanes] = part.astype(BF16)
                    if k == 0:
                        own_ref[:, lanes] = part
            own_load.wait()

        def feed_rows(n_refs, gb_ref, w_ref, ht_ref, back0_ref, back1_ref):
            for i in range(2):
                cut = slice(i * block, (i + 1) * block)
                rows = n_refs[i][...]
                gate = dot(w_ref[0:hidden, :], rows, ((1,), (1,)))
                up = dot(w_ref[hidden : 2 * hidden, :], rows, ((1,), (1,)))
                grad_act = dot(w_ref[2 * hidden :, :], gb_ref[cut, :], ((1,), (1,)))
                squash = jax.nn.sigmoid(gate)
                soft = gate * squash
                ht_ref[2 * hidden :, cut] = (soft * up).astype(BF16)
                ht_ref[0:hidden, cut] = (
                    grad_act * up * squash * (1.0 + gate * (1.0 - squash))
                ).astype(BF16)
                ht_ref[hidden : 2 * hidden, cut] = (grad_act * soft).astype(BF16)
            back = dot(ht_ref[: 2 * hidden, :], w_ref[: 2 * hidden, :], ((0,), (0,)))
            back0_ref[...] = back[:block]
            back1_ref[...] = back[block:].astype(BF16)

        def far_kernel(meta_ref, n0_ref, n1_ref, gb_ref, *refs):
            own_gu_ref, far_gu_ref, pair_gu_ref, gu_across_ref, gu_rest_ref = refs[:5]
            dn_refs = refs[5 : 5 + n_f]
            ht_ref, back0_ref, back1_ref, w_ref, sems = refs[5 + n_f :]
            gate_up = [own_gu_ref, far_gu_ref, pair_gu_ref.at[0], pair_gu_ref.at[1], gu_across_ref]
            gate_up += [gu_rest_ref.at[s] for s in range(n_f - 1)]
            beside_shift = meta_ref[AT_ME + 2]
            arrivals = [0, 2, beside_shift, n_f - beside_shift]
            down = [ref.at[near] for near in range(n_c) for ref in dn_refs]
            loads = []
            for j in range(n_piece):
                lanes = pl.ds(j * LANES, LANES)
                at = pl.multiple_of((arrivals[j % n_f] + j // n_f * n_f) * LANES, LANES)
                loads.append(
                    pltpu.make_async_copy(
                        gate_up[j],
                        w_ref.at[pl.ds(0, early), pl.ds(at, LANES)],
                        sems.at[j],
                    )
                )
                loads.append(
                    pltpu.make_async_copy(
                        down[j], w_ref.at[pl.ds(early, 3 * hidden - early), lanes], sems.at[n_piece + j]
                    )
                )
            for load in loads:
                load.start()
            for load in loads:
                load.wait()
            feed_rows((n0_ref, n1_ref), gb_ref, w_ref, ht_ref, back0_ref, back1_ref)

        def near_kernel(meta_ref, n0_ref, n1_ref, gb_ref, w_ref, far_ht_ref, ht_ref, *refs):
            back0_ref, back1_ref, *ahead_refs = refs
            feed_rows((n0_ref, n1_ref), gb_ref, w_ref, ht_ref, back0_ref, back1_ref)
            for k, ref in enumerate((ht_ref, far_ht_ref)):
                ahead = dot(ref[2 * hidden :, :], w_ref[2 * hidden :, :], ((0,), (0,)))
                ahead_refs[2 * k][...] = ahead[:block]
                ahead_refs[2 * k + 1][...] = ahead[block:].astype(BF16)

        def weight_grad(refs, start, stop, right):
            hts, n_near, n_far, gbs = refs[0:2], refs[2:4], refs[4:6], refs[6:8]
            total = jnp.zeros((stop - start, width), F32)
            for side in range(2):
                left = hts[side]
                if right == 1:
                    total = total + dot(left[start:stop, :], gbs[side][...], ((1,), (0,)))
                    continue
                for i in range(2):
                    rows = (n_near, n_far)[side][i][...]
                    cut = slice(i * block, (i + 1) * block)
                    total = total + dot(left[start:stop, cut], rows, ((1,), (0,)))
            return total

        def gate_up_grad_kernel(meta_ref, *refs):
            keep_ref, send_ref = refs[8:]
            for k in range(2):
                cut = slice(k * hidden, (k + 1) * hidden)
                total = weight_grad(refs, k * hidden, (k + 1) * hidden, 0)
                keep_ref[cut, :] = total[:, :half_width].astype(BF16)
                send_ref[cut, :] = total[:, half_width:].astype(BF16)

        def down_grad_kernel(meta_ref, *refs):
            keep_ref, send_ref = refs[8:]
            total = weight_grad(refs, 2 * hidden, 3 * hidden, 1)

            def chunk(s, near):
                start = near * half_width + s * LANES
                return total[:, start : start + LANES]

            for near in range(n_c):
                keep_ref[0, near] = chunk(0, near)
                keep_ref[1, near] = chunk(2, near)

            @pl.when(lax.rem(meta_ref[AT_ME + 1], 2) == 0)
            def _():
                for near in range(n_c):
                    send_ref[0, near] = chunk(3, near).astype(BF16)
                    send_ref[1, near] = chunk(1, near).astype(BF16)

            @pl.when(lax.rem(meta_ref[AT_ME + 1], 2) == 1)
            def _():
                for near in range(n_c):
                    send_ref[0, near] = chunk(1, near).astype(BF16)
                    send_ref[1, near] = chunk(3, near).astype(BF16)

        def middle_kernel(
            meta_ref,
            cot_ref,
            back_ref,
            beside_ref,
            across_ref,
            mid_ref,
            gain_ref,
            o0_ref,
            o1_ref,
            mixed_ref,
            dmid_ref,
            gg_ref,
            go_ref,
            keep_ref,
            send_ref,
        ):
            back = back_ref[...] + beside_ref[...].astype(F32) + across_ref[...].astype(F32)
            mid = mid_ref[...]
            inverse = inverse_rms(mid)
            gain = to_arrival(meta_ref, lambda lanes: gain_ref[1:2, lanes])
            normal = mid * inverse
            gains = jnp.sum(back * normal, axis=0, keepdims=True)
            for j in range(n_piece):
                gg_ref[:, column(meta_ref, j)] = jnp.broadcast_to(
                    gains[:, j * LANES : (j + 1) * LANES], (8, LANES)
                )
            scaled = back * gain
            delta = inverse * (
                scaled - normal * jnp.mean(scaled * normal, axis=-1, keepdims=True)
            )
            dmid_ref[...] = delta
            grad = (cot_ref[...] + delta).astype(BF16)
            for lo, ref in enumerate((o0_ref, o1_ref)):
                for hi in range(2):
                    tp = member(meta_ref, lo, hi)
                    cut = slice(hi * o_rows, (hi + 1) * o_rows)
                    go_ref[tp] = dot(ref[cut, :], grad, ((1,), (1,))).astype(BF16)
                    weight = dot(mixed_ref[tp], grad, ((1,), (0,))).astype(BF16)
                    (keep_ref, send_ref)[lo][cut, :] = weight

        def attention_back_kernel(
            part,
            meta_ref,
            first_ref,
            a_ref,
            bq_ref,
            w0_ref,
            w1_ref,
            w2_ref,
            w3_ref,
            w4_ref,
            lse_ref,
            q_ref,
            go_ref,
            *refs,
        ):
            win_ref, bias_ref, wide_ref, p_ref, dp_ref = refs[-5:]
            if part == 0:
                ga_ref, gbq_ref, gwb_ref, gwa_ref = refs[:4]
            else:
                ga_ref, gbq_ref, second_ref, beside_ref, third_ref, own_ref = refs[3:9]
                gwb_ref, gwa_ref = refs[-7:-5]
            set_mask(first_ref, bias_ref)
            widen(meta_ref, (w0_ref, w1_ref, w2_ref, w3_ref, w4_ref), win_ref, wide_ref)
            if part == 0:
                gbq_ref[...] = jnp.zeros_like(gbq_ref)
                gwb_ref[...] = jnp.zeros_like(gwb_ref)
            else:
                gbq_ref[...] = refs[0][...]
                gwb_ref[...] = refs[1][...]
                gwa_ref[...] = refs[2][...]
            spans = [pl.ds(j * block, block) for j in range(windows)]
            first_tp = part * (n_tp // 2)

            def one_group(tp, carry):
                own = a_ref[tp]
                factors = kv_factors(win_ref, tp)
                grad_a = []
                grad_kv = [[] for _ in spans]
                for g in range(group):
                    query = q_ref[tp, g]
                    grad_out = go_ref[tp, g * HEAD_DIM : (g + 1) * HEAD_DIM, :]
                    lse = lse_ref[tp, g : g + 1, :]
                    inner = jnp.zeros((1, block), F32)
                    keys = []
                    for j, span in enumerate(spans):
                        key_rows, value_rows = kv_rows_of(factors, wide_ref, g, j)
                        keys.append(key_rows)
                        scores = dot(key_rows, query, ((0,), (0,))) + bias_ref[span, :]
                        probs = jnp.exp(scores - lse)
                        grad_probs = dot(value_rows, grad_out, ((0,), (0,)))
                        p_ref[g % 2, span, :] = probs
                        dp_ref[g % 2, span, :] = grad_probs
                        inner = inner + jnp.sum(probs * grad_probs, axis=0, keepdims=True)
                    grad_query = jnp.zeros((HEAD_DIM, block), F32)
                    for j, span in enumerate(spans):
                        probs = p_ref[g % 2, span, :]
                        grad_scores = (probs * (dp_ref[g % 2, span, :] - inner)).astype(BF16)
                        grad_query = grad_query + dot(keys[j], grad_scores, ((1,), (0,)))
                        grad_keys = dot(query, grad_scores, ((1,), (1,))) * (1.0 / RANK_KV)
                        grad_values = dot(grad_out, probs.astype(BF16), ((1,), (1,)))
                        grad_values = grad_values * (1.0 / RANK_KV)
                        for r in range(KV):
                            grad = grad_keys if r < RANK_KV else grad_values
                            grad_kv[j].append(
                                jnp.sum(grad * wide_ref[j, r], axis=0, keepdims=True)
                            )
                            gwb_ref[j, r] += factors[j][g * KV + r : g * KV + r + 1] * grad
                    grad_query = grad_query * (HEAD_DIM**-0.5 / RANK_Q)
                    for r in range(RANK_Q):
                        grad_a.append(jnp.sum(grad_query * bq_ref[r], axis=0, keepdims=True))
                        gbq_ref[r] += own[g * RANKS + r : g * RANKS + r + 1] * grad_query
                    grad_a.append(jnp.zeros((KV, block), F32))
                grad_a.append(jnp.zeros((a_pad - a_cols, block), F32))
                ga_ref[tp - first_tp] = jnp.concatenate(grad_a, axis=0)
                start = pl.multiple_of(tp * (group * KV), group * KV)
                for j in range(windows):
                    gwa_ref[j, pl.ds(start, group * KV), :] = jnp.concatenate(grad_kv[j], axis=0)
                return carry

            lax.fori_loop(first_tp, first_tp + n_tp // 2, one_group, 0)
            if part == 0:
                return

            def put(ref, start, j):
                for r in range(KV):
                    row = start + r * HEAD_DIM
                    ref[row : row + HEAD_DIM, :] = gwb_ref[j, r].astype(ref.dtype)
                ref[start + kv_b : start + kv_rows, :] = gwa_ref[j].astype(ref.dtype)

            put(own_ref, 0, 3)
            put(beside_ref, 0, 2)
            put(third_ref, 0, 0)
            put(second_ref, 0, 1)

        def last_kernel(
            meta_ref,
            x_ref,
            own_ref,
            second_ref,
            beside_ref,
            third_ref,
            gbq_ref,
            ga0_ref,
            ga1_ref,
            cos_ref,
            sin_ref,
            wb_ref,
            wa_ref,
            normed_ref,
            gain_ref,
            dmid_ref,
            gg_ref,
            delta_ref,
            keep0_ref,
            keep1_ref,
            send0_ref,
            send1_ref,
            b_buf,
            a_buf,
            d_buf,
            g_buf,
        ):
            total = own_ref[...]
            for ref in (second_ref, beside_ref, third_ref):
                total = total + ref[...].astype(F32)
            cosine, sine = cos_ref[...], -sin_ref[...]
            rows = [rotated(gbq_ref[r], cosine, sine) for r in range(RANK_Q)]
            for r in range(KV):
                part = total[r * HEAD_DIM : (r + 1) * HEAD_DIM]
                rows.append(rotated(part, cosine, sine) if r < RANK_KV else part)
            grad_b = jnp.transpose(jnp.concatenate(rows, axis=0)).astype(BF16)
            normed = normed_ref[...]
            back = dot(grad_b, wb_ref[...], ((1,), (1,)))
            for tp in range(n_tp):
                parts = []
                for g in range(group):
                    start = kv_b + (tp * group + g) * KV
                    parts.append(jnp.zeros((RANK_Q, block), F32))
                    parts.append(total[start : start + KV])
                parts.append(jnp.zeros((a_pad - a_cols, block), F32))
                own_a = (ga0_ref, ga1_ref)[tp // 2][tp % 2]
                grad_a = (own_a + jnp.concatenate(parts, axis=0)).astype(BF16)
                back = back + dot(grad_a, wa_ref[tp], ((0,), (0,)))
                a_buf[tp] = dot(grad_a, normed, ((1,), (0,)))
            b_buf[...] = dot(normed, grad_b, ((0,), (0,)))
            x = x_ref[...]
            inverse = inverse_rms(x)
            normal = x * inverse
            gains = jnp.sum(back * normal, axis=0, keepdims=True)
            g_buf[...] = jnp.broadcast_to(gains, (8, width))
            scaled = back * gain_ref[0:1]
            delta = inverse * (
                scaled - normal * jnp.mean(scaled * normal, axis=-1, keepdims=True)
            )
            d_buf[...] = delta
            for j in range(n_piece):
                lanes = column(meta_ref, j)
                cut = slice(j * LANES, (j + 1) * LANES)
                delta_ref[:, lanes] = (d_buf[:, lanes] + dmid_ref[:, cut]).astype(BF16)
            row_index = lax.broadcasted_iota(jnp.int32, (16, LANES), 0)
            for lo, hi in ((0, 0), (0, 1), (1, 0), (1, 1)):
                outs = ((keep0_ref, keep1_ref), (send0_ref, send1_ref))[lo]
                tp = member(meta_ref, lo, hi)
                for near in range(n_c):
                    out = outs[near]
                    for s in range(n_f):
                        j = near * n_f + s
                        lanes = column(meta_ref, j)
                        row = pl.multiple_of((meta_ref[j] * n_tp + tp) * b_rows, b_rows)
                        for k in range(b_parts):
                            out[hi, s, k * b_rows : (k + 1) * b_rows, :] = b_buf[
                                pl.ds(row, b_rows), k * LANES : (k + 1) * LANES
                            ].astype(BF16)
                        out[hi, s, n_b : n_b + a_pad, :] = a_buf[tp, :, lanes].astype(BF16)
                        pair = jnp.where(
                            row_index == 0, g_buf[0:1, lanes], gg_ref[0:1, lanes]
                        )
                        out[hi, s, n_b + a_pad :, :] = pair.astype(BF16)

        def add_kernel(arrival, meta_ref, x_ref, d0_ref, d1_ref, d2_ref, d3_ref, out_ref):
            step = pl.program_id(0) // 2
            rows = pl.ds(pl.multiple_of((pl.program_id(0) % 2) * (block // 2), 8), block // 2)
            for i, ref in enumerate((d0_ref, d1_ref, d2_ref, d3_ref)):

                @pl.when(step == i)
                def _(ref=ref):
                    if not arrival:
                        out_ref[0] = x_ref[0] + ref[rows, :].astype(F32)
                        return
                    for j in range(n_piece):
                        lanes = column(meta_ref, j)
                        out_ref[0, :, lanes] = x_ref[0, :, lanes] + ref[
                            rows, j * LANES : (j + 1) * LANES
                        ].astype(F32)

        def split_kernel(meta_ref, keep_ref, got_ref, own_ref, send_ref):
            def total(s):
                lanes = slice(s * LANES, (s + 1) * LANES)
                return keep_ref[:, lanes].astype(F32) + got_ref[: keep_ref.shape[0], lanes].astype(
                    F32
                )

            own_ref[0] = total(0)
            own_ref[1] = total(2)

            @pl.when(lax.rem(meta_ref[AT_ME + 1], 2) == 0)
            def _():
                send_ref[0] = total(3).astype(BF16)
                send_ref[1] = total(1).astype(BF16)

            @pl.when(lax.rem(meta_ref[AT_ME + 1], 2) == 1)
            def _():
                send_ref[0] = total(1).astype(BF16)
                send_ref[1] = total(3).astype(BF16)

        def unpack_kernel(
            meta_ref, p_ref, got_ref, b_ref, a_ref, g0_ref, g1_ref, o_ref
        ):
            total = p_ref[...].astype(F32) + got_ref[...].astype(F32)
            for k in range(b_parts):
                b_ref[0, :, k * LANES : (k + 1) * LANES] = total[k * b_rows : (k + 1) * b_rows]
            a_ref[0] = total[n_b : n_b + a_cols]
            rows = total[n_b + a_pad : n_b + a_pad + 8]
            rows = pltpu.roll(rows, (n_tp - meta_ref[AT_ME]) * gain_part, 1)
            g0_ref[...] = rows[0:1, :gain_part]
            g1_ref[...] = rows[1:2, :gain_part]
            o_ref[0] = total[pack_rows:]

        core = lambda v, label="row": swap(v, "tp", n_tp, 1, "core_" + label)
        chip = lambda v, label="row": swap(v, "tp", n_tp, 2, "y_" + label)
        ctx = lambda v, label="row": swap(v, "ctx", n_c, 1, "x_" + label)
        ahead = lambda v, s, label="row": shift(v, "fsdp", n_f, s, "z_" + label)

        (pack,) = call(
            pack_kernel,
            "pack",
            [((pack_rows, LANES), BF16)],
            (w_factor_b, w_factor_a.transpose(0, 2, 1), attn_gains, ffn_gains),
        )
        o_rows_all = w_out[0].astype(BF16)
        pack = jnp.stack([pack] + [ahead(pack, s, "pack") for s in range(1, n_f)])
        o_parts = [o_rows_all] + [ahead(o_rows_all, s, "wo") for s in range(1, n_f)]
        o_parts = jnp.concatenate(o_parts, axis=0)
        gu_in = after(w_gate_up.transpose(0, 1, 3, 2), pack)
        own_gu, own_dn = call(
            big_kernel,
            "big_pack",
            [((early, LANES), BF16), ((3 * hidden - early, LANES), BF16)],
            (gu_in, w_down),
        )
        pack = jnp.stack([pack, ctx(pack, "pack")])
        far_gu = swap(own_gu, "fsdp", n_f, 2, "z_gate_up")
        dn_pair = jnp.stack([own_dn, ctx(own_dn, "down")])
        gu_across = ctx(own_gu, "gate_up")
        o_across = ctx(o_parts, "wo")
        o_parts = jnp.concatenate(
            [
                half[s * o_rows : (s + 1) * o_rows]
                for half in (o_parts, o_across)
                for s in range(n_f)
            ],
            axis=1,
        )
        own_x, own_cot, near_cot, far_cot = call(
            rows_kernel,
            "rows",
            [((block, width), F32)] * 2 + [((2 * block, width), BF16)] * 2,
            (resid_in, cotangent),
            [REMOTE] * 2,
            [pltpu.VMEM((4, block, width), F32), pltpu.SemaphoreType.DMA((5,))],
            scalars=after(meta, o_across),
        )
        pack_across, far_gu, dn_pair, o_parts, near_cot, far_cot = lax.optimization_barrier(
            (chip(pack, "pack"), far_gu, dn_pair, o_parts, near_cot, far_cot)
        )
        pair_gu = swap(jnp.stack([own_gu, far_gu]), "fsdp", n_f, 1, "z_gate_up_pair")
        pack = jnp.stack([pack, pack_across], axis=1)
        other_pack = core(pack, "pack")

        def add_rows(whole, parts, arrival):
            rows = pl.BlockSpec(
                (1, block // 2, width), lambda i, m: (0, 2 * m[AT_TP + i // 2] + i % 2, 0)
            )
            (out,) = call(
                lambda *refs: add_kernel(arrival, *refs),
                "add_rows",
                [(whole.shape, F32)],
                (whole, *parts),
                [rows] + [WHOLE] * 4,
                (),
                (2 * n_tp,),
                [rows],
            )
            return out

        def split(keep, got):
            size = keep.shape[0]
            return call(
                split_kernel,
                "split",
                [((2, size, LANES), F32), ((2, size, LANES), BF16)],
                (keep, got),
            )

        def first_step(send, label):
            return swap(send, "fsdp", n_f, 1, "z1_" + label)

        def second_step(own, got, label):
            total = own + got.astype(F32)
            return total[0], swap(total[1].astype(BF16), "fsdp", n_f, 2, "z2_" + label)

        seg_here = lax.dynamic_slice_in_dim(segment_ids[0], place * block, block, 0)
        first = jnp.sum((segment_ids[0][:, None] < seg_here[None, :]).astype(jnp.int32), axis=0)
        token = place * block + jnp.arange(block, dtype=jnp.int32)
        position = (token - first).astype(F32)
        first = (first - place * block + extra * block).reshape(1, block)
        frequency = 10000.0 ** (-2.0 * jnp.arange(HEAD_DIM // 2, dtype=F32) / HEAD_DIM)
        angles = frequency[:, None] * position[None, :]
        cosine, sine = jnp.cos(angles), jnp.sin(angles)

        weight_b, weight_a, gains, normed, a_rows, b_query, payload = call(
            factor_kernel,
            "factors",
            [
                ((width, b_cols), BF16),
                ((n_tp, a_pad, width), BF16),
                ((16, width), F32),
                ((block, width), BF16),
                ((n_tp, a_pad, block), F32),
                ((RANK_Q, HEAD_DIM, block), F32),
                ((kv_rows, block), BF16),
            ],
            (own_x, pack, other_pack, cosine, sine),
        )
        def places(value, step, chosen, label):
            pairs = [(i, i + step) for i in chosen if 0 <= i + step < n_place]
            with jax.named_scope(label):
                return lax.ppermute(value, ("ctx", "tp"), pairs)

        every, odd, even = range(n_place), range(1, n_place, 2), range(0, n_place, 2)
        second = places(payload, 2, every, "x_kv_second")
        third = places(payload, 3, odd, "x_kv_third")
        beside_kv = core(payload, "kv")
        o_own = jnp.concatenate([o_parts, chip(o_parts, "wo")], axis=0)
        second, pair_gu, gu_across = lax.optimization_barrier((second, pair_gu, gu_across))
        gu_rest = ctx(jnp.concatenate([far_gu[None], pair_gu], axis=0), "gate_up_rest")
        dn_parts = [dn_pair, ahead(dn_pair, 1, "down1")]
        beside_second = core(second, "kv_second")
        tied = lax.optimization_barrier((third, second, beside_second, beside_kv, o_own))
        wins = (*tied[:4], payload)
        o_own = tied[4]
        o_other = core(o_own, "wo")
        window = windows * block
        lse, query, mixed = call(
            attention_kernel,
            "attention",
            [
                ((n_tp, group, block), F32),
                ((n_tp, group, HEAD_DIM, block), BF16),
                ((n_tp, feats, block), BF16),
            ],
            (first, a_rows, b_query, *wins),
            None,
            [
                pltpu.VMEM((windows, kv_rows, block), BF16),
                pltpu.VMEM((window, block), F32),
                pltpu.VMEM((windows, KV, HEAD_DIM, block), F32),
                pltpu.VMEM((group, window, block), F32),
            ],
        )
        dn_parts[1] = after(dn_parts[1], mixed)
        for s in range(2, n_f):
            dn_parts.append(ahead(dn_parts[-1], 1, "down" + str(s)))
        mid, attn_out, normed_ffn = call(
            project_kernel,
            "project",
            [((block, width), F32), ((block, width), F32), ((block, width), BF16)],
            (own_x, mixed, o_own, o_other, gains),
        )

        near_rows = (normed_ffn, core(normed_ffn, "nf"))
        far_own = chip(normed_ffn, "nf")

        far_own, gu_rest = lax.optimization_barrier((far_own, gu_rest))
        far_own, dn_parts[-1], gu_rest = lax.optimization_barrier(
            (far_own, dn_parts[-1], gu_rest)
        )
        pieces = (own_gu, far_gu, pair_gu, gu_across, gu_rest, *dn_parts)
        far_rows = (far_own, core(far_own, "nf_far"))
        whole_ht = ((3 * hidden, 2 * block), BF16)
        two_sums = [((block, width), F32), ((block, width), BF16)]
        far_ht, far_back, far_back1, weights = call(
            far_kernel,
            "feed_far",
            [whole_ht, *two_sums, ((3 * hidden, width), BF16)],
            (*far_rows, far_cot, *pieces),
            [WHOLE] * 3 + [REMOTE] * len(pieces),
            [pltpu.SemaphoreType.DMA((2 * n_piece,))],
            room=12,
        )
        across = (far_back + core(far_back1, "dn_far").astype(F32)).astype(BF16)
        near_ht, near_back, near_back1, near_out, near_out1, far_out, far_out1 = call(
            near_kernel,
            "feed_near",
            [whole_ht, *two_sums * 3],
            (after(near_rows[0], across), near_rows[1], near_cot, weights, far_ht),
            room=12,
        )
        across = chip(across, "dn")
        beside = core(near_back1, "dn_near")

        grad_args = (near_ht, far_ht, *near_rows, *far_rows, near_cot, far_cot)
        own_d, send_d = call(
            down_grad_kernel,
            "down_grad",
            [((2, n_c, hidden, LANES), F32), ((2, n_c, hidden, LANES), BF16)],
            grad_args,
            room=12,
        )
        got_d = first_step(send_d, "d")
        keep_a, send_a = call(
            gate_up_grad_kernel,
            "gate_up_grad",
            [((2 * hidden, half_width), BF16)] * 2,
            (after(grad_args[0], send_d), *grad_args[1:]),
            room=12,
        )
        got_a = ctx(send_a, "grads_a")
        across = after(across, send_a)

        delta_mid, gain_grad, grad_mixed, keep_o, send_o = call(
            middle_kernel,
            "middle",
            [
                ((block, width), F32),
                ((8, width), F32),
                ((n_tp, feats, block), BF16),
                ((2 * o_rows, width), BF16),
                ((2 * o_rows, width), BF16),
            ],
            (own_cot, near_back, beside, across, mid, gains, o_own, o_other, mixed),
        )
        near_sum = attn_out + near_out + core(after(near_out1, across), "out_near").astype(F32)
        far_sum = far_out + core(after(far_out1, across), "out_far").astype(F32)
        out_send = jnp.stack([far_sum, near_sum]).astype(BF16)
        grad_mixed = after(grad_mixed, out_send)
        rows_got = core(send_o, "go")
        out_got = chip(out_send, "out")
        back_args = (first, a_rows, b_query, *wins, lse, query, grad_mixed)
        sums = [
            ((RANK_Q, HEAD_DIM, block), F32),
            ((windows, KV, HEAD_DIM, block), F32),
            ((windows, heads * KV, block), F32),
        ]
        grad_a_out = ((n_tp // 2, a_pad, block), F32)
        back_scratch = [
            pltpu.VMEM((windows, kv_rows, block), BF16),
            pltpu.VMEM((window, block), F32),
            pltpu.VMEM((windows, KV, HEAD_DIM, block), F32),
            pltpu.VMEM((2, window, block), F32),
            pltpu.VMEM((2, window, block), F32),
        ]
        grad_a0, *sums_out = call(
            lambda *refs: attention_back_kernel(0, *refs),
            "attention_back_a",
            [grad_a_out] + sums,
            back_args,
            None,
            back_scratch,
        )
        sums_out[0], own_d, got_d, _ = lax.optimization_barrier(
            (sums_out[0], own_d, got_d, grad_a0)
        )
        own_d, got_d = second_step(own_d, got_d, "d")
        grad_a1, grad_bq, *sends = call(
            lambda *refs: attention_back_kernel(1, *refs),
            "attention_back_b",
            [
                grad_a_out,
                sums[0],
                ((kv_rows, block), BF16),
                ((kv_rows, block), BF16),
                ((kv_rows, block), BF16),
                ((kv_rows, block), F32),
            ],
            (*back_args, *sums_out),
            None,
            [pltpu.VMEM(shape, kind) for shape, kind in sums[1:]] + back_scratch,
        )
        *sends[:3], out_got, rows_got = lax.optimization_barrier((*sends[:3], out_got, rows_got))
        second_got = places(sends[0], -2, every, "x_kv_back_second")
        beside_got = places(sends[1], -1, every, "x_kv_back_beside")
        third_got = places(sends[2], -3, every, "x_kv_back_third")
        own_a, send_a = split(after(keep_a, sends[0]), got_a)
        got_a = first_step(send_a, "a")
        rows_o = keep_o.astype(F32) + after(rows_got, send_a).astype(F32)
        rows_keep, rows_send = rows_o[:o_rows], rows_o[o_rows:].astype(BF16)
        rows_got = chip(rows_send, "go")
        *got, got_d = lax.optimization_barrier((second_got, beside_got, third_got, got_d))
        out_rows = (out_send[::-1].astype(F32) + out_got.astype(F32)).astype(BF16)

        delta, keep0, keep1, send0, send1 = call(
            last_kernel,
            "last",
            [
                ((block, width), BF16),
                *[((2, n_f, pack_rows, LANES), BF16)] * 4,
            ],
            (
                own_x,
                sends[3],
                *got,
                grad_bq,
                grad_a0,
                grad_a1,
                cosine,
                sine,
                weight_b,
                weight_a,
                normed,
                gains,
                delta_mid,
                gain_grad,
            ),
            [WHOLE] * 16,
            [
                pltpu.VMEM((width, b_cols), F32),
                pltpu.VMEM((n_tp, a_pad, width), F32),
                pltpu.VMEM((block, width), F32),
                pltpu.VMEM((8, width), F32),
            ],
        )

        part_send = (keep1.astype(F32) + core(send1, "gp").astype(F32)).astype(BF16)
        total_d = own_d + got_d.astype(F32)
        part_send, got_a = lax.optimization_barrier((part_send, got_a))
        part_got = ctx(part_send, "gp")
        own_a, got_a = second_step(own_a, got_a, "a")
        part = keep0.astype(F32) + core(after(send0, part_send), "gp_near").astype(F32)
        rows_got, part = lax.optimization_barrier((rows_got, part))
        rows_o = rows_keep + rows_got.astype(F32)
        rows_keep, rows_send = rows_o[:, :half_width], rows_o[:, half_width:].astype(BF16)
        across_delta = chip(delta, "delta")
        rows_go = ctx(rows_send, "go")
        out_rows = after(out_rows, part_send)
        out_beside = core(out_rows, "out_rows")
        block_out = add_rows(
            resid_in, (out_rows[0], out_rows[1], out_beside[0], out_beside[1]), True
        )
        part_got, across_delta = lax.optimization_barrier((part_got, across_delta, block_out))[:2]
        part = part + part_got.astype(F32)
        part_send = part[1].astype(BF16)
        part_got = chip(part_send, "gp")
        across_delta = after(across_delta, part_send)
        beside_delta = core(after(delta, part_send), "delta")
        got_last = ctx(after(total_d[1], part_send).astype(BF16), "d")
        part_got, rows_go, got_a = lax.optimization_barrier((part_got, rows_go, got_a))
        part = part[0] + part_got.astype(F32)
        rows_o = rows_keep + rows_go.astype(F32)
        part = [
            jnp.concatenate([part[s], rows_o[:, s * LANES : (s + 1) * LANES]], axis=0)
            for s in range(n_f)
        ]
        is_even_f = f_index % 2 == 0
        part_send = [
            jnp.where(is_even_f, part[3], part[1]),
            jnp.where(is_even_f, part[1], part[3]),
        ]
        part_send = jnp.stack(part_send).astype(BF16)
        part_own, part_got = second_step(
            jnp.stack([part[0], part[2]]), first_step(part_send, "gp"), "gp"
        )
        across_delta = after(across_delta, part_send)
        resid_grad = add_rows(
            cotangent,
            (delta, across_delta, beside_delta, core(across_delta, "delta_far")),
            False,
        )
        part_got, got_last = lax.optimization_barrier((part_got, got_last, resid_grad))[:2]
        grad_down = total_d[0] + got_last.astype(F32)
        grad_gate_up = (own_a + got_a.astype(F32)).reshape(1, 2, hidden, fc_cols)
        part_b, part_a, part_g0, part_g1, grad_out = call(
            unpack_kernel,
            "unpack",
            [
                ((1, b_rows, b_cols), F32),
                ((1, a_cols, fc_cols), F32),
                ((1, gain_part), F32),
                ((1, gain_part), F32),
                ((1, o_rows, LANES), F32),
            ],
            (part_own, part_got),
        )
        return (
            block_out,
            resid_grad,
            part_a.transpose(0, 2, 1),
            part_b,
            grad_out,
            grad_gate_up.transpose(0, 1, 3, 2),
            grad_down[None],
            part_g0,
            part_g1,
        )

    return shards


def make_shards(mesh):
    fused, general = make_fused(mesh), make_general(mesh)
    fits = mesh.shape["fsdp"] == 4 and mesh.shape["ctx"] == 2 and mesh.shape["tp"] == 4

    def shards(*args):
        return (fused if fits and args[7].shape[2] == LANES else general)(*args)

    return shards


def solution(mesh):
    return jax.shard_map(
        make_shards(mesh),
        mesh=mesh,
        in_specs=(
            P("fsdp", "ctx", None),
            P("fsdp", None),
            P("fsdp", "ctx", None),
            P(None, ("fsdp", "ctx"), "tp"),
            P(None, ("fsdp", "ctx", "tp"), None),
            P(None, "tp", ("fsdp", "ctx")),
            P(None, None, ("fsdp", "ctx"), "tp"),
            P(None, "tp", ("fsdp", "ctx")),
            P(None, ("fsdp", "ctx", "tp")),
            P(None, ("fsdp", "ctx", "tp")),
        ),
        out_specs=(
            P("fsdp", "ctx", None),
            P("fsdp", "ctx", None),
            P(None, ("fsdp", "ctx"), "tp"),
            P(None, ("fsdp", "ctx", "tp"), None),
            P(None, "tp", ("fsdp", "ctx")),
            P(None, None, ("fsdp", "ctx"), "tp"),
            P(None, "tp", ("fsdp", "ctx")),
            P(None, ("fsdp", "ctx", "tp")),
            P(None, ("fsdp", "ctx", "tp")),
        ),
        check_vma=False,
    )
```

```python
import math

import jax
import jax.numpy as jnp
from jax import lax
from jax.experimental import pallas as pl
from jax.experimental.pallas import tpu as pltpu
from jax.sharding import PartitionSpec as P

HEAD_DIM = 64
RANK_Q = 6
RANK_KV = 2
RANKS = 10
KV = 2 * RANK_KV
MOST_DOC = 768
EPSILON = 1e-05
LANES = 128
BF16 = jnp.bfloat16
F32 = jnp.float32
MASKED = -1e30


def inverse_rms(values):
    return lax.rsqrt(jnp.mean(values * values, axis=-1, keepdims=True) + EPSILON)


def norm_back(grad_value, values, inverse, gain):
    scaled = grad_value * gain
    normal = values * inverse
    return inverse * (scaled - normal * jnp.mean(scaled * normal, axis=-1, keepdims=True))


def dot(left, right, dims):
    return lax.dot_general(left, right, (dims, ((), ())), preferred_element_type=F32)


def shift(value, axes, size, step, label="shift"):
    with jax.named_scope(label):
        return lax.ppermute(value, axes, [(i, (i + step) % size) for i in range(size)])


def swap(value, axis, size, bit, label="swap"):
    with jax.named_scope(label):
        return lax.ppermute(value, axis, [(i, i ^ bit) for i in range(size)])


def gather_direct(value, axis, size):
    me = lax.axis_index(axis)
    parts = [(me, value)]
    for step in range(1, size):
        parts.append(((me - step) % size, shift(value, axis, size, step)))
    out = jnp.zeros((size,) + value.shape, value.dtype)
    for place, part in parts:
        out = lax.dynamic_update_slice(out, part[None], (place,) + (0,) * value.ndim)
    return out


def gather_pair(value, axis, size, bit):
    mine = (lax.axis_index(axis) // bit) % 2 == 0
    other = swap(value, axis, size, bit)
    return jnp.stack([jnp.where(mine, value, other), jnp.where(mine, other, value)])


def after(value, *others):
    return lax.optimization_barrier((value,) + others)[0]


def take(value, index):
    return lax.dynamic_index_in_dim(value, index, 0, keepdims=False)


def scatter_direct(value, axis, size):
    me = lax.axis_index(axis)
    got = [
        shift(take(value, (me + step) % size), axis, size, step) for step in range(1, size)
    ]
    total = take(value, me).astype(F32)
    for part in got:
        total = total + part.astype(F32)
    return total


def scatter_pair(value, axis, size, bit):
    mine = (lax.axis_index(axis) // bit) % 2
    got = swap(take(value, 1 - mine).astype(BF16), axis, size, bit)
    return take(value, mine).astype(F32) + got.astype(F32)


def attention_mask(first_ref, window, block):
    start = first_ref[...]
    place = lax.broadcasted_iota(jnp.int32, (window, block), 0)
    query_place = lax.broadcasted_iota(jnp.int32, (window, block), 1) + (window - block)
    return jnp.where((place >= start) & (place <= query_place), 0.0, MASKED)


def head_rows(wa_ref, wide_ref, head):
    factors = wa_ref[head].astype(F32)
    key_rows = (factors[0:1] * wide_ref[0] + factors[1:2] * wide_ref[1]) * (1.0 / RANK_KV)
    value_rows = (factors[2:3] * wide_ref[2] + factors[3:4] * wide_ref[3]) * (1.0 / RANK_KV)
    return factors, key_rows.astype(BF16), value_rows.astype(BF16)


def forward_kernel(
    first_ref, a_ref, bq_ref, wa_ref, wb_ref, mixed_ref, lse_ref, q_ref, bias_ref, wide_ref, s_ref
):
    heads = a_ref.shape[0]
    window, block = bias_ref.shape
    bias_ref[...] = attention_mask(first_ref, window, block)
    wide_ref[...] = wb_ref[...].astype(F32)
    spans = [pl.ds(j * block, block) for j in range(window // block)]

    def one_head(head, carry):
        factors = a_ref[head]
        query = factors[0:1] * bq_ref[0]
        for r in range(1, RANK_Q):
            query = query + factors[r : r + 1] * bq_ref[r]
        query = (query * (1.0 / RANK_Q)).astype(BF16) * jnp.asarray(HEAD_DIM**-0.5, BF16)
        q_ref[head] = query
        _, key_rows, value_rows = head_rows(wa_ref, wide_ref, head)
        top = jnp.full((1, block), MASKED, F32)
        for j, span in enumerate(spans):
            keys = key_rows[:, j * block : (j + 1) * block]
            scores = dot(keys, query, ((0,), (0,))) + bias_ref[span, :]
            s_ref[span, :] = scores
            top = jnp.maximum(top, jnp.max(scores, axis=0, keepdims=True))
        total = jnp.zeros((1, block), F32)
        for span in spans:
            weight = jnp.exp(s_ref[span, :] - top)
            s_ref[span, :] = weight
            total = total + jnp.sum(weight, axis=0, keepdims=True)
        lse_ref[head] = top + jnp.log(total)
        scale = 1.0 / total
        mixed = jnp.zeros((HEAD_DIM, block), F32)
        for j, span in enumerate(spans):
            probs = (s_ref[span, :] * scale).astype(BF16)
            mixed = mixed + dot(
                value_rows[:, j * block : (j + 1) * block], probs, ((1,), (0,))
            )
        mixed_ref[head] = mixed.astype(BF16)
        return carry

    lax.fori_loop(0, heads, one_head, 0)


def backward_kernel(
    first_ref,
    a_ref,
    bq_ref,
    wa_ref,
    wb_ref,
    lse_ref,
    q_ref,
    go_ref,
    ga_ref,
    gbq_ref,
    gwa_ref,
    gwb_ref,
    bias_ref,
    wide_ref,
    p_ref,
    dp_ref,
):
    heads = a_ref.shape[0]
    window, block = bias_ref.shape
    bias_ref[...] = attention_mask(first_ref, window, block)
    wide_ref[...] = wb_ref[...].astype(F32)
    gbq_ref[...] = jnp.zeros_like(gbq_ref)
    gwb_ref[...] = jnp.zeros_like(gwb_ref)
    count = window // block
    spans = [pl.ds(j * block, block) for j in range(count)]

    def one_head(head, carry):
        factors, key_rows, value_rows = head_rows(wa_ref, wide_ref, head)
        query = q_ref[head]
        grad_out = go_ref[head]
        lse = lse_ref[head]
        inner = jnp.zeros((1, block), F32)
        for j, span in enumerate(spans):
            cut = slice(j * block, (j + 1) * block)
            scores = dot(key_rows[:, cut], query, ((0,), (0,))) + bias_ref[span, :]
            probs = jnp.exp(scores - lse)
            grad_probs = dot(value_rows[:, cut], grad_out, ((0,), (0,)))
            p_ref[span, :] = probs
            dp_ref[span, :] = grad_probs
            inner = inner + jnp.sum(probs * grad_probs, axis=0, keepdims=True)
        grad_query = jnp.zeros((HEAD_DIM, block), F32)
        for j, span in enumerate(spans):
            cut = slice(j * block, (j + 1) * block)
            probs = p_ref[span, :]
            grad_scores = (probs * (dp_ref[span, :] - inner)).astype(BF16)
            grad_query = grad_query + dot(key_rows[:, cut], grad_scores, ((1,), (0,)))
            grad_keys = dot(query, grad_scores, ((1,), (1,))) * (1.0 / RANK_KV)
            grad_values = dot(grad_out, probs.astype(BF16), ((1,), (1,))) * (1.0 / RANK_KV)
            rows = []
            for r in range(KV):
                grad = grad_keys if r < RANK_KV else grad_values
                rows.append(jnp.sum(grad * wide_ref[r, :, span], axis=0, keepdims=True))
                gwb_ref[r, :, span] += factors[r : r + 1, cut] * grad
            gwa_ref[head, :, span] = jnp.concatenate(rows, axis=0)
        grad_query = grad_query * (HEAD_DIM**-0.5 / RANK_Q)
        own = a_ref[head]
        rows = []
        for r in range(RANK_Q):
            rows.append(jnp.sum(grad_query * bq_ref[r], axis=0, keepdims=True))
            gbq_ref[r] += own[r : r + 1] * grad_query
        ga_ref[head] = jnp.concatenate(rows, axis=0)
        return carry

    lax.fori_loop(0, heads, one_head, 0)


VMEM_LIMIT = 56 * 1024 * 1024


def whole_specs(count):
    return [pl.BlockSpec(memory_space=pltpu.VMEM)] * count


def attend_forward(first, a_rows, b_query, win_a, win_b):
    heads, _, block = a_rows.shape
    window = win_a.shape[-1]
    return pl.pallas_call(
        forward_kernel,
        out_shape=(
            jax.ShapeDtypeStruct((heads, HEAD_DIM, block), BF16),
            jax.ShapeDtypeStruct((heads, 1, block), F32),
            jax.ShapeDtypeStruct((heads, HEAD_DIM, block), BF16),
        ),
        in_specs=whole_specs(5),
        out_specs=tuple(whole_specs(3)),
        scratch_shapes=[
            pltpu.VMEM((window, block), F32),
            pltpu.VMEM((KV, HEAD_DIM, window), F32),
            pltpu.VMEM((window, block), F32),
        ],
        compiler_params=pltpu.CompilerParams(vmem_limit_bytes=VMEM_LIMIT),
        name="attend_forward",
    )(first, a_rows, b_query, win_a, win_b)


def attend_backward(first, a_rows, b_query, win_a, win_b, lse, query, grad_mixed):
    heads, _, block = a_rows.shape
    window = win_a.shape[-1]
    return pl.pallas_call(
        backward_kernel,
        out_shape=(
            jax.ShapeDtypeStruct((heads, RANK_Q, block), F32),
            jax.ShapeDtypeStruct((RANK_Q, HEAD_DIM, block), F32),
            jax.ShapeDtypeStruct((heads, KV, window), F32),
            jax.ShapeDtypeStruct((KV, HEAD_DIM, window), F32),
        ),
        in_specs=whole_specs(8),
        out_specs=tuple(whole_specs(4)),
        scratch_shapes=[
            pltpu.VMEM((window, block), F32),
            pltpu.VMEM((KV, HEAD_DIM, window), F32),
            pltpu.VMEM((window, block), F32),
            pltpu.VMEM((window, block), F32),
        ],
        compiler_params=pltpu.CompilerParams(vmem_limit_bytes=VMEM_LIMIT),
        name="attend_backward",
    )(first, a_rows, b_query, win_a, win_b, lse, query, grad_mixed)


def rotate(rows, cosine, sine):
    half = HEAD_DIM // 2
    lower, upper = rows[:, :half], rows[:, half:]
    return jnp.concatenate(
        [lower * cosine - upper * sine, lower * sine + upper * cosine], axis=1
    )


def make_general(mesh):
    n_f, n_c, n_tp = mesh.shape["fsdp"], mesh.shape["ctx"], mesh.shape["tp"]
    n_hi, n_lo = 2, n_tp // 2

    def shards(
        resid_in,
        segment_ids,
        cotangent,
        w_factor_a,
        w_factor_b,
        w_out,
        w_gate_up,
        w_down,
        attn_gains,
        ffn_gains,
    ):
        seq_count, local_len, width = resid_in.shape
        assert seq_count == 1 and w_factor_a.shape[0] == 1 and n_lo == 2
        full_len = segment_ids.shape[1]
        block = local_len // n_tp
        extra = -(-(MOST_DOC - 1) // block)
        window = (extra + 1) * block
        a_cols = w_factor_a.shape[2]
        heads = n_tp * a_cols // RANKS
        b_cols = w_factor_b.shape[2]
        b_rows = w_factor_b.shape[1]
        b_parts = b_cols // LANES
        fc_cols = w_down.shape[2]
        hidden = w_down.shape[1]
        o_rows = w_out.shape[1]

        f_index, c_index, t_index = (
            lax.axis_index("fsdp"),
            lax.axis_index("ctx"),
            lax.axis_index("tp"),
        )
        hi, lo = t_index // 2, t_index % 2
        place = c_index * n_tp + t_index
        n_place = n_c * n_tp

        gains = jnp.concatenate([attn_gains, ffn_gains], axis=1).astype(BF16)
        gain_count = gains.shape[1]
        gain_rows = 16 * (-(-gain_count // (16 * LANES)))
        gains = jnp.pad(gains.reshape(-1), (0, gain_rows * LANES - gain_count))
        b_shard = w_factor_b[0].astype(BF16).reshape(b_rows, b_parts, LANES)
        a_shard = w_factor_a[0].astype(BF16).T
        pack = jnp.concatenate(
            [
                b_shard.transpose(1, 0, 2).reshape(-1, LANES),
                a_shard.reshape(-1, LANES),
                gains.reshape(-1, LANES),
            ],
            axis=0,
        )
        n_b = b_parts * b_rows
        n_a = a_cols * fc_cols // LANES
        pack = gather_direct(pack, "fsdp", n_f)
        after_pack = pack
        pack = gather_pair(pack, "ctx", n_c, 1)
        pack = gather_pair(pack, "tp", n_tp, 2)
        pack = gather_pair(pack, "tp", n_tp, 1)
        pack = pack.transpose(3, 2, 1, 0, 4, 5)
        weight_b = pack[:, :, :, :, :n_b].reshape(-1, b_parts, b_rows, LANES)
        weight_b = weight_b.transpose(0, 2, 1, 3).reshape(width, b_cols)
        weight_a = pack[:, :, :, :, n_b : n_b + n_a].reshape(n_f, n_c, n_tp, a_cols, fc_cols)
        weight_a = weight_a.transpose(2, 3, 0, 1, 4).reshape(n_tp * a_cols, width)
        gains_all = pack[:, :, :, :, n_b + n_a :].reshape(-1, gain_rows * LANES)[:, :gain_count]
        gains_all = gains_all.reshape(-1, 2, gain_count // 2).transpose(1, 0, 2)
        gains_all = gains_all.reshape(2, width).astype(F32)
        gain_attn, gain_ffn = gains_all[0:1], gains_all[1:2]

        big = jnp.concatenate(
            [
                w_gate_up[0, 0].astype(BF16).T,
                w_gate_up[0, 1].astype(BF16).T,
                w_down[0].astype(BF16),
                w_out[0].astype(BF16),
            ],
            axis=0,
        )
        big, _ = lax.optimization_barrier((big, after_pack))
        big = gather_direct(big, "fsdp", n_f)
        big = gather_pair(big, "ctx", n_c, 1)
        big = big.transpose(2, 1, 0, 3).reshape(-1, width)
        weight_g = big[:hidden]
        weight_u = big[hidden : 2 * hidden]
        weight_d = big[2 * hidden : 3 * hidden]
        weight_o = gather_pair(big[3 * hidden :], "tp", n_tp, 2)
        weight_o = gather_pair(weight_o, "tp", n_tp, 1)
        weight_o = weight_o.transpose(1, 0, 2, 3).reshape(n_tp * o_rows, width)

        seg_here = lax.dynamic_slice_in_dim(segment_ids[0], place * block, block, 0)
        first = jnp.sum((segment_ids[0][:, None] < seg_here[None, :]).astype(jnp.int32), axis=0)
        token = place * block + jnp.arange(block, dtype=jnp.int32)
        position = (token - first).astype(F32)
        first = (first - place * block + extra * block).reshape(1, block)
        frequency = 10000.0 ** (
            -2.0 * jnp.arange(HEAD_DIM // 2, dtype=F32) / HEAD_DIM
        )
        angles = frequency[:, None] * position[None, :]
        cosine, sine = jnp.cos(angles)[None], jnp.sin(angles)[None]

        stream = resid_in[0].reshape(n_tp, block, width)
        own = take(stream, t_index)
        inverse_attn = inverse_rms(own)
        normed = (own * inverse_attn * gain_attn).astype(BF16)
        a_rows = dot(weight_a, normed, ((1,), (1,))).reshape(heads, RANKS, block)
        b_raw = dot(weight_b, normed, ((0,), (1,))).reshape(RANKS, HEAD_DIM, block)
        b_rot = rotate(b_raw[: RANK_Q + RANK_KV], cosine, sine)
        b_query = b_rot[:RANK_Q]
        b_kv = jnp.concatenate([b_rot[RANK_Q:], b_raw[RANK_Q + RANK_KV :]], axis=0)
        payload = jnp.concatenate(
            [
                b_kv.reshape(KV * HEAD_DIM, block),
                a_rows[:, RANK_Q:].reshape(heads * KV, block),
            ],
            axis=0,
        ).astype(BF16)
        around = [
            lax.ppermute(
                payload, ("ctx", "tp"), [(i, i + step) for i in range(n_place - step)]
            )
            for step in range(extra, 0, -1)
        ]
        win = jnp.concatenate(around + [payload], axis=1)
        win_b = win[: KV * HEAD_DIM].reshape(KV, HEAD_DIM, window)
        win_a = win[KV * HEAD_DIM :].reshape(heads, KV, window)

        mixed, lse, query = attend_forward(first, a_rows, b_query, win_a, win_b)
        mixed = mixed.reshape(heads * HEAD_DIM, block)
        attn_out = dot(mixed, weight_o, ((0,), (0,)))
        mid = own + attn_out
        inverse_ffn = inverse_rms(mid)
        normed_ffn = (mid * inverse_ffn * gain_ffn).astype(BF16)

        near_rows = gather_pair(normed_ffn, "tp", n_tp, 1)
        far_rows = gather_pair(swap(normed_ffn, "tp", n_tp, 2), "tp", n_tp, 1)
        grad_all = cotangent[0].reshape(n_hi, n_lo * block, width)

        def half(rows, grad_rows):
            rows = rows.reshape(n_lo * block, width)
            gate = dot(rows, weight_g, ((1,), (1,)))
            up = dot(rows, weight_u, ((1,), (1,)))
            grad_act = dot(grad_rows, weight_d, ((1,), (1,)))
            squash = jax.nn.sigmoid(gate)
            act = (gate * squash * up).astype(BF16)
            grad_gate = (grad_act * up * squash * (1.0 + gate * (1.0 - squash))).astype(BF16)
            grad_up = (grad_act * gate * squash).astype(BF16)
            back = dot(grad_gate, weight_g, ((1,), (0,))) + dot(grad_up, weight_u, ((1,), (0,)))
            ahead = dot(act, weight_d, ((1,), (0,)))
            both = lambda v: v.reshape(n_lo, block, width)
            return rows, act, grad_gate, grad_up, both(back), both(ahead)

        grad_near = take(grad_all, hi).astype(BF16)
        grad_far = take(grad_all, 1 - hi).astype(BF16)
        near = half(near_rows, grad_near)
        far = half(far_rows, grad_far)
        back_far = scatter_pair(far[4], "tp", n_tp, 1).astype(BF16)
        back_far = swap(back_far, "tp", n_tp, 2)
        grad_normed_ffn = scatter_pair(near[4], "tp", n_tp, 1) + back_far.astype(F32)
        ahead_far = scatter_pair(far[5], "tp", n_tp, 1).astype(BF16)
        ahead_far = swap(ahead_far, "tp", n_tp, 2)
        ffn_out = scatter_pair(near[5], "tp", n_tp, 1) + ahead_far.astype(F32)

        def spread(value):
            beside = swap(value, "tp", n_tp, 1)
            across = swap(value, "tp", n_tp, 2)
            diagonal = swap(across, "tp", n_tp, 1)
            out = jnp.zeros((n_tp,) + value.shape, value.dtype)
            for bit, part in enumerate((value, beside, across, diagonal)):
                out = lax.dynamic_update_slice(out, part[None], (t_index ^ bit, 0, 0))
            return out.reshape(local_len, width).astype(F32)

        block_out = resid_in + spread((attn_out + ffn_out).astype(BF16))[None]

        def columns(value, which):
            value = value.reshape(value.shape[0], n_f, n_c, fc_cols)
            value = lax.dynamic_index_in_dim(value, which, 2, keepdims=False)
            return value.reshape(value.shape[0], n_f * fc_cols)

        rows_all = jnp.concatenate([near[0], far[0]], axis=0)
        act_all = jnp.concatenate([near[1], far[1]], axis=0)
        gate_all = jnp.concatenate([near[2], far[2]], axis=0)
        up_all = jnp.concatenate([near[3], far[3]], axis=0)
        cot_all = jnp.concatenate([grad_near, grad_far], axis=0)

        def big_grads(which):
            rows_cut = columns(rows_all, which)
            cot_cut = columns(cot_all, which)
            return jnp.concatenate(
                [
                    dot(gate_all, rows_cut, ((0,), (0,))),
                    dot(up_all, rows_cut, ((0,), (0,))),
                    dot(act_all, cot_cut, ((0,), (0,))),
                ],
                axis=0,
            )

        def over_fc(send, keep):
            total = keep + swap(send.astype(BF16), "ctx", n_c, 1).astype(F32)
            total = total.astype(BF16).reshape(-1, n_f, fc_cols).transpose(1, 0, 2)
            return scatter_direct(total, "fsdp", n_f)

        grad_big = over_fc(big_grads(1 - c_index), big_grads(c_index))
        grad_gate_w = grad_big[:hidden].T
        grad_up_w = grad_big[hidden : 2 * hidden].T
        grad_down_w = grad_big[2 * hidden :]

        own_cot = take(cotangent[0].reshape(n_tp, block, width), t_index)
        gain_grad_ffn = jnp.sum(grad_normed_ffn * mid * inverse_ffn, axis=0)
        delta_mid = norm_back(grad_normed_ffn, mid, inverse_ffn, gain_ffn)
        grad_attn = (own_cot + delta_mid).astype(BF16)
        grad_out = dot(mixed, grad_attn, ((1,), (0,))).reshape(n_hi, n_lo, o_rows, width)
        grad_out = scatter_pair(grad_out.transpose(1, 0, 2, 3), "tp", n_tp, 1)
        grad_out = scatter_pair(grad_out, "tp", n_tp, 2)
        grad_out = over_fc(columns(grad_out, 1 - c_index), columns(grad_out, c_index))

        grad_mixed = dot(weight_o, grad_attn, ((1,), (1,))).astype(BF16)
        ga_q, gb_q, gw_a, gw_b = attend_backward(
            first,
            a_rows,
            b_query,
            win_a,
            win_b,
            lse,
            query,
            grad_mixed.reshape(heads, HEAD_DIM, block),
        )
        gw = jnp.concatenate(
            [gw_b.reshape(KV * HEAD_DIM, window), gw_a.reshape(heads * KV, window)], axis=0
        )
        total = gw[:, extra * block :]
        for step in range(1, extra + 1):
            part = gw[:, (extra - step) * block : (extra - step + 1) * block].astype(BF16)
            part = lax.ppermute(
                part, ("ctx", "tp"), [(i + step, i) for i in range(n_place - step)]
            )
            total = total + part.astype(F32)
        gb_kv = total[: KV * HEAD_DIM].reshape(KV, HEAD_DIM, block)
        ga_kv = total[KV * HEAD_DIM :].reshape(heads, KV, block)
        grad_b = jnp.concatenate(
            [
                rotate(jnp.concatenate([gb_q, gb_kv[:RANK_KV]], axis=0), cosine, -sine),
                gb_kv[RANK_KV:],
            ],
            axis=0,
        )
        grad_b = grad_b.reshape(b_cols, block).astype(BF16)
        grad_a = jnp.concatenate([ga_q, ga_kv], axis=1).reshape(heads * RANKS, block).astype(BF16)
        grad_normed = dot(grad_a, weight_a, ((0,), (0,))) + dot(grad_b, weight_b, ((0,), (1,)))
        gain_grad_attn = jnp.sum(grad_normed * own * inverse_attn, axis=0)
        delta = delta_mid + norm_back(grad_normed, own, inverse_attn, gain_attn)
        resid_grad = cotangent + spread(delta.astype(BF16))[None]

        grad_wa = dot(grad_a, normed, ((1,), (0,))).astype(BF16)
        grad_wa = grad_wa.reshape(n_hi, n_lo, a_cols, n_f, n_c, fc_cols)
        grad_wa = grad_wa.transpose(1, 0, 4, 3, 2, 5).reshape(n_lo, n_hi, n_c, n_f, n_a, LANES)
        grad_wb = jnp.einsum(
            "pkt,td->pdk",
            grad_b.reshape(b_parts, LANES, block),
            normed,
            preferred_element_type=F32,
        ).astype(BF16)
        grad_wb = grad_wb.reshape(b_parts, n_f, n_c, n_hi, n_lo, b_rows, LANES)
        grad_wb = grad_wb.transpose(4, 3, 2, 1, 0, 5, 6)
        grad_wb = grad_wb.reshape(n_lo, n_hi, n_c, n_f, n_b, LANES)
        gain_grads = jnp.stack([gain_grad_attn, gain_grad_ffn]).astype(BF16)
        gain_grads = gain_grads.reshape(2, n_f, n_c, n_hi, n_lo, gain_count // 2)
        gain_grads = gain_grads.transpose(4, 3, 2, 1, 0, 5).reshape(
            n_lo, n_hi, n_c, n_f, gain_count
        )
        gain_grads = jnp.pad(
            gain_grads, [(0, 0)] * 4 + [(0, gain_rows * LANES - gain_count)]
        ).reshape(n_lo, n_hi, n_c, n_f, gain_rows, LANES)
        pack = jnp.concatenate([grad_wb, grad_wa, gain_grads], axis=4)
        pack = scatter_pair(pack, "tp", n_tp, 1)
        pack = scatter_pair(pack, "tp", n_tp, 2)
        pack = scatter_pair(pack, "ctx", n_c, 1).astype(BF16)
        pack = scatter_direct(pack, "fsdp", n_f)
        part_b = pack[:n_b].reshape(b_parts, b_rows, LANES).transpose(1, 0, 2)
        part_b = part_b.reshape(1, b_rows, b_cols)
        part_a = pack[n_b : n_b + n_a].reshape(a_cols, fc_cols).T[None]
        part_gain = pack[n_b + n_a :].reshape(-1)[:gain_count].reshape(2, 1, gain_count // 2)
        return (
            block_out,
            resid_grad,
            part_a,
            part_b,
            grad_out[None],
            jnp.stack([grad_gate_w, grad_up_w])[None],
            grad_down_w[None],
            part_gain[0],
            part_gain[1],
        )

    return shards


def rotated(rows, cosine, sine):
    half = HEAD_DIM // 2
    lower, upper = rows[:half], rows[half:]
    return jnp.concatenate([lower * cosine - upper * sine, lower * sine + upper * cosine], axis=0)


def make_fused(mesh):
    n_f, n_c, n_tp = mesh.shape["fsdp"], mesh.shape["ctx"], mesh.shape["tp"]
    n_piece = n_f * n_c
    AT_TP = n_piece
    AT_ME = n_piece + n_tp

    def shards(
        resid_in,
        segment_ids,
        cotangent,
        w_factor_a,
        w_factor_b,
        w_out,
        w_gate_up,
        w_down,
        attn_gains,
        ffn_gains,
    ):
        _, local_len, width = resid_in.shape
        block = local_len // n_tp
        extra = -(-(MOST_DOC - 1) // block)
        windows = extra + 1
        a_cols = w_factor_a.shape[2]
        group = a_cols // RANKS
        heads = n_tp * group
        feats = group * HEAD_DIM
        a_pad = 16 * (-(-a_cols // 16))
        b_rows, b_cols = w_factor_b.shape[1:]
        b_parts = b_cols // LANES
        n_b = b_parts * b_rows
        pack_rows = n_b + a_pad + 16
        fc_cols = w_down.shape[2]
        hidden = w_down.shape[1]
        o_rows = w_out.shape[1]
        gain_part = attn_gains.shape[1]
        kv_b = KV * HEAD_DIM
        kv_rows = kv_b + heads * KV
        half_width = width // n_c
        pairs = heads // 2
        pair_rows = 8 * (-(-2 * RANKS // 8))
        early = 2 * hidden + 16 * (hidden // 64)
        assert n_f == 4 and fc_cols == LANES and o_rows == feats and n_tp == 4 and n_c == 2

        f_index, c_index, t_index = (
            lax.axis_index("fsdp"),
            lax.axis_index("ctx"),
            lax.axis_index("tp"),
        )
        place = c_index * n_tp + t_index
        n_place = n_c * n_tp
        columns = [
            ((f_index - s) % n_f) * n_c + (c_index if near == 0 else 1 - c_index)
            for near in range(n_c)
            for s in range(n_f)
        ]
        members = [t_index ^ (lo + 2 * hi) for lo in range(2) for hi in range(2)]
        beside_shift = jnp.where(f_index % 2 == 0, n_f - 1, 1)
        meta = jnp.stack(columns + members + [t_index, f_index, beside_shift]).astype(jnp.int32)

        resid_in = pltpu.with_memory_space_constraint(resid_in, pltpu.HBM)
        cotangent = pltpu.with_memory_space_constraint(cotangent, pltpu.HBM)

        def column(meta_ref, j):
            return pl.ds(pl.multiple_of(meta_ref[j] * LANES, LANES), LANES)

        def member(meta_ref, lo, hi):
            return meta_ref[AT_TP + 2 * lo + hi]

        def to_arrival(meta_ref, load):
            return jnp.concatenate([load(column(meta_ref, j)) for j in range(n_piece)], axis=1)

        WHOLE = pl.BlockSpec(memory_space=pltpu.VMEM)
        REMOTE = pl.BlockSpec(memory_space=pl.ANY)

        def call(
            kernel, name, outs, args, specs=None, scratch=(), grid=(1,), out_specs=None, room=4,
            scalars=meta,
        ):
            held = 0
            for arg, spec in zip((*args, *args[:1]), (specs or []) + (out_specs or [])):
                if spec.block_shape:
                    held += 2 * math.prod(spec.block_shape) * arg.dtype.itemsize
            for item in scratch:
                if hasattr(item, "shape") and item.memory_space == pltpu.VMEM:
                    held += math.prod(item.shape) * jnp.dtype(item.dtype).itemsize
            limit = min(held + room * 2**20, VMEM_LIMIT)
            return pl.pallas_call(
                kernel,
                out_shape=[jax.ShapeDtypeStruct(s, d) for s, d in outs],
                grid_spec=pltpu.PrefetchScalarGridSpec(
                    num_scalar_prefetch=1,
                    grid=grid,
                    in_specs=specs or [WHOLE] * len(args),
                    out_specs=out_specs or [WHOLE] * len(outs),
                    scratch_shapes=list(scratch),
                ),
                compiler_params=pltpu.CompilerParams(vmem_limit_bytes=limit),
                name=name,
            )(scalars, *args)


        def pack_kernel(meta_ref, b_ref, a_ref, g0_ref, g1_ref, out_ref):
            for k in range(b_parts):
                out_ref[k * b_rows : (k + 1) * b_rows, :] = b_ref[
                    0, :, k * LANES : (k + 1) * LANES
                ].astype(BF16)
            a_shard = jnp.concatenate([a_ref[0], jnp.zeros((a_pad - a_cols, LANES), F32)], axis=0)
            out_ref[n_b : n_b + a_pad, :] = a_shard.astype(BF16)
            both = jnp.concatenate([g0_ref[...], g1_ref[...]], axis=0)
            both = jnp.concatenate([both, jnp.zeros((6, gain_part), F32)], axis=0)
            both = jnp.concatenate([both, jnp.zeros((8, LANES - gain_part), F32)], axis=1)
            both = pltpu.roll(both, meta_ref[AT_ME] * gain_part, 1)
            both = jnp.concatenate([both, jnp.zeros((8, LANES), F32)], axis=0)
            out_ref[n_b + a_pad :, :] = both.astype(BF16)

        def big_kernel(meta_ref, gu_ref, d_ref, gu_out_ref, d_out_ref):
            for k in range(2):
                gu_out_ref[k * hidden : (k + 1) * hidden, :] = gu_ref[0, k].astype(BF16)
            gu_out_ref[2 * hidden :, :] = d_ref[0, : early - 2 * hidden, :].astype(BF16)
            d_out_ref[...] = d_ref[0, early - 2 * hidden :, :].astype(BF16)

        def factor_kernel(
            meta_ref,
            x_ref,
            p0_ref,
            p1_ref,
            cos_ref,
            sin_ref,
            wb_ref,
            wa_ref,
            gain_ref,
            normed_ref,
            a_ref,
            bq_ref,
            pay_ref,
        ):
            gain_ref[...] = jnp.zeros_like(gain_ref)
            for lo, hi in ((0, 0), (0, 1), (1, 0), (1, 1)):
                part = (p0_ref, p1_ref)[lo]
                tp = member(meta_ref, lo, hi)
                for near in range(n_c):
                    for s in range(n_f):
                        j = near * n_f + s
                        lanes = column(meta_ref, j)
                        row = pl.multiple_of((meta_ref[j] * n_tp + tp) * b_rows, b_rows)
                        for k in range(b_parts):
                            wb_ref[pl.ds(row, b_rows), k * LANES : (k + 1) * LANES] = part[
                                near, hi, s, k * b_rows : (k + 1) * b_rows, :
                            ]
                        wa_ref[tp, :, lanes] = part[near, hi, s, n_b : n_b + a_pad, :]
                        gain_ref[:, lanes] += part[near, hi, s, n_b + a_pad :, :].astype(F32)
            x = x_ref[...]
            normed = (x * inverse_rms(x) * gain_ref[0:1]).astype(BF16)
            normed_ref[...] = normed
            cosine, sine = cos_ref[...], sin_ref[...]
            b_raw = jnp.transpose(dot(normed, wb_ref[...], ((1,), (0,))))
            for r in range(RANK_Q):
                bq_ref[r] = rotated(b_raw[r * HEAD_DIM : (r + 1) * HEAD_DIM], cosine, sine)
            for r in range(KV):
                rows = b_raw[(RANK_Q + r) * HEAD_DIM : (RANK_Q + r + 1) * HEAD_DIM]
                if r < RANK_KV:
                    rows = rotated(rows, cosine, sine)
                pay_ref[r * HEAD_DIM : (r + 1) * HEAD_DIM, :] = rows.astype(BF16)
            for tp in range(n_tp):
                a_raw = dot(wa_ref[tp], normed, ((1,), (1,)))
                a_ref[tp] = a_raw
                kv = [a_raw[g * RANKS + RANK_Q : (g + 1) * RANKS] for g in range(group)]
                start = kv_b + tp * group * KV
                pay_ref[start : start + group * KV, :] = jnp.concatenate(kv, axis=0).astype(BF16)

        def set_mask(first_ref, bias_ref):
            bias_ref[...] = attention_mask(first_ref, windows * block, block)

        def is_even(meta_ref):
            return lax.rem(meta_ref[AT_ME], 2) == 0

        def widen(meta_ref, arrived, win_ref, wide_ref):
            third, second, beside_second, beside, own = arrived
            win_ref[1] = second[...]
            win_ref[3] = own[...]

            @pl.when(is_even(meta_ref))
            def _():
                win_ref[0] = third[...]
                win_ref[2] = beside_second[...]

            @pl.when(jnp.logical_not(is_even(meta_ref)))
            def _():
                win_ref[0] = beside_second[...]
                win_ref[2] = beside[...]

            for j in range(windows):
                for r in range(KV):
                    wide_ref[j, r] = win_ref[j, r * HEAD_DIM : (r + 1) * HEAD_DIM, :].astype(F32)

        def spread_factors(a_ref, win_ref, own_ref, kv_ref):
            for pair in range(pairs):
                start = pair % (group // 2) * 2 * RANKS
                own_ref[pair, : 2 * RANKS, :] = a_ref[pair * 2 // group, start : start + 2 * RANKS, :]
            for j in range(windows):
                kv_ref[j] = win_ref[j, kv_b:, :].astype(F32)

        def kv_factors(kv_ref, pair):
            start = pl.multiple_of(pair * (2 * KV), 2 * KV)
            return [kv_ref[j, pl.ds(start, 2 * KV), :] for j in range(windows)]

        def head_place(pair, g):
            tp, half = pair // (group // 2), lax.rem(pair, group // 2)
            return tp, 2 * half + g, pl.ds(pl.multiple_of((2 * half + g) * HEAD_DIM, HEAD_DIM), HEAD_DIM)

        def kv_rows_of(factors, wide_ref, g, j):
            def mix(r):
                a0 = factors[j][g * KV + r : g * KV + r + 1]
                a1 = factors[j][g * KV + r + 1 : g * KV + r + 2]
                rows = a0 * wide_ref[j, r] + a1 * wide_ref[j, r + 1]
                return (rows * (1.0 / RANK_KV)).astype(BF16)

            return mix(0), mix(RANK_KV)

        def attention_kernel(
            meta_ref,
            first_ref,
            a_ref,
            bq_ref,
            w0_ref,
            w1_ref,
            w2_ref,
            w3_ref,
            w4_ref,
            lse_ref,
            q_ref,
            mixed_ref,
            win_ref,
            bias_ref,
            wide_ref,
            s_ref,
            own_ref,
            kv_ref,
        ):
            set_mask(first_ref, bias_ref)
            widen(meta_ref, (w0_ref, w1_ref, w2_ref, w3_ref, w4_ref), win_ref, wide_ref)
            spread_factors(a_ref, win_ref, own_ref, kv_ref)
            spans = [pl.ds(j * block, block) for j in range(windows)]

            def one_pair(pair, carry):
                own = own_ref[pair]
                factors = kv_factors(kv_ref, pair)
                for g in range(2):
                    tp, head, rows = head_place(pair, g)
                    query = own[g * RANKS : g * RANKS + 1] * bq_ref[0]
                    for r in range(1, RANK_Q):
                        query = query + own[g * RANKS + r : g * RANKS + r + 1] * bq_ref[r]
                    query = (query * (1.0 / RANK_Q)).astype(BF16)
                    query = query * jnp.asarray(HEAD_DIM**-0.5, BF16)
                    q_ref[tp, head] = query
                    top = jnp.full((1, block), MASKED, F32)
                    values = []
                    for j, span in enumerate(spans):
                        keys, value_rows = kv_rows_of(factors, wide_ref, g, j)
                        values.append(value_rows)
                        scores = dot(keys, query, ((0,), (0,))) + bias_ref[span, :]
                        s_ref[g, span, :] = scores
                        top = jnp.maximum(top, jnp.max(scores, axis=0, keepdims=True))
                    total = jnp.zeros((1, block), F32)
                    for span in spans:
                        weight = jnp.exp(s_ref[g, span, :] - top)
                        s_ref[g, span, :] = weight
                        total = total + jnp.sum(weight, axis=0, keepdims=True)
                    lse_ref[pair, g : g + 1, :] = top + jnp.log(total)
                    scale = 1.0 / total
                    mixed = jnp.zeros((HEAD_DIM, block), F32)
                    for j, span in enumerate(spans):
                        probs = (s_ref[g, span, :] * scale).astype(BF16)
                        mixed = mixed + dot(values[j], probs, ((1,), (0,)))
                    mixed_ref[tp, rows, :] = mixed.astype(BF16)
                return carry

            lax.fori_loop(0, pairs, one_pair, 0)

        def project_kernel(
            meta_ref, x_ref, mixed_ref, o0_ref, o1_ref, gain_ref, mid_ref, attn_ref, nf_ref
        ):
            attn = jnp.zeros((block, width), F32)
            for lo, ref in enumerate((o0_ref, o1_ref)):
                for hi in range(2):
                    rows = mixed_ref[member(meta_ref, lo, hi)]
                    attn = attn + dot(rows, ref[hi * o_rows : (hi + 1) * o_rows, :], ((0,), (0,)))
            attn_ref[...] = attn
            mid = to_arrival(meta_ref, lambda lanes: x_ref[:, lanes]) + attn
            mid_ref[...] = mid
            gain = to_arrival(meta_ref, lambda lanes: gain_ref[1:2, lanes])
            nf_ref[...] = (mid * inverse_rms(mid) * gain).astype(BF16)

        def rows_kernel(
            meta_ref, x_hbm, cot_ref, x_ref, own_ref, near_ref, far_ref, cot_buf, sems
        ):
            row = pl.multiple_of(meta_ref[AT_ME] * block, block)
            own_load = pltpu.make_async_copy(x_hbm.at[0, pl.ds(row, block), :], x_ref, sems.at[4])
            own_load.start()
            loads = []
            for side in range(2):
                for i in range(2):
                    row = pl.multiple_of(member(meta_ref, i, side) * block, block)
                    k = 2 * side + i
                    loads.append(
                        pltpu.make_async_copy(
                            cot_ref.at[0, pl.ds(row, block), :], cot_buf.at[k], sems.at[k]
                        )
                    )
                    loads[-1].start()
            for k, load in enumerate(loads):
                load.wait()
                out_ref = (near_ref, far_ref)[k // 2]
                rows = slice(k % 2 * block, (k % 2 + 1) * block)
                for j in range(n_piece):
                    lanes = slice(j * LANES, (j + 1) * LANES)
                    part = cot_buf[k, :, column(meta_ref, j)]
                    out_ref[rows, lanes] = part.astype(BF16)
                    if k == 0:
                        own_ref[:, lanes] = part
            own_load.wait()

        def feed_rows(n_refs, gb_ref, w_ref, ht_ref, back0_ref, back1_ref):
            for i in range(2):
                cut = slice(i * block, (i + 1) * block)
                rows = n_refs[i][...]
                gate = dot(w_ref[0:hidden, :], rows, ((1,), (1,)))
                up = dot(w_ref[hidden : 2 * hidden, :], rows, ((1,), (1,)))
                grad_act = dot(w_ref[2 * hidden :, :], gb_ref[cut, :], ((1,), (1,)))
                squash = jax.nn.sigmoid(gate)
                soft = gate * squash
                ht_ref[2 * hidden :, cut] = (soft * up).astype(BF16)
                ht_ref[0:hidden, cut] = (
                    grad_act * up * squash * (1.0 + gate * (1.0 - squash))
                ).astype(BF16)
                ht_ref[hidden : 2 * hidden, cut] = (grad_act * soft).astype(BF16)
            back = dot(ht_ref[: 2 * hidden, :], w_ref[: 2 * hidden, :], ((0,), (0,)))
            back0_ref[...] = back[:block]
            back1_ref[...] = back[block:].astype(BF16)

        def far_kernel(meta_ref, n0_ref, n1_ref, gb_ref, *refs):
            own_gu_ref, far_gu_ref, pair_gu_ref, gu_across_ref, gu_rest_ref = refs[:5]
            dn_refs = refs[5 : 5 + n_f]
            ht_ref, back0_ref, back1_ref, w_ref, sems = refs[5 + n_f :]
            gate_up = [own_gu_ref, far_gu_ref, pair_gu_ref.at[0], pair_gu_ref.at[1], gu_across_ref]
            gate_up += [gu_rest_ref.at[s] for s in range(n_f - 1)]
            beside_shift = meta_ref[AT_ME + 2]
            arrivals = [0, 2, beside_shift, n_f - beside_shift]
            down = [ref.at[near] for near in range(n_c) for ref in dn_refs]
            loads = []
            for j in range(n_piece):
                lanes = pl.ds(j * LANES, LANES)
                at = pl.multiple_of((arrivals[j % n_f] + j // n_f * n_f) * LANES, LANES)
                loads.append(
                    pltpu.make_async_copy(
                        gate_up[j],
                        w_ref.at[pl.ds(0, early), pl.ds(at, LANES)],
                        sems.at[j],
                    )
                )
                loads.append(
                    pltpu.make_async_copy(
                        down[j], w_ref.at[pl.ds(early, 3 * hidden - early), lanes], sems.at[n_piece + j]
                    )
                )
            for load in loads:
                load.start()
            for load in loads:
                load.wait()
            feed_rows((n0_ref, n1_ref), gb_ref, w_ref, ht_ref, back0_ref, back1_ref)

        def near_kernel(meta_ref, n0_ref, n1_ref, gb_ref, w_ref, far_ht_ref, ht_ref, *refs):
            back0_ref, back1_ref, *ahead_refs = refs
            feed_rows((n0_ref, n1_ref), gb_ref, w_ref, ht_ref, back0_ref, back1_ref)
            for k, ref in enumerate((ht_ref, far_ht_ref)):
                ahead = dot(ref[2 * hidden :, :], w_ref[2 * hidden :, :], ((0,), (0,)))
                ahead_refs[2 * k][...] = ahead[:block]
                ahead_refs[2 * k + 1][...] = ahead[block:].astype(BF16)

        def weight_grad(refs, start, stop, right):
            hts, n_near, n_far, gbs = refs[0:2], refs[2:4], refs[4:6], refs[6:8]
            total = jnp.zeros((stop - start, width), F32)
            for side in range(2):
                left = hts[side]
                if right == 1:
                    total = total + dot(left[start:stop, :], gbs[side][...], ((1,), (0,)))
                    continue
                for i in range(2):
                    rows = (n_near, n_far)[side][i][...]
                    cut = slice(i * block, (i + 1) * block)
                    total = total + dot(left[start:stop, cut], rows, ((1,), (0,)))
            return total

        def gate_up_grad_kernel(meta_ref, *refs):
            keep_ref, send_ref = refs[8:]
            for k in range(2):
                cut = slice(k * hidden, (k + 1) * hidden)
                total = weight_grad(refs, k * hidden, (k + 1) * hidden, 0)
                keep_ref[cut, :] = total[:, :half_width].astype(BF16)
                send_ref[cut, :] = total[:, half_width:].astype(BF16)

        def down_grad_kernel(meta_ref, *refs):
            keep_ref, send_ref = refs[8:]
            total = weight_grad(refs, 2 * hidden, 3 * hidden, 1)

            def chunk(s, near):
                start = near * half_width + s * LANES
                return total[:, start : start + LANES]

            for near in range(n_c):
                keep_ref[0, near] = chunk(0, near)
                keep_ref[1, near] = chunk(2, near)

            @pl.when(lax.rem(meta_ref[AT_ME + 1], 2) == 0)
            def _():
                for near in range(n_c):
                    send_ref[0, near] = chunk(3, near).astype(BF16)
                    send_ref[1, near] = chunk(1, near).astype(BF16)

            @pl.when(lax.rem(meta_ref[AT_ME + 1], 2) == 1)
            def _():
                for near in range(n_c):
                    send_ref[0, near] = chunk(1, near).astype(BF16)
                    send_ref[1, near] = chunk(3, near).astype(BF16)

        def middle_kernel(
            meta_ref,
            cot_ref,
            back_ref,
            beside_ref,
            across_ref,
            mid_ref,
            gain_ref,
            o0_ref,
            o1_ref,
            mixed_ref,
            dmid_ref,
            gg_ref,
            go_ref,
            keep_ref,
            send_ref,
        ):
            back = back_ref[...] + beside_ref[...].astype(F32) + across_ref[...].astype(F32)
            mid = mid_ref[...]
            inverse = inverse_rms(mid)
            gain = to_arrival(meta_ref, lambda lanes: gain_ref[1:2, lanes])
            normal = mid * inverse
            gains = jnp.sum(back * normal, axis=0, keepdims=True)
            for j in range(n_piece):
                gg_ref[:, column(meta_ref, j)] = jnp.broadcast_to(
                    gains[:, j * LANES : (j + 1) * LANES], (8, LANES)
                )
            scaled = back * gain
            delta = inverse * (
                scaled - normal * jnp.mean(scaled * normal, axis=-1, keepdims=True)
            )
            dmid_ref[...] = delta
            grad = (cot_ref[...] + delta).astype(BF16)
            for lo, ref in enumerate((o0_ref, o1_ref)):
                for hi in range(2):
                    tp = member(meta_ref, lo, hi)
                    cut = slice(hi * o_rows, (hi + 1) * o_rows)
                    go_ref[tp] = dot(ref[cut, :], grad, ((1,), (1,))).astype(BF16)
                    weight = dot(mixed_ref[tp], grad, ((1,), (0,))).astype(BF16)
                    (keep_ref, send_ref)[lo][cut, :] = weight

        def attention_back_kernel(
            part,
            meta_ref,
            first_ref,
            a_ref,
            bq_ref,
            w0_ref,
            w1_ref,
            w2_ref,
            w3_ref,
            w4_ref,
            lse_ref,
            q_ref,
            go_ref,
            *refs,
        ):
            win_ref, bias_ref, wide_ref, p_ref, dp_ref, own_ref, kv_ref = refs[-7:]
            if part == 0:
                ga_ref, gbq_ref, gwb_ref, gwa_ref = refs[:4]
            else:
                ga_ref, gbq_ref, second_ref, beside_ref, third_ref, own_out_ref = refs[3:9]
                gwb_ref, gwa_ref = refs[-9:-7]
            set_mask(first_ref, bias_ref)
            widen(meta_ref, (w0_ref, w1_ref, w2_ref, w3_ref, w4_ref), win_ref, wide_ref)
            spread_factors(a_ref, win_ref, own_ref, kv_ref)
            if part == 0:
                gbq_ref[...] = jnp.zeros_like(gbq_ref)
                gwb_ref[...] = jnp.zeros_like(gwb_ref)
            else:
                gbq_ref[...] = refs[0][...]
                gwb_ref[...] = refs[1][...]
                gwa_ref[...] = refs[2][...]
            spans = [pl.ds(j * block, block) for j in range(windows)]
            first_pair = part * (pairs // 2)

            def one_pair(pair, carry):
                own = own_ref[pair]
                factors = kv_factors(kv_ref, pair)
                grad_a = []
                grad_kv = [[] for _ in spans]
                for g in range(2):
                    tp, head, rows = head_place(pair, g)
                    query = q_ref[tp, head]
                    grad_out = go_ref[tp, rows, :]
                    lse = lse_ref[pair, g : g + 1, :]
                    inner = jnp.zeros((1, block), F32)
                    keys = []
                    for j, span in enumerate(spans):
                        key_rows, value_rows = kv_rows_of(factors, wide_ref, g, j)
                        keys.append(key_rows)
                        scores = dot(key_rows, query, ((0,), (0,))) + bias_ref[span, :]
                        probs = jnp.exp(scores - lse)
                        grad_probs = dot(value_rows, grad_out, ((0,), (0,)))
                        p_ref[g % 2, span, :] = probs
                        dp_ref[g % 2, span, :] = grad_probs
                        inner = inner + jnp.sum(probs * grad_probs, axis=0, keepdims=True)
                    grad_query = jnp.zeros((HEAD_DIM, block), F32)
                    for j, span in enumerate(spans):
                        probs = p_ref[g % 2, span, :]
                        grad_scores = (probs * (dp_ref[g % 2, span, :] - inner)).astype(BF16)
                        grad_query = grad_query + dot(keys[j], grad_scores, ((1,), (0,)))
                        grad_keys = dot(query, grad_scores, ((1,), (1,))) * (1.0 / RANK_KV)
                        grad_values = dot(grad_out, probs.astype(BF16), ((1,), (1,)))
                        grad_values = grad_values * (1.0 / RANK_KV)
                        for r in range(KV):
                            grad = grad_keys if r < RANK_KV else grad_values
                            grad_kv[j].append(
                                jnp.sum(grad * wide_ref[j, r], axis=0, keepdims=True)
                            )
                            gwb_ref[j, r] += factors[j][g * KV + r : g * KV + r + 1] * grad
                    grad_query = grad_query * (HEAD_DIM**-0.5 / RANK_Q)
                    for r in range(RANK_Q):
                        grad_a.append(jnp.sum(grad_query * bq_ref[r], axis=0, keepdims=True))
                        gbq_ref[r] += own[g * RANKS + r : g * RANKS + r + 1] * grad_query
                    grad_a.append(jnp.zeros((KV, block), F32))
                grad_a.append(jnp.zeros((pair_rows - 2 * RANKS, block), F32))
                ga_ref[pair - first_pair] = jnp.concatenate(grad_a, axis=0)
                start = pl.multiple_of(pair * (2 * KV), 2 * KV)
                for j in range(windows):
                    gwa_ref[j, pl.ds(start, 2 * KV), :] = jnp.concatenate(grad_kv[j], axis=0)
                return carry

            lax.fori_loop(first_pair, first_pair + pairs // 2, one_pair, 0)
            if part == 0:
                return

            def put(ref, start, j):
                for r in range(KV):
                    row = start + r * HEAD_DIM
                    ref[row : row + HEAD_DIM, :] = gwb_ref[j, r].astype(ref.dtype)
                ref[start + kv_b : start + kv_rows, :] = gwa_ref[j].astype(ref.dtype)

            put(own_out_ref, 0, 3)
            put(beside_ref, 0, 2)
            put(third_ref, 0, 0)
            put(second_ref, 0, 1)

        def last_kernel(
            meta_ref,
            x_ref,
            own_ref,
            second_ref,
            beside_ref,
            third_ref,
            gbq_ref,
            ga0_ref,
            ga1_ref,
            cos_ref,
            sin_ref,
            wb_ref,
            wa_ref,
            normed_ref,
            gain_ref,
            dmid_ref,
            gg_ref,
            delta_ref,
            keep0_ref,
            keep1_ref,
            send0_ref,
            send1_ref,
            b_buf,
            a_buf,
            d_buf,
            g_buf,
        ):
            total = own_ref[...]
            for ref in (second_ref, beside_ref, third_ref):
                total = total + ref[...].astype(F32)
            cosine, sine = cos_ref[...], -sin_ref[...]
            rows = [rotated(gbq_ref[r], cosine, sine) for r in range(RANK_Q)]
            for r in range(KV):
                part = total[r * HEAD_DIM : (r + 1) * HEAD_DIM]
                rows.append(rotated(part, cosine, sine) if r < RANK_KV else part)
            grad_b = jnp.transpose(jnp.concatenate(rows, axis=0)).astype(BF16)
            normed = normed_ref[...]
            back = dot(grad_b, wb_ref[...], ((1,), (1,)))
            for tp in range(n_tp):
                parts = []
                for g in range(group):
                    start = kv_b + (tp * group + g) * KV
                    parts.append(jnp.zeros((RANK_Q, block), F32))
                    parts.append(total[start : start + KV])
                parts.append(jnp.zeros((a_pad - a_cols, block), F32))
                half = group // 2
                at = [tp * half + k for k in range(half)]
                own_a = [
                    (ga0_ref, ga1_ref)[k * 2 // pairs][k % (pairs // 2), : 2 * RANKS, :] for k in at
                ]
                own_a.append(jnp.zeros((a_pad - a_cols, block), F32))
                own_a = jnp.concatenate(own_a, axis=0)
                grad_a = (own_a + jnp.concatenate(parts, axis=0)).astype(BF16)
                back = back + dot(grad_a, wa_ref[tp], ((0,), (0,)))
                a_buf[tp] = dot(grad_a, normed, ((1,), (0,)))
            b_buf[...] = dot(normed, grad_b, ((0,), (0,)))
            x = x_ref[...]
            inverse = inverse_rms(x)
            normal = x * inverse
            gains = jnp.sum(back * normal, axis=0, keepdims=True)
            g_buf[...] = jnp.broadcast_to(gains, (8, width))
            scaled = back * gain_ref[0:1]
            delta = inverse * (
                scaled - normal * jnp.mean(scaled * normal, axis=-1, keepdims=True)
            )
            d_buf[...] = delta
            for j in range(n_piece):
                lanes = column(meta_ref, j)
                cut = slice(j * LANES, (j + 1) * LANES)
                delta_ref[:, lanes] = (d_buf[:, lanes] + dmid_ref[:, cut]).astype(BF16)
            row_index = lax.broadcasted_iota(jnp.int32, (16, LANES), 0)
            for lo, hi in ((0, 0), (0, 1), (1, 0), (1, 1)):
                outs = ((keep0_ref, keep1_ref), (send0_ref, send1_ref))[lo]
                tp = member(meta_ref, lo, hi)
                for near in range(n_c):
                    out = outs[near]
                    for s in range(n_f):
                        j = near * n_f + s
                        lanes = column(meta_ref, j)
                        row = pl.multiple_of((meta_ref[j] * n_tp + tp) * b_rows, b_rows)
                        for k in range(b_parts):
                            out[hi, s, k * b_rows : (k + 1) * b_rows, :] = b_buf[
                                pl.ds(row, b_rows), k * LANES : (k + 1) * LANES
                            ].astype(BF16)
                        out[hi, s, n_b : n_b + a_pad, :] = a_buf[tp, :, lanes].astype(BF16)
                        pair = jnp.where(
                            row_index == 0, g_buf[0:1, lanes], gg_ref[0:1, lanes]
                        )
                        out[hi, s, n_b + a_pad :, :] = pair.astype(BF16)

        def add_kernel(arrival, meta_ref, x_ref, d0_ref, d1_ref, d2_ref, d3_ref, out_ref):
            step = pl.program_id(0) // 2
            rows = pl.ds(pl.multiple_of((pl.program_id(0) % 2) * (block // 2), 8), block // 2)
            for i, ref in enumerate((d0_ref, d1_ref, d2_ref, d3_ref)):

                @pl.when(step == i)
                def _(ref=ref):
                    if not arrival:
                        out_ref[0] = x_ref[0] + ref[rows, :].astype(F32)
                        return
                    for j in range(n_piece):
                        lanes = column(meta_ref, j)
                        out_ref[0, :, lanes] = x_ref[0, :, lanes] + ref[
                            rows, j * LANES : (j + 1) * LANES
                        ].astype(F32)

        def split_kernel(meta_ref, keep_ref, got_ref, own_ref, send_ref):
            def total(s):
                lanes = slice(s * LANES, (s + 1) * LANES)
                return keep_ref[:, lanes].astype(F32) + got_ref[: keep_ref.shape[0], lanes].astype(
                    F32
                )

            own_ref[0] = total(0)
            own_ref[1] = total(2)

            @pl.when(lax.rem(meta_ref[AT_ME + 1], 2) == 0)
            def _():
                send_ref[0] = total(3).astype(BF16)
                send_ref[1] = total(1).astype(BF16)

            @pl.when(lax.rem(meta_ref[AT_ME + 1], 2) == 1)
            def _():
                send_ref[0] = total(1).astype(BF16)
                send_ref[1] = total(3).astype(BF16)

        def unpack_kernel(
            meta_ref, p_ref, got_ref, b_ref, a_ref, g0_ref, g1_ref, o_ref
        ):
            total = p_ref[...].astype(F32) + got_ref[...].astype(F32)
            for k in range(b_parts):
                b_ref[0, :, k * LANES : (k + 1) * LANES] = total[k * b_rows : (k + 1) * b_rows]
            a_ref[0] = total[n_b : n_b + a_cols]
            rows = total[n_b + a_pad : n_b + a_pad + 8]
            rows = pltpu.roll(rows, (n_tp - meta_ref[AT_ME]) * gain_part, 1)
            g0_ref[...] = rows[0:1, :gain_part]
            g1_ref[...] = rows[1:2, :gain_part]
            o_ref[0] = total[pack_rows:]

        core = lambda v, label="row": swap(v, "tp", n_tp, 1, "core_" + label)
        chip = lambda v, label="row": swap(v, "tp", n_tp, 2, "y_" + label)
        ctx = lambda v, label="row": swap(v, "ctx", n_c, 1, "x_" + label)
        ahead = lambda v, s, label="row": shift(v, "fsdp", n_f, s, "z_" + label)

        (pack,) = call(
            pack_kernel,
            "pack",
            [((pack_rows, LANES), BF16)],
            (w_factor_b, w_factor_a.transpose(0, 2, 1), attn_gains, ffn_gains),
        )
        o_rows_all = w_out[0].astype(BF16)
        pack = jnp.stack([pack] + [ahead(pack, s, "pack") for s in range(1, n_f)])
        o_parts = [o_rows_all] + [ahead(o_rows_all, s, "wo") for s in range(1, n_f)]
        o_parts = jnp.concatenate(o_parts, axis=0)
        gu_in = after(w_gate_up.transpose(0, 1, 3, 2), pack)
        own_gu, own_dn = call(
            big_kernel,
            "big_pack",
            [((early, LANES), BF16), ((3 * hidden - early, LANES), BF16)],
            (gu_in, w_down),
        )
        pack = jnp.stack([pack, ctx(pack, "pack")])
        far_gu = swap(own_gu, "fsdp", n_f, 2, "z_gate_up")
        dn_pair = jnp.stack([own_dn, ctx(own_dn, "down")])
        gu_across = ctx(own_gu, "gate_up")
        o_across = ctx(o_parts, "wo")
        o_parts = jnp.concatenate(
            [
                half[s * o_rows : (s + 1) * o_rows]
                for half in (o_parts, o_across)
                for s in range(n_f)
            ],
            axis=1,
        )
        own_x, own_cot, near_cot, far_cot = call(
            rows_kernel,
            "rows",
            [((block, width), F32)] * 2 + [((2 * block, width), BF16)] * 2,
            (resid_in, cotangent),
            [REMOTE] * 2,
            [pltpu.VMEM((4, block, width), F32), pltpu.SemaphoreType.DMA((5,))],
            scalars=after(meta, o_across),
        )
        pack_across, far_gu, dn_pair, o_parts, near_cot, far_cot = lax.optimization_barrier(
            (chip(pack, "pack"), far_gu, dn_pair, o_parts, near_cot, far_cot)
        )
        pair_gu = swap(jnp.stack([own_gu, far_gu]), "fsdp", n_f, 1, "z_gate_up_pair")
        pack = jnp.stack([pack, pack_across], axis=1)
        other_pack = core(pack, "pack")

        def add_rows(whole, parts, arrival):
            rows = pl.BlockSpec(
                (1, block // 2, width), lambda i, m: (0, 2 * m[AT_TP + i // 2] + i % 2, 0)
            )
            (out,) = call(
                lambda *refs: add_kernel(arrival, *refs),
                "add_rows",
                [(whole.shape, F32)],
                (whole, *parts),
                [rows] + [WHOLE] * 4,
                (),
                (2 * n_tp,),
                [rows],
            )
            return out

        def split(keep, got):
            size = keep.shape[0]
            return call(
                split_kernel,
                "split",
                [((2, size, LANES), F32), ((2, size, LANES), BF16)],
                (keep, got),
            )

        def first_step(send, label):
            return swap(send, "fsdp", n_f, 1, "z1_" + label)

        def second_step(own, got, label):
            total = own + got.astype(F32)
            return total[0], swap(total[1].astype(BF16), "fsdp", n_f, 2, "z2_" + label)

        seg_here = lax.dynamic_slice_in_dim(segment_ids[0], place * block, block, 0)
        first = jnp.sum((segment_ids[0][:, None] < seg_here[None, :]).astype(jnp.int32), axis=0)
        token = place * block + jnp.arange(block, dtype=jnp.int32)
        position = (token - first).astype(F32)
        first = (first - place * block + extra * block).reshape(1, block)
        frequency = 10000.0 ** (-2.0 * jnp.arange(HEAD_DIM // 2, dtype=F32) / HEAD_DIM)
        angles = frequency[:, None] * position[None, :]
        cosine, sine = jnp.cos(angles), jnp.sin(angles)

        weight_b, weight_a, gains, normed, a_rows, b_query, payload = call(
            factor_kernel,
            "factors",
            [
                ((width, b_cols), BF16),
                ((n_tp, a_pad, width), BF16),
                ((16, width), F32),
                ((block, width), BF16),
                ((n_tp, a_pad, block), F32),
                ((RANK_Q, HEAD_DIM, block), F32),
                ((kv_rows, block), BF16),
            ],
            (own_x, pack, other_pack, cosine, sine),
        )
        def places(value, step, chosen, label):
            pairs = [(i, i + step) for i in chosen if 0 <= i + step < n_place]
            with jax.named_scope(label):
                return lax.ppermute(value, ("ctx", "tp"), pairs)

        every, odd, even = range(n_place), range(1, n_place, 2), range(0, n_place, 2)
        second = places(payload, 2, every, "x_kv_second")
        third = places(payload, 3, odd, "x_kv_third")
        beside_kv = core(payload, "kv")
        o_own = jnp.concatenate([o_parts, chip(o_parts, "wo")], axis=0)
        second, pair_gu, gu_across = lax.optimization_barrier((second, pair_gu, gu_across))
        gu_rest = ctx(jnp.concatenate([far_gu[None], pair_gu], axis=0), "gate_up_rest")
        dn_parts = [dn_pair, ahead(dn_pair, 1, "down1")]
        beside_second = core(second, "kv_second")
        tied = lax.optimization_barrier((third, second, beside_second, beside_kv, o_own))
        wins = (*tied[:4], payload)
        o_own = tied[4]
        o_other = core(o_own, "wo")
        window = windows * block
        factor_scratch = [
            pltpu.VMEM((pairs, pair_rows, block), F32),
            pltpu.VMEM((windows, heads * KV, block), F32),
        ]
        lse, query, mixed = call(
            attention_kernel,
            "attention",
            [
                ((pairs, 2, block), F32),
                ((n_tp, group, HEAD_DIM, block), BF16),
                ((n_tp, feats, block), BF16),
            ],
            (first, a_rows, b_query, *wins),
            None,
            [
                pltpu.VMEM((windows, kv_rows, block), BF16),
                pltpu.VMEM((window, block), F32),
                pltpu.VMEM((windows, KV, HEAD_DIM, block), F32),
                pltpu.VMEM((2, window, block), F32),
                *factor_scratch,
            ],
        )
        dn_parts[1] = after(dn_parts[1], mixed)
        for s in range(2, n_f):
            dn_parts.append(ahead(dn_parts[-1], 1, "down" + str(s)))
        mid, attn_out, normed_ffn = call(
            project_kernel,
            "project",
            [((block, width), F32), ((block, width), F32), ((block, width), BF16)],
            (own_x, mixed, o_own, o_other, gains),
        )

        near_rows = (normed_ffn, core(normed_ffn, "nf"))
        far_own = chip(normed_ffn, "nf")

        far_own, gu_rest = lax.optimization_barrier((far_own, gu_rest))
        far_own, dn_parts[-1], gu_rest = lax.optimization_barrier(
            (far_own, dn_parts[-1], gu_rest)
        )
        pieces = (own_gu, far_gu, pair_gu, gu_across, gu_rest, *dn_parts)
        far_rows = (far_own, core(far_own, "nf_far"))
        whole_ht = ((3 * hidden, 2 * block), BF16)
        two_sums = [((block, width), F32), ((block, width), BF16)]
        far_ht, far_back, far_back1, weights = call(
            far_kernel,
            "feed_far",
            [whole_ht, *two_sums, ((3 * hidden, width), BF16)],
            (*far_rows, far_cot, *pieces),
            [WHOLE] * 3 + [REMOTE] * len(pieces),
            [pltpu.SemaphoreType.DMA((2 * n_piece,))],
            room=12,
        )
        across = (far_back + core(far_back1, "dn_far").astype(F32)).astype(BF16)
        near_ht, near_back, near_back1, near_out, near_out1, far_out, far_out1 = call(
            near_kernel,
            "feed_near",
            [whole_ht, *two_sums * 3],
            (after(near_rows[0], across), near_rows[1], near_cot, weights, far_ht),
            room=12,
        )
        across = chip(across, "dn")
        beside = core(near_back1, "dn_near")

        grad_args = (near_ht, far_ht, *near_rows, *far_rows, near_cot, far_cot)
        own_d, send_d = call(
            down_grad_kernel,
            "down_grad",
            [((2, n_c, hidden, LANES), F32), ((2, n_c, hidden, LANES), BF16)],
            grad_args,
            room=12,
        )
        got_d = first_step(send_d, "d")
        keep_a, send_a = call(
            gate_up_grad_kernel,
            "gate_up_grad",
            [((2 * hidden, half_width), BF16)] * 2,
            (after(grad_args[0], send_d), *grad_args[1:]),
            room=12,
        )
        got_a = ctx(send_a, "grads_a")
        across = after(across, send_a)

        delta_mid, gain_grad, grad_mixed, keep_o, send_o = call(
            middle_kernel,
            "middle",
            [
                ((block, width), F32),
                ((8, width), F32),
                ((n_tp, feats, block), BF16),
                ((2 * o_rows, width), BF16),
                ((2 * o_rows, width), BF16),
            ],
            (own_cot, near_back, beside, across, mid, gains, o_own, o_other, mixed),
        )
        near_sum = attn_out + near_out + core(after(near_out1, across), "out_near").astype(F32)
        far_sum = far_out + core(after(far_out1, across), "out_far").astype(F32)
        out_send = jnp.stack([far_sum, near_sum]).astype(BF16)
        grad_mixed = after(grad_mixed, out_send)
        rows_got = core(send_o, "go")
        out_got = chip(out_send, "out")
        back_args = (first, a_rows, b_query, *wins, lse, query, grad_mixed)
        sums = [
            ((RANK_Q, HEAD_DIM, block), F32),
            ((windows, KV, HEAD_DIM, block), F32),
            ((windows, heads * KV, block), F32),
        ]
        grad_a_out = ((pairs // 2, pair_rows, block), F32)
        back_scratch = [
            pltpu.VMEM((windows, kv_rows, block), BF16),
            pltpu.VMEM((window, block), F32),
            pltpu.VMEM((windows, KV, HEAD_DIM, block), F32),
            pltpu.VMEM((2, window, block), F32),
            pltpu.VMEM((2, window, block), F32),
            *factor_scratch,
        ]
        grad_a0, *sums_out = call(
            lambda *refs: attention_back_kernel(0, *refs),
            "attention_back_a",
            [grad_a_out] + sums,
            back_args,
            None,
            back_scratch,
        )
        sums_out[0], own_d, got_d, _ = lax.optimization_barrier(
            (sums_out[0], own_d, got_d, grad_a0)
        )
        own_d, got_d = second_step(own_d, got_d, "d")
        grad_a1, grad_bq, *sends = call(
            lambda *refs: attention_back_kernel(1, *refs),
            "attention_back_b",
            [
                grad_a_out,
                sums[0],
                ((kv_rows, block), BF16),
                ((kv_rows, block), BF16),
                ((kv_rows, block), BF16),
                ((kv_rows, block), F32),
            ],
            (*back_args, *sums_out),
            None,
            [pltpu.VMEM(shape, kind) for shape, kind in sums[1:]] + back_scratch,
        )
        *sends[:3], out_got, rows_got = lax.optimization_barrier((*sends[:3], out_got, rows_got))
        second_got = places(sends[0], -2, every, "x_kv_back_second")
        beside_got = places(sends[1], -1, every, "x_kv_back_beside")
        third_got = places(sends[2], -3, every, "x_kv_back_third")
        own_a, send_a = split(after(keep_a, sends[0]), got_a)
        got_a = first_step(send_a, "a")
        rows_o = keep_o.astype(F32) + after(rows_got, send_a).astype(F32)
        rows_keep, rows_send = rows_o[:o_rows], rows_o[o_rows:].astype(BF16)
        rows_got = chip(rows_send, "go")
        *got, got_d = lax.optimization_barrier((second_got, beside_got, third_got, got_d))
        out_rows = (out_send[::-1].astype(F32) + out_got.astype(F32)).astype(BF16)

        delta, keep0, keep1, send0, send1 = call(
            last_kernel,
            "last",
            [
                ((block, width), BF16),
                *[((2, n_f, pack_rows, LANES), BF16)] * 4,
            ],
            (
                own_x,
                sends[3],
                *got,
                grad_bq,
                grad_a0,
                grad_a1,
                cosine,
                sine,
                weight_b,
                weight_a,
                normed,
                gains,
                delta_mid,
                gain_grad,
            ),
            [WHOLE] * 16,
            [
                pltpu.VMEM((width, b_cols), F32),
                pltpu.VMEM((n_tp, a_pad, width), F32),
                pltpu.VMEM((block, width), F32),
                pltpu.VMEM((8, width), F32),
            ],
        )

        part_send = (keep1.astype(F32) + core(send1, "gp").astype(F32)).astype(BF16)
        total_d = own_d + got_d.astype(F32)
        part_send, got_a = lax.optimization_barrier((part_send, got_a))
        part_got = ctx(part_send, "gp")
        own_a, got_a = second_step(own_a, got_a, "a")
        part = keep0.astype(F32) + core(after(send0, part_send), "gp_near").astype(F32)
        rows_got, part = lax.optimization_barrier((rows_got, part))
        rows_o = rows_keep + rows_got.astype(F32)
        rows_keep, rows_send = rows_o[:, :half_width], rows_o[:, half_width:].astype(BF16)
        across_delta = chip(delta, "delta")
        rows_go = ctx(rows_send, "go")
        out_rows = after(out_rows, part_send)
        out_beside = core(out_rows, "out_rows")
        block_out = add_rows(
            resid_in, (out_rows[0], out_rows[1], out_beside[0], out_beside[1]), True
        )
        part_got, across_delta = lax.optimization_barrier((part_got, across_delta, block_out))[:2]
        part = part + part_got.astype(F32)
        part_send = part[1].astype(BF16)
        part_got = chip(part_send, "gp")
        across_delta = after(across_delta, part_send)
        beside_delta = core(after(delta, part_send), "delta")
        got_last = ctx(after(total_d[1], part_send).astype(BF16), "d")
        part_got, rows_go, got_a = lax.optimization_barrier((part_got, rows_go, got_a))
        part = part[0] + part_got.astype(F32)
        rows_o = rows_keep + rows_go.astype(F32)
        part = [
            jnp.concatenate([part[s], rows_o[:, s * LANES : (s + 1) * LANES]], axis=0)
            for s in range(n_f)
        ]
        is_even_f = f_index % 2 == 0
        part_send = [
            jnp.where(is_even_f, part[3], part[1]),
            jnp.where(is_even_f, part[1], part[3]),
        ]
        part_send = jnp.stack(part_send).astype(BF16)
        part_own, part_got = second_step(
            jnp.stack([part[0], part[2]]), first_step(part_send, "gp"), "gp"
        )
        across_delta = after(across_delta, part_send)
        resid_grad = add_rows(
            cotangent,
            (delta, across_delta, beside_delta, core(across_delta, "delta_far")),
            False,
        )
        part_got, got_last = lax.optimization_barrier((part_got, got_last, resid_grad))[:2]
        grad_down = total_d[0] + got_last.astype(F32)
        grad_gate_up = (own_a + got_a.astype(F32)).reshape(1, 2, hidden, fc_cols)
        part_b, part_a, part_g0, part_g1, grad_out = call(
            unpack_kernel,
            "unpack",
            [
                ((1, b_rows, b_cols), F32),
                ((1, a_cols, fc_cols), F32),
                ((1, gain_part), F32),
                ((1, gain_part), F32),
                ((1, o_rows, LANES), F32),
            ],
            (part_own, part_got),
        )
        return (
            block_out,
            resid_grad,
            part_a.transpose(0, 2, 1),
            part_b,
            grad_out,
            grad_gate_up.transpose(0, 1, 3, 2),
            grad_down[None],
            part_g0,
            part_g1,
        )

    return shards


def make_shards(mesh):
    fused, general = make_fused(mesh), make_general(mesh)
    fits = mesh.shape["fsdp"] == 4 and mesh.shape["ctx"] == 2 and mesh.shape["tp"] == 4

    def shards(*args):
        return (fused if fits and args[7].shape[2] == LANES else general)(*args)

    return shards


def solution(mesh):
    return jax.shard_map(
        make_shards(mesh),
        mesh=mesh,
        in_specs=(
            P("fsdp", "ctx", None),
            P("fsdp", None),
            P("fsdp", "ctx", None),
            P(None, ("fsdp", "ctx"), "tp"),
            P(None, ("fsdp", "ctx", "tp"), None),
            P(None, "tp", ("fsdp", "ctx")),
            P(None, None, ("fsdp", "ctx"), "tp"),
            P(None, "tp", ("fsdp", "ctx")),
            P(None, ("fsdp", "ctx", "tp")),
            P(None, ("fsdp", "ctx", "tp")),
        ),
        out_specs=(
            P("fsdp", "ctx", None),
            P("fsdp", "ctx", None),
            P(None, ("fsdp", "ctx"), "tp"),
            P(None, ("fsdp", "ctx", "tp"), None),
            P(None, "tp", ("fsdp", "ctx")),
            P(None, None, ("fsdp", "ctx"), "tp"),
            P(None, "tp", ("fsdp", "ctx")),
            P(None, ("fsdp", "ctx", "tp")),
            P(None, ("fsdp", "ctx", "tp")),
        ),
        check_vma=False,
    )
```

```python
import math

import jax
import jax.numpy as jnp
from jax import lax
from jax.experimental import pallas as pl
from jax.experimental.pallas import tpu as pltpu
from jax.sharding import PartitionSpec as P

HEAD_DIM = 64
RANK_Q = 6
RANK_KV = 2
RANKS = 10
KV = 2 * RANK_KV
MOST_DOC = 768
EPSILON = 1e-05
LANES = 128
BF16 = jnp.bfloat16
F32 = jnp.float32
MASKED = -1e30


def inverse_rms(values):
    return lax.rsqrt(jnp.mean(values * values, axis=-1, keepdims=True) + EPSILON)


def norm_back(grad_value, values, inverse, gain):
    scaled = grad_value * gain
    normal = values * inverse
    return inverse * (scaled - normal * jnp.mean(scaled * normal, axis=-1, keepdims=True))


def dot(left, right, dims):
    return lax.dot_general(left, right, (dims, ((), ())), preferred_element_type=F32)


def shift(value, axes, size, step, label="shift"):
    with jax.named_scope(label):
        return lax.ppermute(value, axes, [(i, (i + step) % size) for i in range(size)])


def swap(value, axis, size, bit, label="swap"):
    with jax.named_scope(label):
        return lax.ppermute(value, axis, [(i, i ^ bit) for i in range(size)])


def gather_direct(value, axis, size):
    me = lax.axis_index(axis)
    parts = [(me, value)]
    for step in range(1, size):
        parts.append(((me - step) % size, shift(value, axis, size, step)))
    out = jnp.zeros((size,) + value.shape, value.dtype)
    for place, part in parts:
        out = lax.dynamic_update_slice(out, part[None], (place,) + (0,) * value.ndim)
    return out


def gather_pair(value, axis, size, bit):
    mine = (lax.axis_index(axis) // bit) % 2 == 0
    other = swap(value, axis, size, bit)
    return jnp.stack([jnp.where(mine, value, other), jnp.where(mine, other, value)])


def after(value, *others):
    return lax.optimization_barrier((value,) + others)[0]


def take(value, index):
    return lax.dynamic_index_in_dim(value, index, 0, keepdims=False)


def scatter_direct(value, axis, size):
    me = lax.axis_index(axis)
    got = [
        shift(take(value, (me + step) % size), axis, size, step) for step in range(1, size)
    ]
    total = take(value, me).astype(F32)
    for part in got:
        total = total + part.astype(F32)
    return total


def scatter_pair(value, axis, size, bit):
    mine = (lax.axis_index(axis) // bit) % 2
    got = swap(take(value, 1 - mine).astype(BF16), axis, size, bit)
    return take(value, mine).astype(F32) + got.astype(F32)


def attention_mask(first_ref, window, block):
    start = first_ref[...]
    place = lax.broadcasted_iota(jnp.int32, (window, block), 0)
    query_place = lax.broadcasted_iota(jnp.int32, (window, block), 1) + (window - block)
    return jnp.where((place >= start) & (place <= query_place), 0.0, MASKED)


def head_rows(wa_ref, wide_ref, head):
    factors = wa_ref[head].astype(F32)
    key_rows = (factors[0:1] * wide_ref[0] + factors[1:2] * wide_ref[1]) * (1.0 / RANK_KV)
    value_rows = (factors[2:3] * wide_ref[2] + factors[3:4] * wide_ref[3]) * (1.0 / RANK_KV)
    return factors, key_rows.astype(BF16), value_rows.astype(BF16)


def forward_kernel(
    first_ref, a_ref, bq_ref, wa_ref, wb_ref, mixed_ref, lse_ref, q_ref, bias_ref, wide_ref, s_ref
):
    heads = a_ref.shape[0]
    window, block = bias_ref.shape
    bias_ref[...] = attention_mask(first_ref, window, block)
    wide_ref[...] = wb_ref[...].astype(F32)
    spans = [pl.ds(j * block, block) for j in range(window // block)]

    def one_head(head, carry):
        factors = a_ref[head]
        query = factors[0:1] * bq_ref[0]
        for r in range(1, RANK_Q):
            query = query + factors[r : r + 1] * bq_ref[r]
        query = (query * (1.0 / RANK_Q)).astype(BF16) * jnp.asarray(HEAD_DIM**-0.5, BF16)
        q_ref[head] = query
        _, key_rows, value_rows = head_rows(wa_ref, wide_ref, head)
        top = jnp.full((1, block), MASKED, F32)
        for j, span in enumerate(spans):
            keys = key_rows[:, j * block : (j + 1) * block]
            scores = dot(keys, query, ((0,), (0,))) + bias_ref[span, :]
            s_ref[span, :] = scores
            top = jnp.maximum(top, jnp.max(scores, axis=0, keepdims=True))
        total = jnp.zeros((1, block), F32)
        for span in spans:
            weight = jnp.exp(s_ref[span, :] - top)
            s_ref[span, :] = weight
            total = total + jnp.sum(weight, axis=0, keepdims=True)
        lse_ref[head] = top + jnp.log(total)
        scale = 1.0 / total
        mixed = jnp.zeros((HEAD_DIM, block), F32)
        for j, span in enumerate(spans):
            probs = (s_ref[span, :] * scale).astype(BF16)
            mixed = mixed + dot(
                value_rows[:, j * block : (j + 1) * block], probs, ((1,), (0,))
            )
        mixed_ref[head] = mixed.astype(BF16)
        return carry

    lax.fori_loop(0, heads, one_head, 0)


def backward_kernel(
    first_ref,
    a_ref,
    bq_ref,
    wa_ref,
    wb_ref,
    lse_ref,
    q_ref,
    go_ref,
    ga_ref,
    gbq_ref,
    gwa_ref,
    gwb_ref,
    bias_ref,
    wide_ref,
    p_ref,
    dp_ref,
):
    heads = a_ref.shape[0]
    window, block = bias_ref.shape
    bias_ref[...] = attention_mask(first_ref, window, block)
    wide_ref[...] = wb_ref[...].astype(F32)
    gbq_ref[...] = jnp.zeros_like(gbq_ref)
    gwb_ref[...] = jnp.zeros_like(gwb_ref)
    count = window // block
    spans = [pl.ds(j * block, block) for j in range(count)]

    def one_head(head, carry):
        factors, key_rows, value_rows = head_rows(wa_ref, wide_ref, head)
        query = q_ref[head]
        grad_out = go_ref[head]
        lse = lse_ref[head]
        inner = jnp.zeros((1, block), F32)
        for j, span in enumerate(spans):
            cut = slice(j * block, (j + 1) * block)
            scores = dot(key_rows[:, cut], query, ((0,), (0,))) + bias_ref[span, :]
            probs = jnp.exp(scores - lse)
            grad_probs = dot(value_rows[:, cut], grad_out, ((0,), (0,)))
            p_ref[span, :] = probs
            dp_ref[span, :] = grad_probs
            inner = inner + jnp.sum(probs * grad_probs, axis=0, keepdims=True)
        grad_query = jnp.zeros((HEAD_DIM, block), F32)
        for j, span in enumerate(spans):
            cut = slice(j * block, (j + 1) * block)
            probs = p_ref[span, :]
            grad_scores = (probs * (dp_ref[span, :] - inner)).astype(BF16)
            grad_query = grad_query + dot(key_rows[:, cut], grad_scores, ((1,), (0,)))
            grad_keys = dot(query, grad_scores, ((1,), (1,))) * (1.0 / RANK_KV)
            grad_values = dot(grad_out, probs.astype(BF16), ((1,), (1,))) * (1.0 / RANK_KV)
            rows = []
            for r in range(KV):
                grad = grad_keys if r < RANK_KV else grad_values
                rows.append(jnp.sum(grad * wide_ref[r, :, span], axis=0, keepdims=True))
                gwb_ref[r, :, span] += factors[r : r + 1, cut] * grad
            gwa_ref[head, :, span] = jnp.concatenate(rows, axis=0)
        grad_query = grad_query * (HEAD_DIM**-0.5 / RANK_Q)
        own = a_ref[head]
        rows = []
        for r in range(RANK_Q):
            rows.append(jnp.sum(grad_query * bq_ref[r], axis=0, keepdims=True))
            gbq_ref[r] += own[r : r + 1] * grad_query
        ga_ref[head] = jnp.concatenate(rows, axis=0)
        return carry

    lax.fori_loop(0, heads, one_head, 0)


VMEM_LIMIT = 56 * 1024 * 1024


def whole_specs(count):
    return [pl.BlockSpec(memory_space=pltpu.VMEM)] * count


def attend_forward(first, a_rows, b_query, win_a, win_b):
    heads, _, block = a_rows.shape
    window = win_a.shape[-1]
    return pl.pallas_call(
        forward_kernel,
        out_shape=(
            jax.ShapeDtypeStruct((heads, HEAD_DIM, block), BF16),
            jax.ShapeDtypeStruct((heads, 1, block), F32),
            jax.ShapeDtypeStruct((heads, HEAD_DIM, block), BF16),
        ),
        in_specs=whole_specs(5),
        out_specs=tuple(whole_specs(3)),
        scratch_shapes=[
            pltpu.VMEM((window, block), F32),
            pltpu.VMEM((KV, HEAD_DIM, window), F32),
            pltpu.VMEM((window, block), F32),
        ],
        compiler_params=pltpu.CompilerParams(vmem_limit_bytes=VMEM_LIMIT),
        name="attend_forward",
    )(first, a_rows, b_query, win_a, win_b)


def attend_backward(first, a_rows, b_query, win_a, win_b, lse, query, grad_mixed):
    heads, _, block = a_rows.shape
    window = win_a.shape[-1]
    return pl.pallas_call(
        backward_kernel,
        out_shape=(
            jax.ShapeDtypeStruct((heads, RANK_Q, block), F32),
            jax.ShapeDtypeStruct((RANK_Q, HEAD_DIM, block), F32),
            jax.ShapeDtypeStruct((heads, KV, window), F32),
            jax.ShapeDtypeStruct((KV, HEAD_DIM, window), F32),
        ),
        in_specs=whole_specs(8),
        out_specs=tuple(whole_specs(4)),
        scratch_shapes=[
            pltpu.VMEM((window, block), F32),
            pltpu.VMEM((KV, HEAD_DIM, window), F32),
            pltpu.VMEM((window, block), F32),
            pltpu.VMEM((window, block), F32),
        ],
        compiler_params=pltpu.CompilerParams(vmem_limit_bytes=VMEM_LIMIT),
        name="attend_backward",
    )(first, a_rows, b_query, win_a, win_b, lse, query, grad_mixed)


def rotate(rows, cosine, sine):
    half = HEAD_DIM // 2
    lower, upper = rows[:, :half], rows[:, half:]
    return jnp.concatenate(
        [lower * cosine - upper * sine, lower * sine + upper * cosine], axis=1
    )


def make_general(mesh):
    n_f, n_c, n_tp = mesh.shape["fsdp"], mesh.shape["ctx"], mesh.shape["tp"]
    n_hi, n_lo = 2, n_tp // 2

    def shards(
        resid_in,
        segment_ids,
        cotangent,
        w_factor_a,
        w_factor_b,
        w_out,
        w_gate_up,
        w_down,
        attn_gains,
        ffn_gains,
    ):
        seq_count, local_len, width = resid_in.shape
        assert seq_count == 1 and w_factor_a.shape[0] == 1 and n_lo == 2
        full_len = segment_ids.shape[1]
        block = local_len // n_tp
        extra = -(-(MOST_DOC - 1) // block)
        window = (extra + 1) * block
        a_cols = w_factor_a.shape[2]
        heads = n_tp * a_cols // RANKS
        b_cols = w_factor_b.shape[2]
        b_rows = w_factor_b.shape[1]
        b_parts = b_cols // LANES
        fc_cols = w_down.shape[2]
        hidden = w_down.shape[1]
        o_rows = w_out.shape[1]

        f_index, c_index, t_index = (
            lax.axis_index("fsdp"),
            lax.axis_index("ctx"),
            lax.axis_index("tp"),
        )
        hi, lo = t_index // 2, t_index % 2
        place = c_index * n_tp + t_index
        n_place = n_c * n_tp

        gains = jnp.concatenate([attn_gains, ffn_gains], axis=1).astype(BF16)
        gain_count = gains.shape[1]
        gain_rows = 16 * (-(-gain_count // (16 * LANES)))
        gains = jnp.pad(gains.reshape(-1), (0, gain_rows * LANES - gain_count))
        b_shard = w_factor_b[0].astype(BF16).reshape(b_rows, b_parts, LANES)
        a_shard = w_factor_a[0].astype(BF16).T
        pack = jnp.concatenate(
            [
                b_shard.transpose(1, 0, 2).reshape(-1, LANES),
                a_shard.reshape(-1, LANES),
                gains.reshape(-1, LANES),
            ],
            axis=0,
        )
        n_b = b_parts * b_rows
        n_a = a_cols * fc_cols // LANES
        pack = gather_direct(pack, "fsdp", n_f)
        after_pack = pack
        pack = gather_pair(pack, "ctx", n_c, 1)
        pack = gather_pair(pack, "tp", n_tp, 2)
        pack = gather_pair(pack, "tp", n_tp, 1)
        pack = pack.transpose(3, 2, 1, 0, 4, 5)
        weight_b = pack[:, :, :, :, :n_b].reshape(-1, b_parts, b_rows, LANES)
        weight_b = weight_b.transpose(0, 2, 1, 3).reshape(width, b_cols)
        weight_a = pack[:, :, :, :, n_b : n_b + n_a].reshape(n_f, n_c, n_tp, a_cols, fc_cols)
        weight_a = weight_a.transpose(2, 3, 0, 1, 4).reshape(n_tp * a_cols, width)
        gains_all = pack[:, :, :, :, n_b + n_a :].reshape(-1, gain_rows * LANES)[:, :gain_count]
        gains_all = gains_all.reshape(-1, 2, gain_count // 2).transpose(1, 0, 2)
        gains_all = gains_all.reshape(2, width).astype(F32)
        gain_attn, gain_ffn = gains_all[0:1], gains_all[1:2]

        big = jnp.concatenate(
            [
                w_gate_up[0, 0].astype(BF16).T,
                w_gate_up[0, 1].astype(BF16).T,
                w_down[0].astype(BF16),
                w_out[0].astype(BF16),
            ],
            axis=0,
        )
        big, _ = lax.optimization_barrier((big, after_pack))
        big = gather_direct(big, "fsdp", n_f)
        big = gather_pair(big, "ctx", n_c, 1)
        big = big.transpose(2, 1, 0, 3).reshape(-1, width)
        weight_g = big[:hidden]
        weight_u = big[hidden : 2 * hidden]
        weight_d = big[2 * hidden : 3 * hidden]
        weight_o = gather_pair(big[3 * hidden :], "tp", n_tp, 2)
        weight_o = gather_pair(weight_o, "tp", n_tp, 1)
        weight_o = weight_o.transpose(1, 0, 2, 3).reshape(n_tp * o_rows, width)

        seg_here = lax.dynamic_slice_in_dim(segment_ids[0], place * block, block, 0)
        first = jnp.sum((segment_ids[0][:, None] < seg_here[None, :]).astype(jnp.int32), axis=0)
        token = place * block + jnp.arange(block, dtype=jnp.int32)
        position = (token - first).astype(F32)
        first = (first - place * block + extra * block).reshape(1, block)
        frequency = 10000.0 ** (
            -2.0 * jnp.arange(HEAD_DIM // 2, dtype=F32) / HEAD_DIM
        )
        angles = frequency[:, None] * position[None, :]
        cosine, sine = jnp.cos(angles)[None], jnp.sin(angles)[None]

        stream = resid_in[0].reshape(n_tp, block, width)
        own = take(stream, t_index)
        inverse_attn = inverse_rms(own)
        normed = (own * inverse_attn * gain_attn).astype(BF16)
        a_rows = dot(weight_a, normed, ((1,), (1,))).reshape(heads, RANKS, block)
        b_raw = dot(weight_b, normed, ((0,), (1,))).reshape(RANKS, HEAD_DIM, block)
        b_rot = rotate(b_raw[: RANK_Q + RANK_KV], cosine, sine)
        b_query = b_rot[:RANK_Q]
        b_kv = jnp.concatenate([b_rot[RANK_Q:], b_raw[RANK_Q + RANK_KV :]], axis=0)
        payload = jnp.concatenate(
            [
                b_kv.reshape(KV * HEAD_DIM, block),
                a_rows[:, RANK_Q:].reshape(heads * KV, block),
            ],
            axis=0,
        ).astype(BF16)
        around = [
            lax.ppermute(
                payload, ("ctx", "tp"), [(i, i + step) for i in range(n_place - step)]
            )
            for step in range(extra, 0, -1)
        ]
        win = jnp.concatenate(around + [payload], axis=1)
        win_b = win[: KV * HEAD_DIM].reshape(KV, HEAD_DIM, window)
        win_a = win[KV * HEAD_DIM :].reshape(heads, KV, window)

        mixed, lse, query = attend_forward(first, a_rows, b_query, win_a, win_b)
        mixed = mixed.reshape(heads * HEAD_DIM, block)
        attn_out = dot(mixed, weight_o, ((0,), (0,)))
        mid = own + attn_out
        inverse_ffn = inverse_rms(mid)
        normed_ffn = (mid * inverse_ffn * gain_ffn).astype(BF16)

        near_rows = gather_pair(normed_ffn, "tp", n_tp, 1)
        far_rows = gather_pair(swap(normed_ffn, "tp", n_tp, 2), "tp", n_tp, 1)
        grad_all = cotangent[0].reshape(n_hi, n_lo * block, width)

        def half(rows, grad_rows):
            rows = rows.reshape(n_lo * block, width)
            gate = dot(rows, weight_g, ((1,), (1,)))
            up = dot(rows, weight_u, ((1,), (1,)))
            grad_act = dot(grad_rows, weight_d, ((1,), (1,)))
            squash = jax.nn.sigmoid(gate)
            act = (gate * squash * up).astype(BF16)
            grad_gate = (grad_act * up * squash * (1.0 + gate * (1.0 - squash))).astype(BF16)
            grad_up = (grad_act * gate * squash).astype(BF16)
            back = dot(grad_gate, weight_g, ((1,), (0,))) + dot(grad_up, weight_u, ((1,), (0,)))
            ahead = dot(act, weight_d, ((1,), (0,)))
            both = lambda v: v.reshape(n_lo, block, width)
            return rows, act, grad_gate, grad_up, both(back), both(ahead)

        grad_near = take(grad_all, hi).astype(BF16)
        grad_far = take(grad_all, 1 - hi).astype(BF16)
        near = half(near_rows, grad_near)
        far = half(far_rows, grad_far)
        back_far = scatter_pair(far[4], "tp", n_tp, 1).astype(BF16)
        back_far = swap(back_far, "tp", n_tp, 2)
        grad_normed_ffn = scatter_pair(near[4], "tp", n_tp, 1) + back_far.astype(F32)
        ahead_far = scatter_pair(far[5], "tp", n_tp, 1).astype(BF16)
        ahead_far = swap(ahead_far, "tp", n_tp, 2)
        ffn_out = scatter_pair(near[5], "tp", n_tp, 1) + ahead_far.astype(F32)

        def spread(value):
            beside = swap(value, "tp", n_tp, 1)
            across = swap(value, "tp", n_tp, 2)
            diagonal = swap(across, "tp", n_tp, 1)
            out = jnp.zeros((n_tp,) + value.shape, value.dtype)
            for bit, part in enumerate((value, beside, across, diagonal)):
                out = lax.dynamic_update_slice(out, part[None], (t_index ^ bit, 0, 0))
            return out.reshape(local_len, width).astype(F32)

        block_out = resid_in + spread((attn_out + ffn_out).astype(BF16))[None]

        def columns(value, which):
            value = value.reshape(value.shape[0], n_f, n_c, fc_cols)
            value = lax.dynamic_index_in_dim(value, which, 2, keepdims=False)
            return value.reshape(value.shape[0], n_f * fc_cols)

        rows_all = jnp.concatenate([near[0], far[0]], axis=0)
        act_all = jnp.concatenate([near[1], far[1]], axis=0)
        gate_all = jnp.concatenate([near[2], far[2]], axis=0)
        up_all = jnp.concatenate([near[3], far[3]], axis=0)
        cot_all = jnp.concatenate([grad_near, grad_far], axis=0)

        def big_grads(which):
            rows_cut = columns(rows_all, which)
            cot_cut = columns(cot_all, which)
            return jnp.concatenate(
                [
                    dot(gate_all, rows_cut, ((0,), (0,))),
                    dot(up_all, rows_cut, ((0,), (0,))),
                    dot(act_all, cot_cut, ((0,), (0,))),
                ],
                axis=0,
            )

        def over_fc(send, keep):
            total = keep + swap(send.astype(BF16), "ctx", n_c, 1).astype(F32)
            total = total.astype(BF16).reshape(-1, n_f, fc_cols).transpose(1, 0, 2)
            return scatter_direct(total, "fsdp", n_f)

        grad_big = over_fc(big_grads(1 - c_index), big_grads(c_index))
        grad_gate_w = grad_big[:hidden].T
        grad_up_w = grad_big[hidden : 2 * hidden].T
        grad_down_w = grad_big[2 * hidden :]

        own_cot = take(cotangent[0].reshape(n_tp, block, width), t_index)
        gain_grad_ffn = jnp.sum(grad_normed_ffn * mid * inverse_ffn, axis=0)
        delta_mid = norm_back(grad_normed_ffn, mid, inverse_ffn, gain_ffn)
        grad_attn = (own_cot + delta_mid).astype(BF16)
        grad_out = dot(mixed, grad_attn, ((1,), (0,))).reshape(n_hi, n_lo, o_rows, width)
        grad_out = scatter_pair(grad_out.transpose(1, 0, 2, 3), "tp", n_tp, 1)
        grad_out = scatter_pair(grad_out, "tp", n_tp, 2)
        grad_out = over_fc(columns(grad_out, 1 - c_index), columns(grad_out, c_index))

        grad_mixed = dot(weight_o, grad_attn, ((1,), (1,))).astype(BF16)
        ga_q, gb_q, gw_a, gw_b = attend_backward(
            first,
            a_rows,
            b_query,
            win_a,
            win_b,
            lse,
            query,
            grad_mixed.reshape(heads, HEAD_DIM, block),
        )
        gw = jnp.concatenate(
            [gw_b.reshape(KV * HEAD_DIM, window), gw_a.reshape(heads * KV, window)], axis=0
        )
        total = gw[:, extra * block :]
        for step in range(1, extra + 1):
            part = gw[:, (extra - step) * block : (extra - step + 1) * block].astype(BF16)
            part = lax.ppermute(
                part, ("ctx", "tp"), [(i + step, i) for i in range(n_place - step)]
            )
            total = total + part.astype(F32)
        gb_kv = total[: KV * HEAD_DIM].reshape(KV, HEAD_DIM, block)
        ga_kv = total[KV * HEAD_DIM :].reshape(heads, KV, block)
        grad_b = jnp.concatenate(
            [
                rotate(jnp.concatenate([gb_q, gb_kv[:RANK_KV]], axis=0), cosine, -sine),
                gb_kv[RANK_KV:],
            ],
            axis=0,
        )
        grad_b = grad_b.reshape(b_cols, block).astype(BF16)
        grad_a = jnp.concatenate([ga_q, ga_kv], axis=1).reshape(heads * RANKS, block).astype(BF16)
        grad_normed = dot(grad_a, weight_a, ((0,), (0,))) + dot(grad_b, weight_b, ((0,), (1,)))
        gain_grad_attn = jnp.sum(grad_normed * own * inverse_attn, axis=0)
        delta = delta_mid + norm_back(grad_normed, own, inverse_attn, gain_attn)
        resid_grad = cotangent + spread(delta.astype(BF16))[None]

        grad_wa = dot(grad_a, normed, ((1,), (0,))).astype(BF16)
        grad_wa = grad_wa.reshape(n_hi, n_lo, a_cols, n_f, n_c, fc_cols)
        grad_wa = grad_wa.transpose(1, 0, 4, 3, 2, 5).reshape(n_lo, n_hi, n_c, n_f, n_a, LANES)
        grad_wb = jnp.einsum(
            "pkt,td->pdk",
            grad_b.reshape(b_parts, LANES, block),
            normed,
            preferred_element_type=F32,
        ).astype(BF16)
        grad_wb = grad_wb.reshape(b_parts, n_f, n_c, n_hi, n_lo, b_rows, LANES)
        grad_wb = grad_wb.transpose(4, 3, 2, 1, 0, 5, 6)
        grad_wb = grad_wb.reshape(n_lo, n_hi, n_c, n_f, n_b, LANES)
        gain_grads = jnp.stack([gain_grad_attn, gain_grad_ffn]).astype(BF16)
        gain_grads = gain_grads.reshape(2, n_f, n_c, n_hi, n_lo, gain_count // 2)
        gain_grads = gain_grads.transpose(4, 3, 2, 1, 0, 5).reshape(
            n_lo, n_hi, n_c, n_f, gain_count
        )
        gain_grads = jnp.pad(
            gain_grads, [(0, 0)] * 4 + [(0, gain_rows * LANES - gain_count)]
        ).reshape(n_lo, n_hi, n_c, n_f, gain_rows, LANES)
        pack = jnp.concatenate([grad_wb, grad_wa, gain_grads], axis=4)
        pack = scatter_pair(pack, "tp", n_tp, 1)
        pack = scatter_pair(pack, "tp", n_tp, 2)
        pack = scatter_pair(pack, "ctx", n_c, 1).astype(BF16)
        pack = scatter_direct(pack, "fsdp", n_f)
        part_b = pack[:n_b].reshape(b_parts, b_rows, LANES).transpose(1, 0, 2)
        part_b = part_b.reshape(1, b_rows, b_cols)
        part_a = pack[n_b : n_b + n_a].reshape(a_cols, fc_cols).T[None]
        part_gain = pack[n_b + n_a :].reshape(-1)[:gain_count].reshape(2, 1, gain_count // 2)
        return (
            block_out,
            resid_grad,
            part_a,
            part_b,
            grad_out[None],
            jnp.stack([grad_gate_w, grad_up_w])[None],
            grad_down_w[None],
            part_gain[0],
            part_gain[1],
        )

    return shards


def rotated(rows, cosine, sine):
    half = HEAD_DIM // 2
    lower, upper = rows[:half], rows[half:]
    return jnp.concatenate([lower * cosine - upper * sine, lower * sine + upper * cosine], axis=0)


def make_fused(mesh):
    n_f, n_c, n_tp = mesh.shape["fsdp"], mesh.shape["ctx"], mesh.shape["tp"]
    n_piece = n_f * n_c
    AT_TP = n_piece
    AT_ME = n_piece + n_tp

    def shards(
        resid_in,
        segment_ids,
        cotangent,
        w_factor_a,
        w_factor_b,
        w_out,
        w_gate_up,
        w_down,
        attn_gains,
        ffn_gains,
    ):
        _, local_len, width = resid_in.shape
        block = local_len // n_tp
        extra = -(-(MOST_DOC - 1) // block)
        windows = extra + 1
        a_cols = w_factor_a.shape[2]
        group = a_cols // RANKS
        heads = n_tp * group
        feats = group * HEAD_DIM
        a_pad = 16 * (-(-a_cols // 16))
        b_rows, b_cols = w_factor_b.shape[1:]
        b_parts = b_cols // LANES
        n_b = b_parts * b_rows
        pack_rows = n_b + a_pad + 16
        fc_cols = w_down.shape[2]
        hidden = w_down.shape[1]
        o_rows = w_out.shape[1]
        gain_part = attn_gains.shape[1]
        kv_b = KV * HEAD_DIM
        kv_rows = kv_b + heads * KV
        half_width = width // n_c
        pairs = heads // 2
        first_part = 5 * pairs // 8
        pair_rows = 8 * (-(-2 * RANKS // 8))
        early = 2 * hidden + 16 * (hidden // 64)
        assert n_f == 4 and fc_cols == LANES and o_rows == feats and n_tp == 4 and n_c == 2

        f_index, c_index, t_index = (
            lax.axis_index("fsdp"),
            lax.axis_index("ctx"),
            lax.axis_index("tp"),
        )
        place = c_index * n_tp + t_index
        n_place = n_c * n_tp
        columns = [
            ((f_index - s) % n_f) * n_c + (c_index if near == 0 else 1 - c_index)
            for near in range(n_c)
            for s in range(n_f)
        ]
        members = [t_index ^ (lo + 2 * hi) for lo in range(2) for hi in range(2)]
        beside_shift = jnp.where(f_index % 2 == 0, n_f - 1, 1)
        meta = jnp.stack(columns + members + [t_index, f_index, beside_shift]).astype(jnp.int32)

        resid_in = pltpu.with_memory_space_constraint(resid_in, pltpu.HBM)
        cotangent = pltpu.with_memory_space_constraint(cotangent, pltpu.HBM)

        def column(meta_ref, j):
            return pl.ds(pl.multiple_of(meta_ref[j] * LANES, LANES), LANES)

        def member(meta_ref, lo, hi):
            return meta_ref[AT_TP + 2 * lo + hi]

        def to_arrival(meta_ref, load):
            return jnp.concatenate([load(column(meta_ref, j)) for j in range(n_piece)], axis=1)

        WHOLE = pl.BlockSpec(memory_space=pltpu.VMEM)
        REMOTE = pl.BlockSpec(memory_space=pl.ANY)

        def call(
            kernel, name, outs, args, specs=None, scratch=(), grid=(1,), out_specs=None, room=4,
            scalars=meta,
        ):
            held = 0
            for arg, spec in zip((*args, *args[:1]), (specs or []) + (out_specs or [])):
                if spec.block_shape:
                    held += 2 * math.prod(spec.block_shape) * arg.dtype.itemsize
            for item in scratch:
                if hasattr(item, "shape") and item.memory_space == pltpu.VMEM:
                    held += math.prod(item.shape) * jnp.dtype(item.dtype).itemsize
            limit = min(held + room * 2**20, VMEM_LIMIT)
            return pl.pallas_call(
                kernel,
                out_shape=[jax.ShapeDtypeStruct(s, d) for s, d in outs],
                grid_spec=pltpu.PrefetchScalarGridSpec(
                    num_scalar_prefetch=1,
                    grid=grid,
                    in_specs=specs or [WHOLE] * len(args),
                    out_specs=out_specs or [WHOLE] * len(outs),
                    scratch_shapes=list(scratch),
                ),
                compiler_params=pltpu.CompilerParams(vmem_limit_bytes=limit),
                name=name,
            )(scalars, *args)


        def pack_kernel(meta_ref, b_ref, a_ref, g0_ref, g1_ref, out_ref):
            for k in range(b_parts):
                out_ref[k * b_rows : (k + 1) * b_rows, :] = b_ref[
                    0, :, k * LANES : (k + 1) * LANES
                ].astype(BF16)
            a_shard = jnp.concatenate([a_ref[0], jnp.zeros((a_pad - a_cols, LANES), F32)], axis=0)
            out_ref[n_b : n_b + a_pad, :] = a_shard.astype(BF16)
            both = jnp.concatenate([g0_ref[...], g1_ref[...]], axis=0)
            both = jnp.concatenate([both, jnp.zeros((6, gain_part), F32)], axis=0)
            both = jnp.concatenate([both, jnp.zeros((8, LANES - gain_part), F32)], axis=1)
            both = pltpu.roll(both, meta_ref[AT_ME] * gain_part, 1)
            both = jnp.concatenate([both, jnp.zeros((8, LANES), F32)], axis=0)
            out_ref[n_b + a_pad :, :] = both.astype(BF16)

        def big_kernel(meta_ref, gu_ref, d_ref, gu_out_ref, d_out_ref):
            for k in range(2):
                gu_out_ref[k * hidden : (k + 1) * hidden, :] = gu_ref[0, k].astype(BF16)
            gu_out_ref[2 * hidden :, :] = d_ref[0, : early - 2 * hidden, :].astype(BF16)
            d_out_ref[...] = d_ref[0, early - 2 * hidden :, :].astype(BF16)

        def factor_kernel(
            meta_ref,
            x_ref,
            p0_ref,
            p1_ref,
            cos_ref,
            sin_ref,
            wb_ref,
            wa_ref,
            gain_ref,
            normed_ref,
            a_ref,
            bq_ref,
            pay_ref,
        ):
            gain_ref[...] = jnp.zeros_like(gain_ref)
            for lo, hi in ((0, 0), (0, 1), (1, 0), (1, 1)):
                part = (p0_ref, p1_ref)[lo]
                tp = member(meta_ref, lo, hi)
                for near in range(n_c):
                    for s in range(n_f):
                        j = near * n_f + s
                        lanes = column(meta_ref, j)
                        row = pl.multiple_of((meta_ref[j] * n_tp + tp) * b_rows, b_rows)
                        for k in range(b_parts):
                            wb_ref[pl.ds(row, b_rows), k * LANES : (k + 1) * LANES] = part[
                                near, hi, s, k * b_rows : (k + 1) * b_rows, :
                            ]
                        wa_ref[tp, :, lanes] = part[near, hi, s, n_b : n_b + a_pad, :]
                        gain_ref[:, lanes] += part[near, hi, s, n_b + a_pad :, :].astype(F32)
            x = x_ref[...]
            normed = (x * inverse_rms(x) * gain_ref[0:1]).astype(BF16)
            normed_ref[...] = normed
            cosine, sine = cos_ref[...], sin_ref[...]
            b_raw = jnp.transpose(dot(normed, wb_ref[...], ((1,), (0,))))
            for r in range(RANK_Q):
                bq_ref[r] = rotated(b_raw[r * HEAD_DIM : (r + 1) * HEAD_DIM], cosine, sine)
            for r in range(KV):
                rows = b_raw[(RANK_Q + r) * HEAD_DIM : (RANK_Q + r + 1) * HEAD_DIM]
                if r < RANK_KV:
                    rows = rotated(rows, cosine, sine)
                pay_ref[r * HEAD_DIM : (r + 1) * HEAD_DIM, :] = rows.astype(BF16)
            for tp in range(n_tp):
                a_raw = dot(wa_ref[tp], normed, ((1,), (1,)))
                a_ref[tp] = a_raw
                kv = [a_raw[g * RANKS + RANK_Q : (g + 1) * RANKS] for g in range(group)]
                start = kv_b + tp * group * KV
                pay_ref[start : start + group * KV, :] = jnp.concatenate(kv, axis=0).astype(BF16)

        def set_mask(first_ref, bias_ref):
            bias_ref[...] = attention_mask(first_ref, windows * block, block)

        def is_even(meta_ref):
            return lax.rem(meta_ref[AT_ME], 2) == 0

        def widen(meta_ref, arrived, win_ref, wide_ref):
            third, second, beside_second, beside, own = arrived
            win_ref[1] = second[...]
            win_ref[3] = own[...]

            @pl.when(is_even(meta_ref))
            def _():
                win_ref[0] = third[...]
                win_ref[2] = beside_second[...]

            @pl.when(jnp.logical_not(is_even(meta_ref)))
            def _():
                win_ref[0] = beside_second[...]
                win_ref[2] = beside[...]

            for j in range(windows):
                for r in range(KV):
                    wide_ref[j, r] = win_ref[j, r * HEAD_DIM : (r + 1) * HEAD_DIM, :].astype(F32)

        def spread_factors(a_ref, win_ref, own_ref, kv_ref):
            for pair in range(pairs):
                start = pair % (group // 2) * 2 * RANKS
                own_ref[pair, : 2 * RANKS, :] = a_ref[pair * 2 // group, start : start + 2 * RANKS, :]
            for j in range(windows):
                kv_ref[j] = win_ref[j, kv_b:, :].astype(F32)

        def kv_factors(kv_ref, pair):
            start = pl.multiple_of(pair * (2 * KV), 2 * KV)
            return [kv_ref[j, pl.ds(start, 2 * KV), :] for j in range(windows)]

        def head_place(pair, g):
            tp, half = pair // (group // 2), lax.rem(pair, group // 2)
            return tp, 2 * half + g, pl.ds(pl.multiple_of((2 * half + g) * HEAD_DIM, HEAD_DIM), HEAD_DIM)

        def kv_rows_of(factors, wide_ref, g, j):
            def mix(r):
                a0 = factors[j][g * KV + r : g * KV + r + 1]
                a1 = factors[j][g * KV + r + 1 : g * KV + r + 2]
                rows = a0 * wide_ref[j, r] + a1 * wide_ref[j, r + 1]
                return (rows * (1.0 / RANK_KV)).astype(BF16)

            return mix(0), mix(RANK_KV)

        def attention_kernel(
            meta_ref,
            first_ref,
            a_ref,
            bq_ref,
            w0_ref,
            w1_ref,
            w2_ref,
            w3_ref,
            w4_ref,
            lse_ref,
            q_ref,
            mixed_ref,
            win_ref,
            bias_ref,
            wide_ref,
            s_ref,
            own_ref,
            kv_ref,
        ):
            set_mask(first_ref, bias_ref)
            widen(meta_ref, (w0_ref, w1_ref, w2_ref, w3_ref, w4_ref), win_ref, wide_ref)
            spread_factors(a_ref, win_ref, own_ref, kv_ref)
            spans = [pl.ds(j * block, block) for j in range(windows)]

            def one_pair(pair, slot):
                own = own_ref[pair]
                factors = kv_factors(kv_ref, pair)
                for g in range(2):
                    tp, head, rows = head_place(pair, g)
                    query = own[g * RANKS : g * RANKS + 1] * bq_ref[0]
                    for r in range(1, RANK_Q):
                        query = query + own[g * RANKS + r : g * RANKS + r + 1] * bq_ref[r]
                    query = (query * (1.0 / RANK_Q)).astype(BF16)
                    query = query * jnp.asarray(HEAD_DIM**-0.5, BF16)
                    q_ref[tp, head] = query
                    top = jnp.full((1, block), MASKED, F32)
                    values = []
                    for j, span in enumerate(spans):
                        keys, value_rows = kv_rows_of(factors, wide_ref, g, j)
                        values.append(value_rows)
                        scores = dot(keys, query, ((0,), (0,))) + bias_ref[span, :]
                        s_ref[slot + g, span, :] = scores
                        top = jnp.maximum(top, jnp.max(scores, axis=0, keepdims=True))
                    total = jnp.zeros((1, block), F32)
                    for span in spans:
                        weight = jnp.exp(s_ref[slot + g, span, :] - top)
                        s_ref[slot + g, span, :] = weight
                        total = total + jnp.sum(weight, axis=0, keepdims=True)
                    lse_ref[pair, g : g + 1, :] = top + jnp.log(total)
                    scale = 1.0 / total
                    mixed = jnp.zeros((HEAD_DIM, block), F32)
                    for j, span in enumerate(spans):
                        probs = (s_ref[slot + g, span, :] * scale).astype(BF16)
                        mixed = mixed + dot(values[j], probs, ((1,), (0,)))
                    mixed_ref[tp, rows, :] = mixed.astype(BF16)

            def one_member(tp, carry):
                for k in range(group // 2):
                    one_pair(tp * (group // 2) + k, 2 * k)
                return carry

            lax.fori_loop(0, n_tp, one_member, 0)

        def project_kernel(
            meta_ref, x_ref, mixed_ref, o0_ref, o1_ref, gain_ref, mid_ref, attn_ref, nf_ref
        ):
            attn = jnp.zeros((block, width), F32)
            for lo, ref in enumerate((o0_ref, o1_ref)):
                for hi in range(2):
                    rows = mixed_ref[member(meta_ref, lo, hi)]
                    attn = attn + dot(rows, ref[hi * o_rows : (hi + 1) * o_rows, :], ((0,), (0,)))
            attn_ref[...] = attn
            mid = to_arrival(meta_ref, lambda lanes: x_ref[:, lanes]) + attn
            mid_ref[...] = mid
            gain = to_arrival(meta_ref, lambda lanes: gain_ref[1:2, lanes])
            nf_ref[...] = (mid * inverse_rms(mid) * gain).astype(BF16)

        def rows_kernel(
            meta_ref, x_hbm, cot_ref, x_ref, own_ref, near_ref, far_ref, cot_buf, sems
        ):
            row = pl.multiple_of(meta_ref[AT_ME] * block, block)
            own_load = pltpu.make_async_copy(x_hbm.at[0, pl.ds(row, block), :], x_ref, sems.at[4])
            own_load.start()
            loads = []
            for side in range(2):
                for i in range(2):
                    row = pl.multiple_of(member(meta_ref, i, side) * block, block)
                    k = 2 * side + i
                    loads.append(
                        pltpu.make_async_copy(
                            cot_ref.at[0, pl.ds(row, block), :], cot_buf.at[k], sems.at[k]
                        )
                    )
                    loads[-1].start()
            for k, load in enumerate(loads):
                load.wait()
                out_ref = (near_ref, far_ref)[k // 2]
                rows = slice(k % 2 * block, (k % 2 + 1) * block)
                for j in range(n_piece):
                    lanes = slice(j * LANES, (j + 1) * LANES)
                    part = cot_buf[k, :, column(meta_ref, j)]
                    out_ref[rows, lanes] = part.astype(BF16)
                    if k == 0:
                        own_ref[:, lanes] = part
            own_load.wait()

        def feed_rows(n_refs, gb_ref, w_ref, ht_ref, back0_ref, back1_ref, rows_ref):
            for i in range(2):
                rows_ref[i] = n_refs[i][...]

            def one_block(i, carry):
                cut = pl.ds(pl.multiple_of(i * block, block), block)
                rows = rows_ref[i]
                gate = dot(w_ref[0:hidden, :], rows, ((1,), (1,)))
                up = dot(w_ref[hidden : 2 * hidden, :], rows, ((1,), (1,)))
                grad_act = dot(w_ref[2 * hidden :, :], gb_ref[cut, :], ((1,), (1,)))
                squash = jax.nn.sigmoid(gate)
                soft = gate * squash
                ht_ref[2 * hidden :, cut] = (soft * up).astype(BF16)
                ht_ref[0:hidden, cut] = (
                    grad_act * up * squash * (1.0 + gate * (1.0 - squash))
                ).astype(BF16)
                ht_ref[hidden : 2 * hidden, cut] = (grad_act * soft).astype(BF16)
                return carry

            lax.fori_loop(0, 2, one_block, 0)
            back = dot(ht_ref[: 2 * hidden, :], w_ref[: 2 * hidden, :], ((0,), (0,)))
            back0_ref[...] = back[:block]
            back1_ref[...] = back[block:].astype(BF16)

        def far_kernel(meta_ref, n0_ref, n1_ref, gb_ref, *refs):
            own_gu_ref, far_gu_ref, pair_gu_ref, gu_across_ref, gu_rest_ref = refs[:5]
            dn_refs = refs[5 : 5 + n_f]
            ht_ref, back0_ref, back1_ref, w_ref, rows_ref, sems = refs[5 + n_f :]
            gate_up = [own_gu_ref, far_gu_ref, pair_gu_ref.at[0], pair_gu_ref.at[1], gu_across_ref]
            gate_up += [gu_rest_ref.at[s] for s in range(n_f - 1)]
            beside_shift = meta_ref[AT_ME + 2]
            arrivals = [0, 2, beside_shift, n_f - beside_shift]
            down = [ref.at[near] for near in range(n_c) for ref in dn_refs]
            loads = []
            for j in range(n_piece):
                lanes = pl.ds(j * LANES, LANES)
                at = pl.multiple_of((arrivals[j % n_f] + j // n_f * n_f) * LANES, LANES)
                loads.append(
                    pltpu.make_async_copy(
                        gate_up[j],
                        w_ref.at[pl.ds(0, early), pl.ds(at, LANES)],
                        sems.at[j],
                    )
                )
                loads.append(
                    pltpu.make_async_copy(
                        down[j], w_ref.at[pl.ds(early, 3 * hidden - early), lanes], sems.at[n_piece + j]
                    )
                )
            for load in loads:
                load.start()
            for load in loads:
                load.wait()
            feed_rows((n0_ref, n1_ref), gb_ref, w_ref, ht_ref, back0_ref, back1_ref, rows_ref)

        def near_kernel(meta_ref, n0_ref, n1_ref, gb_ref, w_ref, far_ht_ref, ht_ref, *refs):
            back0_ref, back1_ref, *ahead_refs, rows_ref = refs
            feed_rows((n0_ref, n1_ref), gb_ref, w_ref, ht_ref, back0_ref, back1_ref, rows_ref)
            for k, ref in enumerate((ht_ref, far_ht_ref)):
                ahead = dot(ref[2 * hidden :, :], w_ref[2 * hidden :, :], ((0,), (0,)))
                ahead_refs[2 * k][...] = ahead[:block]
                ahead_refs[2 * k + 1][...] = ahead[block:].astype(BF16)

        def weight_grad(refs, start, stop, right):
            hts, n_near, n_far, gbs = refs[0:2], refs[2:4], refs[4:6], refs[6:8]
            total = jnp.zeros((stop - start, width), F32)
            for side in range(2):
                left = hts[side]
                if right == 1:
                    total = total + dot(left[start:stop, :], gbs[side][...], ((1,), (0,)))
                    continue
                for i in range(2):
                    rows = (n_near, n_far)[side][i][...]
                    cut = slice(i * block, (i + 1) * block)
                    total = total + dot(left[start:stop, cut], rows, ((1,), (0,)))
            return total

        def gate_up_grad_kernel(meta_ref, *refs):
            keep_ref, send_ref = refs[8:]
            for k in range(2):
                cut = slice(k * hidden, (k + 1) * hidden)
                total = weight_grad(refs, k * hidden, (k + 1) * hidden, 0)
                keep_ref[cut, :] = total[:, :half_width].astype(BF16)
                send_ref[cut, :] = total[:, half_width:].astype(BF16)

        def down_grad_kernel(meta_ref, *refs):
            keep_ref, send_ref = refs[8:]
            total = weight_grad(refs, 2 * hidden, 3 * hidden, 1)

            def chunk(s, near):
                start = near * half_width + s * LANES
                return total[:, start : start + LANES]

            for near in range(n_c):
                keep_ref[0, near] = chunk(0, near)
                keep_ref[1, near] = chunk(2, near)

            @pl.when(lax.rem(meta_ref[AT_ME + 1], 2) == 0)
            def _():
                for near in range(n_c):
                    send_ref[0, near] = chunk(3, near).astype(BF16)
                    send_ref[1, near] = chunk(1, near).astype(BF16)

            @pl.when(lax.rem(meta_ref[AT_ME + 1], 2) == 1)
            def _():
                for near in range(n_c):
                    send_ref[0, near] = chunk(1, near).astype(BF16)
                    send_ref[1, near] = chunk(3, near).astype(BF16)

        def middle_kernel(
            meta_ref,
            cot_ref,
            back_ref,
            beside_ref,
            across_ref,
            mid_ref,
            gain_ref,
            o0_ref,
            o1_ref,
            mixed_ref,
            dmid_ref,
            gg_ref,
            go_ref,
            keep_ref,
            send_ref,
        ):
            back = back_ref[...] + beside_ref[...].astype(F32) + across_ref[...].astype(F32)
            mid = mid_ref[...]
            inverse = inverse_rms(mid)
            gain = to_arrival(meta_ref, lambda lanes: gain_ref[1:2, lanes])
            normal = mid * inverse
            gains = jnp.sum(back * normal, axis=0, keepdims=True)
            for j in range(n_piece):
                gg_ref[:, column(meta_ref, j)] = jnp.broadcast_to(
                    gains[:, j * LANES : (j + 1) * LANES], (8, LANES)
                )
            scaled = back * gain
            delta = inverse * (
                scaled - normal * jnp.mean(scaled * normal, axis=-1, keepdims=True)
            )
            dmid_ref[...] = delta
            grad = (cot_ref[...] + delta).astype(BF16)
            for lo, ref in enumerate((o0_ref, o1_ref)):
                for hi in range(2):
                    tp = member(meta_ref, lo, hi)
                    cut = slice(hi * o_rows, (hi + 1) * o_rows)
                    go_ref[tp] = dot(ref[cut, :], grad, ((1,), (1,))).astype(BF16)
                    weight = dot(mixed_ref[tp], grad, ((1,), (0,))).astype(BF16)
                    (keep_ref, send_ref)[lo][cut, :] = weight

        def attention_back_kernel(
            part,
            meta_ref,
            first_ref,
            a_ref,
            bq_ref,
            w0_ref,
            w1_ref,
            w2_ref,
            w3_ref,
            w4_ref,
            lse_ref,
            q_ref,
            go_ref,
            *refs,
        ):
            win_ref, bias_ref, wide_ref, p_ref, dp_ref, own_ref, kv_ref = refs[-7:]
            if part == 0:
                ga_ref, gbq_ref, gwb_ref, gwa_ref = refs[:4]
            else:
                ga_ref, gbq_ref, second_ref, beside_ref, third_ref, own_out_ref = refs[3:9]
                gwb_ref, gwa_ref = refs[-9:-7]
            set_mask(first_ref, bias_ref)
            widen(meta_ref, (w0_ref, w1_ref, w2_ref, w3_ref, w4_ref), win_ref, wide_ref)
            spread_factors(a_ref, win_ref, own_ref, kv_ref)
            if part == 0:
                gbq_ref[...] = jnp.zeros_like(gbq_ref)
                gwb_ref[...] = jnp.zeros_like(gwb_ref)
            else:
                gbq_ref[...] = refs[0][...]
                gwb_ref[...] = refs[1][...]
                gwa_ref[...] = refs[2][...]
            spans = [pl.ds(j * block, block) for j in range(windows)]
            first_pair, stop_pair = ((0, first_part), (first_part, pairs))[part]

            def one_pair(pair, carry):
                own = own_ref[pair]
                factors = kv_factors(kv_ref, pair)
                grad_a = []
                grad_kv = [[] for _ in spans]
                for g in range(2):
                    tp, head, rows = head_place(pair, g)
                    query = q_ref[tp, head]
                    grad_out = go_ref[tp, rows, :]
                    lse = lse_ref[pair, g : g + 1, :]
                    inner = jnp.zeros((1, block), F32)
                    keys = []
                    for j, span in enumerate(spans):
                        key_rows, value_rows = kv_rows_of(factors, wide_ref, g, j)
                        keys.append(key_rows)
                        scores = dot(key_rows, query, ((0,), (0,))) + bias_ref[span, :]
                        probs = jnp.exp(scores - lse)
                        grad_probs = dot(value_rows, grad_out, ((0,), (0,)))
                        p_ref[g % 2, span, :] = probs
                        dp_ref[g % 2, span, :] = grad_probs
                        inner = inner + jnp.sum(probs * grad_probs, axis=0, keepdims=True)
                    grad_query = jnp.zeros((HEAD_DIM, block), F32)
                    for j, span in enumerate(spans):
                        probs = p_ref[g % 2, span, :]
                        grad_scores = (probs * (dp_ref[g % 2, span, :] - inner)).astype(BF16)
                        grad_query = grad_query + dot(keys[j], grad_scores, ((1,), (0,)))
                        grad_keys = dot(query, grad_scores, ((1,), (1,))) * (1.0 / RANK_KV)
                        grad_values = dot(grad_out, probs.astype(BF16), ((1,), (1,)))
                        grad_values = grad_values * (1.0 / RANK_KV)
                        for r in range(KV):
                            grad = grad_keys if r < RANK_KV else grad_values
                            grad_kv[j].append(
                                jnp.sum(grad * wide_ref[j, r], axis=0, keepdims=True)
                            )
                            gwb_ref[j, r] += factors[j][g * KV + r : g * KV + r + 1] * grad
                    grad_query = grad_query * (HEAD_DIM**-0.5 / RANK_Q)
                    for r in range(RANK_Q):
                        grad_a.append(jnp.sum(grad_query * bq_ref[r], axis=0, keepdims=True))
                        gbq_ref[r] += own[g * RANKS + r : g * RANKS + r + 1] * grad_query
                    grad_a.append(jnp.zeros((KV, block), F32))
                grad_a.append(jnp.zeros((pair_rows - 2 * RANKS, block), F32))
                ga_ref[pair - first_pair] = jnp.concatenate(grad_a, axis=0)
                start = pl.multiple_of(pair * (2 * KV), 2 * KV)
                for j in range(windows):
                    gwa_ref[j, pl.ds(start, 2 * KV), :] = jnp.concatenate(grad_kv[j], axis=0)
                return carry

            lax.fori_loop(first_pair, stop_pair, one_pair, 0)
            if part == 0:
                return

            def put(ref, start, j):
                for r in range(KV):
                    row = start + r * HEAD_DIM
                    ref[row : row + HEAD_DIM, :] = gwb_ref[j, r].astype(ref.dtype)
                ref[start + kv_b : start + kv_rows, :] = gwa_ref[j].astype(ref.dtype)

            put(own_out_ref, 0, 3)
            put(beside_ref, 0, 2)
            put(third_ref, 0, 0)
            put(second_ref, 0, 1)

        def last_kernel(
            meta_ref,
            x_ref,
            own_ref,
            second_ref,
            beside_ref,
            third_ref,
            gbq_ref,
            ga0_ref,
            ga1_ref,
            cos_ref,
            sin_ref,
            wb_ref,
            wa_ref,
            normed_ref,
            gain_ref,
            dmid_ref,
            gg_ref,
            delta_ref,
            keep0_ref,
            keep1_ref,
            send0_ref,
            send1_ref,
            b_buf,
            a_buf,
            d_buf,
            g_buf,
        ):
            total = own_ref[...]
            for ref in (second_ref, beside_ref, third_ref):
                total = total + ref[...].astype(F32)
            cosine, sine = cos_ref[...], -sin_ref[...]
            rows = [rotated(gbq_ref[r], cosine, sine) for r in range(RANK_Q)]
            for r in range(KV):
                part = total[r * HEAD_DIM : (r + 1) * HEAD_DIM]
                rows.append(rotated(part, cosine, sine) if r < RANK_KV else part)
            grad_b = jnp.transpose(jnp.concatenate(rows, axis=0)).astype(BF16)
            normed = normed_ref[...]
            back = dot(grad_b, wb_ref[...], ((1,), (1,)))
            for tp in range(n_tp):
                parts = []
                for g in range(group):
                    start = kv_b + (tp * group + g) * KV
                    parts.append(jnp.zeros((RANK_Q, block), F32))
                    parts.append(total[start : start + KV])
                parts.append(jnp.zeros((a_pad - a_cols, block), F32))
                half = group // 2
                at = [tp * half + k for k in range(half)]
                own_a = [
                    ga0_ref[k, : 2 * RANKS, :]
                    if k < first_part
                    else ga1_ref[k - first_part, : 2 * RANKS, :]
                    for k in at
                ]
                own_a.append(jnp.zeros((a_pad - a_cols, block), F32))
                own_a = jnp.concatenate(own_a, axis=0)
                grad_a = (own_a + jnp.concatenate(parts, axis=0)).astype(BF16)
                back = back + dot(grad_a, wa_ref[tp], ((0,), (0,)))
                a_buf[tp] = dot(grad_a, normed, ((1,), (0,)))
            b_buf[...] = dot(normed, grad_b, ((0,), (0,)))
            x = x_ref[...]
            inverse = inverse_rms(x)
            normal = x * inverse
            gains = jnp.sum(back * normal, axis=0, keepdims=True)
            g_buf[...] = jnp.broadcast_to(gains, (8, width))
            scaled = back * gain_ref[0:1]
            delta = inverse * (
                scaled - normal * jnp.mean(scaled * normal, axis=-1, keepdims=True)
            )
            d_buf[...] = delta
            for j in range(n_piece):
                lanes = column(meta_ref, j)
                cut = slice(j * LANES, (j + 1) * LANES)
                delta_ref[:, lanes] = (d_buf[:, lanes] + dmid_ref[:, cut]).astype(BF16)
            row_index = lax.broadcasted_iota(jnp.int32, (16, LANES), 0)
            for lo, hi in ((0, 0), (0, 1), (1, 0), (1, 1)):
                outs = ((keep0_ref, keep1_ref), (send0_ref, send1_ref))[lo]
                tp = member(meta_ref, lo, hi)
                for near in range(n_c):
                    out = outs[near]
                    for s in range(n_f):
                        j = near * n_f + s
                        lanes = column(meta_ref, j)
                        row = pl.multiple_of((meta_ref[j] * n_tp + tp) * b_rows, b_rows)
                        for k in range(b_parts):
                            out[hi, s, k * b_rows : (k + 1) * b_rows, :] = b_buf[
                                pl.ds(row, b_rows), k * LANES : (k + 1) * LANES
                            ].astype(BF16)
                        out[hi, s, n_b : n_b + a_pad, :] = a_buf[tp, :, lanes].astype(BF16)
                        pair = jnp.where(
                            row_index == 0, g_buf[0:1, lanes], gg_ref[0:1, lanes]
                        )
                        out[hi, s, n_b + a_pad :, :] = pair.astype(BF16)

        def add_kernel(arrival, meta_ref, x_ref, d0_ref, d1_ref, d2_ref, d3_ref, out_ref):
            step = pl.program_id(0) // 2
            rows = pl.ds(pl.multiple_of((pl.program_id(0) % 2) * (block // 2), 8), block // 2)
            for i, ref in enumerate((d0_ref, d1_ref, d2_ref, d3_ref)):

                @pl.when(step == i)
                def _(ref=ref):
                    if not arrival:
                        out_ref[0] = x_ref[0] + ref[rows, :].astype(F32)
                        return
                    for j in range(n_piece):
                        lanes = column(meta_ref, j)
                        out_ref[0, :, lanes] = x_ref[0, :, lanes] + ref[
                            rows, j * LANES : (j + 1) * LANES
                        ].astype(F32)

        def split_kernel(meta_ref, keep_ref, got_ref, own_ref, send_ref):
            def total(s):
                lanes = slice(s * LANES, (s + 1) * LANES)
                return keep_ref[:, lanes].astype(F32) + got_ref[: keep_ref.shape[0], lanes].astype(
                    F32
                )

            own_ref[0] = total(0)
            own_ref[1] = total(2)

            @pl.when(lax.rem(meta_ref[AT_ME + 1], 2) == 0)
            def _():
                send_ref[0] = total(3).astype(BF16)
                send_ref[1] = total(1).astype(BF16)

            @pl.when(lax.rem(meta_ref[AT_ME + 1], 2) == 1)
            def _():
                send_ref[0] = total(1).astype(BF16)
                send_ref[1] = total(3).astype(BF16)

        def unpack_kernel(
            meta_ref, p_ref, got_ref, b_ref, a_ref, g0_ref, g1_ref, o_ref
        ):
            total = p_ref[...].astype(F32) + got_ref[...].astype(F32)
            for k in range(b_parts):
                b_ref[0, :, k * LANES : (k + 1) * LANES] = total[k * b_rows : (k + 1) * b_rows]
            a_ref[0] = total[n_b : n_b + a_cols]
            rows = total[n_b + a_pad : n_b + a_pad + 8]
            rows = pltpu.roll(rows, (n_tp - meta_ref[AT_ME]) * gain_part, 1)
            g0_ref[...] = rows[0:1, :gain_part]
            g1_ref[...] = rows[1:2, :gain_part]
            o_ref[0] = total[pack_rows:]

        core = lambda v, label="row": swap(v, "tp", n_tp, 1, "core_" + label)
        chip = lambda v, label="row": swap(v, "tp", n_tp, 2, "y_" + label)
        ctx = lambda v, label="row": swap(v, "ctx", n_c, 1, "x_" + label)
        ahead = lambda v, s, label="row": shift(v, "fsdp", n_f, s, "z_" + label)

        (pack,) = call(
            pack_kernel,
            "pack",
            [((pack_rows, LANES), BF16)],
            (w_factor_b, w_factor_a.transpose(0, 2, 1), attn_gains, ffn_gains),
        )
        o_rows_all = w_out[0].astype(BF16)
        pack = jnp.stack([pack] + [ahead(pack, s, "pack") for s in range(1, n_f)])
        o_parts = [o_rows_all] + [ahead(o_rows_all, s, "wo") for s in range(1, n_f)]
        o_parts = jnp.concatenate(o_parts, axis=0)
        gu_in = after(w_gate_up.transpose(0, 1, 3, 2), pack)
        own_gu, own_dn = call(
            big_kernel,
            "big_pack",
            [((early, LANES), BF16), ((3 * hidden - early, LANES), BF16)],
            (gu_in, w_down),
        )
        pack = jnp.stack([pack, ctx(pack, "pack")])
        far_gu = swap(own_gu, "fsdp", n_f, 2, "z_gate_up")
        dn_pair = jnp.stack([own_dn, ctx(own_dn, "down")])
        gu_across = ctx(own_gu, "gate_up")
        o_across = ctx(o_parts, "wo")
        o_parts = jnp.concatenate(
            [
                half[s * o_rows : (s + 1) * o_rows]
                for half in (o_parts, o_across)
                for s in range(n_f)
            ],
            axis=1,
        )
        own_x, own_cot, near_cot, far_cot = call(
            rows_kernel,
            "rows",
            [((block, width), F32)] * 2 + [((2 * block, width), BF16)] * 2,
            (resid_in, cotangent),
            [REMOTE] * 2,
            [pltpu.VMEM((4, block, width), F32), pltpu.SemaphoreType.DMA((5,))],
            scalars=after(meta, o_across),
        )
        pack_across, far_gu, dn_pair, o_parts, near_cot, far_cot = lax.optimization_barrier(
            (chip(pack, "pack"), far_gu, dn_pair, o_parts, near_cot, far_cot)
        )
        pair_gu = swap(jnp.stack([own_gu, far_gu]), "fsdp", n_f, 1, "z_gate_up_pair")
        pack = jnp.stack([pack, pack_across], axis=1)
        other_pack = core(pack, "pack")

        def add_rows(whole, parts, arrival):
            rows = pl.BlockSpec(
                (1, block // 2, width), lambda i, m: (0, 2 * m[AT_TP + i // 2] + i % 2, 0)
            )
            (out,) = call(
                lambda *refs: add_kernel(arrival, *refs),
                "add_rows",
                [(whole.shape, F32)],
                (whole, *parts),
                [rows] + [WHOLE] * 4,
                (),
                (2 * n_tp,),
                [rows],
            )
            return out

        def split(keep, got):
            size = keep.shape[0]
            return call(
                split_kernel,
                "split",
                [((2, size, LANES), F32), ((2, size, LANES), BF16)],
                (keep, got),
            )

        def first_step(send, label):
            return swap(send, "fsdp", n_f, 1, "z1_" + label)

        def second_step(own, got, label):
            total = own + got.astype(F32)
            return total[0], swap(total[1].astype(BF16), "fsdp", n_f, 2, "z2_" + label)

        seg_here = lax.dynamic_slice_in_dim(segment_ids[0], place * block, block, 0)
        first = jnp.sum((segment_ids[0][:, None] < seg_here[None, :]).astype(jnp.int32), axis=0)
        token = place * block + jnp.arange(block, dtype=jnp.int32)
        position = (token - first).astype(F32)
        first = (first - place * block + extra * block).reshape(1, block)
        frequency = 10000.0 ** (-2.0 * jnp.arange(HEAD_DIM // 2, dtype=F32) / HEAD_DIM)
        angles = frequency[:, None] * position[None, :]
        cosine, sine = jnp.cos(angles), jnp.sin(angles)

        weight_b, weight_a, gains, normed, a_rows, b_query, payload = call(
            factor_kernel,
            "factors",
            [
                ((width, b_cols), BF16),
                ((n_tp, a_pad, width), BF16),
                ((16, width), F32),
                ((block, width), BF16),
                ((n_tp, a_pad, block), F32),
                ((RANK_Q, HEAD_DIM, block), F32),
                ((kv_rows, block), BF16),
            ],
            (own_x, pack, other_pack, cosine, sine),
        )
        def places(value, step, chosen, label):
            pairs = [(i, i + step) for i in chosen if 0 <= i + step < n_place]
            with jax.named_scope(label):
                return lax.ppermute(value, ("ctx", "tp"), pairs)

        every, odd, even = range(n_place), range(1, n_place, 2), range(0, n_place, 2)
        second = places(payload, 2, every, "x_kv_second")
        third = places(payload, 3, odd, "x_kv_third")
        beside_kv = core(payload, "kv")
        o_own = jnp.concatenate([o_parts, chip(o_parts, "wo")], axis=0)
        second, pair_gu, gu_across = lax.optimization_barrier((second, pair_gu, gu_across))
        gu_rest = ctx(jnp.concatenate([far_gu[None], pair_gu], axis=0), "gate_up_rest")
        dn_parts = [dn_pair, ahead(dn_pair, 1, "down1")]
        beside_second = core(second, "kv_second")
        tied = lax.optimization_barrier((third, second, beside_second, beside_kv, o_own))
        wins = (*tied[:4], payload)
        o_own = tied[4]
        o_other = core(o_own, "wo")
        window = windows * block
        factor_scratch = [
            pltpu.VMEM((pairs, pair_rows, block), F32),
            pltpu.VMEM((windows, heads * KV, block), F32),
        ]
        lse, query, mixed = call(
            attention_kernel,
            "attention",
            [
                ((pairs, 2, block), F32),
                ((n_tp, group, HEAD_DIM, block), BF16),
                ((n_tp, feats, block), BF16),
            ],
            (first, a_rows, b_query, *wins),
            None,
            [
                pltpu.VMEM((windows, kv_rows, block), BF16),
                pltpu.VMEM((window, block), F32),
                pltpu.VMEM((windows, KV, HEAD_DIM, block), F32),
                pltpu.VMEM((group, window, block), F32),
                *factor_scratch,
            ],
        )
        dn_parts[1] = after(dn_parts[1], mixed)
        for s in range(2, n_f):
            dn_parts.append(ahead(dn_parts[-1], 1, "down" + str(s)))
        mid, attn_out, normed_ffn = call(
            project_kernel,
            "project",
            [((block, width), F32), ((block, width), F32), ((block, width), BF16)],
            (own_x, mixed, o_own, o_other, gains),
        )

        near_rows = (normed_ffn, core(normed_ffn, "nf"))
        far_own = chip(normed_ffn, "nf")

        far_own, gu_rest = lax.optimization_barrier((far_own, gu_rest))
        far_own, dn_parts[-1], gu_rest = lax.optimization_barrier(
            (far_own, dn_parts[-1], gu_rest)
        )
        pieces = (own_gu, far_gu, pair_gu, gu_across, gu_rest, *dn_parts)
        far_rows = (far_own, core(far_own, "nf_far"))
        whole_ht = ((3 * hidden, 2 * block), BF16)
        two_sums = [((block, width), F32), ((block, width), BF16)]
        far_ht, far_back, far_back1, weights = call(
            far_kernel,
            "feed_far",
            [whole_ht, *two_sums, ((3 * hidden, width), BF16)],
            (*far_rows, far_cot, *pieces),
            [WHOLE] * 3 + [REMOTE] * len(pieces),
            [pltpu.VMEM((2, block, width), BF16), pltpu.SemaphoreType.DMA((2 * n_piece,))],
            room=12,
        )
        across = (far_back + core(far_back1, "dn_far").astype(F32)).astype(BF16)
        near_ht, near_back, near_back1, near_out, near_out1, far_out, far_out1 = call(
            near_kernel,
            "feed_near",
            [whole_ht, *two_sums * 3],
            (after(near_rows[0], across), near_rows[1], near_cot, weights, far_ht),
            None,
            [pltpu.VMEM((2, block, width), BF16)],
            room=12,
        )
        across = chip(across, "dn")
        beside = core(near_back1, "dn_near")

        grad_args = (near_ht, far_ht, *near_rows, *far_rows, near_cot, far_cot)
        own_d, send_d = call(
            down_grad_kernel,
            "down_grad",
            [((2, n_c, hidden, LANES), F32), ((2, n_c, hidden, LANES), BF16)],
            grad_args,
            room=12,
        )
        got_d = first_step(send_d, "d")
        keep_a, send_a = call(
            gate_up_grad_kernel,
            "gate_up_grad",
            [((2 * hidden, half_width), BF16)] * 2,
            (after(grad_args[0], send_d), *grad_args[1:]),
            room=12,
        )
        got_a = ctx(send_a, "grads_a")
        across = after(across, send_a)

        delta_mid, gain_grad, grad_mixed, keep_o, send_o = call(
            middle_kernel,
            "middle",
            [
                ((block, width), F32),
                ((8, width), F32),
                ((n_tp, feats, block), BF16),
                ((2 * o_rows, width), BF16),
                ((2 * o_rows, width), BF16),
            ],
            (own_cot, near_back, beside, across, mid, gains, o_own, o_other, mixed),
        )
        near_sum = attn_out + near_out + core(after(near_out1, across), "out_near").astype(F32)
        far_sum = far_out + core(after(far_out1, across), "out_far").astype(F32)
        out_send = jnp.stack([far_sum, near_sum]).astype(BF16)
        grad_mixed = after(grad_mixed, out_send)
        rows_got = core(send_o, "go")
        out_got = chip(out_send, "out")
        back_args = (first, a_rows, b_query, *wins, lse, query, grad_mixed)
        sums = [
            ((RANK_Q, HEAD_DIM, block), F32),
            ((windows, KV, HEAD_DIM, block), F32),
            ((windows, heads * KV, block), F32),
        ]
        back_scratch = [
            pltpu.VMEM((windows, kv_rows, block), BF16),
            pltpu.VMEM((window, block), F32),
            pltpu.VMEM((windows, KV, HEAD_DIM, block), F32),
            pltpu.VMEM((2, window, block), F32),
            pltpu.VMEM((2, window, block), F32),
            *factor_scratch,
        ]
        grad_a0, *sums_out = call(
            lambda *refs: attention_back_kernel(0, *refs),
            "attention_back_a",
            [((first_part, pair_rows, block), F32)] + sums,
            back_args,
            None,
            back_scratch,
        )
        sums_out[0], own_d, got_d, _ = lax.optimization_barrier(
            (sums_out[0], own_d, got_d, grad_a0)
        )
        own_d, got_d = second_step(own_d, got_d, "d")
        grad_a1, grad_bq, *sends = call(
            lambda *refs: attention_back_kernel(1, *refs),
            "attention_back_b",
            [
                ((pairs - first_part, pair_rows, block), F32),
                sums[0],
                ((kv_rows, block), BF16),
                ((kv_rows, block), BF16),
                ((kv_rows, block), BF16),
                ((kv_rows, block), F32),
            ],
            (*back_args, *sums_out),
            None,
            [pltpu.VMEM(shape, kind) for shape, kind in sums[1:]] + back_scratch,
        )
        *sends[:3], out_got, rows_got = lax.optimization_barrier((*sends[:3], out_got, rows_got))
        second_got = places(sends[0], -2, every, "x_kv_back_second")
        beside_got = places(sends[1], -1, every, "x_kv_back_beside")
        third_got = places(sends[2], -3, every, "x_kv_back_third")
        own_a, send_a = split(after(keep_a, sends[0]), got_a)
        got_a = first_step(send_a, "a")
        rows_o = keep_o.astype(F32) + after(rows_got, send_a).astype(F32)
        rows_keep, rows_send = rows_o[:o_rows], rows_o[o_rows:].astype(BF16)
        rows_got = chip(rows_send, "go")
        *got, got_d = lax.optimization_barrier((second_got, beside_got, third_got, got_d))
        out_rows = (out_send[::-1].astype(F32) + out_got.astype(F32)).astype(BF16)

        delta, keep0, keep1, send0, send1 = call(
            last_kernel,
            "last",
            [
                ((block, width), BF16),
                *[((2, n_f, pack_rows, LANES), BF16)] * 4,
            ],
            (
                own_x,
                sends[3],
                *got,
                grad_bq,
                grad_a0,
                grad_a1,
                cosine,
                sine,
                weight_b,
                weight_a,
                normed,
                gains,
                delta_mid,
                gain_grad,
            ),
            [WHOLE] * 16,
            [
                pltpu.VMEM((width, b_cols), F32),
                pltpu.VMEM((n_tp, a_pad, width), F32),
                pltpu.VMEM((block, width), F32),
                pltpu.VMEM((8, width), F32),
            ],
        )

        part_send = (keep1.astype(F32) + core(send1, "gp").astype(F32)).astype(BF16)
        total_d = own_d + got_d.astype(F32)
        part_send, got_a = lax.optimization_barrier((part_send, got_a))
        part_got = ctx(part_send, "gp")
        own_a, got_a = second_step(own_a, got_a, "a")
        part = keep0.astype(F32) + core(after(send0, part_send), "gp_near").astype(F32)
        rows_got, part = lax.optimization_barrier((rows_got, part))
        rows_o = rows_keep + rows_got.astype(F32)
        rows_keep, rows_send = rows_o[:, :half_width], rows_o[:, half_width:].astype(BF16)
        across_delta = chip(delta, "delta")
        rows_go = ctx(rows_send, "go")
        out_rows = after(out_rows, part_send)
        out_beside = core(out_rows, "out_rows")
        block_out = add_rows(
            resid_in, (out_rows[0], out_rows[1], out_beside[0], out_beside[1]), True
        )
        part_got, across_delta = lax.optimization_barrier((part_got, across_delta, block_out))[:2]
        part = part + part_got.astype(F32)
        part_send = part[1].astype(BF16)
        part_got = chip(part_send, "gp")
        across_delta = after(across_delta, part_send)
        beside_delta = core(after(delta, part_send), "delta")
        got_last = ctx(after(total_d[1], part_send).astype(BF16), "d")
        part_got, rows_go, got_a = lax.optimization_barrier((part_got, rows_go, got_a))
        part = part[0] + part_got.astype(F32)
        rows_o = rows_keep + rows_go.astype(F32)
        part = [
            jnp.concatenate([part[s], rows_o[:, s * LANES : (s + 1) * LANES]], axis=0)
            for s in range(n_f)
        ]
        is_even_f = f_index % 2 == 0
        part_send = [
            jnp.where(is_even_f, part[3], part[1]),
            jnp.where(is_even_f, part[1], part[3]),
        ]
        part_send = jnp.stack(part_send).astype(BF16)
        part_own, part_got = second_step(
            jnp.stack([part[0], part[2]]), first_step(part_send, "gp"), "gp"
        )
        across_delta = after(across_delta, part_send)
        resid_grad = add_rows(
            cotangent,
            (delta, across_delta, beside_delta, core(across_delta, "delta_far")),
            False,
        )
        part_got, got_last = lax.optimization_barrier((part_got, got_last, resid_grad))[:2]
        grad_down = total_d[0] + got_last.astype(F32)
        grad_gate_up = (own_a + got_a.astype(F32)).reshape(1, 2, hidden, fc_cols)
        part_b, part_a, part_g0, part_g1, grad_out = call(
            unpack_kernel,
            "unpack",
            [
                ((1, b_rows, b_cols), F32),
                ((1, a_cols, fc_cols), F32),
                ((1, gain_part), F32),
                ((1, gain_part), F32),
                ((1, o_rows, LANES), F32),
            ],
            (part_own, part_got),
        )
        return (
            block_out,
            resid_grad,
            part_a.transpose(0, 2, 1),
            part_b,
            grad_out,
            grad_gate_up.transpose(0, 1, 3, 2),
            grad_down[None],
            part_g0,
            part_g1,
        )

    return shards


def make_shards(mesh):
    fused, general = make_fused(mesh), make_general(mesh)
    fits = mesh.shape["fsdp"] == 4 and mesh.shape["ctx"] == 2 and mesh.shape["tp"] == 4

    def shards(*args):
        return (fused if fits and args[7].shape[2] == LANES else general)(*args)

    return shards


def solution(mesh):
    return jax.shard_map(
        make_shards(mesh),
        mesh=mesh,
        in_specs=(
            P("fsdp", "ctx", None),
            P("fsdp", None),
            P("fsdp", "ctx", None),
            P(None, ("fsdp", "ctx"), "tp"),
            P(None, ("fsdp", "ctx", "tp"), None),
            P(None, "tp", ("fsdp", "ctx")),
            P(None, None, ("fsdp", "ctx"), "tp"),
            P(None, "tp", ("fsdp", "ctx")),
            P(None, ("fsdp", "ctx", "tp")),
            P(None, ("fsdp", "ctx", "tp")),
        ),
        out_specs=(
            P("fsdp", "ctx", None),
            P("fsdp", "ctx", None),
            P(None, ("fsdp", "ctx"), "tp"),
            P(None, ("fsdp", "ctx", "tp"), None),
            P(None, "tp", ("fsdp", "ctx")),
            P(None, None, ("fsdp", "ctx"), "tp"),
            P(None, "tp", ("fsdp", "ctx")),
            P(None, ("fsdp", "ctx", "tp")),
            P(None, ("fsdp", "ctx", "tp")),
        ),
        check_vma=False,
    )
```

```python
import math

import jax
import jax.numpy as jnp
from jax import lax
from jax.experimental import pallas as pl
from jax.experimental.pallas import tpu as pltpu
from jax.sharding import PartitionSpec as P

HEAD_DIM = 64
RANK_Q = 6
RANK_KV = 2
RANKS = 10
KV = 2 * RANK_KV
MOST_DOC = 768
EPSILON = 1e-05
LANES = 128
BF16 = jnp.bfloat16
F32 = jnp.float32
MASKED = -1e30


def inverse_rms(values):
    return lax.rsqrt(jnp.mean(values * values, axis=-1, keepdims=True) + EPSILON)


def norm_back(grad_value, values, inverse, gain):
    scaled = grad_value * gain
    normal = values * inverse
    return inverse * (scaled - normal * jnp.mean(scaled * normal, axis=-1, keepdims=True))


def dot(left, right, dims):
    return lax.dot_general(left, right, (dims, ((), ())), preferred_element_type=F32)


def shift(value, axes, size, step, label="shift"):
    with jax.named_scope(label):
        return lax.ppermute(value, axes, [(i, (i + step) % size) for i in range(size)])


def swap(value, axis, size, bit, label="swap"):
    with jax.named_scope(label):
        return lax.ppermute(value, axis, [(i, i ^ bit) for i in range(size)])


def gather_direct(value, axis, size):
    me = lax.axis_index(axis)
    parts = [(me, value)]
    for step in range(1, size):
        parts.append(((me - step) % size, shift(value, axis, size, step)))
    out = jnp.zeros((size,) + value.shape, value.dtype)
    for place, part in parts:
        out = lax.dynamic_update_slice(out, part[None], (place,) + (0,) * value.ndim)
    return out


def gather_pair(value, axis, size, bit):
    mine = (lax.axis_index(axis) // bit) % 2 == 0
    other = swap(value, axis, size, bit)
    return jnp.stack([jnp.where(mine, value, other), jnp.where(mine, other, value)])


def after(value, *others):
    return lax.optimization_barrier((value,) + others)[0]


def take(value, index):
    return lax.dynamic_index_in_dim(value, index, 0, keepdims=False)


def scatter_direct(value, axis, size):
    me = lax.axis_index(axis)
    got = [
        shift(take(value, (me + step) % size), axis, size, step) for step in range(1, size)
    ]
    total = take(value, me).astype(F32)
    for part in got:
        total = total + part.astype(F32)
    return total


def scatter_pair(value, axis, size, bit):
    mine = (lax.axis_index(axis) // bit) % 2
    got = swap(take(value, 1 - mine).astype(BF16), axis, size, bit)
    return take(value, mine).astype(F32) + got.astype(F32)


def attention_mask(first_ref, window, block):
    start = first_ref[...]
    place = lax.broadcasted_iota(jnp.int32, (window, block), 0)
    query_place = lax.broadcasted_iota(jnp.int32, (window, block), 1) + (window - block)
    return jnp.where((place >= start) & (place <= query_place), 0.0, MASKED)


def head_rows(wa_ref, wide_ref, head):
    factors = wa_ref[head].astype(F32)
    key_rows = (factors[0:1] * wide_ref[0] + factors[1:2] * wide_ref[1]) * (1.0 / RANK_KV)
    value_rows = (factors[2:3] * wide_ref[2] + factors[3:4] * wide_ref[3]) * (1.0 / RANK_KV)
    return factors, key_rows.astype(BF16), value_rows.astype(BF16)


def forward_kernel(
    first_ref, a_ref, bq_ref, wa_ref, wb_ref, mixed_ref, lse_ref, q_ref, bias_ref, wide_ref, s_ref
):
    heads = a_ref.shape[0]
    window, block = bias_ref.shape
    bias_ref[...] = attention_mask(first_ref, window, block)
    wide_ref[...] = wb_ref[...].astype(F32)
    spans = [pl.ds(j * block, block) for j in range(window // block)]

    def one_head(head, carry):
        factors = a_ref[head]
        query = factors[0:1] * bq_ref[0]
        for r in range(1, RANK_Q):
            query = query + factors[r : r + 1] * bq_ref[r]
        query = (query * (1.0 / RANK_Q)).astype(BF16) * jnp.asarray(HEAD_DIM**-0.5, BF16)
        q_ref[head] = query
        _, key_rows, value_rows = head_rows(wa_ref, wide_ref, head)
        top = jnp.full((1, block), MASKED, F32)
        for j, span in enumerate(spans):
            keys = key_rows[:, j * block : (j + 1) * block]
            scores = dot(keys, query, ((0,), (0,))) + bias_ref[span, :]
            s_ref[span, :] = scores
            top = jnp.maximum(top, jnp.max(scores, axis=0, keepdims=True))
        total = jnp.zeros((1, block), F32)
        for span in spans:
            weight = jnp.exp(s_ref[span, :] - top)
            s_ref[span, :] = weight
            total = total + jnp.sum(weight, axis=0, keepdims=True)
        lse_ref[head] = top + jnp.log(total)
        scale = 1.0 / total
        mixed = jnp.zeros((HEAD_DIM, block), F32)
        for j, span in enumerate(spans):
            probs = (s_ref[span, :] * scale).astype(BF16)
            mixed = mixed + dot(
                value_rows[:, j * block : (j + 1) * block], probs, ((1,), (0,))
            )
        mixed_ref[head] = mixed.astype(BF16)
        return carry

    lax.fori_loop(0, heads, one_head, 0)


def backward_kernel(
    first_ref,
    a_ref,
    bq_ref,
    wa_ref,
    wb_ref,
    lse_ref,
    q_ref,
    go_ref,
    ga_ref,
    gbq_ref,
    gwa_ref,
    gwb_ref,
    bias_ref,
    wide_ref,
    p_ref,
    dp_ref,
):
    heads = a_ref.shape[0]
    window, block = bias_ref.shape
    bias_ref[...] = attention_mask(first_ref, window, block)
    wide_ref[...] = wb_ref[...].astype(F32)
    gbq_ref[...] = jnp.zeros_like(gbq_ref)
    gwb_ref[...] = jnp.zeros_like(gwb_ref)
    count = window // block
    spans = [pl.ds(j * block, block) for j in range(count)]

    def one_head(head, carry):
        factors, key_rows, value_rows = head_rows(wa_ref, wide_ref, head)
        query = q_ref[head]
        grad_out = go_ref[head]
        lse = lse_ref[head]
        inner = jnp.zeros((1, block), F32)
        for j, span in enumerate(spans):
            cut = slice(j * block, (j + 1) * block)
            scores = dot(key_rows[:, cut], query, ((0,), (0,))) + bias_ref[span, :]
            probs = jnp.exp(scores - lse)
            grad_probs = dot(value_rows[:, cut], grad_out, ((0,), (0,)))
            p_ref[span, :] = probs
            dp_ref[span, :] = grad_probs
            inner = inner + jnp.sum(probs * grad_probs, axis=0, keepdims=True)
        grad_query = jnp.zeros((HEAD_DIM, block), F32)
        for j, span in enumerate(spans):
            cut = slice(j * block, (j + 1) * block)
            probs = p_ref[span, :]
            grad_scores = (probs * (dp_ref[span, :] - inner)).astype(BF16)
            grad_query = grad_query + dot(key_rows[:, cut], grad_scores, ((1,), (0,)))
            grad_keys = dot(query, grad_scores, ((1,), (1,))) * (1.0 / RANK_KV)
            grad_values = dot(grad_out, probs.astype(BF16), ((1,), (1,))) * (1.0 / RANK_KV)
            rows = []
            for r in range(KV):
                grad = grad_keys if r < RANK_KV else grad_values
                rows.append(jnp.sum(grad * wide_ref[r, :, span], axis=0, keepdims=True))
                gwb_ref[r, :, span] += factors[r : r + 1, cut] * grad
            gwa_ref[head, :, span] = jnp.concatenate(rows, axis=0)
        grad_query = grad_query * (HEAD_DIM**-0.5 / RANK_Q)
        own = a_ref[head]
        rows = []
        for r in range(RANK_Q):
            rows.append(jnp.sum(grad_query * bq_ref[r], axis=0, keepdims=True))
            gbq_ref[r] += own[r : r + 1] * grad_query
        ga_ref[head] = jnp.concatenate(rows, axis=0)
        return carry

    lax.fori_loop(0, heads, one_head, 0)


VMEM_LIMIT = 56 * 1024 * 1024


def whole_specs(count):
    return [pl.BlockSpec(memory_space=pltpu.VMEM)] * count


def attend_forward(first, a_rows, b_query, win_a, win_b):
    heads, _, block = a_rows.shape
    window = win_a.shape[-1]
    return pl.pallas_call(
        forward_kernel,
        out_shape=(
            jax.ShapeDtypeStruct((heads, HEAD_DIM, block), BF16),
            jax.ShapeDtypeStruct((heads, 1, block), F32),
            jax.ShapeDtypeStruct((heads, HEAD_DIM, block), BF16),
        ),
        in_specs=whole_specs(5),
        out_specs=tuple(whole_specs(3)),
        scratch_shapes=[
            pltpu.VMEM((window, block), F32),
            pltpu.VMEM((KV, HEAD_DIM, window), F32),
            pltpu.VMEM((window, block), F32),
        ],
        compiler_params=pltpu.CompilerParams(vmem_limit_bytes=VMEM_LIMIT),
        name="attend_forward",
    )(first, a_rows, b_query, win_a, win_b)


def attend_backward(first, a_rows, b_query, win_a, win_b, lse, query, grad_mixed):
    heads, _, block = a_rows.shape
    window = win_a.shape[-1]
    return pl.pallas_call(
        backward_kernel,
        out_shape=(
            jax.ShapeDtypeStruct((heads, RANK_Q, block), F32),
            jax.ShapeDtypeStruct((RANK_Q, HEAD_DIM, block), F32),
            jax.ShapeDtypeStruct((heads, KV, window), F32),
            jax.ShapeDtypeStruct((KV, HEAD_DIM, window), F32),
        ),
        in_specs=whole_specs(8),
        out_specs=tuple(whole_specs(4)),
        scratch_shapes=[
            pltpu.VMEM((window, block), F32),
            pltpu.VMEM((KV, HEAD_DIM, window), F32),
            pltpu.VMEM((window, block), F32),
            pltpu.VMEM((window, block), F32),
        ],
        compiler_params=pltpu.CompilerParams(vmem_limit_bytes=VMEM_LIMIT),
        name="attend_backward",
    )(first, a_rows, b_query, win_a, win_b, lse, query, grad_mixed)


def rotate(rows, cosine, sine):
    half = HEAD_DIM // 2
    lower, upper = rows[:, :half], rows[:, half:]
    return jnp.concatenate(
        [lower * cosine - upper * sine, lower * sine + upper * cosine], axis=1
    )


def make_general(mesh):
    n_f, n_c, n_tp = mesh.shape["fsdp"], mesh.shape["ctx"], mesh.shape["tp"]
    n_hi, n_lo = 2, n_tp // 2

    def shards(
        resid_in,
        segment_ids,
        cotangent,
        w_factor_a,
        w_factor_b,
        w_out,
        w_gate_up,
        w_down,
        attn_gains,
        ffn_gains,
    ):
        seq_count, local_len, width = resid_in.shape
        assert seq_count == 1 and w_factor_a.shape[0] == 1 and n_lo == 2
        full_len = segment_ids.shape[1]
        block = local_len // n_tp
        extra = -(-(MOST_DOC - 1) // block)
        window = (extra + 1) * block
        a_cols = w_factor_a.shape[2]
        heads = n_tp * a_cols // RANKS
        b_cols = w_factor_b.shape[2]
        b_rows = w_factor_b.shape[1]
        b_parts = b_cols // LANES
        fc_cols = w_down.shape[2]
        hidden = w_down.shape[1]
        o_rows = w_out.shape[1]

        f_index, c_index, t_index = (
            lax.axis_index("fsdp"),
            lax.axis_index("ctx"),
            lax.axis_index("tp"),
        )
        hi, lo = t_index // 2, t_index % 2
        place = c_index * n_tp + t_index
        n_place = n_c * n_tp

        gains = jnp.concatenate([attn_gains, ffn_gains], axis=1).astype(BF16)
        gain_count = gains.shape[1]
        gain_rows = 16 * (-(-gain_count // (16 * LANES)))
        gains = jnp.pad(gains.reshape(-1), (0, gain_rows * LANES - gain_count))
        b_shard = w_factor_b[0].astype(BF16).reshape(b_rows, b_parts, LANES)
        a_shard = w_factor_a[0].astype(BF16).T
        pack = jnp.concatenate(
            [
                b_shard.transpose(1, 0, 2).reshape(-1, LANES),
                a_shard.reshape(-1, LANES),
                gains.reshape(-1, LANES),
            ],
            axis=0,
        )
        n_b = b_parts * b_rows
        n_a = a_cols * fc_cols // LANES
        pack = gather_direct(pack, "fsdp", n_f)
        after_pack = pack
        pack = gather_pair(pack, "ctx", n_c, 1)
        pack = gather_pair(pack, "tp", n_tp, 2)
        pack = gather_pair(pack, "tp", n_tp, 1)
        pack = pack.transpose(3, 2, 1, 0, 4, 5)
        weight_b = pack[:, :, :, :, :n_b].reshape(-1, b_parts, b_rows, LANES)
        weight_b = weight_b.transpose(0, 2, 1, 3).reshape(width, b_cols)
        weight_a = pack[:, :, :, :, n_b : n_b + n_a].reshape(n_f, n_c, n_tp, a_cols, fc_cols)
        weight_a = weight_a.transpose(2, 3, 0, 1, 4).reshape(n_tp * a_cols, width)
        gains_all = pack[:, :, :, :, n_b + n_a :].reshape(-1, gain_rows * LANES)[:, :gain_count]
        gains_all = gains_all.reshape(-1, 2, gain_count // 2).transpose(1, 0, 2)
        gains_all = gains_all.reshape(2, width).astype(F32)
        gain_attn, gain_ffn = gains_all[0:1], gains_all[1:2]

        big = jnp.concatenate(
            [
                w_gate_up[0, 0].astype(BF16).T,
                w_gate_up[0, 1].astype(BF16).T,
                w_down[0].astype(BF16),
                w_out[0].astype(BF16),
            ],
            axis=0,
        )
        big, _ = lax.optimization_barrier((big, after_pack))
        big = gather_direct(big, "fsdp", n_f)
        big = gather_pair(big, "ctx", n_c, 1)
        big = big.transpose(2, 1, 0, 3).reshape(-1, width)
        weight_g = big[:hidden]
        weight_u = big[hidden : 2 * hidden]
        weight_d = big[2 * hidden : 3 * hidden]
        weight_o = gather_pair(big[3 * hidden :], "tp", n_tp, 2)
        weight_o = gather_pair(weight_o, "tp", n_tp, 1)
        weight_o = weight_o.transpose(1, 0, 2, 3).reshape(n_tp * o_rows, width)

        seg_here = lax.dynamic_slice_in_dim(segment_ids[0], place * block, block, 0)
        first = jnp.sum((segment_ids[0][:, None] < seg_here[None, :]).astype(jnp.int32), axis=0)
        token = place * block + jnp.arange(block, dtype=jnp.int32)
        position = (token - first).astype(F32)
        first = (first - place * block + extra * block).reshape(1, block)
        frequency = 10000.0 ** (
            -2.0 * jnp.arange(HEAD_DIM // 2, dtype=F32) / HEAD_DIM
        )
        angles = frequency[:, None] * position[None, :]
        cosine, sine = jnp.cos(angles)[None], jnp.sin(angles)[None]

        stream = resid_in[0].reshape(n_tp, block, width)
        own = take(stream, t_index)
        inverse_attn = inverse_rms(own)
        normed = (own * inverse_attn * gain_attn).astype(BF16)
        a_rows = dot(weight_a, normed, ((1,), (1,))).reshape(heads, RANKS, block)
        b_raw = dot(weight_b, normed, ((0,), (1,))).reshape(RANKS, HEAD_DIM, block)
        b_rot = rotate(b_raw[: RANK_Q + RANK_KV], cosine, sine)
        b_query = b_rot[:RANK_Q]
        b_kv = jnp.concatenate([b_rot[RANK_Q:], b_raw[RANK_Q + RANK_KV :]], axis=0)
        payload = jnp.concatenate(
            [
                b_kv.reshape(KV * HEAD_DIM, block),
                a_rows[:, RANK_Q:].reshape(heads * KV, block),
            ],
            axis=0,
        ).astype(BF16)
        around = [
            lax.ppermute(
                payload, ("ctx", "tp"), [(i, i + step) for i in range(n_place - step)]
            )
            for step in range(extra, 0, -1)
        ]
        win = jnp.concatenate(around + [payload], axis=1)
        win_b = win[: KV * HEAD_DIM].reshape(KV, HEAD_DIM, window)
        win_a = win[KV * HEAD_DIM :].reshape(heads, KV, window)

        mixed, lse, query = attend_forward(first, a_rows, b_query, win_a, win_b)
        mixed = mixed.reshape(heads * HEAD_DIM, block)
        attn_out = dot(mixed, weight_o, ((0,), (0,)))
        mid = own + attn_out
        inverse_ffn = inverse_rms(mid)
        normed_ffn = (mid * inverse_ffn * gain_ffn).astype(BF16)

        near_rows = gather_pair(normed_ffn, "tp", n_tp, 1)
        far_rows = gather_pair(swap(normed_ffn, "tp", n_tp, 2), "tp", n_tp, 1)
        grad_all = cotangent[0].reshape(n_hi, n_lo * block, width)

        def half(rows, grad_rows):
            rows = rows.reshape(n_lo * block, width)
            gate = dot(rows, weight_g, ((1,), (1,)))
            up = dot(rows, weight_u, ((1,), (1,)))
            grad_act = dot(grad_rows, weight_d, ((1,), (1,)))
            squash = jax.nn.sigmoid(gate)
            act = (gate * squash * up).astype(BF16)
            grad_gate = (grad_act * up * squash * (1.0 + gate * (1.0 - squash))).astype(BF16)
            grad_up = (grad_act * gate * squash).astype(BF16)
            back = dot(grad_gate, weight_g, ((1,), (0,))) + dot(grad_up, weight_u, ((1,), (0,)))
            ahead = dot(act, weight_d, ((1,), (0,)))
            both = lambda v: v.reshape(n_lo, block, width)
            return rows, act, grad_gate, grad_up, both(back), both(ahead)

        grad_near = take(grad_all, hi).astype(BF16)
        grad_far = take(grad_all, 1 - hi).astype(BF16)
        near = half(near_rows, grad_near)
        far = half(far_rows, grad_far)
        back_far = scatter_pair(far[4], "tp", n_tp, 1).astype(BF16)
        back_far = swap(back_far, "tp", n_tp, 2)
        grad_normed_ffn = scatter_pair(near[4], "tp", n_tp, 1) + back_far.astype(F32)
        ahead_far = scatter_pair(far[5], "tp", n_tp, 1).astype(BF16)
        ahead_far = swap(ahead_far, "tp", n_tp, 2)
        ffn_out = scatter_pair(near[5], "tp", n_tp, 1) + ahead_far.astype(F32)

        def spread(value):
            beside = swap(value, "tp", n_tp, 1)
            across = swap(value, "tp", n_tp, 2)
            diagonal = swap(across, "tp", n_tp, 1)
            out = jnp.zeros((n_tp,) + value.shape, value.dtype)
            for bit, part in enumerate((value, beside, across, diagonal)):
                out = lax.dynamic_update_slice(out, part[None], (t_index ^ bit, 0, 0))
            return out.reshape(local_len, width).astype(F32)

        block_out = resid_in + spread((attn_out + ffn_out).astype(BF16))[None]

        def columns(value, which):
            value = value.reshape(value.shape[0], n_f, n_c, fc_cols)
            value = lax.dynamic_index_in_dim(value, which, 2, keepdims=False)
            return value.reshape(value.shape[0], n_f * fc_cols)

        rows_all = jnp.concatenate([near[0], far[0]], axis=0)
        act_all = jnp.concatenate([near[1], far[1]], axis=0)
        gate_all = jnp.concatenate([near[2], far[2]], axis=0)
        up_all = jnp.concatenate([near[3], far[3]], axis=0)
        cot_all = jnp.concatenate([grad_near, grad_far], axis=0)

        def big_grads(which):
            rows_cut = columns(rows_all, which)
            cot_cut = columns(cot_all, which)
            return jnp.concatenate(
                [
                    dot(gate_all, rows_cut, ((0,), (0,))),
                    dot(up_all, rows_cut, ((0,), (0,))),
                    dot(act_all, cot_cut, ((0,), (0,))),
                ],
                axis=0,
            )

        def over_fc(send, keep):
            total = keep + swap(send.astype(BF16), "ctx", n_c, 1).astype(F32)
            total = total.astype(BF16).reshape(-1, n_f, fc_cols).transpose(1, 0, 2)
            return scatter_direct(total, "fsdp", n_f)

        grad_big = over_fc(big_grads(1 - c_index), big_grads(c_index))
        grad_gate_w = grad_big[:hidden].T
        grad_up_w = grad_big[hidden : 2 * hidden].T
        grad_down_w = grad_big[2 * hidden :]

        own_cot = take(cotangent[0].reshape(n_tp, block, width), t_index)
        gain_grad_ffn = jnp.sum(grad_normed_ffn * mid * inverse_ffn, axis=0)
        delta_mid = norm_back(grad_normed_ffn, mid, inverse_ffn, gain_ffn)
        grad_attn = (own_cot + delta_mid).astype(BF16)
        grad_out = dot(mixed, grad_attn, ((1,), (0,))).reshape(n_hi, n_lo, o_rows, width)
        grad_out = scatter_pair(grad_out.transpose(1, 0, 2, 3), "tp", n_tp, 1)
        grad_out = scatter_pair(grad_out, "tp", n_tp, 2)
        grad_out = over_fc(columns(grad_out, 1 - c_index), columns(grad_out, c_index))

        grad_mixed = dot(weight_o, grad_attn, ((1,), (1,))).astype(BF16)
        ga_q, gb_q, gw_a, gw_b = attend_backward(
            first,
            a_rows,
            b_query,
            win_a,
            win_b,
            lse,
            query,
            grad_mixed.reshape(heads, HEAD_DIM, block),
        )
        gw = jnp.concatenate(
            [gw_b.reshape(KV * HEAD_DIM, window), gw_a.reshape(heads * KV, window)], axis=0
        )
        total = gw[:, extra * block :]
        for step in range(1, extra + 1):
            part = gw[:, (extra - step) * block : (extra - step + 1) * block].astype(BF16)
            part = lax.ppermute(
                part, ("ctx", "tp"), [(i + step, i) for i in range(n_place - step)]
            )
            total = total + part.astype(F32)
        gb_kv = total[: KV * HEAD_DIM].reshape(KV, HEAD_DIM, block)
        ga_kv = total[KV * HEAD_DIM :].reshape(heads, KV, block)
        grad_b = jnp.concatenate(
            [
                rotate(jnp.concatenate([gb_q, gb_kv[:RANK_KV]], axis=0), cosine, -sine),
                gb_kv[RANK_KV:],
            ],
            axis=0,
        )
        grad_b = grad_b.reshape(b_cols, block).astype(BF16)
        grad_a = jnp.concatenate([ga_q, ga_kv], axis=1).reshape(heads * RANKS, block).astype(BF16)
        grad_normed = dot(grad_a, weight_a, ((0,), (0,))) + dot(grad_b, weight_b, ((0,), (1,)))
        gain_grad_attn = jnp.sum(grad_normed * own * inverse_attn, axis=0)
        delta = delta_mid + norm_back(grad_normed, own, inverse_attn, gain_attn)
        resid_grad = cotangent + spread(delta.astype(BF16))[None]

        grad_wa = dot(grad_a, normed, ((1,), (0,))).astype(BF16)
        grad_wa = grad_wa.reshape(n_hi, n_lo, a_cols, n_f, n_c, fc_cols)
        grad_wa = grad_wa.transpose(1, 0, 4, 3, 2, 5).reshape(n_lo, n_hi, n_c, n_f, n_a, LANES)
        grad_wb = jnp.einsum(
            "pkt,td->pdk",
            grad_b.reshape(b_parts, LANES, block),
            normed,
            preferred_element_type=F32,
        ).astype(BF16)
        grad_wb = grad_wb.reshape(b_parts, n_f, n_c, n_hi, n_lo, b_rows, LANES)
        grad_wb = grad_wb.transpose(4, 3, 2, 1, 0, 5, 6)
        grad_wb = grad_wb.reshape(n_lo, n_hi, n_c, n_f, n_b, LANES)
        gain_grads = jnp.stack([gain_grad_attn, gain_grad_ffn]).astype(BF16)
        gain_grads = gain_grads.reshape(2, n_f, n_c, n_hi, n_lo, gain_count // 2)
        gain_grads = gain_grads.transpose(4, 3, 2, 1, 0, 5).reshape(
            n_lo, n_hi, n_c, n_f, gain_count
        )
        gain_grads = jnp.pad(
            gain_grads, [(0, 0)] * 4 + [(0, gain_rows * LANES - gain_count)]
        ).reshape(n_lo, n_hi, n_c, n_f, gain_rows, LANES)
        pack = jnp.concatenate([grad_wb, grad_wa, gain_grads], axis=4)
        pack = scatter_pair(pack, "tp", n_tp, 1)
        pack = scatter_pair(pack, "tp", n_tp, 2)
        pack = scatter_pair(pack, "ctx", n_c, 1).astype(BF16)
        pack = scatter_direct(pack, "fsdp", n_f)
        part_b = pack[:n_b].reshape(b_parts, b_rows, LANES).transpose(1, 0, 2)
        part_b = part_b.reshape(1, b_rows, b_cols)
        part_a = pack[n_b : n_b + n_a].reshape(a_cols, fc_cols).T[None]
        part_gain = pack[n_b + n_a :].reshape(-1)[:gain_count].reshape(2, 1, gain_count // 2)
        return (
            block_out,
            resid_grad,
            part_a,
            part_b,
            grad_out[None],
            jnp.stack([grad_gate_w, grad_up_w])[None],
            grad_down_w[None],
            part_gain[0],
            part_gain[1],
        )

    return shards


def rotated(rows, cosine, sine):
    half = HEAD_DIM // 2
    lower, upper = rows[:half], rows[half:]
    return jnp.concatenate([lower * cosine - upper * sine, lower * sine + upper * cosine], axis=0)


def make_fused(mesh):
    n_f, n_c, n_tp = mesh.shape["fsdp"], mesh.shape["ctx"], mesh.shape["tp"]
    n_piece = n_f * n_c
    AT_TP = n_piece
    AT_ME = n_piece + n_tp

    def shards(
        resid_in,
        segment_ids,
        cotangent,
        w_factor_a,
        w_factor_b,
        w_out,
        w_gate_up,
        w_down,
        attn_gains,
        ffn_gains,
    ):
        _, local_len, width = resid_in.shape
        block = local_len // n_tp
        extra = -(-(MOST_DOC - 1) // block)
        windows = extra + 1
        a_cols = w_factor_a.shape[2]
        group = a_cols // RANKS
        heads = n_tp * group
        feats = group * HEAD_DIM
        a_pad = 16 * (-(-a_cols // 16))
        b_rows, b_cols = w_factor_b.shape[1:]
        b_parts = b_cols // LANES
        n_b = b_parts * b_rows
        pack_rows = n_b + a_pad + 16
        fc_cols = w_down.shape[2]
        hidden = w_down.shape[1]
        o_rows = w_out.shape[1]
        gain_part = attn_gains.shape[1]
        kv_b = KV * HEAD_DIM
        kv_rows = kv_b + heads * KV
        half_width = width // n_c
        pairs = heads // 2
        first_part = 5 * pairs // 8
        pair_rows = 8 * (-(-2 * RANKS // 8))
        early = 2 * hidden + 16 * (hidden // 64)
        assert n_f == 4 and fc_cols == LANES and o_rows == feats and n_tp == 4 and n_c == 2

        f_index, c_index, t_index = (
            lax.axis_index("fsdp"),
            lax.axis_index("ctx"),
            lax.axis_index("tp"),
        )
        place = c_index * n_tp + t_index
        n_place = n_c * n_tp
        columns = [
            ((f_index - s) % n_f) * n_c + (c_index if near == 0 else 1 - c_index)
            for near in range(n_c)
            for s in range(n_f)
        ]
        members = [t_index ^ (lo + 2 * hi) for lo in range(2) for hi in range(2)]
        beside_shift = jnp.where(f_index % 2 == 0, n_f - 1, 1)
        meta = jnp.stack(columns + members + [t_index, f_index, beside_shift]).astype(jnp.int32)

        resid_in = pltpu.with_memory_space_constraint(resid_in, pltpu.HBM)
        cotangent = pltpu.with_memory_space_constraint(cotangent, pltpu.HBM)

        def column(meta_ref, j):
            return pl.ds(pl.multiple_of(meta_ref[j] * LANES, LANES), LANES)

        def member(meta_ref, lo, hi):
            return meta_ref[AT_TP + 2 * lo + hi]

        def to_arrival(meta_ref, load):
            return jnp.concatenate([load(column(meta_ref, j)) for j in range(n_piece)], axis=1)

        WHOLE = pl.BlockSpec(memory_space=pltpu.VMEM)
        REMOTE = pl.BlockSpec(memory_space=pl.ANY)

        def call(
            kernel, name, outs, args, specs=None, scratch=(), grid=(1,), out_specs=None, room=4,
            scalars=meta,
        ):
            held = 0
            for arg, spec in zip((*args, *args[:1]), (specs or []) + (out_specs or [])):
                if spec.block_shape:
                    held += 2 * math.prod(spec.block_shape) * arg.dtype.itemsize
            for item in scratch:
                if hasattr(item, "shape") and item.memory_space == pltpu.VMEM:
                    held += math.prod(item.shape) * jnp.dtype(item.dtype).itemsize
            limit = min(held + room * 2**20, VMEM_LIMIT)
            return pl.pallas_call(
                kernel,
                out_shape=[jax.ShapeDtypeStruct(s, d) for s, d in outs],
                grid_spec=pltpu.PrefetchScalarGridSpec(
                    num_scalar_prefetch=1,
                    grid=grid,
                    in_specs=specs or [WHOLE] * len(args),
                    out_specs=out_specs or [WHOLE] * len(outs),
                    scratch_shapes=list(scratch),
                ),
                compiler_params=pltpu.CompilerParams(vmem_limit_bytes=limit),
                name=name,
            )(scalars, *args)


        def pack_kernel(meta_ref, b_ref, a_ref, g0_ref, g1_ref, out_ref):
            for k in range(b_parts):
                out_ref[k * b_rows : (k + 1) * b_rows, :] = b_ref[
                    0, :, k * LANES : (k + 1) * LANES
                ].astype(BF16)
            a_shard = jnp.concatenate([a_ref[0], jnp.zeros((a_pad - a_cols, LANES), F32)], axis=0)
            out_ref[n_b : n_b + a_pad, :] = a_shard.astype(BF16)
            both = jnp.concatenate([g0_ref[...], g1_ref[...]], axis=0)
            both = jnp.concatenate([both, jnp.zeros((6, gain_part), F32)], axis=0)
            both = jnp.concatenate([both, jnp.zeros((8, LANES - gain_part), F32)], axis=1)
            both = pltpu.roll(both, meta_ref[AT_ME] * gain_part, 1)
            both = jnp.concatenate([both, jnp.zeros((8, LANES), F32)], axis=0)
            out_ref[n_b + a_pad :, :] = both.astype(BF16)

        def big_kernel(meta_ref, gu_ref, d_ref, gu_out_ref, d_out_ref):
            for k in range(2):
                gu_out_ref[k * hidden : (k + 1) * hidden, :] = gu_ref[0, k].astype(BF16)
            gu_out_ref[2 * hidden :, :] = d_ref[0, : early - 2 * hidden, :].astype(BF16)
            d_out_ref[...] = d_ref[0, early - 2 * hidden :, :].astype(BF16)

        def factor_kernel(
            meta_ref,
            x_ref,
            p0_ref,
            p1_ref,
            cos_ref,
            sin_ref,
            wb_ref,
            wa_ref,
            gain_ref,
            normed_ref,
            a_ref,
            bq_ref,
            pay_ref,
        ):
            gain_ref[...] = jnp.zeros_like(gain_ref)
            for lo, hi in ((0, 0), (0, 1), (1, 0), (1, 1)):
                part = (p0_ref, p1_ref)[lo]
                tp = member(meta_ref, lo, hi)
                for near in range(n_c):
                    for s in range(n_f):
                        j = near * n_f + s
                        lanes = column(meta_ref, j)
                        row = pl.multiple_of((meta_ref[j] * n_tp + tp) * b_rows, b_rows)
                        for k in range(b_parts):
                            wb_ref[pl.ds(row, b_rows), k * LANES : (k + 1) * LANES] = part[
                                near, hi, s, k * b_rows : (k + 1) * b_rows, :
                            ]
                        wa_ref[tp, :, lanes] = part[near, hi, s, n_b : n_b + a_pad, :]
                        gain_ref[:, lanes] += part[near, hi, s, n_b + a_pad :, :].astype(F32)
            x = x_ref[...]
            normed = (x * inverse_rms(x) * gain_ref[0:1]).astype(BF16)
            normed_ref[...] = normed
            cosine, sine = cos_ref[...], sin_ref[...]
            b_raw = jnp.transpose(dot(normed, wb_ref[...], ((1,), (0,))))
            for r in range(RANK_Q):
                bq_ref[r] = rotated(b_raw[r * HEAD_DIM : (r + 1) * HEAD_DIM], cosine, sine)
            for r in range(KV):
                rows = b_raw[(RANK_Q + r) * HEAD_DIM : (RANK_Q + r + 1) * HEAD_DIM]
                if r < RANK_KV:
                    rows = rotated(rows, cosine, sine)
                pay_ref[r * HEAD_DIM : (r + 1) * HEAD_DIM, :] = rows.astype(BF16)
            for tp in range(n_tp):
                a_raw = dot(wa_ref[tp], normed, ((1,), (1,)))
                a_ref[tp] = a_raw
                kv = [a_raw[g * RANKS + RANK_Q : (g + 1) * RANKS] for g in range(group)]
                start = kv_b + tp * group * KV
                pay_ref[start : start + group * KV, :] = jnp.concatenate(kv, axis=0).astype(BF16)

        def set_mask(first_ref, bias_ref):
            bias_ref[...] = attention_mask(first_ref, windows * block, block)

        def is_even(meta_ref):
            return lax.rem(meta_ref[AT_ME], 2) == 0

        def widen(meta_ref, arrived, win_ref, wide_ref):
            third, second, beside_second, beside, own = arrived
            win_ref[1] = second[...]
            win_ref[3] = own[...]

            @pl.when(is_even(meta_ref))
            def _():
                win_ref[0] = third[...]
                win_ref[2] = beside_second[...]

            @pl.when(jnp.logical_not(is_even(meta_ref)))
            def _():
                win_ref[0] = beside_second[...]
                win_ref[2] = beside[...]

            for j in range(windows):
                for r in range(KV):
                    wide_ref[j, r] = win_ref[j, r * HEAD_DIM : (r + 1) * HEAD_DIM, :].astype(F32)

        def spread_factors(a_ref, win_ref, own_ref, kv_ref):
            for pair in range(pairs):
                start = pair % (group // 2) * 2 * RANKS
                own_ref[pair, : 2 * RANKS, :] = a_ref[pair * 2 // group, start : start + 2 * RANKS, :]
            for j in range(windows):
                kv_ref[j] = win_ref[j, kv_b:, :].astype(F32)

        def kv_factors(kv_ref, pair):
            start = pl.multiple_of(pair * (2 * KV), 2 * KV)
            return [kv_ref[j, pl.ds(start, 2 * KV), :] for j in range(windows)]

        def head_place(pair, g):
            tp, half = pair // (group // 2), lax.rem(pair, group // 2)
            return tp, 2 * half + g, pl.ds(pl.multiple_of((2 * half + g) * HEAD_DIM, HEAD_DIM), HEAD_DIM)

        def kv_rows_of(factors, wide_ref, g, j):
            def mix(r):
                a0 = factors[j][g * KV + r : g * KV + r + 1]
                a1 = factors[j][g * KV + r + 1 : g * KV + r + 2]
                rows = a0 * wide_ref[j, r] + a1 * wide_ref[j, r + 1]
                return (rows * (1.0 / RANK_KV)).astype(BF16)

            return mix(0), mix(RANK_KV)

        def attention_kernel(
            meta_ref,
            first_ref,
            a_ref,
            bq_ref,
            w0_ref,
            w1_ref,
            w2_ref,
            w3_ref,
            w4_ref,
            lse_ref,
            q_ref,
            mixed_ref,
            win_ref,
            bias_ref,
            wide_ref,
            s_ref,
            own_ref,
            kv_ref,
        ):
            set_mask(first_ref, bias_ref)
            widen(meta_ref, (w0_ref, w1_ref, w2_ref, w3_ref, w4_ref), win_ref, wide_ref)
            spread_factors(a_ref, win_ref, own_ref, kv_ref)
            spans = [pl.ds(j * block, block) for j in range(windows)]

            def one_pair(pair, slot):
                own = own_ref[pair]
                factors = kv_factors(kv_ref, pair)
                for g in range(2):
                    tp, head, rows = head_place(pair, g)
                    query = own[g * RANKS : g * RANKS + 1] * bq_ref[0]
                    for r in range(1, RANK_Q):
                        query = query + own[g * RANKS + r : g * RANKS + r + 1] * bq_ref[r]
                    query = (query * (1.0 / RANK_Q)).astype(BF16)
                    query = query * jnp.asarray(HEAD_DIM**-0.5, BF16)
                    q_ref[tp, head] = query
                    top = jnp.full((1, block), MASKED, F32)
                    values = []
                    for j, span in enumerate(spans):
                        keys, value_rows = kv_rows_of(factors, wide_ref, g, j)
                        values.append(value_rows)
                        scores = dot(keys, query, ((0,), (0,))) + bias_ref[span, :]
                        s_ref[slot + g, span, :] = scores
                        top = jnp.maximum(top, jnp.max(scores, axis=0, keepdims=True))
                    total = jnp.zeros((1, block), F32)
                    for span in spans:
                        weight = jnp.exp(s_ref[slot + g, span, :] - top)
                        s_ref[slot + g, span, :] = weight
                        total = total + jnp.sum(weight, axis=0, keepdims=True)
                    lse_ref[pair, g : g + 1, :] = top + jnp.log(total)
                    scale = 1.0 / total
                    mixed = jnp.zeros((HEAD_DIM, block), F32)
                    for j, span in enumerate(spans):
                        probs = (s_ref[slot + g, span, :] * scale).astype(BF16)
                        mixed = mixed + dot(values[j], probs, ((1,), (0,)))
                    mixed_ref[tp, rows, :] = mixed.astype(BF16)

            def one_member(tp, carry):
                for k in range(group // 2):
                    one_pair(tp * (group // 2) + k, 2 * k)
                return carry

            lax.fori_loop(0, n_tp, one_member, 0)

        def project_kernel(
            meta_ref, x_ref, mixed_ref, o0_ref, o1_ref, gain_ref, mid_ref, attn_ref, nf_ref
        ):
            attn = jnp.zeros((block, width), F32)
            for lo, ref in enumerate((o0_ref, o1_ref)):
                for hi in range(2):
                    rows = mixed_ref[member(meta_ref, lo, hi)]
                    attn = attn + dot(rows, ref[hi * o_rows : (hi + 1) * o_rows, :], ((0,), (0,)))
            attn_ref[...] = attn
            mid = to_arrival(meta_ref, lambda lanes: x_ref[:, lanes]) + attn
            mid_ref[...] = mid
            gain = to_arrival(meta_ref, lambda lanes: gain_ref[1:2, lanes])
            nf_ref[...] = (mid * inverse_rms(mid) * gain).astype(BF16)

        def rows_kernel(
            meta_ref, x_hbm, cot_ref, x_ref, own_ref, near_ref, far_ref, cot_buf, sems
        ):
            row = pl.multiple_of(meta_ref[AT_ME] * block, block)
            own_load = pltpu.make_async_copy(x_hbm.at[0, pl.ds(row, block), :], x_ref, sems.at[4])
            own_load.start()
            loads = []
            for side in range(2):
                for i in range(2):
                    row = pl.multiple_of(member(meta_ref, i, side) * block, block)
                    k = 2 * side + i
                    loads.append(
                        pltpu.make_async_copy(
                            cot_ref.at[0, pl.ds(row, block), :], cot_buf.at[k], sems.at[k]
                        )
                    )
                    loads[-1].start()
            for k, load in enumerate(loads):
                load.wait()
                out_ref = (near_ref, far_ref)[k // 2]
                rows = slice(k % 2 * block, (k % 2 + 1) * block)
                for j in range(n_piece):
                    lanes = slice(j * LANES, (j + 1) * LANES)
                    part = cot_buf[k, :, column(meta_ref, j)]
                    out_ref[rows, lanes] = part.astype(BF16)
                    if k == 0:
                        own_ref[:, lanes] = part
            own_load.wait()

        def feed_rows(n_refs, gb_ref, w_ref, ht_ref, back0_ref, back1_ref, rows_ref=None):
            if rows_ref is not None:
                for i in range(2):
                    rows_ref[i] = n_refs[i][...]

            def one_block(i, carry):
                if rows_ref is None:
                    cut, rows = pl.ds(i * block, block), n_refs[i][...]
                else:
                    cut, rows = pl.ds(pl.multiple_of(i * block, block), block), rows_ref[i]
                gate = dot(w_ref[0:hidden, :], rows, ((1,), (1,)))
                up = dot(w_ref[hidden : 2 * hidden, :], rows, ((1,), (1,)))
                grad_act = dot(w_ref[2 * hidden :, :], gb_ref[cut, :], ((1,), (1,)))
                squash = jax.nn.sigmoid(gate)
                soft = gate * squash
                ht_ref[2 * hidden :, cut] = (soft * up).astype(BF16)
                ht_ref[0:hidden, cut] = (
                    grad_act * up * squash * (1.0 + gate * (1.0 - squash))
                ).astype(BF16)
                ht_ref[hidden : 2 * hidden, cut] = (grad_act * soft).astype(BF16)
                return carry

            if rows_ref is None:
                for i in range(2):
                    one_block(i, 0)
            else:
                lax.fori_loop(0, 2, one_block, 0)
            back = dot(ht_ref[: 2 * hidden, :], w_ref[: 2 * hidden, :], ((0,), (0,)))
            back0_ref[...] = back[:block]
            back1_ref[...] = back[block:].astype(BF16)

        def far_kernel(meta_ref, n0_ref, n1_ref, gb_ref, *refs):
            own_gu_ref, far_gu_ref, pair_gu_ref, gu_across_ref, gu_rest_ref = refs[:5]
            dn_refs = refs[5 : 5 + n_f]
            ht_ref, back0_ref, back1_ref, w_ref, sems = refs[5 + n_f :]
            gate_up = [own_gu_ref, far_gu_ref, pair_gu_ref.at[0], pair_gu_ref.at[1], gu_across_ref]
            gate_up += [gu_rest_ref.at[s] for s in range(n_f - 1)]
            beside_shift = meta_ref[AT_ME + 2]
            arrivals = [0, 2, beside_shift, n_f - beside_shift]
            down = [ref.at[near] for near in range(n_c) for ref in dn_refs]
            loads = []
            for j in range(n_piece):
                lanes = pl.ds(j * LANES, LANES)
                at = pl.multiple_of((arrivals[j % n_f] + j // n_f * n_f) * LANES, LANES)
                loads.append(
                    pltpu.make_async_copy(
                        gate_up[j],
                        w_ref.at[pl.ds(0, early), pl.ds(at, LANES)],
                        sems.at[j],
                    )
                )
                loads.append(
                    pltpu.make_async_copy(
                        down[j], w_ref.at[pl.ds(early, 3 * hidden - early), lanes], sems.at[n_piece + j]
                    )
                )
            for load in loads:
                load.start()
            for load in loads:
                load.wait()
            feed_rows((n0_ref, n1_ref), gb_ref, w_ref, ht_ref, back0_ref, back1_ref)

        def near_kernel(meta_ref, n0_ref, n1_ref, gb_ref, w_ref, far_ht_ref, ht_ref, *refs):
            back0_ref, back1_ref, *ahead_refs, rows_ref = refs
            feed_rows((n0_ref, n1_ref), gb_ref, w_ref, ht_ref, back0_ref, back1_ref, rows_ref)
            for k, ref in enumerate((ht_ref, far_ht_ref)):
                ahead = dot(ref[2 * hidden :, :], w_ref[2 * hidden :, :], ((0,), (0,)))
                ahead_refs[2 * k][...] = ahead[:block]
                ahead_refs[2 * k + 1][...] = ahead[block:].astype(BF16)

        def weight_grad(refs, start, stop, right):
            hts, n_near, n_far, gbs = refs[0:2], refs[2:4], refs[4:6], refs[6:8]
            total = jnp.zeros((stop - start, width), F32)
            for side in range(2):
                left = hts[side]
                if right == 1:
                    total = total + dot(left[start:stop, :], gbs[side][...], ((1,), (0,)))
                    continue
                for i in range(2):
                    rows = (n_near, n_far)[side][i][...]
                    cut = slice(i * block, (i + 1) * block)
                    total = total + dot(left[start:stop, cut], rows, ((1,), (0,)))
            return total

        def gate_up_grad_kernel(meta_ref, *refs):
            keep_ref, send_ref = refs[8:]
            for k in range(2):
                cut = slice(k * hidden, (k + 1) * hidden)
                total = weight_grad(refs, k * hidden, (k + 1) * hidden, 0)
                keep_ref[cut, :] = total[:, :half_width].astype(BF16)
                send_ref[cut, :] = total[:, half_width:].astype(BF16)

        def down_grad_kernel(meta_ref, *refs):
            keep_ref, send_ref = refs[8:]
            total = weight_grad(refs, 2 * hidden, 3 * hidden, 1)

            def chunk(s, near):
                start = near * half_width + s * LANES
                return total[:, start : start + LANES]

            for near in range(n_c):
                keep_ref[0, near] = chunk(0, near)
                keep_ref[1, near] = chunk(2, near)

            @pl.when(lax.rem(meta_ref[AT_ME + 1], 2) == 0)
            def _():
                for near in range(n_c):
                    send_ref[0, near] = chunk(3, near).astype(BF16)
                    send_ref[1, near] = chunk(1, near).astype(BF16)

            @pl.when(lax.rem(meta_ref[AT_ME + 1], 2) == 1)
            def _():
                for near in range(n_c):
                    send_ref[0, near] = chunk(1, near).astype(BF16)
                    send_ref[1, near] = chunk(3, near).astype(BF16)

        def middle_kernel(
            meta_ref,
            cot_ref,
            back_ref,
            beside_ref,
            across_ref,
            mid_ref,
            gain_ref,
            o0_ref,
            o1_ref,
            mixed_ref,
            dmid_ref,
            gg_ref,
            go_ref,
            keep_ref,
            send_ref,
        ):
            back = back_ref[...] + beside_ref[...].astype(F32) + across_ref[...].astype(F32)
            mid = mid_ref[...]
            inverse = inverse_rms(mid)
            gain = to_arrival(meta_ref, lambda lanes: gain_ref[1:2, lanes])
            normal = mid * inverse
            gains = jnp.sum(back * normal, axis=0, keepdims=True)
            for j in range(n_piece):
                gg_ref[:, column(meta_ref, j)] = jnp.broadcast_to(
                    gains[:, j * LANES : (j + 1) * LANES], (8, LANES)
                )
            scaled = back * gain
            delta = inverse * (
                scaled - normal * jnp.mean(scaled * normal, axis=-1, keepdims=True)
            )
            dmid_ref[...] = delta
            grad = (cot_ref[...] + delta).astype(BF16)
            for lo, ref in enumerate((o0_ref, o1_ref)):
                for hi in range(2):
                    tp = member(meta_ref, lo, hi)
                    cut = slice(hi * o_rows, (hi + 1) * o_rows)
                    go_ref[tp] = dot(ref[cut, :], grad, ((1,), (1,))).astype(BF16)
                    weight = dot(mixed_ref[tp], grad, ((1,), (0,))).astype(BF16)
                    (keep_ref, send_ref)[lo][cut, :] = weight

        def attention_back_kernel(
            part,
            meta_ref,
            first_ref,
            a_ref,
            bq_ref,
            w0_ref,
            w1_ref,
            w2_ref,
            w3_ref,
            w4_ref,
            lse_ref,
            q_ref,
            go_ref,
            *refs,
        ):
            win_ref, bias_ref, wide_ref, p_ref, dp_ref, own_ref, kv_ref = refs[-7:]
            if part == 0:
                ga_ref, gbq_ref, gwb_ref, gwa_ref = refs[:4]
            else:
                ga_ref, gbq_ref, second_ref, beside_ref, third_ref, own_out_ref = refs[3:9]
                gwb_ref, gwa_ref = refs[-9:-7]
            set_mask(first_ref, bias_ref)
            widen(meta_ref, (w0_ref, w1_ref, w2_ref, w3_ref, w4_ref), win_ref, wide_ref)
            spread_factors(a_ref, win_ref, own_ref, kv_ref)
            if part == 0:
                gbq_ref[...] = jnp.zeros_like(gbq_ref)
                gwb_ref[...] = jnp.zeros_like(gwb_ref)
            else:
                gbq_ref[...] = refs[0][...]
                gwb_ref[...] = refs[1][...]
                gwa_ref[...] = refs[2][...]
            spans = [pl.ds(j * block, block) for j in range(windows)]
            first_pair, stop_pair = ((0, first_part), (first_part, pairs))[part]

            def one_pair(pair, carry):
                own = own_ref[pair]
                factors = kv_factors(kv_ref, pair)
                grad_a = []
                grad_kv = [[] for _ in spans]
                for g in range(2):
                    tp, head, rows = head_place(pair, g)
                    query = q_ref[tp, head]
                    grad_out = go_ref[tp, rows, :]
                    lse = lse_ref[pair, g : g + 1, :]
                    inner = jnp.zeros((1, block), F32)
                    keys = []
                    for j, span in enumerate(spans):
                        key_rows, value_rows = kv_rows_of(factors, wide_ref, g, j)
                        keys.append(key_rows)
                        scores = dot(key_rows, query, ((0,), (0,))) + bias_ref[span, :]
                        probs = jnp.exp(scores - lse)
                        grad_probs = dot(value_rows, grad_out, ((0,), (0,)))
                        p_ref[g % 2, span, :] = probs
                        dp_ref[g % 2, span, :] = grad_probs
                        inner = inner + jnp.sum(probs * grad_probs, axis=0, keepdims=True)
                    grad_query = jnp.zeros((HEAD_DIM, block), F32)
                    for j, span in enumerate(spans):
                        probs = p_ref[g % 2, span, :]
                        grad_scores = (probs * (dp_ref[g % 2, span, :] - inner)).astype(BF16)
                        grad_query = grad_query + dot(keys[j], grad_scores, ((1,), (0,)))
                        grad_keys = dot(query, grad_scores, ((1,), (1,))) * (1.0 / RANK_KV)
                        grad_values = dot(grad_out, probs.astype(BF16), ((1,), (1,)))
                        grad_values = grad_values * (1.0 / RANK_KV)
                        for r in range(KV):
                            grad = grad_keys if r < RANK_KV else grad_values
                            grad_kv[j].append(
                                jnp.sum(grad * wide_ref[j, r], axis=0, keepdims=True)
                            )
                            gwb_ref[j, r] += factors[j][g * KV + r : g * KV + r + 1] * grad
                    grad_query = grad_query * (HEAD_DIM**-0.5 / RANK_Q)
                    for r in range(RANK_Q):
                        grad_a.append(jnp.sum(grad_query * bq_ref[r], axis=0, keepdims=True))
                        gbq_ref[r] += own[g * RANKS + r : g * RANKS + r + 1] * grad_query
                    grad_a.append(jnp.zeros((KV, block), F32))
                grad_a.append(jnp.zeros((pair_rows - 2 * RANKS, block), F32))
                ga_ref[pair - first_pair] = jnp.concatenate(grad_a, axis=0)
                start = pl.multiple_of(pair * (2 * KV), 2 * KV)
                for j in range(windows):
                    gwa_ref[j, pl.ds(start, 2 * KV), :] = jnp.concatenate(grad_kv[j], axis=0)
                return carry

            lax.fori_loop(first_pair, stop_pair, one_pair, 0)
            if part == 0:
                return

            def put(ref, start, j):
                for r in range(KV):
                    row = start + r * HEAD_DIM
                    ref[row : row + HEAD_DIM, :] = gwb_ref[j, r].astype(ref.dtype)
                ref[start + kv_b : start + kv_rows, :] = gwa_ref[j].astype(ref.dtype)

            put(own_out_ref, 0, 3)
            put(beside_ref, 0, 2)
            put(third_ref, 0, 0)
            put(second_ref, 0, 1)

        def last_kernel(
            meta_ref,
            x_ref,
            own_ref,
            second_ref,
            beside_ref,
            third_ref,
            gbq_ref,
            ga0_ref,
            ga1_ref,
            cos_ref,
            sin_ref,
            wb_ref,
            wa_ref,
            normed_ref,
            gain_ref,
            dmid_ref,
            gg_ref,
            delta_ref,
            keep0_ref,
            keep1_ref,
            send0_ref,
            send1_ref,
            b_buf,
            a_buf,
            d_buf,
            g_buf,
        ):
            total = own_ref[...]
            for ref in (second_ref, beside_ref, third_ref):
                total = total + ref[...].astype(F32)
            cosine, sine = cos_ref[...], -sin_ref[...]
            rows = [rotated(gbq_ref[r], cosine, sine) for r in range(RANK_Q)]
            for r in range(KV):
                part = total[r * HEAD_DIM : (r + 1) * HEAD_DIM]
                rows.append(rotated(part, cosine, sine) if r < RANK_KV else part)
            grad_b = jnp.transpose(jnp.concatenate(rows, axis=0)).astype(BF16)
            normed = normed_ref[...]
            back = dot(grad_b, wb_ref[...], ((1,), (1,)))
            for tp in range(n_tp):
                parts = []
                for g in range(group):
                    start = kv_b + (tp * group + g) * KV
                    parts.append(jnp.zeros((RANK_Q, block), F32))
                    parts.append(total[start : start + KV])
                parts.append(jnp.zeros((a_pad - a_cols, block), F32))
                half = group // 2
                at = [tp * half + k for k in range(half)]
                own_a = [
                    ga0_ref[k, : 2 * RANKS, :]
                    if k < first_part
                    else ga1_ref[k - first_part, : 2 * RANKS, :]
                    for k in at
                ]
                own_a.append(jnp.zeros((a_pad - a_cols, block), F32))
                own_a = jnp.concatenate(own_a, axis=0)
                grad_a = (own_a + jnp.concatenate(parts, axis=0)).astype(BF16)
                back = back + dot(grad_a, wa_ref[tp], ((0,), (0,)))
                a_buf[tp] = dot(grad_a, normed, ((1,), (0,)))
            b_buf[...] = dot(normed, grad_b, ((0,), (0,)))
            x = x_ref[...]
            inverse = inverse_rms(x)
            normal = x * inverse
            gains = jnp.sum(back * normal, axis=0, keepdims=True)
            g_buf[...] = jnp.broadcast_to(gains, (8, width))
            scaled = back * gain_ref[0:1]
            delta = inverse * (
                scaled - normal * jnp.mean(scaled * normal, axis=-1, keepdims=True)
            )
            d_buf[...] = delta
            for j in range(n_piece):
                lanes = column(meta_ref, j)
                cut = slice(j * LANES, (j + 1) * LANES)
                delta_ref[:, lanes] = (d_buf[:, lanes] + dmid_ref[:, cut]).astype(BF16)
            row_index = lax.broadcasted_iota(jnp.int32, (16, LANES), 0)
            for lo, hi in ((0, 0), (0, 1), (1, 0), (1, 1)):
                outs = ((keep0_ref, keep1_ref), (send0_ref, send1_ref))[lo]
                tp = member(meta_ref, lo, hi)
                for near in range(n_c):
                    out = outs[near]
                    for s in range(n_f):
                        j = near * n_f + s
                        lanes = column(meta_ref, j)
                        row = pl.multiple_of((meta_ref[j] * n_tp + tp) * b_rows, b_rows)
                        for k in range(b_parts):
                            out[hi, s, k * b_rows : (k + 1) * b_rows, :] = b_buf[
                                pl.ds(row, b_rows), k * LANES : (k + 1) * LANES
                            ].astype(BF16)
                        out[hi, s, n_b : n_b + a_pad, :] = a_buf[tp, :, lanes].astype(BF16)
                        pair = jnp.where(
                            row_index == 0, g_buf[0:1, lanes], gg_ref[0:1, lanes]
                        )
                        out[hi, s, n_b + a_pad :, :] = pair.astype(BF16)

        def add_kernel(arrival, meta_ref, x_ref, d0_ref, d1_ref, d2_ref, d3_ref, out_ref):
            step = pl.program_id(0) // 2
            rows = pl.ds(pl.multiple_of((pl.program_id(0) % 2) * (block // 2), 8), block // 2)
            for i, ref in enumerate((d0_ref, d1_ref, d2_ref, d3_ref)):

                @pl.when(step == i)
                def _(ref=ref):
                    if not arrival:
                        out_ref[0] = x_ref[0] + ref[rows, :].astype(F32)
                        return
                    for j in range(n_piece):
                        lanes = column(meta_ref, j)
                        out_ref[0, :, lanes] = x_ref[0, :, lanes] + ref[
                            rows, j * LANES : (j + 1) * LANES
                        ].astype(F32)

        def split_kernel(meta_ref, keep_ref, got_ref, own_ref, send_ref):
            def total(s):
                lanes = slice(s * LANES, (s + 1) * LANES)
                return keep_ref[:, lanes].astype(F32) + got_ref[: keep_ref.shape[0], lanes].astype(
                    F32
                )

            own_ref[0] = total(0)
            own_ref[1] = total(2)

            @pl.when(lax.rem(meta_ref[AT_ME + 1], 2) == 0)
            def _():
                send_ref[0] = total(3).astype(BF16)
                send_ref[1] = total(1).astype(BF16)

            @pl.when(lax.rem(meta_ref[AT_ME + 1], 2) == 1)
            def _():
                send_ref[0] = total(1).astype(BF16)
                send_ref[1] = total(3).astype(BF16)

        def unpack_kernel(
            meta_ref, p_ref, got_ref, b_ref, a_ref, g0_ref, g1_ref, o_ref
        ):
            total = p_ref[...].astype(F32) + got_ref[...].astype(F32)
            for k in range(b_parts):
                b_ref[0, :, k * LANES : (k + 1) * LANES] = total[k * b_rows : (k + 1) * b_rows]
            a_ref[0] = total[n_b : n_b + a_cols]
            rows = total[n_b + a_pad : n_b + a_pad + 8]
            rows = pltpu.roll(rows, (n_tp - meta_ref[AT_ME]) * gain_part, 1)
            g0_ref[...] = rows[0:1, :gain_part]
            g1_ref[...] = rows[1:2, :gain_part]
            o_ref[0] = total[pack_rows:]

        core = lambda v, label="row": swap(v, "tp", n_tp, 1, "core_" + label)
        chip = lambda v, label="row": swap(v, "tp", n_tp, 2, "y_" + label)
        ctx = lambda v, label="row": swap(v, "ctx", n_c, 1, "x_" + label)
        ahead = lambda v, s, label="row": shift(v, "fsdp", n_f, s, "z_" + label)

        (pack,) = call(
            pack_kernel,
            "pack",
            [((pack_rows, LANES), BF16)],
            (w_factor_b, w_factor_a.transpose(0, 2, 1), attn_gains, ffn_gains),
        )
        o_rows_all = w_out[0].astype(BF16)
        pack = jnp.stack([pack] + [ahead(pack, s, "pack") for s in range(1, n_f)])
        o_parts = [o_rows_all] + [ahead(o_rows_all, s, "wo") for s in range(1, n_f)]
        o_parts = jnp.concatenate(o_parts, axis=0)
        gu_in = after(w_gate_up.transpose(0, 1, 3, 2), pack)
        own_gu, own_dn = call(
            big_kernel,
            "big_pack",
            [((early, LANES), BF16), ((3 * hidden - early, LANES), BF16)],
            (gu_in, w_down),
        )
        pack = jnp.stack([pack, ctx(pack, "pack")])
        far_gu = swap(own_gu, "fsdp", n_f, 2, "z_gate_up")
        dn_pair = jnp.stack([own_dn, ctx(own_dn, "down")])
        gu_across = ctx(own_gu, "gate_up")
        o_across = ctx(o_parts, "wo")
        o_parts = jnp.concatenate(
            [
                half[s * o_rows : (s + 1) * o_rows]
                for half in (o_parts, o_across)
                for s in range(n_f)
            ],
            axis=1,
        )
        own_x, own_cot, near_cot, far_cot = call(
            rows_kernel,
            "rows",
            [((block, width), F32)] * 2 + [((2 * block, width), BF16)] * 2,
            (resid_in, cotangent),
            [REMOTE] * 2,
            [pltpu.VMEM((4, block, width), F32), pltpu.SemaphoreType.DMA((5,))],
            scalars=after(meta, o_across),
        )
        pack_across, far_gu, dn_pair, o_parts, near_cot, far_cot = lax.optimization_barrier(
            (chip(pack, "pack"), far_gu, dn_pair, o_parts, near_cot, far_cot)
        )
        pair_gu = swap(jnp.stack([own_gu, far_gu]), "fsdp", n_f, 1, "z_gate_up_pair")
        pack = jnp.stack([pack, pack_across], axis=1)
        other_pack = core(pack, "pack")

        def add_rows(whole, parts, arrival):
            rows = pl.BlockSpec(
                (1, block // 2, width), lambda i, m: (0, 2 * m[AT_TP + i // 2] + i % 2, 0)
            )
            (out,) = call(
                lambda *refs: add_kernel(arrival, *refs),
                "add_rows",
                [(whole.shape, F32)],
                (whole, *parts),
                [rows] + [WHOLE] * 4,
                (),
                (2 * n_tp,),
                [rows],
            )
            return out

        def split(keep, got):
            size = keep.shape[0]
            return call(
                split_kernel,
                "split",
                [((2, size, LANES), F32), ((2, size, LANES), BF16)],
                (keep, got),
            )

        def first_step(send, label):
            return swap(send, "fsdp", n_f, 1, "z1_" + label)

        def second_step(own, got, label):
            total = own + got.astype(F32)
            return total[0], swap(total[1].astype(BF16), "fsdp", n_f, 2, "z2_" + label)

        seg_here = lax.dynamic_slice_in_dim(segment_ids[0], place * block, block, 0)
        first = jnp.sum((segment_ids[0][:, None] < seg_here[None, :]).astype(jnp.int32), axis=0)
        token = place * block + jnp.arange(block, dtype=jnp.int32)
        position = (token - first).astype(F32)
        first = (first - place * block + extra * block).reshape(1, block)
        frequency = 10000.0 ** (-2.0 * jnp.arange(HEAD_DIM // 2, dtype=F32) / HEAD_DIM)
        angles = frequency[:, None] * position[None, :]
        cosine, sine = jnp.cos(angles), jnp.sin(angles)

        weight_b, weight_a, gains, normed, a_rows, b_query, payload = call(
            factor_kernel,
            "factors",
            [
                ((width, b_cols), BF16),
                ((n_tp, a_pad, width), BF16),
                ((16, width), F32),
                ((block, width), BF16),
                ((n_tp, a_pad, block), F32),
                ((RANK_Q, HEAD_DIM, block), F32),
                ((kv_rows, block), BF16),
            ],
            (own_x, pack, other_pack, cosine, sine),
        )
        def places(value, step, chosen, label):
            pairs = [(i, i + step) for i in chosen if 0 <= i + step < n_place]
            with jax.named_scope(label):
                return lax.ppermute(value, ("ctx", "tp"), pairs)

        every, odd, even = range(n_place), range(1, n_place, 2), range(0, n_place, 2)
        second = places(payload, 2, every, "x_kv_second")
        third = places(payload, 3, odd, "x_kv_third")
        beside_kv = core(payload, "kv")
        o_own = jnp.concatenate([o_parts, chip(o_parts, "wo")], axis=0)
        second, pair_gu, gu_across = lax.optimization_barrier((second, pair_gu, gu_across))
        gu_rest = ctx(jnp.concatenate([far_gu[None], pair_gu], axis=0), "gate_up_rest")
        dn_parts = [dn_pair, ahead(dn_pair, 1, "down1")]
        beside_second = core(second, "kv_second")
        tied = lax.optimization_barrier((third, second, beside_second, beside_kv, o_own))
        wins = (*tied[:4], payload)
        o_own = tied[4]
        o_other = core(o_own, "wo")
        window = windows * block
        factor_scratch = [
            pltpu.VMEM((pairs, pair_rows, block), F32),
            pltpu.VMEM((windows, heads * KV, block), F32),
        ]
        lse, query, mixed = call(
            attention_kernel,
            "attention",
            [
                ((pairs, 2, block), F32),
                ((n_tp, group, HEAD_DIM, block), BF16),
                ((n_tp, feats, block), BF16),
            ],
            (first, a_rows, b_query, *wins),
            None,
            [
                pltpu.VMEM((windows, kv_rows, block), BF16),
                pltpu.VMEM((window, block), F32),
                pltpu.VMEM((windows, KV, HEAD_DIM, block), F32),
                pltpu.VMEM((group, window, block), F32),
                *factor_scratch,
            ],
        )
        dn_parts[1] = after(dn_parts[1], mixed)
        for s in range(2, n_f):
            dn_parts.append(ahead(dn_parts[-1], 1, "down" + str(s)))
        mid, attn_out, normed_ffn = call(
            project_kernel,
            "project",
            [((block, width), F32), ((block, width), F32), ((block, width), BF16)],
            (own_x, mixed, o_own, o_other, gains),
        )

        near_rows = (normed_ffn, core(normed_ffn, "nf"))
        far_own = chip(normed_ffn, "nf")

        far_own, gu_rest = lax.optimization_barrier((far_own, gu_rest))
        far_own, dn_parts[-1], gu_rest = lax.optimization_barrier(
            (far_own, dn_parts[-1], gu_rest)
        )
        pieces = (own_gu, far_gu, pair_gu, gu_across, gu_rest, *dn_parts)
        far_rows = (far_own, core(far_own, "nf_far"))
        whole_ht = ((3 * hidden, 2 * block), BF16)
        two_sums = [((block, width), F32), ((block, width), BF16)]
        far_ht, far_back, far_back1, weights = call(
            far_kernel,
            "feed_far",
            [whole_ht, *two_sums, ((3 * hidden, width), BF16)],
            (*far_rows, far_cot, *pieces),
            [WHOLE] * 3 + [REMOTE] * len(pieces),
            [pltpu.SemaphoreType.DMA((2 * n_piece,))],
            room=12,
        )
        across = (far_back + core(far_back1, "dn_far").astype(F32)).astype(BF16)
        near_ht, near_back, near_back1, near_out, near_out1, far_out, far_out1 = call(
            near_kernel,
            "feed_near",
            [whole_ht, *two_sums * 3],
            (after(near_rows[0], across), near_rows[1], near_cot, weights, far_ht),
            None,
            [pltpu.VMEM((2, block, width), BF16)],
            room=12,
        )
        across = chip(across, "dn")
        beside = core(near_back1, "dn_near")

        grad_args = (near_ht, far_ht, *near_rows, *far_rows, near_cot, far_cot)
        own_d, send_d = call(
            down_grad_kernel,
            "down_grad",
            [((2, n_c, hidden, LANES), F32), ((2, n_c, hidden, LANES), BF16)],
            grad_args,
            room=12,
        )
        got_d = first_step(send_d, "d")
        keep_a, send_a = call(
            gate_up_grad_kernel,
            "gate_up_grad",
            [((2 * hidden, half_width), BF16)] * 2,
            (after(grad_args[0], send_d), *grad_args[1:]),
            room=12,
        )
        got_a = ctx(send_a, "grads_a")
        across = after(across, send_a)

        delta_mid, gain_grad, grad_mixed, keep_o, send_o = call(
            middle_kernel,
            "middle",
            [
                ((block, width), F32),
                ((8, width), F32),
                ((n_tp, feats, block), BF16),
                ((2 * o_rows, width), BF16),
                ((2 * o_rows, width), BF16),
            ],
            (own_cot, near_back, beside, across, mid, gains, o_own, o_other, mixed),
        )
        near_sum = attn_out + near_out + core(after(near_out1, across), "out_near").astype(F32)
        far_sum = far_out + core(after(far_out1, across), "out_far").astype(F32)
        out_send = jnp.stack([far_sum, near_sum]).astype(BF16)
        grad_mixed = after(grad_mixed, out_send)
        rows_got = core(send_o, "go")
        out_got = chip(out_send, "out")
        back_args = (first, a_rows, b_query, *wins, lse, query, grad_mixed)
        sums = [
            ((RANK_Q, HEAD_DIM, block), F32),
            ((windows, KV, HEAD_DIM, block), F32),
            ((windows, heads * KV, block), F32),
        ]
        back_scratch = [
            pltpu.VMEM((windows, kv_rows, block), BF16),
            pltpu.VMEM((window, block), F32),
            pltpu.VMEM((windows, KV, HEAD_DIM, block), F32),
            pltpu.VMEM((2, window, block), F32),
            pltpu.VMEM((2, window, block), F32),
            *factor_scratch,
        ]
        grad_a0, *sums_out = call(
            lambda *refs: attention_back_kernel(0, *refs),
            "attention_back_a",
            [((first_part, pair_rows, block), F32)] + sums,
            back_args,
            None,
            back_scratch,
        )
        sums_out[0], own_d, got_d, _ = lax.optimization_barrier(
            (sums_out[0], own_d, got_d, grad_a0)
        )
        own_d, got_d = second_step(own_d, got_d, "d")
        grad_a1, grad_bq, *sends = call(
            lambda *refs: attention_back_kernel(1, *refs),
            "attention_back_b",
            [
                ((pairs - first_part, pair_rows, block), F32),
                sums[0],
                ((kv_rows, block), BF16),
                ((kv_rows, block), BF16),
                ((kv_rows, block), BF16),
                ((kv_rows, block), F32),
            ],
            (*back_args, *sums_out),
            None,
            [pltpu.VMEM(shape, kind) for shape, kind in sums[1:]] + back_scratch,
        )
        *sends[:3], out_got, rows_got = lax.optimization_barrier((*sends[:3], out_got, rows_got))
        second_got = places(sends[0], -2, every, "x_kv_back_second")
        beside_got = places(sends[1], -1, every, "x_kv_back_beside")
        third_got = places(sends[2], -3, every, "x_kv_back_third")
        own_a, send_a = split(after(keep_a, sends[0]), got_a)
        got_a = first_step(send_a, "a")
        rows_o = keep_o.astype(F32) + after(rows_got, send_a).astype(F32)
        rows_keep, rows_send = rows_o[:o_rows], rows_o[o_rows:].astype(BF16)
        rows_got = chip(rows_send, "go")
        *got, got_d = lax.optimization_barrier((second_got, beside_got, third_got, got_d))
        out_rows = (out_send[::-1].astype(F32) + out_got.astype(F32)).astype(BF16)

        delta, keep0, keep1, send0, send1 = call(
            last_kernel,
            "last",
            [
                ((block, width), BF16),
                *[((2, n_f, pack_rows, LANES), BF16)] * 4,
            ],
            (
                own_x,
                sends[3],
                *got,
                grad_bq,
                grad_a0,
                grad_a1,
                cosine,
                sine,
                weight_b,
                weight_a,
                normed,
                gains,
                delta_mid,
                gain_grad,
            ),
            [WHOLE] * 16,
            [
                pltpu.VMEM((width, b_cols), F32),
                pltpu.VMEM((n_tp, a_pad, width), F32),
                pltpu.VMEM((block, width), F32),
                pltpu.VMEM((8, width), F32),
            ],
        )

        part_send = (keep1.astype(F32) + core(send1, "gp").astype(F32)).astype(BF16)
        total_d = own_d + got_d.astype(F32)
        part_send, got_a = lax.optimization_barrier((part_send, got_a))
        part_got = ctx(part_send, "gp")
        own_a, got_a = second_step(own_a, got_a, "a")
        part = keep0.astype(F32) + core(after(send0, part_send), "gp_near").astype(F32)
        rows_got, part = lax.optimization_barrier((rows_got, part))
        rows_o = rows_keep + rows_got.astype(F32)
        rows_keep, rows_send = rows_o[:, :half_width], rows_o[:, half_width:].astype(BF16)
        across_delta = chip(delta, "delta")
        rows_go = ctx(rows_send, "go")
        out_rows = after(out_rows, part_send)
        out_beside = core(out_rows, "out_rows")
        block_out = add_rows(
            resid_in, (out_rows[0], out_rows[1], out_beside[0], out_beside[1]), True
        )
        part_got, across_delta = lax.optimization_barrier((part_got, across_delta, block_out))[:2]
        part = part + part_got.astype(F32)
        part_send = part[1].astype(BF16)
        part_got = chip(part_send, "gp")
        across_delta = after(across_delta, part_send)
        beside_delta = core(after(delta, part_send), "delta")
        got_last = ctx(after(total_d[1], part_send).astype(BF16), "d")
        part_got, rows_go, got_a = lax.optimization_barrier((part_got, rows_go, got_a))
        part = part[0] + part_got.astype(F32)
        rows_o = rows_keep + rows_go.astype(F32)
        part = [
            jnp.concatenate([part[s], rows_o[:, s * LANES : (s + 1) * LANES]], axis=0)
            for s in range(n_f)
        ]
        is_even_f = f_index % 2 == 0
        part_send = [
            jnp.where(is_even_f, part[3], part[1]),
            jnp.where(is_even_f, part[1], part[3]),
        ]
        part_send = jnp.stack(part_send).astype(BF16)
        part_own, part_got = second_step(
            jnp.stack([part[0], part[2]]), first_step(part_send, "gp"), "gp"
        )
        across_delta = after(across_delta, part_send)
        resid_grad = add_rows(
            cotangent,
            (delta, across_delta, beside_delta, core(across_delta, "delta_far")),
            False,
        )
        part_got, got_last = lax.optimization_barrier((part_got, got_last, resid_grad))[:2]
        grad_down = total_d[0] + got_last.astype(F32)
        grad_gate_up = (own_a + got_a.astype(F32)).reshape(1, 2, hidden, fc_cols)
        part_b, part_a, part_g0, part_g1, grad_out = call(
            unpack_kernel,
            "unpack",
            [
                ((1, b_rows, b_cols), F32),
                ((1, a_cols, fc_cols), F32),
                ((1, gain_part), F32),
                ((1, gain_part), F32),
                ((1, o_rows, LANES), F32),
            ],
            (part_own, part_got),
        )
        return (
            block_out,
            resid_grad,
            part_a.transpose(0, 2, 1),
            part_b,
            grad_out,
            grad_gate_up.transpose(0, 1, 3, 2),
            grad_down[None],
            part_g0,
            part_g1,
        )

    return shards


def make_shards(mesh):
    fused, general = make_fused(mesh), make_general(mesh)
    fits = mesh.shape["fsdp"] == 4 and mesh.shape["ctx"] == 2 and mesh.shape["tp"] == 4

    def shards(*args):
        return (fused if fits and args[7].shape[2] == LANES else general)(*args)

    return shards


def solution(mesh):
    return jax.shard_map(
        make_shards(mesh),
        mesh=mesh,
        in_specs=(
            P("fsdp", "ctx", None),
            P("fsdp", None),
            P("fsdp", "ctx", None),
            P(None, ("fsdp", "ctx"), "tp"),
            P(None, ("fsdp", "ctx", "tp"), None),
            P(None, "tp", ("fsdp", "ctx")),
            P(None, None, ("fsdp", "ctx"), "tp"),
            P(None, "tp", ("fsdp", "ctx")),
            P(None, ("fsdp", "ctx", "tp")),
            P(None, ("fsdp", "ctx", "tp")),
        ),
        out_specs=(
            P("fsdp", "ctx", None),
            P("fsdp", "ctx", None),
            P(None, ("fsdp", "ctx"), "tp"),
            P(None, ("fsdp", "ctx", "tp"), None),
            P(None, "tp", ("fsdp", "ctx")),
            P(None, None, ("fsdp", "ctx"), "tp"),
            P(None, "tp", ("fsdp", "ctx")),
            P(None, ("fsdp", "ctx", "tp")),
            P(None, ("fsdp", "ctx", "tp")),
        ),
        check_vma=False,
    )
```

```python
import math

import jax
import jax.numpy as jnp
from jax import lax
from jax.experimental import pallas as pl
from jax.experimental.pallas import tpu as pltpu
from jax.sharding import PartitionSpec as P

HEAD_DIM = 64
RANK_Q = 6
RANK_KV = 2
RANKS = 10
KV = 2 * RANK_KV
MOST_DOC = 768
EPSILON = 1e-05
LANES = 128
BF16 = jnp.bfloat16
F32 = jnp.float32
MASKED = -1e30


def inverse_rms(values):
    return lax.rsqrt(jnp.mean(values * values, axis=-1, keepdims=True) + EPSILON)


def norm_back(grad_value, values, inverse, gain):
    scaled = grad_value * gain
    normal = values * inverse
    return inverse * (scaled - normal * jnp.mean(scaled * normal, axis=-1, keepdims=True))


def dot(left, right, dims):
    return lax.dot_general(left, right, (dims, ((), ())), preferred_element_type=F32)


def shift(value, axes, size, step, label="shift"):
    with jax.named_scope(label):
        return lax.ppermute(value, axes, [(i, (i + step) % size) for i in range(size)])


def swap(value, axis, size, bit, label="swap"):
    with jax.named_scope(label):
        return lax.ppermute(value, axis, [(i, i ^ bit) for i in range(size)])


def gather_direct(value, axis, size):
    me = lax.axis_index(axis)
    parts = [(me, value)]
    for step in range(1, size):
        parts.append(((me - step) % size, shift(value, axis, size, step)))
    out = jnp.zeros((size,) + value.shape, value.dtype)
    for place, part in parts:
        out = lax.dynamic_update_slice(out, part[None], (place,) + (0,) * value.ndim)
    return out


def gather_pair(value, axis, size, bit):
    mine = (lax.axis_index(axis) // bit) % 2 == 0
    other = swap(value, axis, size, bit)
    return jnp.stack([jnp.where(mine, value, other), jnp.where(mine, other, value)])


def after(value, *others):
    return lax.optimization_barrier((value,) + others)[0]


def take(value, index):
    return lax.dynamic_index_in_dim(value, index, 0, keepdims=False)


def scatter_direct(value, axis, size):
    me = lax.axis_index(axis)
    got = [
        shift(take(value, (me + step) % size), axis, size, step) for step in range(1, size)
    ]
    total = take(value, me).astype(F32)
    for part in got:
        total = total + part.astype(F32)
    return total


def scatter_pair(value, axis, size, bit):
    mine = (lax.axis_index(axis) // bit) % 2
    got = swap(take(value, 1 - mine).astype(BF16), axis, size, bit)
    return take(value, mine).astype(F32) + got.astype(F32)


def attention_mask(first_ref, window, block):
    start = first_ref[...]
    place = lax.broadcasted_iota(jnp.int32, (window, block), 0)
    query_place = lax.broadcasted_iota(jnp.int32, (window, block), 1) + (window - block)
    return jnp.where((place >= start) & (place <= query_place), 0.0, MASKED)


def head_rows(wa_ref, wide_ref, head):
    factors = wa_ref[head].astype(F32)
    key_rows = (factors[0:1] * wide_ref[0] + factors[1:2] * wide_ref[1]) * (1.0 / RANK_KV)
    value_rows = (factors[2:3] * wide_ref[2] + factors[3:4] * wide_ref[3]) * (1.0 / RANK_KV)
    return factors, key_rows.astype(BF16), value_rows.astype(BF16)


def forward_kernel(
    first_ref, a_ref, bq_ref, wa_ref, wb_ref, mixed_ref, lse_ref, q_ref, bias_ref, wide_ref, s_ref
):
    heads = a_ref.shape[0]
    window, block = bias_ref.shape
    bias_ref[...] = attention_mask(first_ref, window, block)
    wide_ref[...] = wb_ref[...].astype(F32)
    spans = [pl.ds(j * block, block) for j in range(window // block)]

    def one_head(head, carry):
        factors = a_ref[head]
        query = factors[0:1] * bq_ref[0]
        for r in range(1, RANK_Q):
            query = query + factors[r : r + 1] * bq_ref[r]
        query = (query * (1.0 / RANK_Q)).astype(BF16) * jnp.asarray(HEAD_DIM**-0.5, BF16)
        q_ref[head] = query
        _, key_rows, value_rows = head_rows(wa_ref, wide_ref, head)
        top = jnp.full((1, block), MASKED, F32)
        for j, span in enumerate(spans):
            keys = key_rows[:, j * block : (j + 1) * block]
            scores = dot(keys, query, ((0,), (0,))) + bias_ref[span, :]
            s_ref[span, :] = scores
            top = jnp.maximum(top, jnp.max(scores, axis=0, keepdims=True))
        total = jnp.zeros((1, block), F32)
        for span in spans:
            weight = jnp.exp(s_ref[span, :] - top)
            s_ref[span, :] = weight
            total = total + jnp.sum(weight, axis=0, keepdims=True)
        lse_ref[head] = top + jnp.log(total)
        scale = 1.0 / total
        mixed = jnp.zeros((HEAD_DIM, block), F32)
        for j, span in enumerate(spans):
            probs = (s_ref[span, :] * scale).astype(BF16)
            mixed = mixed + dot(
                value_rows[:, j * block : (j + 1) * block], probs, ((1,), (0,))
            )
        mixed_ref[head] = mixed.astype(BF16)
        return carry

    lax.fori_loop(0, heads, one_head, 0)


def backward_kernel(
    first_ref,
    a_ref,
    bq_ref,
    wa_ref,
    wb_ref,
    lse_ref,
    q_ref,
    go_ref,
    ga_ref,
    gbq_ref,
    gwa_ref,
    gwb_ref,
    bias_ref,
    wide_ref,
    p_ref,
    dp_ref,
):
    heads = a_ref.shape[0]
    window, block = bias_ref.shape
    bias_ref[...] = attention_mask(first_ref, window, block)
    wide_ref[...] = wb_ref[...].astype(F32)
    gbq_ref[...] = jnp.zeros_like(gbq_ref)
    gwb_ref[...] = jnp.zeros_like(gwb_ref)
    count = window // block
    spans = [pl.ds(j * block, block) for j in range(count)]

    def one_head(head, carry):
        factors, key_rows, value_rows = head_rows(wa_ref, wide_ref, head)
        query = q_ref[head]
        grad_out = go_ref[head]
        lse = lse_ref[head]
        inner = jnp.zeros((1, block), F32)
        for j, span in enumerate(spans):
            cut = slice(j * block, (j + 1) * block)
            scores = dot(key_rows[:, cut], query, ((0,), (0,))) + bias_ref[span, :]
            probs = jnp.exp(scores - lse)
            grad_probs = dot(value_rows[:, cut], grad_out, ((0,), (0,)))
            p_ref[span, :] = probs
            dp_ref[span, :] = grad_probs
            inner = inner + jnp.sum(probs * grad_probs, axis=0, keepdims=True)
        grad_query = jnp.zeros((HEAD_DIM, block), F32)
        for j, span in enumerate(spans):
            cut = slice(j * block, (j + 1) * block)
            probs = p_ref[span, :]
            grad_scores = (probs * (dp_ref[span, :] - inner)).astype(BF16)
            grad_query = grad_query + dot(key_rows[:, cut], grad_scores, ((1,), (0,)))
            grad_keys = dot(query, grad_scores, ((1,), (1,))) * (1.0 / RANK_KV)
            grad_values = dot(grad_out, probs.astype(BF16), ((1,), (1,))) * (1.0 / RANK_KV)
            rows = []
            for r in range(KV):
                grad = grad_keys if r < RANK_KV else grad_values
                rows.append(jnp.sum(grad * wide_ref[r, :, span], axis=0, keepdims=True))
                gwb_ref[r, :, span] += factors[r : r + 1, cut] * grad
            gwa_ref[head, :, span] = jnp.concatenate(rows, axis=0)
        grad_query = grad_query * (HEAD_DIM**-0.5 / RANK_Q)
        own = a_ref[head]
        rows = []
        for r in range(RANK_Q):
            rows.append(jnp.sum(grad_query * bq_ref[r], axis=0, keepdims=True))
            gbq_ref[r] += own[r : r + 1] * grad_query
        ga_ref[head] = jnp.concatenate(rows, axis=0)
        return carry

    lax.fori_loop(0, heads, one_head, 0)


VMEM_LIMIT = 56 * 1024 * 1024


def whole_specs(count):
    return [pl.BlockSpec(memory_space=pltpu.VMEM)] * count


def attend_forward(first, a_rows, b_query, win_a, win_b):
    heads, _, block = a_rows.shape
    window = win_a.shape[-1]
    return pl.pallas_call(
        forward_kernel,
        out_shape=(
            jax.ShapeDtypeStruct((heads, HEAD_DIM, block), BF16),
            jax.ShapeDtypeStruct((heads, 1, block), F32),
            jax.ShapeDtypeStruct((heads, HEAD_DIM, block), BF16),
        ),
        in_specs=whole_specs(5),
        out_specs=tuple(whole_specs(3)),
        scratch_shapes=[
            pltpu.VMEM((window, block), F32),
            pltpu.VMEM((KV, HEAD_DIM, window), F32),
            pltpu.VMEM((window, block), F32),
        ],
        compiler_params=pltpu.CompilerParams(vmem_limit_bytes=VMEM_LIMIT),
        name="attend_forward",
    )(first, a_rows, b_query, win_a, win_b)


def attend_backward(first, a_rows, b_query, win_a, win_b, lse, query, grad_mixed):
    heads, _, block = a_rows.shape
    window = win_a.shape[-1]
    return pl.pallas_call(
        backward_kernel,
        out_shape=(
            jax.ShapeDtypeStruct((heads, RANK_Q, block), F32),
            jax.ShapeDtypeStruct((RANK_Q, HEAD_DIM, block), F32),
            jax.ShapeDtypeStruct((heads, KV, window), F32),
            jax.ShapeDtypeStruct((KV, HEAD_DIM, window), F32),
        ),
        in_specs=whole_specs(8),
        out_specs=tuple(whole_specs(4)),
        scratch_shapes=[
            pltpu.VMEM((window, block), F32),
            pltpu.VMEM((KV, HEAD_DIM, window), F32),
            pltpu.VMEM((window, block), F32),
            pltpu.VMEM((window, block), F32),
        ],
        compiler_params=pltpu.CompilerParams(vmem_limit_bytes=VMEM_LIMIT),
        name="attend_backward",
    )(first, a_rows, b_query, win_a, win_b, lse, query, grad_mixed)


def rotate(rows, cosine, sine):
    half = HEAD_DIM // 2
    lower, upper = rows[:, :half], rows[:, half:]
    return jnp.concatenate(
        [lower * cosine - upper * sine, lower * sine + upper * cosine], axis=1
    )


def make_general(mesh):
    n_f, n_c, n_tp = mesh.shape["fsdp"], mesh.shape["ctx"], mesh.shape["tp"]
    n_hi, n_lo = 2, n_tp // 2

    def shards(
        resid_in,
        segment_ids,
        cotangent,
        w_factor_a,
        w_factor_b,
        w_out,
        w_gate_up,
        w_down,
        attn_gains,
        ffn_gains,
    ):
        seq_count, local_len, width = resid_in.shape
        assert seq_count == 1 and w_factor_a.shape[0] == 1 and n_lo == 2
        full_len = segment_ids.shape[1]
        block = local_len // n_tp
        extra = -(-(MOST_DOC - 1) // block)
        window = (extra + 1) * block
        a_cols = w_factor_a.shape[2]
        heads = n_tp * a_cols // RANKS
        b_cols = w_factor_b.shape[2]
        b_rows = w_factor_b.shape[1]
        b_parts = b_cols // LANES
        fc_cols = w_down.shape[2]
        hidden = w_down.shape[1]
        o_rows = w_out.shape[1]

        f_index, c_index, t_index = (
            lax.axis_index("fsdp"),
            lax.axis_index("ctx"),
            lax.axis_index("tp"),
        )
        hi, lo = t_index // 2, t_index % 2
        place = c_index * n_tp + t_index
        n_place = n_c * n_tp

        gains = jnp.concatenate([attn_gains, ffn_gains], axis=1).astype(BF16)
        gain_count = gains.shape[1]
        gain_rows = 16 * (-(-gain_count // (16 * LANES)))
        gains = jnp.pad(gains.reshape(-1), (0, gain_rows * LANES - gain_count))
        b_shard = w_factor_b[0].astype(BF16).reshape(b_rows, b_parts, LANES)
        a_shard = w_factor_a[0].astype(BF16).T
        pack = jnp.concatenate(
            [
                b_shard.transpose(1, 0, 2).reshape(-1, LANES),
                a_shard.reshape(-1, LANES),
                gains.reshape(-1, LANES),
            ],
            axis=0,
        )
        n_b = b_parts * b_rows
        n_a = a_cols * fc_cols // LANES
        pack = gather_direct(pack, "fsdp", n_f)
        after_pack = pack
        pack = gather_pair(pack, "ctx", n_c, 1)
        pack = gather_pair(pack, "tp", n_tp, 2)
        pack = gather_pair(pack, "tp", n_tp, 1)
        pack = pack.transpose(3, 2, 1, 0, 4, 5)
        weight_b = pack[:, :, :, :, :n_b].reshape(-1, b_parts, b_rows, LANES)
        weight_b = weight_b.transpose(0, 2, 1, 3).reshape(width, b_cols)
        weight_a = pack[:, :, :, :, n_b : n_b + n_a].reshape(n_f, n_c, n_tp, a_cols, fc_cols)
        weight_a = weight_a.transpose(2, 3, 0, 1, 4).reshape(n_tp * a_cols, width)
        gains_all = pack[:, :, :, :, n_b + n_a :].reshape(-1, gain_rows * LANES)[:, :gain_count]
        gains_all = gains_all.reshape(-1, 2, gain_count // 2).transpose(1, 0, 2)
        gains_all = gains_all.reshape(2, width).astype(F32)
        gain_attn, gain_ffn = gains_all[0:1], gains_all[1:2]

        big = jnp.concatenate(
            [
                w_gate_up[0, 0].astype(BF16).T,
                w_gate_up[0, 1].astype(BF16).T,
                w_down[0].astype(BF16),
                w_out[0].astype(BF16),
            ],
            axis=0,
        )
        big, _ = lax.optimization_barrier((big, after_pack))
        big = gather_direct(big, "fsdp", n_f)
        big = gather_pair(big, "ctx", n_c, 1)
        big = big.transpose(2, 1, 0, 3).reshape(-1, width)
        weight_g = big[:hidden]
        weight_u = big[hidden : 2 * hidden]
        weight_d = big[2 * hidden : 3 * hidden]
        weight_o = gather_pair(big[3 * hidden :], "tp", n_tp, 2)
        weight_o = gather_pair(weight_o, "tp", n_tp, 1)
        weight_o = weight_o.transpose(1, 0, 2, 3).reshape(n_tp * o_rows, width)

        seg_here = lax.dynamic_slice_in_dim(segment_ids[0], place * block, block, 0)
        first = jnp.sum((segment_ids[0][:, None] < seg_here[None, :]).astype(jnp.int32), axis=0)
        token = place * block + jnp.arange(block, dtype=jnp.int32)
        position = (token - first).astype(F32)
        first = (first - place * block + extra * block).reshape(1, block)
        frequency = 10000.0 ** (
            -2.0 * jnp.arange(HEAD_DIM // 2, dtype=F32) / HEAD_DIM
        )
        angles = frequency[:, None] * position[None, :]
        cosine, sine = jnp.cos(angles)[None], jnp.sin(angles)[None]

        stream = resid_in[0].reshape(n_tp, block, width)
        own = take(stream, t_index)
        inverse_attn = inverse_rms(own)
        normed = (own * inverse_attn * gain_attn).astype(BF16)
        a_rows = dot(weight_a, normed, ((1,), (1,))).reshape(heads, RANKS, block)
        b_raw = dot(weight_b, normed, ((0,), (1,))).reshape(RANKS, HEAD_DIM, block)
        b_rot = rotate(b_raw[: RANK_Q + RANK_KV], cosine, sine)
        b_query = b_rot[:RANK_Q]
        b_kv = jnp.concatenate([b_rot[RANK_Q:], b_raw[RANK_Q + RANK_KV :]], axis=0)
        payload = jnp.concatenate(
            [
                b_kv.reshape(KV * HEAD_DIM, block),
                a_rows[:, RANK_Q:].reshape(heads * KV, block),
            ],
            axis=0,
        ).astype(BF16)
        around = [
            lax.ppermute(
                payload, ("ctx", "tp"), [(i, i + step) for i in range(n_place - step)]
            )
            for step in range(extra, 0, -1)
        ]
        win = jnp.concatenate(around + [payload], axis=1)
        win_b = win[: KV * HEAD_DIM].reshape(KV, HEAD_DIM, window)
        win_a = win[KV * HEAD_DIM :].reshape(heads, KV, window)

        mixed, lse, query = attend_forward(first, a_rows, b_query, win_a, win_b)
        mixed = mixed.reshape(heads * HEAD_DIM, block)
        attn_out = dot(mixed, weight_o, ((0,), (0,)))
        mid = own + attn_out
        inverse_ffn = inverse_rms(mid)
        normed_ffn = (mid * inverse_ffn * gain_ffn).astype(BF16)

        near_rows = gather_pair(normed_ffn, "tp", n_tp, 1)
        far_rows = gather_pair(swap(normed_ffn, "tp", n_tp, 2), "tp", n_tp, 1)
        grad_all = cotangent[0].reshape(n_hi, n_lo * block, width)

        def half(rows, grad_rows):
            rows = rows.reshape(n_lo * block, width)
            gate = dot(rows, weight_g, ((1,), (1,)))
            up = dot(rows, weight_u, ((1,), (1,)))
            grad_act = dot(grad_rows, weight_d, ((1,), (1,)))
            squash = jax.nn.sigmoid(gate)
            act = (gate * squash * up).astype(BF16)
            grad_gate = (grad_act * up * squash * (1.0 + gate * (1.0 - squash))).astype(BF16)
            grad_up = (grad_act * gate * squash).astype(BF16)
            back = dot(grad_gate, weight_g, ((1,), (0,))) + dot(grad_up, weight_u, ((1,), (0,)))
            ahead = dot(act, weight_d, ((1,), (0,)))
            both = lambda v: v.reshape(n_lo, block, width)
            return rows, act, grad_gate, grad_up, both(back), both(ahead)

        grad_near = take(grad_all, hi).astype(BF16)
        grad_far = take(grad_all, 1 - hi).astype(BF16)
        near = half(near_rows, grad_near)
        far = half(far_rows, grad_far)
        back_far = scatter_pair(far[4], "tp", n_tp, 1).astype(BF16)
        back_far = swap(back_far, "tp", n_tp, 2)
        grad_normed_ffn = scatter_pair(near[4], "tp", n_tp, 1) + back_far.astype(F32)
        ahead_far = scatter_pair(far[5], "tp", n_tp, 1).astype(BF16)
        ahead_far = swap(ahead_far, "tp", n_tp, 2)
        ffn_out = scatter_pair(near[5], "tp", n_tp, 1) + ahead_far.astype(F32)

        def spread(value):
            beside = swap(value, "tp", n_tp, 1)
            across = swap(value, "tp", n_tp, 2)
            diagonal = swap(across, "tp", n_tp, 1)
            out = jnp.zeros((n_tp,) + value.shape, value.dtype)
            for bit, part in enumerate((value, beside, across, diagonal)):
                out = lax.dynamic_update_slice(out, part[None], (t_index ^ bit, 0, 0))
            return out.reshape(local_len, width).astype(F32)

        block_out = resid_in + spread((attn_out + ffn_out).astype(BF16))[None]

        def columns(value, which):
            value = value.reshape(value.shape[0], n_f, n_c, fc_cols)
            value = lax.dynamic_index_in_dim(value, which, 2, keepdims=False)
            return value.reshape(value.shape[0], n_f * fc_cols)

        rows_all = jnp.concatenate([near[0], far[0]], axis=0)
        act_all = jnp.concatenate([near[1], far[1]], axis=0)
        gate_all = jnp.concatenate([near[2], far[2]], axis=0)
        up_all = jnp.concatenate([near[3], far[3]], axis=0)
        cot_all = jnp.concatenate([grad_near, grad_far], axis=0)

        def big_grads(which):
            rows_cut = columns(rows_all, which)
            cot_cut = columns(cot_all, which)
            return jnp.concatenate(
                [
                    dot(gate_all, rows_cut, ((0,), (0,))),
                    dot(up_all, rows_cut, ((0,), (0,))),
                    dot(act_all, cot_cut, ((0,), (0,))),
                ],
                axis=0,
            )

        def over_fc(send, keep):
            total = keep + swap(send.astype(BF16), "ctx", n_c, 1).astype(F32)
            total = total.astype(BF16).reshape(-1, n_f, fc_cols).transpose(1, 0, 2)
            return scatter_direct(total, "fsdp", n_f)

        grad_big = over_fc(big_grads(1 - c_index), big_grads(c_index))
        grad_gate_w = grad_big[:hidden].T
        grad_up_w = grad_big[hidden : 2 * hidden].T
        grad_down_w = grad_big[2 * hidden :]

        own_cot = take(cotangent[0].reshape(n_tp, block, width), t_index)
        gain_grad_ffn = jnp.sum(grad_normed_ffn * mid * inverse_ffn, axis=0)
        delta_mid = norm_back(grad_normed_ffn, mid, inverse_ffn, gain_ffn)
        grad_attn = (own_cot + delta_mid).astype(BF16)
        grad_out = dot(mixed, grad_attn, ((1,), (0,))).reshape(n_hi, n_lo, o_rows, width)
        grad_out = scatter_pair(grad_out.transpose(1, 0, 2, 3), "tp", n_tp, 1)
        grad_out = scatter_pair(grad_out, "tp", n_tp, 2)
        grad_out = over_fc(columns(grad_out, 1 - c_index), columns(grad_out, c_index))

        grad_mixed = dot(weight_o, grad_attn, ((1,), (1,))).astype(BF16)
        ga_q, gb_q, gw_a, gw_b = attend_backward(
            first,
            a_rows,
            b_query,
            win_a,
            win_b,
            lse,
            query,
            grad_mixed.reshape(heads, HEAD_DIM, block),
        )
        gw = jnp.concatenate(
            [gw_b.reshape(KV * HEAD_DIM, window), gw_a.reshape(heads * KV, window)], axis=0
        )
        total = gw[:, extra * block :]
        for step in range(1, extra + 1):
            part = gw[:, (extra - step) * block : (extra - step + 1) * block].astype(BF16)
            part = lax.ppermute(
                part, ("ctx", "tp"), [(i + step, i) for i in range(n_place - step)]
            )
            total = total + part.astype(F32)
        gb_kv = total[: KV * HEAD_DIM].reshape(KV, HEAD_DIM, block)
        ga_kv = total[KV * HEAD_DIM :].reshape(heads, KV, block)
        grad_b = jnp.concatenate(
            [
                rotate(jnp.concatenate([gb_q, gb_kv[:RANK_KV]], axis=0), cosine, -sine),
                gb_kv[RANK_KV:],
            ],
            axis=0,
        )
        grad_b = grad_b.reshape(b_cols, block).astype(BF16)
        grad_a = jnp.concatenate([ga_q, ga_kv], axis=1).reshape(heads * RANKS, block).astype(BF16)
        grad_normed = dot(grad_a, weight_a, ((0,), (0,))) + dot(grad_b, weight_b, ((0,), (1,)))
        gain_grad_attn = jnp.sum(grad_normed * own * inverse_attn, axis=0)
        delta = delta_mid + norm_back(grad_normed, own, inverse_attn, gain_attn)
        resid_grad = cotangent + spread(delta.astype(BF16))[None]

        grad_wa = dot(grad_a, normed, ((1,), (0,))).astype(BF16)
        grad_wa = grad_wa.reshape(n_hi, n_lo, a_cols, n_f, n_c, fc_cols)
        grad_wa = grad_wa.transpose(1, 0, 4, 3, 2, 5).reshape(n_lo, n_hi, n_c, n_f, n_a, LANES)
        grad_wb = jnp.einsum(
            "pkt,td->pdk",
            grad_b.reshape(b_parts, LANES, block),
            normed,
            preferred_element_type=F32,
        ).astype(BF16)
        grad_wb = grad_wb.reshape(b_parts, n_f, n_c, n_hi, n_lo, b_rows, LANES)
        grad_wb = grad_wb.transpose(4, 3, 2, 1, 0, 5, 6)
        grad_wb = grad_wb.reshape(n_lo, n_hi, n_c, n_f, n_b, LANES)
        gain_grads = jnp.stack([gain_grad_attn, gain_grad_ffn]).astype(BF16)
        gain_grads = gain_grads.reshape(2, n_f, n_c, n_hi, n_lo, gain_count // 2)
        gain_grads = gain_grads.transpose(4, 3, 2, 1, 0, 5).reshape(
            n_lo, n_hi, n_c, n_f, gain_count
        )
        gain_grads = jnp.pad(
            gain_grads, [(0, 0)] * 4 + [(0, gain_rows * LANES - gain_count)]
        ).reshape(n_lo, n_hi, n_c, n_f, gain_rows, LANES)
        pack = jnp.concatenate([grad_wb, grad_wa, gain_grads], axis=4)
        pack = scatter_pair(pack, "tp", n_tp, 1)
        pack = scatter_pair(pack, "tp", n_tp, 2)
        pack = scatter_pair(pack, "ctx", n_c, 1).astype(BF16)
        pack = scatter_direct(pack, "fsdp", n_f)
        part_b = pack[:n_b].reshape(b_parts, b_rows, LANES).transpose(1, 0, 2)
        part_b = part_b.reshape(1, b_rows, b_cols)
        part_a = pack[n_b : n_b + n_a].reshape(a_cols, fc_cols).T[None]
        part_gain = pack[n_b + n_a :].reshape(-1)[:gain_count].reshape(2, 1, gain_count // 2)
        return (
            block_out,
            resid_grad,
            part_a,
            part_b,
            grad_out[None],
            jnp.stack([grad_gate_w, grad_up_w])[None],
            grad_down_w[None],
            part_gain[0],
            part_gain[1],
        )

    return shards


def rotated(rows, cosine, sine):
    half = HEAD_DIM // 2
    lower, upper = rows[:half], rows[half:]
    return jnp.concatenate([lower * cosine - upper * sine, lower * sine + upper * cosine], axis=0)


def make_fused(mesh):
    n_f, n_c, n_tp = mesh.shape["fsdp"], mesh.shape["ctx"], mesh.shape["tp"]
    n_piece = n_f * n_c
    AT_TP = n_piece
    AT_ME = n_piece + n_tp

    def shards(
        resid_in,
        segment_ids,
        cotangent,
        w_factor_a,
        w_factor_b,
        w_out,
        w_gate_up,
        w_down,
        attn_gains,
        ffn_gains,
    ):
        _, local_len, width = resid_in.shape
        block = local_len // n_tp
        extra = -(-(MOST_DOC - 1) // block)
        windows = extra + 1
        a_cols = w_factor_a.shape[2]
        group = a_cols // RANKS
        heads = n_tp * group
        feats = group * HEAD_DIM
        a_pad = 16 * (-(-a_cols // 16))
        b_rows, b_cols = w_factor_b.shape[1:]
        b_parts = b_cols // LANES
        n_b = b_parts * b_rows
        pack_rows = n_b + a_pad + 16
        fc_cols = w_down.shape[2]
        hidden = w_down.shape[1]
        o_rows = w_out.shape[1]
        gain_part = attn_gains.shape[1]
        kv_b = KV * HEAD_DIM
        kv_rows = kv_b + heads * KV
        half_width = width // n_c
        pairs = heads // 2
        first_part = 5 * pairs // 8
        pair_rows = 8 * (-(-2 * RANKS // 8))
        early = 2 * hidden + 16 * (hidden // 64)
        assert n_f == 4 and fc_cols == LANES and o_rows == feats and n_tp == 4 and n_c == 2

        f_index, c_index, t_index = (
            lax.axis_index("fsdp"),
            lax.axis_index("ctx"),
            lax.axis_index("tp"),
        )
        place = c_index * n_tp + t_index
        n_place = n_c * n_tp
        columns = [
            ((f_index - s) % n_f) * n_c + (c_index if near == 0 else 1 - c_index)
            for near in range(n_c)
            for s in range(n_f)
        ]
        members = [t_index ^ (lo + 2 * hi) for lo in range(2) for hi in range(2)]
        beside_shift = jnp.where(f_index % 2 == 0, n_f - 1, 1)
        meta = jnp.stack(columns + members + [t_index, f_index, beside_shift]).astype(jnp.int32)

        resid_in = pltpu.with_memory_space_constraint(resid_in, pltpu.HBM)
        cotangent = pltpu.with_memory_space_constraint(cotangent, pltpu.HBM)

        def column(meta_ref, j):
            return pl.ds(pl.multiple_of(meta_ref[j] * LANES, LANES), LANES)

        def member(meta_ref, lo, hi):
            return meta_ref[AT_TP + 2 * lo + hi]

        def to_arrival(meta_ref, load):
            return jnp.concatenate([load(column(meta_ref, j)) for j in range(n_piece)], axis=1)

        WHOLE = pl.BlockSpec(memory_space=pltpu.VMEM)
        REMOTE = pl.BlockSpec(memory_space=pl.ANY)

        def call(
            kernel, name, outs, args, specs=None, scratch=(), grid=(1,), out_specs=None, room=4,
            scalars=meta,
        ):
            held = 0
            for arg, spec in zip((*args, *args[:1]), (specs or []) + (out_specs or [])):
                if spec.block_shape:
                    held += 2 * math.prod(spec.block_shape) * arg.dtype.itemsize
            for item in scratch:
                if hasattr(item, "shape") and item.memory_space == pltpu.VMEM:
                    held += math.prod(item.shape) * jnp.dtype(item.dtype).itemsize
            limit = min(held + room * 2**20, VMEM_LIMIT)
            return pl.pallas_call(
                kernel,
                out_shape=[jax.ShapeDtypeStruct(s, d) for s, d in outs],
                grid_spec=pltpu.PrefetchScalarGridSpec(
                    num_scalar_prefetch=1,
                    grid=grid,
                    in_specs=specs or [WHOLE] * len(args),
                    out_specs=out_specs or [WHOLE] * len(outs),
                    scratch_shapes=list(scratch),
                ),
                compiler_params=pltpu.CompilerParams(vmem_limit_bytes=limit),
                name=name,
            )(scalars, *args)


        def pack_kernel(meta_ref, b_ref, a_ref, g0_ref, g1_ref, out_ref):
            for k in range(b_parts):
                out_ref[k * b_rows : (k + 1) * b_rows, :] = b_ref[
                    0, :, k * LANES : (k + 1) * LANES
                ].astype(BF16)
            a_shard = jnp.concatenate([a_ref[0], jnp.zeros((a_pad - a_cols, LANES), F32)], axis=0)
            out_ref[n_b : n_b + a_pad, :] = a_shard.astype(BF16)
            both = jnp.concatenate([g0_ref[...], g1_ref[...]], axis=0)
            both = jnp.concatenate([both, jnp.zeros((6, gain_part), F32)], axis=0)
            both = jnp.concatenate([both, jnp.zeros((8, LANES - gain_part), F32)], axis=1)
            both = pltpu.roll(both, meta_ref[AT_ME] * gain_part, 1)
            both = jnp.concatenate([both, jnp.zeros((8, LANES), F32)], axis=0)
            out_ref[n_b + a_pad :, :] = both.astype(BF16)

        def big_kernel(meta_ref, gu_ref, d_ref, gu_out_ref, d_out_ref):
            for k in range(2):
                gu_out_ref[k * hidden : (k + 1) * hidden, :] = gu_ref[0, k].astype(BF16)
            gu_out_ref[2 * hidden :, :] = d_ref[0, : early - 2 * hidden, :].astype(BF16)
            d_out_ref[...] = d_ref[0, early - 2 * hidden :, :].astype(BF16)

        def factor_kernel(
            meta_ref,
            x_ref,
            p0_ref,
            p1_ref,
            cos_ref,
            sin_ref,
            wb_ref,
            wa_ref,
            gain_ref,
            normed_ref,
            a_ref,
            bq_ref,
            pay_ref,
        ):
            gain_ref[...] = jnp.zeros_like(gain_ref)
            for lo, hi in ((0, 0), (0, 1), (1, 0), (1, 1)):
                part = (p0_ref, p1_ref)[lo]
                tp = member(meta_ref, lo, hi)
                for near in range(n_c):
                    for s in range(n_f):
                        j = near * n_f + s
                        lanes = column(meta_ref, j)
                        row = pl.multiple_of((meta_ref[j] * n_tp + tp) * b_rows, b_rows)
                        for k in range(b_parts):
                            wb_ref[pl.ds(row, b_rows), k * LANES : (k + 1) * LANES] = part[
                                near, hi, s, k * b_rows : (k + 1) * b_rows, :
                            ]
                        wa_ref[tp, :, lanes] = part[near, hi, s, n_b : n_b + a_pad, :]
                        gain_ref[:, lanes] += part[near, hi, s, n_b + a_pad :, :].astype(F32)
            x = x_ref[...]
            normed = (x * inverse_rms(x) * gain_ref[0:1]).astype(BF16)
            normed_ref[...] = normed
            cosine, sine = cos_ref[...], sin_ref[...]
            b_raw = jnp.transpose(dot(normed, wb_ref[...], ((1,), (0,))))
            for r in range(RANK_Q):
                bq_ref[r] = rotated(b_raw[r * HEAD_DIM : (r + 1) * HEAD_DIM], cosine, sine)
            for r in range(KV):
                rows = b_raw[(RANK_Q + r) * HEAD_DIM : (RANK_Q + r + 1) * HEAD_DIM]
                if r < RANK_KV:
                    rows = rotated(rows, cosine, sine)
                pay_ref[r * HEAD_DIM : (r + 1) * HEAD_DIM, :] = rows.astype(BF16)
            for tp in range(n_tp):
                a_raw = dot(wa_ref[tp], normed, ((1,), (1,)))
                a_ref[tp] = a_raw
                kv = [a_raw[g * RANKS + RANK_Q : (g + 1) * RANKS] for g in range(group)]
                start = kv_b + tp * group * KV
                pay_ref[start : start + group * KV, :] = jnp.concatenate(kv, axis=0).astype(BF16)

        def set_mask(first_ref, bias_ref):
            bias_ref[...] = attention_mask(first_ref, windows * block, block)

        def is_even(meta_ref):
            return lax.rem(meta_ref[AT_ME], 2) == 0

        def widen(meta_ref, arrived, win_ref, wide_ref):
            third, second, beside_second, beside, own = arrived
            win_ref[1] = second[...]
            win_ref[3] = own[...]

            @pl.when(is_even(meta_ref))
            def _():
                win_ref[0] = third[...]
                win_ref[2] = beside_second[...]

            @pl.when(jnp.logical_not(is_even(meta_ref)))
            def _():
                win_ref[0] = beside_second[...]
                win_ref[2] = beside[...]

            for j in range(windows):
                for r in range(KV):
                    wide_ref[j, r] = win_ref[j, r * HEAD_DIM : (r + 1) * HEAD_DIM, :].astype(F32)

        def spread_factors(a_ref, win_ref, own_ref, kv_ref):
            for pair in range(pairs):
                start = pair % (group // 2) * 2 * RANKS
                own_ref[pair, : 2 * RANKS, :] = a_ref[pair * 2 // group, start : start + 2 * RANKS, :]
            for j in range(windows):
                kv_ref[j] = win_ref[j, kv_b:, :].astype(F32)

        def kv_factors(kv_ref, pair):
            start = pl.multiple_of(pair * (2 * KV), 2 * KV)
            return [kv_ref[j, pl.ds(start, 2 * KV), :] for j in range(windows)]

        def head_place(pair, g):
            tp, half = pair // (group // 2), lax.rem(pair, group // 2)
            return tp, 2 * half + g, pl.ds(pl.multiple_of((2 * half + g) * HEAD_DIM, HEAD_DIM), HEAD_DIM)

        def kv_rows_of(factors, wide_ref, g, j):
            def mix(r):
                a0 = factors[j][g * KV + r : g * KV + r + 1]
                a1 = factors[j][g * KV + r + 1 : g * KV + r + 2]
                rows = a0 * wide_ref[j, r] + a1 * wide_ref[j, r + 1]
                return (rows * (1.0 / RANK_KV)).astype(BF16)

            return mix(0), mix(RANK_KV)

        def attention_kernel(
            meta_ref,
            first_ref,
            a_ref,
            bq_ref,
            w0_ref,
            w1_ref,
            w2_ref,
            w3_ref,
            w4_ref,
            lse_ref,
            q_ref,
            mixed_ref,
            win_ref,
            bias_ref,
            wide_ref,
            s_ref,
            own_ref,
            kv_ref,
        ):
            set_mask(first_ref, bias_ref)
            widen(meta_ref, (w0_ref, w1_ref, w2_ref, w3_ref, w4_ref), win_ref, wide_ref)
            spread_factors(a_ref, win_ref, own_ref, kv_ref)
            spans = [pl.ds(j * block, block) for j in range(windows)]

            def one_pair(pair, slot):
                own = own_ref[pair]
                factors = kv_factors(kv_ref, pair)
                for g in range(2):
                    tp, head, rows = head_place(pair, g)
                    query = own[g * RANKS : g * RANKS + 1] * bq_ref[0]
                    for r in range(1, RANK_Q):
                        query = query + own[g * RANKS + r : g * RANKS + r + 1] * bq_ref[r]
                    query = (query * (1.0 / RANK_Q)).astype(BF16)
                    query = query * jnp.asarray(HEAD_DIM**-0.5, BF16)
                    q_ref[tp, head] = query
                    top = jnp.full((1, block), MASKED, F32)
                    values = []
                    for j, span in enumerate(spans):
                        keys, value_rows = kv_rows_of(factors, wide_ref, g, j)
                        values.append(value_rows)
                        scores = dot(keys, query, ((0,), (0,))) + bias_ref[span, :]
                        s_ref[slot + g, span, :] = scores
                        top = jnp.maximum(top, jnp.max(scores, axis=0, keepdims=True))
                    total = jnp.zeros((1, block), F32)
                    for span in spans:
                        weight = jnp.exp(s_ref[slot + g, span, :] - top)
                        s_ref[slot + g, span, :] = weight
                        total = total + jnp.sum(weight, axis=0, keepdims=True)
                    lse_ref[pair, g : g + 1, :] = top + jnp.log(total)
                    scale = 1.0 / total
                    mixed = jnp.zeros((HEAD_DIM, block), F32)
                    for j, span in enumerate(spans):
                        probs = (s_ref[slot + g, span, :] * scale).astype(BF16)
                        mixed = mixed + dot(values[j], probs, ((1,), (0,)))
                    mixed_ref[tp, rows, :] = mixed.astype(BF16)

            def one_member(tp, carry):
                for k in range(group // 2):
                    one_pair(tp * (group // 2) + k, 2 * k)
                return carry

            lax.fori_loop(0, n_tp, one_member, 0)

        def project_kernel(
            meta_ref, x_ref, mixed_ref, o0_ref, o1_ref, gain_ref, mid_ref, attn_ref, nf_ref
        ):
            attn = jnp.zeros((block, width), F32)
            for lo, ref in enumerate((o0_ref, o1_ref)):
                for hi in range(2):
                    rows = mixed_ref[member(meta_ref, lo, hi)]
                    attn = attn + dot(rows, ref[hi * o_rows : (hi + 1) * o_rows, :], ((0,), (0,)))
            attn_ref[...] = attn
            mid = to_arrival(meta_ref, lambda lanes: x_ref[:, lanes]) + attn
            mid_ref[...] = mid
            gain = to_arrival(meta_ref, lambda lanes: gain_ref[1:2, lanes])
            nf_ref[...] = (mid * inverse_rms(mid) * gain).astype(BF16)

        def rows_kernel(
            meta_ref, x_hbm, cot_ref, x_ref, own_ref, near_ref, far_ref, cot_buf, sems
        ):
            row = pl.multiple_of(meta_ref[AT_ME] * block, block)
            own_load = pltpu.make_async_copy(x_hbm.at[0, pl.ds(row, block), :], x_ref, sems.at[4])
            own_load.start()
            loads = []
            for side in range(2):
                for i in range(2):
                    row = pl.multiple_of(member(meta_ref, i, side) * block, block)
                    k = 2 * side + i
                    loads.append(
                        pltpu.make_async_copy(
                            cot_ref.at[0, pl.ds(row, block), :], cot_buf.at[k], sems.at[k]
                        )
                    )
                    loads[-1].start()
            for k, load in enumerate(loads):
                load.wait()
                out_ref = (near_ref, far_ref)[k // 2]
                rows = slice(k % 2 * block, (k % 2 + 1) * block)
                for j in range(n_piece):
                    lanes = slice(j * LANES, (j + 1) * LANES)
                    part = cot_buf[k, :, column(meta_ref, j)]
                    out_ref[rows, lanes] = part.astype(BF16)
                    if k == 0:
                        own_ref[:, lanes] = part
            own_load.wait()

        def feed_rows(n_refs, gb_ref, w_ref, ht_ref, back0_ref, back1_ref, rows_ref):
            for i in range(2):
                rows_ref[i] = n_refs[i][...]

            def one_block(i, carry):
                cut = pl.ds(pl.multiple_of(i * block, block), block)
                rows = rows_ref[i]
                gate = dot(w_ref[0:hidden, :], rows, ((1,), (1,)))
                up = dot(w_ref[hidden : 2 * hidden, :], rows, ((1,), (1,)))
                grad_act = dot(w_ref[2 * hidden :, :], gb_ref[cut, :], ((1,), (1,)))
                squash = jax.nn.sigmoid(gate)
                soft = gate * squash
                ht_ref[2 * hidden :, cut] = (soft * up).astype(BF16)
                ht_ref[0:hidden, cut] = (
                    grad_act * up * squash * (1.0 + gate * (1.0 - squash))
                ).astype(BF16)
                ht_ref[hidden : 2 * hidden, cut] = (grad_act * soft).astype(BF16)
                return carry

            lax.fori_loop(0, 2, one_block, 0)
            back = dot(ht_ref[: 2 * hidden, :], w_ref[: 2 * hidden, :], ((0,), (0,)))
            back0_ref[...] = back[:block]
            back1_ref[...] = back[block:].astype(BF16)

        def far_kernel(meta_ref, n0_ref, n1_ref, gb_ref, *refs):
            own_gu_ref, far_gu_ref, pair_gu_ref, gu_across_ref, gu_rest_ref = refs[:5]
            dn_refs = refs[5 : 5 + n_f]
            ht_ref, back0_ref, back1_ref, w_ref, rows_ref, sems = refs[5 + n_f :]
            gate_up = [own_gu_ref, far_gu_ref, pair_gu_ref.at[0], pair_gu_ref.at[1], gu_across_ref]
            gate_up += [gu_rest_ref.at[s] for s in range(n_f - 1)]
            beside_shift = meta_ref[AT_ME + 2]
            arrivals = [0, 2, beside_shift, n_f - beside_shift]
            down = [ref.at[near] for near in range(n_c) for ref in dn_refs]
            loads = []
            for j in range(n_piece):
                lanes = pl.ds(j * LANES, LANES)
                at = pl.multiple_of((arrivals[j % n_f] + j // n_f * n_f) * LANES, LANES)
                loads.append(
                    pltpu.make_async_copy(
                        gate_up[j],
                        w_ref.at[pl.ds(0, early), pl.ds(at, LANES)],
                        sems.at[j],
                    )
                )
                loads.append(
                    pltpu.make_async_copy(
                        down[j], w_ref.at[pl.ds(early, 3 * hidden - early), lanes], sems.at[n_piece + j]
                    )
                )
            for load in loads:
                load.start()
            for load in loads:
                load.wait()
            feed_rows((n0_ref, n1_ref), gb_ref, w_ref, ht_ref, back0_ref, back1_ref, rows_ref)

        def near_kernel(meta_ref, n0_ref, n1_ref, gb_ref, w_ref, far_ht_ref, ht_ref, *refs):
            back0_ref, back1_ref, *ahead_refs, rows_ref = refs
            feed_rows((n0_ref, n1_ref), gb_ref, w_ref, ht_ref, back0_ref, back1_ref, rows_ref)
            for k, ref in enumerate((ht_ref, far_ht_ref)):
                ahead = dot(ref[2 * hidden :, :], w_ref[2 * hidden :, :], ((0,), (0,)))
                ahead_refs[2 * k][...] = ahead[:block]
                ahead_refs[2 * k + 1][...] = ahead[block:].astype(BF16)

        def weight_grad(refs, start, stop, right):
            hts, n_near, n_far, gbs = refs[0:2], refs[2:4], refs[4:6], refs[6:8]
            total = jnp.zeros((stop - start, width), F32)
            for side in range(2):
                left = hts[side]
                if right == 1:
                    total = total + dot(left[start:stop, :], gbs[side][...], ((1,), (0,)))
                    continue
                for i in range(2):
                    rows = (n_near, n_far)[side][i][...]
                    cut = slice(i * block, (i + 1) * block)
                    total = total + dot(left[start:stop, cut], rows, ((1,), (0,)))
            return total

        def gate_up_grad_kernel(meta_ref, *refs):
            keep_ref, send_ref = refs[8:]
            for k in range(2):
                cut = slice(k * hidden, (k + 1) * hidden)
                total = weight_grad(refs, k * hidden, (k + 1) * hidden, 0)
                keep_ref[cut, :] = total[:, :half_width].astype(BF16)
                send_ref[cut, :] = total[:, half_width:].astype(BF16)

        def down_grad_kernel(meta_ref, *refs):
            keep_ref, send_ref = refs[8:]
            total = weight_grad(refs, 2 * hidden, 3 * hidden, 1)

            def chunk(s, near):
                start = near * half_width + s * LANES
                return total[:, start : start + LANES]

            for near in range(n_c):
                keep_ref[0, near] = chunk(0, near)
                keep_ref[1, near] = chunk(2, near)

            @pl.when(lax.rem(meta_ref[AT_ME + 1], 2) == 0)
            def _():
                for near in range(n_c):
                    send_ref[0, near] = chunk(3, near).astype(BF16)
                    send_ref[1, near] = chunk(1, near).astype(BF16)

            @pl.when(lax.rem(meta_ref[AT_ME + 1], 2) == 1)
            def _():
                for near in range(n_c):
                    send_ref[0, near] = chunk(1, near).astype(BF16)
                    send_ref[1, near] = chunk(3, near).astype(BF16)

        def middle_kernel(
            meta_ref,
            cot_ref,
            back_ref,
            beside_ref,
            across_ref,
            mid_ref,
            gain_ref,
            o0_ref,
            o1_ref,
            mixed_ref,
            dmid_ref,
            gg_ref,
            go_ref,
            keep_ref,
            send_ref,
        ):
            back = back_ref[...] + beside_ref[...].astype(F32) + across_ref[...].astype(F32)
            mid = mid_ref[...]
            inverse = inverse_rms(mid)
            gain = to_arrival(meta_ref, lambda lanes: gain_ref[1:2, lanes])
            normal = mid * inverse
            gains = jnp.sum(back * normal, axis=0, keepdims=True)
            for j in range(n_piece):
                gg_ref[:, column(meta_ref, j)] = jnp.broadcast_to(
                    gains[:, j * LANES : (j + 1) * LANES], (8, LANES)
                )
            scaled = back * gain
            delta = inverse * (
                scaled - normal * jnp.mean(scaled * normal, axis=-1, keepdims=True)
            )
            dmid_ref[...] = delta
            grad = (cot_ref[...] + delta).astype(BF16)
            for lo, ref in enumerate((o0_ref, o1_ref)):
                for hi in range(2):
                    tp = member(meta_ref, lo, hi)
                    cut = slice(hi * o_rows, (hi + 1) * o_rows)
                    go_ref[tp] = dot(ref[cut, :], grad, ((1,), (1,))).astype(BF16)
                    weight = dot(mixed_ref[tp], grad, ((1,), (0,))).astype(BF16)
                    (keep_ref, send_ref)[lo][cut, :] = weight

        def attention_back_kernel(
            part,
            meta_ref,
            first_ref,
            a_ref,
            bq_ref,
            w0_ref,
            w1_ref,
            w2_ref,
            w3_ref,
            w4_ref,
            lse_ref,
            q_ref,
            go_ref,
            *refs,
        ):
            win_ref, bias_ref, wide_ref, p_ref, dp_ref, own_ref, kv_ref = refs[-7:]
            if part == 0:
                ga_ref, gbq_ref, gwb_ref, gwa_ref = refs[:4]
            else:
                ga_ref, gbq_ref, second_ref, beside_ref, third_ref, own_out_ref = refs[3:9]
                gwb_ref, gwa_ref = refs[-9:-7]
            set_mask(first_ref, bias_ref)
            widen(meta_ref, (w0_ref, w1_ref, w2_ref, w3_ref, w4_ref), win_ref, wide_ref)
            spread_factors(a_ref, win_ref, own_ref, kv_ref)
            if part == 0:
                gbq_ref[...] = jnp.zeros_like(gbq_ref)
                gwb_ref[...] = jnp.zeros_like(gwb_ref)
            else:
                gbq_ref[...] = refs[0][...]
                gwb_ref[...] = refs[1][...]
                gwa_ref[...] = refs[2][...]
            spans = [pl.ds(j * block, block) for j in range(windows)]
            first_pair, stop_pair = ((0, first_part), (first_part, pairs))[part]

            def one_pair(pair, carry):
                own = own_ref[pair]
                factors = kv_factors(kv_ref, pair)
                grad_a = []
                grad_kv = [[] for _ in spans]
                for g in range(2):
                    tp, head, rows = head_place(pair, g)
                    query = q_ref[tp, head]
                    grad_out = go_ref[tp, rows, :]
                    lse = lse_ref[pair, g : g + 1, :]
                    inner = jnp.zeros((1, block), F32)
                    keys = []
                    for j, span in enumerate(spans):
                        key_rows, value_rows = kv_rows_of(factors, wide_ref, g, j)
                        keys.append(key_rows)
                        scores = dot(key_rows, query, ((0,), (0,))) + bias_ref[span, :]
                        probs = jnp.exp(scores - lse)
                        grad_probs = dot(value_rows, grad_out, ((0,), (0,)))
                        p_ref[g % 2, span, :] = probs
                        dp_ref[g % 2, span, :] = grad_probs
                        inner = inner + jnp.sum(probs * grad_probs, axis=0, keepdims=True)
                    grad_query = jnp.zeros((HEAD_DIM, block), F32)
                    for j, span in enumerate(spans):
                        probs = p_ref[g % 2, span, :]
                        grad_scores = (probs * (dp_ref[g % 2, span, :] - inner)).astype(BF16)
                        grad_query = grad_query + dot(keys[j], grad_scores, ((1,), (0,)))
                        grad_keys = dot(query, grad_scores, ((1,), (1,))) * (1.0 / RANK_KV)
                        grad_values = dot(grad_out, probs.astype(BF16), ((1,), (1,)))
                        grad_values = grad_values * (1.0 / RANK_KV)
                        for r in range(KV):
                            grad = grad_keys if r < RANK_KV else grad_values
                            grad_kv[j].append(
                                jnp.sum(grad * wide_ref[j, r], axis=0, keepdims=True)
                            )
                            gwb_ref[j, r] += factors[j][g * KV + r : g * KV + r + 1] * grad
                    grad_query = grad_query * (HEAD_DIM**-0.5 / RANK_Q)
                    for r in range(RANK_Q):
                        grad_a.append(jnp.sum(grad_query * bq_ref[r], axis=0, keepdims=True))
                        gbq_ref[r] += own[g * RANKS + r : g * RANKS + r + 1] * grad_query
                    grad_a.append(jnp.zeros((KV, block), F32))
                grad_a.append(jnp.zeros((pair_rows - 2 * RANKS, block), F32))
                ga_ref[pair - first_pair] = jnp.concatenate(grad_a, axis=0)
                start = pl.multiple_of(pair * (2 * KV), 2 * KV)
                for j in range(windows):
                    gwa_ref[j, pl.ds(start, 2 * KV), :] = jnp.concatenate(grad_kv[j], axis=0)
                return carry

            lax.fori_loop(first_pair, stop_pair, one_pair, 0)
            if part == 0:
                return

            def put(ref, start, j):
                for r in range(KV):
                    row = start + r * HEAD_DIM
                    ref[row : row + HEAD_DIM, :] = gwb_ref[j, r].astype(ref.dtype)
                ref[start + kv_b : start + kv_rows, :] = gwa_ref[j].astype(ref.dtype)

            put(own_out_ref, 0, 3)
            put(beside_ref, 0, 2)
            put(third_ref, 0, 0)
            put(second_ref, 0, 1)

        def last_kernel(
            meta_ref,
            x_ref,
            own_ref,
            second_ref,
            beside_ref,
            third_ref,
            gbq_ref,
            ga0_ref,
            ga1_ref,
            cos_ref,
            sin_ref,
            wb_ref,
            wa_ref,
            normed_ref,
            gain_ref,
            dmid_ref,
            gg_ref,
            delta_ref,
            keep0_ref,
            keep1_ref,
            send0_ref,
            send1_ref,
            b_buf,
            a_buf,
            d_buf,
            g_buf,
        ):
            total = own_ref[...]
            for ref in (second_ref, beside_ref, third_ref):
                total = total + ref[...].astype(F32)
            cosine, sine = cos_ref[...], -sin_ref[...]
            rows = [rotated(gbq_ref[r], cosine, sine) for r in range(RANK_Q)]
            for r in range(KV):
                part = total[r * HEAD_DIM : (r + 1) * HEAD_DIM]
                rows.append(rotated(part, cosine, sine) if r < RANK_KV else part)
            grad_b = jnp.transpose(jnp.concatenate(rows, axis=0)).astype(BF16)
            normed = normed_ref[...]
            back = dot(grad_b, wb_ref[...], ((1,), (1,)))
            for tp in range(n_tp):
                parts = []
                for g in range(group):
                    start = kv_b + (tp * group + g) * KV
                    parts.append(jnp.zeros((RANK_Q, block), F32))
                    parts.append(total[start : start + KV])
                parts.append(jnp.zeros((a_pad - a_cols, block), F32))
                half = group // 2
                at = [tp * half + k for k in range(half)]
                own_a = [
                    ga0_ref[k, : 2 * RANKS, :]
                    if k < first_part
                    else ga1_ref[k - first_part, : 2 * RANKS, :]
                    for k in at
                ]
                own_a.append(jnp.zeros((a_pad - a_cols, block), F32))
                own_a = jnp.concatenate(own_a, axis=0)
                grad_a = (own_a + jnp.concatenate(parts, axis=0)).astype(BF16)
                back = back + dot(grad_a, wa_ref[tp], ((0,), (0,)))
                a_buf[tp] = dot(grad_a, normed, ((1,), (0,)))
            b_buf[...] = dot(normed, grad_b, ((0,), (0,)))
            x = x_ref[...]
            inverse = inverse_rms(x)
            normal = x * inverse
            gains = jnp.sum(back * normal, axis=0, keepdims=True)
            g_buf[...] = jnp.broadcast_to(gains, (8, width))
            scaled = back * gain_ref[0:1]
            delta = inverse * (
                scaled - normal * jnp.mean(scaled * normal, axis=-1, keepdims=True)
            )
            d_buf[...] = delta
            for j in range(n_piece):
                lanes = column(meta_ref, j)
                cut = slice(j * LANES, (j + 1) * LANES)
                delta_ref[:, lanes] = (d_buf[:, lanes] + dmid_ref[:, cut]).astype(BF16)
            row_index = lax.broadcasted_iota(jnp.int32, (16, LANES), 0)
            for lo, hi in ((0, 0), (0, 1), (1, 0), (1, 1)):
                outs = ((keep0_ref, keep1_ref), (send0_ref, send1_ref))[lo]
                tp = member(meta_ref, lo, hi)
                for near in range(n_c):
                    out = outs[near]
                    for s in range(n_f):
                        j = near * n_f + s
                        lanes = column(meta_ref, j)
                        row = pl.multiple_of((meta_ref[j] * n_tp + tp) * b_rows, b_rows)
                        for k in range(b_parts):
                            out[hi, s, k * b_rows : (k + 1) * b_rows, :] = b_buf[
                                pl.ds(row, b_rows), k * LANES : (k + 1) * LANES
                            ].astype(BF16)
                        out[hi, s, n_b : n_b + a_pad, :] = a_buf[tp, :, lanes].astype(BF16)
                        pair = jnp.where(
                            row_index == 0, g_buf[0:1, lanes], gg_ref[0:1, lanes]
                        )
                        out[hi, s, n_b + a_pad :, :] = pair.astype(BF16)

        def add_kernel(arrival, meta_ref, x_ref, d0_ref, d1_ref, d2_ref, d3_ref, out_ref):
            step = pl.program_id(0)
            rows = pl.ds(0, block)
            for i, ref in enumerate((d0_ref, d1_ref, d2_ref, d3_ref)):

                @pl.when(step == i)
                def _(ref=ref):
                    if not arrival:
                        out_ref[0] = x_ref[0] + ref[rows, :].astype(F32)
                        return
                    for j in range(n_piece):
                        lanes = column(meta_ref, j)
                        out_ref[0, :, lanes] = x_ref[0, :, lanes] + ref[
                            rows, j * LANES : (j + 1) * LANES
                        ].astype(F32)

        def split_kernel(meta_ref, keep_ref, got_ref, own_ref, send_ref):
            def total(s):
                lanes = slice(s * LANES, (s + 1) * LANES)
                return keep_ref[:, lanes].astype(F32) + got_ref[: keep_ref.shape[0], lanes].astype(
                    F32
                )

            own_ref[0] = total(0)
            own_ref[1] = total(2)

            @pl.when(lax.rem(meta_ref[AT_ME + 1], 2) == 0)
            def _():
                send_ref[0] = total(3).astype(BF16)
                send_ref[1] = total(1).astype(BF16)

            @pl.when(lax.rem(meta_ref[AT_ME + 1], 2) == 1)
            def _():
                send_ref[0] = total(1).astype(BF16)
                send_ref[1] = total(3).astype(BF16)

        def unpack_kernel(
            meta_ref, p_ref, got_ref, b_ref, a_ref, g0_ref, g1_ref, o_ref
        ):
            total = p_ref[...].astype(F32) + got_ref[...].astype(F32)
            for k in range(b_parts):
                b_ref[0, :, k * LANES : (k + 1) * LANES] = total[k * b_rows : (k + 1) * b_rows]
            a_ref[0] = total[n_b : n_b + a_cols]
            rows = total[n_b + a_pad : n_b + a_pad + 8]
            rows = pltpu.roll(rows, (n_tp - meta_ref[AT_ME]) * gain_part, 1)
            g0_ref[...] = rows[0:1, :gain_part]
            g1_ref[...] = rows[1:2, :gain_part]
            o_ref[0] = total[pack_rows:]

        core = lambda v, label="row": swap(v, "tp", n_tp, 1, "core_" + label)
        chip = lambda v, label="row": swap(v, "tp", n_tp, 2, "y_" + label)
        ctx = lambda v, label="row": swap(v, "ctx", n_c, 1, "x_" + label)
        ahead = lambda v, s, label="row": shift(v, "fsdp", n_f, s, "z_" + label)

        (pack,) = call(
            pack_kernel,
            "pack",
            [((pack_rows, LANES), BF16)],
            (w_factor_b, w_factor_a.transpose(0, 2, 1), attn_gains, ffn_gains),
        )
        o_rows_all = w_out[0].astype(BF16)
        pack = jnp.stack([pack] + [ahead(pack, s, "pack") for s in range(1, n_f)])
        o_parts = [o_rows_all] + [ahead(o_rows_all, s, "wo") for s in range(1, n_f)]
        o_parts = jnp.concatenate(o_parts, axis=0)
        gu_in = after(w_gate_up.transpose(0, 1, 3, 2), pack)
        own_gu, own_dn = call(
            big_kernel,
            "big_pack",
            [((early, LANES), BF16), ((3 * hidden - early, LANES), BF16)],
            (gu_in, w_down),
        )
        pack = jnp.stack([pack, ctx(pack, "pack")])
        far_gu = swap(own_gu, "fsdp", n_f, 2, "z_gate_up")
        dn_pair = jnp.stack([own_dn, ctx(own_dn, "down")])
        gu_across = ctx(own_gu, "gate_up")
        o_across = ctx(o_parts, "wo")
        o_parts = jnp.concatenate(
            [
                half[s * o_rows : (s + 1) * o_rows]
                for half in (o_parts, o_across)
                for s in range(n_f)
            ],
            axis=1,
        )
        own_x, own_cot, near_cot, far_cot = call(
            rows_kernel,
            "rows",
            [((block, width), F32)] * 2 + [((2 * block, width), BF16)] * 2,
            (resid_in, cotangent),
            [REMOTE] * 2,
            [pltpu.VMEM((4, block, width), F32), pltpu.SemaphoreType.DMA((5,))],
            scalars=after(meta, o_across),
        )
        pack_across, far_gu, dn_pair, o_parts, near_cot, far_cot = lax.optimization_barrier(
            (chip(pack, "pack"), far_gu, dn_pair, o_parts, near_cot, far_cot)
        )
        pair_gu = swap(jnp.stack([own_gu, far_gu]), "fsdp", n_f, 1, "z_gate_up_pair")
        pack = jnp.stack([pack, pack_across], axis=1)
        other_pack = core(pack, "pack")

        def add_rows(whole, parts, arrival):
            rows = pl.BlockSpec(
                (1, block, width), lambda i, m: (0, m[AT_TP + i], 0)
            )
            (out,) = call(
                lambda *refs: add_kernel(arrival, *refs),
                "add_rows",
                [(whole.shape, F32)],
                (whole, *parts),
                [rows] + [WHOLE] * 4,
                (),
                (n_tp,),
                [rows],
            )
            return out

        def split(keep, got):
            size = keep.shape[0]
            return call(
                split_kernel,
                "split",
                [((2, size, LANES), F32), ((2, size, LANES), BF16)],
                (keep, got),
            )

        def first_step(send, label):
            return swap(send, "fsdp", n_f, 1, "z1_" + label)

        def second_step(own, got, label):
            total = own + got.astype(F32)
            return total[0], swap(total[1].astype(BF16), "fsdp", n_f, 2, "z2_" + label)

        seg_here = lax.dynamic_slice_in_dim(segment_ids[0], place * block, block, 0)
        first = jnp.sum((segment_ids[0][:, None] < seg_here[None, :]).astype(jnp.int32), axis=0)
        token = place * block + jnp.arange(block, dtype=jnp.int32)
        position = (token - first).astype(F32)
        first = (first - place * block + extra * block).reshape(1, block)
        frequency = 10000.0 ** (-2.0 * jnp.arange(HEAD_DIM // 2, dtype=F32) / HEAD_DIM)
        angles = frequency[:, None] * position[None, :]
        cosine, sine = jnp.cos(angles), jnp.sin(angles)

        weight_b, weight_a, gains, normed, a_rows, b_query, payload = call(
            factor_kernel,
            "factors",
            [
                ((width, b_cols), BF16),
                ((n_tp, a_pad, width), BF16),
                ((16, width), F32),
                ((block, width), BF16),
                ((n_tp, a_pad, block), F32),
                ((RANK_Q, HEAD_DIM, block), F32),
                ((kv_rows, block), BF16),
            ],
            (own_x, pack, other_pack, cosine, sine),
        )
        def places(value, step, chosen, label):
            pairs = [(i, i + step) for i in chosen if 0 <= i + step < n_place]
            with jax.named_scope(label):
                return lax.ppermute(value, ("ctx", "tp"), pairs)

        every, odd, even = range(n_place), range(1, n_place, 2), range(0, n_place, 2)
        second = places(payload, 2, every, "x_kv_second")
        third = places(payload, 3, odd, "x_kv_third")
        beside_kv = core(payload, "kv")
        o_own = jnp.concatenate([o_parts, chip(o_parts, "wo")], axis=0)
        second, pair_gu, gu_across = lax.optimization_barrier((second, pair_gu, gu_across))
        gu_rest = ctx(jnp.concatenate([far_gu[None], pair_gu], axis=0), "gate_up_rest")
        dn_parts = [dn_pair, ahead(dn_pair, 1, "down1")]
        beside_second = core(second, "kv_second")
        tied = lax.optimization_barrier((third, second, beside_second, beside_kv, o_own))
        wins = (*tied[:4], payload)
        o_own = tied[4]
        o_other = core(o_own, "wo")
        window = windows * block
        factor_scratch = [
            pltpu.VMEM((pairs, pair_rows, block), F32),
            pltpu.VMEM((windows, heads * KV, block), F32),
        ]
        lse, query, mixed = call(
            attention_kernel,
            "attention",
            [
                ((pairs, 2, block), F32),
                ((n_tp, group, HEAD_DIM, block), BF16),
                ((n_tp, feats, block), BF16),
            ],
            (first, a_rows, b_query, *wins),
            None,
            [
                pltpu.VMEM((windows, kv_rows, block), BF16),
                pltpu.VMEM((window, block), F32),
                pltpu.VMEM((windows, KV, HEAD_DIM, block), F32),
                pltpu.VMEM((group, window, block), F32),
                *factor_scratch,
            ],
        )
        dn_parts[1] = after(dn_parts[1], mixed)
        for s in range(2, n_f):
            dn_parts.append(ahead(dn_parts[-1], 1, "down" + str(s)))
        mid, attn_out, normed_ffn = call(
            project_kernel,
            "project",
            [((block, width), F32), ((block, width), F32), ((block, width), BF16)],
            (own_x, mixed, o_own, o_other, gains),
        )

        near_rows = (normed_ffn, core(normed_ffn, "nf"))
        far_own = chip(normed_ffn, "nf")

        far_own, gu_rest = lax.optimization_barrier((far_own, gu_rest))
        far_own, dn_parts[-1], gu_rest = lax.optimization_barrier(
            (far_own, dn_parts[-1], gu_rest)
        )
        pieces = (own_gu, far_gu, pair_gu, gu_across, gu_rest, *dn_parts)
        far_rows = (far_own, core(far_own, "nf_far"))
        whole_ht = ((3 * hidden, 2 * block), BF16)
        two_sums = [((block, width), F32), ((block, width), BF16)]
        far_ht, far_back, far_back1, weights = call(
            far_kernel,
            "feed_far",
            [whole_ht, *two_sums, ((3 * hidden, width), BF16)],
            (*far_rows, far_cot, *pieces),
            [WHOLE] * 3 + [REMOTE] * len(pieces),
            [pltpu.VMEM((2, block, width), BF16), pltpu.SemaphoreType.DMA((2 * n_piece,))],
            room=12,
        )
        across = (far_back + core(far_back1, "dn_far").astype(F32)).astype(BF16)
        near_ht, near_back, near_back1, near_out, near_out1, far_out, far_out1 = call(
            near_kernel,
            "feed_near",
            [whole_ht, *two_sums * 3],
            (after(near_rows[0], across), near_rows[1], near_cot, weights, far_ht),
            None,
            [pltpu.VMEM((2, block, width), BF16)],
            room=12,
        )
        across = chip(across, "dn")
        beside = core(near_back1, "dn_near")

        grad_args = (near_ht, far_ht, *near_rows, *far_rows, near_cot, far_cot)
        own_d, send_d = call(
            down_grad_kernel,
            "down_grad",
            [((2, n_c, hidden, LANES), F32), ((2, n_c, hidden, LANES), BF16)],
            grad_args,
            room=12,
        )
        got_d = first_step(send_d, "d")
        keep_a, send_a = call(
            gate_up_grad_kernel,
            "gate_up_grad",
            [((2 * hidden, half_width), BF16)] * 2,
            (after(grad_args[0], send_d), *grad_args[1:]),
            room=12,
        )
        got_a = ctx(send_a, "grads_a")
        across = after(across, send_a)

        delta_mid, gain_grad, grad_mixed, keep_o, send_o = call(
            middle_kernel,
            "middle",
            [
                ((block, width), F32),
                ((8, width), F32),
                ((n_tp, feats, block), BF16),
                ((2 * o_rows, width), BF16),
                ((2 * o_rows, width), BF16),
            ],
            (own_cot, near_back, beside, across, mid, gains, o_own, o_other, mixed),
        )
        near_sum = attn_out + near_out + core(after(near_out1, across), "out_near").astype(F32)
        far_sum = far_out + core(after(far_out1, across), "out_far").astype(F32)
        out_send = jnp.stack([far_sum, near_sum]).astype(BF16)
        grad_mixed = after(grad_mixed, out_send)
        rows_got = core(send_o, "go")
        out_got = chip(out_send, "out")
        back_args = (first, a_rows, b_query, *wins, lse, query, grad_mixed)
        sums = [
            ((RANK_Q, HEAD_DIM, block), F32),
            ((windows, KV, HEAD_DIM, block), F32),
            ((windows, heads * KV, block), F32),
        ]
        back_scratch = [
            pltpu.VMEM((windows, kv_rows, block), BF16),
            pltpu.VMEM((window, block), F32),
            pltpu.VMEM((windows, KV, HEAD_DIM, block), F32),
            pltpu.VMEM((2, window, block), F32),
            pltpu.VMEM((2, window, block), F32),
            *factor_scratch,
        ]
        grad_a0, *sums_out = call(
            lambda *refs: attention_back_kernel(0, *refs),
            "attention_back_a",
            [((first_part, pair_rows, block), F32)] + sums,
            back_args,
            None,
            back_scratch,
        )
        sums_out[0], own_d, got_d, _ = lax.optimization_barrier(
            (sums_out[0], own_d, got_d, grad_a0)
        )
        own_d, got_d = second_step(own_d, got_d, "d")
        grad_a1, grad_bq, *sends = call(
            lambda *refs: attention_back_kernel(1, *refs),
            "attention_back_b",
            [
                ((pairs - first_part, pair_rows, block), F32),
                sums[0],
                ((kv_rows, block), BF16),
                ((kv_rows, block), BF16),
                ((kv_rows, block), BF16),
                ((kv_rows, block), F32),
            ],
            (*back_args, *sums_out),
            None,
            [pltpu.VMEM(shape, kind) for shape, kind in sums[1:]] + back_scratch,
        )
        *sends[:3], out_got, rows_got = lax.optimization_barrier((*sends[:3], out_got, rows_got))
        second_got = places(sends[0], -2, every, "x_kv_back_second")
        beside_got = places(sends[1], -1, every, "x_kv_back_beside")
        third_got = places(sends[2], -3, every, "x_kv_back_third")
        own_a, send_a = split(after(keep_a, sends[0]), got_a)
        got_a = first_step(send_a, "a")
        rows_o = keep_o.astype(F32) + after(rows_got, send_a).astype(F32)
        rows_keep, rows_send = rows_o[:o_rows], rows_o[o_rows:].astype(BF16)
        rows_got = chip(rows_send, "go")
        *got, got_d = lax.optimization_barrier((second_got, beside_got, third_got, got_d))
        out_rows = (out_send[::-1].astype(F32) + out_got.astype(F32)).astype(BF16)

        delta, keep0, keep1, send0, send1 = call(
            last_kernel,
            "last",
            [
                ((block, width), BF16),
                *[((2, n_f, pack_rows, LANES), BF16)] * 4,
            ],
            (
                own_x,
                sends[3],
                *got,
                grad_bq,
                grad_a0,
                grad_a1,
                cosine,
                sine,
                weight_b,
                weight_a,
                normed,
                gains,
                delta_mid,
                gain_grad,
            ),
            [WHOLE] * 16,
            [
                pltpu.VMEM((width, b_cols), F32),
                pltpu.VMEM((n_tp, a_pad, width), F32),
                pltpu.VMEM((block, width), F32),
                pltpu.VMEM((8, width), F32),
            ],
        )

        part_send = (keep1.astype(F32) + core(send1, "gp").astype(F32)).astype(BF16)
        total_d = own_d + got_d.astype(F32)
        part_send, got_a = lax.optimization_barrier((part_send, got_a))
        part_got = ctx(part_send, "gp")
        own_a, got_a = second_step(own_a, got_a, "a")
        part = keep0.astype(F32) + core(after(send0, part_send), "gp_near").astype(F32)
        rows_got, part = lax.optimization_barrier((rows_got, part))
        rows_o = rows_keep + rows_got.astype(F32)
        rows_keep, rows_send = rows_o[:, :half_width], rows_o[:, half_width:].astype(BF16)
        across_delta = chip(delta, "delta")
        rows_go = ctx(rows_send, "go")
        out_rows = after(out_rows, part_send)
        out_beside = core(out_rows, "out_rows")
        block_out = add_rows(
            resid_in, (out_rows[0], out_rows[1], out_beside[0], out_beside[1]), True
        )
        part_got, across_delta = lax.optimization_barrier((part_got, across_delta, block_out))[:2]
        part = part + part_got.astype(F32)
        part_send = part[1].astype(BF16)
        part_got = chip(part_send, "gp")
        across_delta = after(across_delta, part_send)
        beside_delta = core(after(delta, part_send), "delta")
        got_last = ctx(after(total_d[1], part_send).astype(BF16), "d")
        part_got, rows_go, got_a = lax.optimization_barrier((part_got, rows_go, got_a))
        part = part[0] + part_got.astype(F32)
        rows_o = rows_keep + rows_go.astype(F32)
        part = [
            jnp.concatenate([part[s], rows_o[:, s * LANES : (s + 1) * LANES]], axis=0)
            for s in range(n_f)
        ]
        is_even_f = f_index % 2 == 0
        part_send = [
            jnp.where(is_even_f, part[3], part[1]),
            jnp.where(is_even_f, part[1], part[3]),
        ]
        part_send = jnp.stack(part_send).astype(BF16)
        part_own, part_got = second_step(
            jnp.stack([part[0], part[2]]), first_step(part_send, "gp"), "gp"
        )
        across_delta = after(across_delta, part_send)
        resid_grad = add_rows(
            cotangent,
            (delta, across_delta, beside_delta, core(across_delta, "delta_far")),
            False,
        )
        part_got, got_last = lax.optimization_barrier((part_got, got_last, resid_grad))[:2]
        grad_down = total_d[0] + got_last.astype(F32)
        grad_gate_up = (own_a + got_a.astype(F32)).reshape(1, 2, hidden, fc_cols)
        part_b, part_a, part_g0, part_g1, grad_out = call(
            unpack_kernel,
            "unpack",
            [
                ((1, b_rows, b_cols), F32),
                ((1, a_cols, fc_cols), F32),
                ((1, gain_part), F32),
                ((1, gain_part), F32),
                ((1, o_rows, LANES), F32),
            ],
            (part_own, part_got),
        )
        return (
            block_out,
            resid_grad,
            part_a.transpose(0, 2, 1),
            part_b,
            grad_out,
            grad_gate_up.transpose(0, 1, 3, 2),
            grad_down[None],
            part_g0,
            part_g1,
        )

    return shards


def make_shards(mesh):
    fused, general = make_fused(mesh), make_general(mesh)
    fits = mesh.shape["fsdp"] == 4 and mesh.shape["ctx"] == 2 and mesh.shape["tp"] == 4

    def shards(*args):
        return (fused if fits and args[7].shape[2] == LANES else general)(*args)

    return shards


def solution(mesh):
    return jax.shard_map(
        make_shards(mesh),
        mesh=mesh,
        in_specs=(
            P("fsdp", "ctx", None),
            P("fsdp", None),
            P("fsdp", "ctx", None),
            P(None, ("fsdp", "ctx"), "tp"),
            P(None, ("fsdp", "ctx", "tp"), None),
            P(None, "tp", ("fsdp", "ctx")),
            P(None, None, ("fsdp", "ctx"), "tp"),
            P(None, "tp", ("fsdp", "ctx")),
            P(None, ("fsdp", "ctx", "tp")),
            P(None, ("fsdp", "ctx", "tp")),
        ),
        out_specs=(
            P("fsdp", "ctx", None),
            P("fsdp", "ctx", None),
            P(None, ("fsdp", "ctx"), "tp"),
            P(None, ("fsdp", "ctx", "tp"), None),
            P(None, "tp", ("fsdp", "ctx")),
            P(None, None, ("fsdp", "ctx"), "tp"),
            P(None, "tp", ("fsdp", "ctx")),
            P(None, ("fsdp", "ctx", "tp")),
            P(None, ("fsdp", "ctx", "tp")),
        ),
        check_vma=False,
    )
```
